32 devices in a mesh: ctx: 4 (over y, x), fsdp: 8 (over z, core).
Axes of the slice: x: 2, y: 2, z: 4, core: 2. Of those that a mesh axis runs over, the one named last changes fastest.
Arguments:
- tokens: bfloat16 [8, 2560, 2048], P('fsdp', 'ctx'), may hold values from -6 to 6
- cotangent: bfloat16 [8, 2560, 2048], P('fsdp', 'ctx'), may hold values from -6 to 6
- block_table: int32 [8, 40], P('fsdp'), may hold values from 0 to 39, as said below
- ln_gain: bfloat16 [2048], replicated, may hold values from 0.5 to 1.5
- ln_bias: bfloat16 [2048], replicated, may hold values from -2 to 2
- w_qkv: bfloat16 [2048, 3, 2048], P('fsdp', None, 'ctx'), may hold values from -0.125 to 0.125
- b_qkv: bfloat16 [6144], replicated, may hold values from -2 to 2
- w_dense: bfloat16 [2048, 2048], P('ctx', 'fsdp'), may hold values from -0.5 to 0.5
- b_dense: bfloat16 [2048], replicated, may hold values from -2 to 2
- w_fc1: bfloat16 [2048, 8192], P('fsdp', 'ctx'), may hold values from -0.125 to 0.125
- b_fc1: bfloat16 [8192], replicated, may hold values from -2 to 2
- w_fc2: bfloat16 [8192, 2048], P('ctx', 'fsdp'), may hold values from -0.0625 to 0.0625
- b_fc2: bfloat16 [2048], replicated, may hold values from -2 to 2
Outputs:
- output: bfloat16 [8, 2560, 2048], P('fsdp', 'ctx')
- d_tokens: bfloat16 [8, 2560, 2048], P('fsdp', 'ctx')
- d_ln_gain: float32 [2048], replicated
- d_ln_bias: float32 [2048], replicated
- d_w_qkv: float32 [2048, 3, 2048], P('fsdp', None, 'ctx')
- d_b_qkv: float32 [6144], replicated
- d_w_dense: float32 [2048, 2048], P('ctx', 'fsdp')
- d_b_dense: float32 [2048], replicated
- d_w_fc1: float32 [2048, 8192], P('fsdp', 'ctx')
- d_b_fc1: float32 [8192], replicated
- d_w_fc2: float32 [8192, 2048], P('ctx', 'fsdp')
- d_b_fc2: float32 [2048], replicated
The draws below stay inside these ranges and needn't reach their ends.
Inputs may be any that keep to these rules, and one draw needn't show every extreme that they name: `block_table`: each row lists each of the 40 blocks of its group exactly once.
All inputs are finite; a program needn't handle non-finite values.
Results may differ from the reference program's by a relative error of at most 0.015.
Values may be sent and summed in bfloat16 or wider, within the bound.
No kernel may reach another device: no remote copies, remote signals or barrier semaphores. Data moves between devices by JAX's collectives and lax.ppermute only.
A program may use at most 832 MiB of HBM per device.

```python
import math
import jax
import jax.numpy as jnp
from jax import lax

D = 2048
HEADS = 32
ROT = 32
FF = 8192
PROMPT = 2048
CLEN = 256
BLK = 64
GTOK = 2560
NB = 40
GROUPS = 8


def draw_block_table(key, part):
    group_keys = jax.random.split(key, GROUPS)

    def one_order(group_key):
        return jax.random.permutation(group_key, NB)
    return jax.vmap(one_order)(group_keys).astype(jnp.int32)


def strengthened(values, stream_key, source, target, blocks, factor):
    owner, partner = [(jnp.arange(values.shape[position]) // (values.shape[position] // blocks)).reshape([-1 if axis == position else 1 for axis in range(values.ndim)]) for position in (source, target)]
    chosen = jax.random.permutation(stream_key, blocks)[partner]
    strong = (owner == chosen) | (owner == (partner + blocks // 2) % blocks)
    return jnp.where(strong, factor * values, values)


def steps_of(stream_key, extent, cuts, low, largest):
    def one(position, shards_of):
        steps = jax.random.uniform(jax.random.fold_in(jax.random.fold_in(stream_key, 6), position), (shards_of,), jnp.float32, low / len(cuts), largest / len(cuts))
        return jnp.repeat(jnp.exp(steps), extent[position] // shards_of).reshape((-1,) + (1,) * (len(extent) - position - 1))

    level = one(*cuts[0])
    for cut in cuts[1:]:
        level = level * one(*cut)
    return level


def bell_draw(rng, shape, deviation, limit, shards=(), held_as=jnp.bfloat16):
    drawn = deviation * jax.random.normal(rng, shape, jnp.float32)
    if shards:
        drawn = drawn * steps_of(rng, shape, shards, -0.22, 0.18)
    return jnp.clip(drawn, -limit, limit).astype(held_as)


def gaussian_with(own_key, extent, width, limit, cuts, heavy, kind=jnp.bfloat16):
    values = width * jax.random.normal(own_key, extent, jnp.float32)
    if cuts:
        values = values * steps_of(own_key, extent, cuts, -0.22, 0.18)
    return jnp.clip(strengthened(values, jax.random.fold_in(own_key, 3), *heavy), -limit, limit).astype(kind)


def setup_inputs(seed: int = 0) -> dict:
    splits = jax.random.split(jax.random.key(seed), 14)
    tokens = bell_draw(splits[0], (GROUPS, GTOK, D), 1.0, 6.0, ((0, 8), (1, 4)))
    cotangent = gaussian_with(splits[1], (GROUPS, GTOK, D), 1.0, 6.0, ((0, 8), (1, 4)), (1, 2, 4, 2.0))
    block_table = draw_block_table(jax.random.fold_in(splits[13], 71), 0)
    ln_gain = jnp.clip(1.0 + 0.1 * jax.random.normal(splits[3], (D,), jnp.float32), 0.5, 1.5).astype(jnp.bfloat16)
    ln_bias = bell_draw(splits[4], (D,), 0.3, 2.0)
    w_qkv = bell_draw(splits[5], (D, 3, D), D ** -0.5, 0.125, ((0, 8), (2, 4)))
    b_qkv = bell_draw(splits[6], (3 * D,), 0.3, 2.0)
    w_dense = bell_draw(splits[7], (D, D), (D // 16) ** -0.5, 0.5, ((0, 4), (1, 8)))
    b_dense = bell_draw(splits[8], (D,), 0.3, 2.0)
    w_fc1 = bell_draw(splits[9], (D, FF), D ** -0.5, 0.125, ((0, 8), (1, 4)))
    b_fc1 = bell_draw(splits[10], (FF,), 0.3, 2.0)
    w_fc2 = bell_draw(splits[11], (FF, D), FF ** -0.5, 0.0625, ((0, 4), (1, 8)))
    b_fc2 = bell_draw(splits[12], (D,), 0.3, 2.0)
    return {"tokens": tokens, "cotangent": cotangent, "block_table": block_table, "ln_gain": ln_gain, "ln_bias": ln_bias, "w_qkv": w_qkv, "b_qkv": b_qkv, "w_dense": w_dense, "b_dense": b_dense, "w_fc1": w_fc1, "b_fc1": b_fc1, "w_fc2": w_fc2, "b_fc2": b_fc2}


@jax.custom_vjp
def low(v):
    return lax.optimization_barrier(v.astype(jnp.bfloat16)).astype(jnp.float32)

@jax.custom_vjp
def low_back(v):
    return v

def low_keep(v):
    return (low(v), None)

def low_pass(kept, grad):
    return (grad,)

def back_keep(v):
    return (v, None)

def back_low(kept, grad):
    return (low(grad),)
low.defvjp(low_keep, low_pass)
low_back.defvjp(back_keep, back_low)

def matmul(left, right):
    return jnp.dot(left, right, precision=lax.Precision.HIGHEST, preferred_element_type=jnp.float32)

def layer_norm(values, gain, shift):
    average = lax.optimization_barrier(jnp.mean(values, axis=-1, keepdims=True))
    centred = values - average
    variance = lax.optimization_barrier(jnp.mean(centred * centred, axis=-1, keepdims=True))
    return centred * lax.rsqrt(variance + 1e-05) * gain + shift

def gelu_tanh(values):
    return 0.5 * values * (1.0 + jnp.tanh(math.sqrt(2.0 / math.pi) * (values + 0.044715 * values * values * values)))

def segment_of(places):
    return jnp.where(places < PROMPT, 0, 1 + (places - PROMPT) // CLEN)

def position_of(places):
    return jnp.where(places < PROMPT, places, PROMPT + (places - PROMPT) % CLEN)

def visible(query_places, key_places):
    query_segment = segment_of(query_places)
    key_segment = segment_of(key_places)
    return (key_segment == 0) & (query_segment > 0) | (key_segment == query_segment) & (key_places <= query_places)

def frequencies():
    half_dims = ROT // 2
    return 10000.0 ** (-2.0 * jnp.arange(half_dims, dtype=jnp.float32) / ROT)

def rotate(values, angles, head_dim):
    row_count = values.shape[0]
    by_head = values.reshape(row_count, -1, head_dim)
    half_dims = angles.shape[1]
    cosine = jnp.cos(angles)[:, None, :]
    sine_part = jnp.sin(angles)[:, None, :]
    front = by_head[:, :, :half_dims]
    second = by_head[:, :, half_dims:2 * half_dims]
    turned = jnp.concatenate([front * cosine - second * sine_part, second * cosine + front * sine_part, by_head[:, :, 2 * half_dims:]], axis=-1)
    return turned.reshape(row_count, -1)

def attend(query, key, value, places):
    block_rows = min(512, GTOK)
    head_dim = D // HEADS
    scale = 1.0 / math.sqrt(head_dim)
    query_blocks = query.reshape(GTOK // block_rows, block_rows, HEADS, head_dim)
    place_blocks = places.reshape(GTOK // block_rows, block_rows)
    key_heads = key.reshape(GTOK, HEADS, head_dim)
    value_heads = value.reshape(GTOK, HEADS, head_dim)

    def one_block(operands):
        query_part, query_places = operands
        raw = jnp.einsum('qhe,khe->hqk', query_part, key_heads, precision=lax.Precision.HIGHEST) * scale
        raw = low_back(raw)
        allowed = visible(query_places[:, None], places[None, :])
        masked = jnp.where(allowed[None], raw, -1e+30)
        shifted = jnp.exp(masked - lax.optimization_barrier(jnp.max(masked, axis=-1, keepdims=True)))
        weights = low(shifted / lax.optimization_barrier(jnp.sum(shifted, axis=-1, keepdims=True)))
        return jnp.einsum('hqk,khe->qhe', weights, value_heads, precision=lax.Precision.HIGHEST)
    mixed = lax.map(jax.checkpoint(one_block), (query_blocks, place_blocks))
    return mixed.reshape(GTOK, D)

def group_forward(params, token_rows, table_row):
    ln_gain, ln_bias, w_qkv, b_qkv, w_dense, b_dense, w_fc1, b_fc1, w_fc2, b_fc2 = params
    offsets = jnp.arange(BLK, dtype=jnp.int32)
    places = (table_row[:, None] * BLK + offsets[None, :]).reshape(-1).astype(jnp.int32)
    head_dim = D // HEADS
    normed_low = low(layer_norm(token_rows, ln_gain, ln_bias))
    projected = low_back(matmul(normed_low, w_qkv.reshape(D, 3 * D)) + b_qkv)
    angles = position_of(places).astype(jnp.float32)[:, None] * frequencies()[None, :]
    query = low(rotate(projected[:, :D], angles, head_dim))
    key = low(rotate(projected[:, D:2 * D], angles, head_dim))
    value = low(projected[:, 2 * D:])
    mixed = low(low_back(attend(query, key, value, places)))
    expanded = low_back(matmul(normed_low, w_fc1) + b_fc1)
    activated = low(gelu_tanh(expanded))
    return token_rows + matmul(mixed, w_dense) + b_dense + matmul(activated, w_fc2) + b_fc2

def reference(tokens, cotangent, block_table, ln_gain, ln_bias, w_qkv, b_qkv, w_dense, b_dense, w_fc1, b_fc1, w_fc2, b_fc2):
    params = tuple((item.astype(jnp.float32) for item in (ln_gain, ln_bias, w_qkv, b_qkv, w_dense, b_dense, w_fc1, b_fc1, w_fc2, b_fc2)))

    def whole(token_values, param_tuple):

        def one_group(operands):
            return group_forward(param_tuple, operands[0], operands[1])
        return lax.map(jax.checkpoint(one_group), (token_values, block_table))
    result, pull = jax.vjp(whole, tokens.astype(jnp.float32), params)
    token_grad, param_grads = pull(cotangent.astype(jnp.float32))
    return (result.astype(jnp.bfloat16), token_grad.astype(jnp.bfloat16), param_grads[0], param_grads[1], param_grads[2], param_grads[3], param_grads[4], param_grads[5], param_grads[6], param_grads[7], param_grads[8], param_grads[9])
```

```python
import functools
import math

import jax
import jax.numpy as jnp
from jax import lax
from jax.experimental import pallas as pl
from jax.experimental.pallas import tpu as pltpu
from jax.sharding import PartitionSpec as P

HEADS = 32
ROT = 32
PROMPT = 2048
CLEN = 256
BLK = 64
CHUNK = 256
LANES = 128
NT = (((1,), (1,)), ((), ()))
NN = (((1,), (0,)), ((), ()))
TN = (((0,), (0,)), ((), ()))
LOW = jnp.bfloat16
WIDE = jnp.float32


def dot(left, right, dims):
    return lax.dot_general(left, right, dims, preferred_element_type=WIDE)


def attention_kernel(where_ref, *refs, chunk, chunks, full_chunks, blk, pairs, scale):
    per = chunk // blk
    q_in, k_in, v_in, g_in = (refs[n * per : (n + 1) * per] for n in range(4))
    cos_ref, up_ref, down_ref, att_hbm, grad_hbm = refs[4 * per : 4 * per + 5]
    (
        keys,
        values,
        keys_t,
        values_t,
        probs,
        key_sum,
        value_sum,
        att_stage,
        query_stage,
        key_stage,
        value_stage,
        row_sem,
        col_sem,
    ) = refs[4 * per + 5 :]
    pair, i = pl.program_id(0), pl.program_id(1)
    step = pair * chunks + i
    slot = lax.rem(step, 2)
    last = chunks - 1
    half = LANES // 2
    first = lax.broadcasted_iota(jnp.int32, (1, LANES), 1) < half
    width = pairs * LANES

    def columns(part):
        return pl.ds(pl.multiple_of(part * width + pair * LANES, LANES), LANES)

    def row_copies(which, at):
        stage, target = ((att_stage, att_hbm), (query_stage, grad_hbm))[which]
        return [
            pltpu.make_async_copy(
                stage.at[at, pl.ds(r * blk, blk)],
                target.at[where_ref[i * per + r], :, columns(0)],
                row_sem.at[at, which, r],
            )
            for r in range(per)
        ]

    def col_copies(n):
        block = where_ref[n]
        rows = pl.ds(pl.multiple_of(n * blk, blk), blk)
        return (
            pltpu.make_async_copy(
                key_stage.at[rows], grad_hbm.at[block, :, columns(1)], col_sem.at[0, n]
            ),
            pltpu.make_async_copy(
                value_stage.at[rows], grad_hbm.at[block, :, columns(2)], col_sem.at[1, n]
            ),
        )

    def wait_cols():
        @pl.loop(0, chunks * per)
        def _(n):
            for copy in col_copies(n):
                copy.wait()

    def load(parts):
        return jnp.concatenate([part[0] for part in parts], axis=0)

    def tables(n):
        rows = pl.ds(pl.multiple_of(n * chunk, chunk), chunk)
        return cos_ref[rows], up_ref[rows], down_ref[rows]

    quarter = ROT // 2

    def turn(x, tab):
        return (
            x * tab[0]
            + pltpu.roll(x, quarter, 1) * tab[1]
            + pltpu.roll(x, LANES - quarter, 1) * tab[2]
        )

    def turn_back(x, tab):
        return (
            x * tab[0]
            - pltpu.roll(x, quarter, 1) * tab[1]
            - pltpu.roll(x, LANES - quarter, 1) * tab[2]
        )

    @pl.when(step >= 2)
    def _():
        for which in range(2):
            for copy in row_copies(which, slot):
                copy.wait()

    tab = tables(i)
    query = (turn(load(q_in).astype(WIDE), tab) * scale).astype(LOW)
    key_new = turn(load(k_in).astype(WIDE), tab)
    value_new = load(v_in)
    grad = load(g_in)
    keys[i] = key_new.astype(LOW)
    values[i] = value_new
    keys_t[i] = key_new.T.astype(LOW)
    values_t[i] = value_new.astype(WIDE).T.astype(LOW)
    key_sum[i] = jnp.zeros((chunk, LANES), WIDE)
    value_sum[i] = jnp.zeros((chunk, LANES), WIDE)
    nothing = jnp.zeros_like(query)
    query_of = (jnp.where(first, query, nothing), jnp.where(first, nothing, query))
    grad_of = (jnp.where(first, grad, nothing), jnp.where(first, nothing, grad))
    before = jnp.minimum(i, full_chunks)
    count = before + 1
    key_row = lax.broadcasted_iota(jnp.int32, (chunk, chunk), 0)
    query_col = lax.broadcasted_iota(jnp.int32, (chunk, chunk), 1)

    def fold(values_in, how):
        return how(values_in.reshape(chunk // 8, 8, chunk), axis=0)

    def chunk_of(t):
        return jnp.where(t < before, t, i)

    def score(t, carry):
        j = chunk_of(t)
        key = keys[j]
        out = []
        for h in range(2):
            raw = dot(key, query_of[h], NT)
            raw = jnp.where(key_row <= query_col + (i - j) * chunk, raw, -1e30)
            probs[h, t] = raw
            out.append(jnp.maximum(carry[h], fold(raw, jnp.max)))
        return tuple(out)

    low_start = jnp.full((8, chunk), -1e30, WIDE)
    top = lax.fori_loop(0, count, score, (low_start, low_start))
    top = [jnp.max(x, axis=0, keepdims=True) for x in top]

    def mix(t, carry):
        j = chunk_of(t)
        out = []
        for h in range(2):
            weight = jnp.exp(probs[h, t] - top[h])
            probs[h, t] = weight
            out.append(carry[2 * h] + fold(weight, jnp.sum))
            out.append(
                carry[2 * h + 1]
                + dot(values_t[j, h * half : (h + 1) * half, :], weight.astype(LOW), NN)
            )
        return tuple(out)

    zero_row = jnp.zeros((8, chunk), WIDE)
    zero_mix = jnp.zeros((half, chunk), WIDE)
    mixed = lax.fori_loop(0, count, mix, (zero_row, zero_mix, zero_row, zero_mix))
    inverse = [1.0 / jnp.sum(mixed[2 * h], axis=0, keepdims=True) for h in range(2)]
    attended = jnp.concatenate([mixed[2 * h + 1] * inverse[h] for h in range(2)], axis=0)
    shared = grad.astype(WIDE).T * attended
    inner = [jnp.sum(shared[h * half : (h + 1) * half], axis=0, keepdims=True) for h in range(2)]
    att_stage[slot] = attended.T.astype(LOW)
    for copy in row_copies(0, slot):
        copy.start()

    def back(t, carry):
        j = chunk_of(t)
        value = values[j]
        weights, grads, out = [], [], []
        for h in range(2):
            weight = probs[h, t] * inverse[h]
            weight_grad = dot(value, grad_of[h], NT)
            score_grad = (weight * (weight_grad - inner[h])).astype(LOW)
            out.append(carry[h] + dot(keys_t[j, h * half : (h + 1) * half, :], score_grad, NN))
            weights.append(weight.astype(LOW))
            grads.append(score_grad)
        value_sum[j] += dot(weights[0], grad_of[0], NN) + dot(weights[1], grad_of[1], NN)
        key_sum[j] += dot(grads[0], query_of[0], NN) + dot(grads[1], query_of[1], NN)
        return tuple(out)

    query_grad = lax.fori_loop(0, count, back, (zero_mix, zero_mix))
    query_stage[slot] = turn_back(jnp.concatenate(query_grad, axis=0).T * scale, tab).astype(LOW)
    for copy in row_copies(1, slot):
        copy.start()

    @pl.when(i == last)
    def _():
        @pl.when(pair > 0)
        def _():
            wait_cols()

        @pl.loop(0, chunks)
        def _(n):
            rows = pl.ds(pl.multiple_of(n * chunk, chunk), chunk)
            key_stage[rows] = turn_back(key_sum[n], tables(n)).astype(LOW)
            value_stage[rows] = value_sum[n].astype(LOW)

        @pl.loop(0, chunks * per)
        def _(n):
            for copy in col_copies(n):
                copy.start()

    @pl.when(step == pairs * chunks - 1)
    def _():
        for at in range(2):
            for which in range(2):
                for copy in row_copies(which, at):
                    copy.wait()
        wait_cols()


def attention(qkv, grad, where, tabs, head_dim):
    rows, width = grad.shape
    chunk, blk = CHUNK, BLK
    per, chunks, pairs, blocks = chunk // blk, rows // chunk, width // LANES, rows // blk
    qkv_blocks = qkv.reshape(blocks, blk, 3 * width)
    grad_blocks = grad.reshape(blocks, blk, width)

    def spec(part, r):
        return pl.BlockSpec(
            (1, blk, LANES), lambda p, i, at: (at[i * per + r], 0, part * pairs + p)
        )

    in_specs = [spec(part, r) for part in range(3) for r in range(per)]
    in_specs += [spec(0, r) for r in range(per)]
    in_specs += [pl.BlockSpec((rows, LANES), lambda p, i, at: (0, 0))] * 3
    operands = [qkv_blocks] * (3 * per) + [grad_blocks] * per + list(tabs)
    kernel = functools.partial(
        attention_kernel,
        chunk=chunk,
        chunks=chunks,
        full_chunks=PROMPT // chunk,
        blk=blk,
        pairs=pairs,
        scale=1.0 / math.sqrt(head_dim),
    )
    low_scratch = pltpu.VMEM((chunks, chunk, LANES), LOW)
    low_turned = pltpu.VMEM((chunks, LANES, chunk), LOW)
    wide_scratch = pltpu.VMEM((chunks, chunk, LANES), WIDE)
    attended, grads = pl.pallas_call(
        kernel,
        out_shape=(
            jax.ShapeDtypeStruct((blocks, blk, width), LOW),
            jax.ShapeDtypeStruct((blocks, blk, 3 * width), LOW),
        ),
        grid_spec=pltpu.PrefetchScalarGridSpec(
            num_scalar_prefetch=1,
            grid=(pairs, chunks),
            in_specs=in_specs,
            out_specs=[pl.BlockSpec(memory_space=pl.ANY)] * 2,
            scratch_shapes=[
                low_scratch,
                low_scratch,
                low_turned,
                low_turned,
                pltpu.VMEM((2, PROMPT // chunk + 1, chunk, chunk), WIDE),
                wide_scratch,
                wide_scratch,
                pltpu.VMEM((2, chunk, LANES), LOW),
                pltpu.VMEM((2, chunk, LANES), LOW),
                pltpu.VMEM((rows, LANES), LOW),
                pltpu.VMEM((rows, LANES), LOW),
                pltpu.SemaphoreType.DMA((2, 2, per)),
                pltpu.SemaphoreType.DMA((2, blocks)),
            ],
        ),
        compiler_params=pltpu.CompilerParams(
            dimension_semantics=("arbitrary", "arbitrary"), vmem_limit_bytes=56 << 20
        ),
        cost_estimate=pl.CostEstimate(
            flops=6 * rows * rows * width, bytes_accessed=16 * rows * width, transcendentals=0
        ),
        name="attention",
    )(where, *operands)
    return attended.reshape(rows, width), grads.reshape(rows, 3 * width)


def ring_of(count):
    order = list(range(count // 2)) + list(range(count - 1, count // 2 - 1, -1))
    ahead = [(order[n], order[(n + 1) % count]) for n in range(count)]
    return order, ahead, [(b, a) for a, b in ahead]


def ring_gather(own, axis):
    count = lax.axis_size(axis)
    _, ahead, behind = ring_of(count)
    pieces, half = [own], own.shape[0] // 2
    from_behind = from_ahead = own
    for _ in range(count // 2 - 1):
        from_behind = lax.ppermute(from_behind, axis, ahead)
        from_ahead = lax.ppermute(from_ahead, axis, behind)
        pieces += [from_behind, from_ahead]
    pieces.append(lax.ppermute(from_behind[:half], axis, ahead))
    pieces.append(lax.ppermute(from_ahead[half:], axis, behind))
    return jnp.concatenate(pieces, axis=0)


def ring_rank(offset, count):
    ranks = [0] * count
    for s in range(1, count // 2):
        ranks[s], ranks[count - s] = 2 * s, 2 * s - 1
    ranks[count // 2] = count - 1
    return jnp.asarray(ranks, jnp.int32)[offset]


def ring_reduce(parts, axis):
    count = lax.axis_size(axis)
    _, ahead, behind = ring_of(count)
    rows = parts.shape[0] // count
    half = rows // 2

    def part(rank):
        return parts[rank * rows : (rank + 1) * rows]

    def plus(a, b):
        return (a.astype(WIDE) + b.astype(WIDE)).astype(LOW)

    far = part(count - 1)
    up, down = lax.ppermute(far[:half], axis, ahead), lax.ppermute(far[half:], axis, behind)
    own = part(0).astype(WIDE)
    if count == 2:
        return own + jnp.concatenate([up, down], axis=0).astype(WIDE)
    for s in range(count // 2 - 1, 0, -1):
        to_ahead, to_behind = part(2 * s), part(2 * s - 1)
        if s == count // 2 - 1:
            up = [
                lax.ppermute(plus(to_ahead[:half], up), axis, ahead),
                lax.ppermute(to_ahead[half:], axis, ahead),
            ]
            down = [
                lax.ppermute(to_behind[:half], axis, behind),
                lax.ppermute(plus(to_behind[half:], down), axis, behind),
            ]
            up, down = jnp.concatenate(up, axis=0), jnp.concatenate(down, axis=0)
        else:
            up = lax.ppermute(plus(to_ahead, up), axis, ahead)
            down = lax.ppermute(plus(to_behind, down), axis, behind)
    return own + up.astype(WIDE) + down.astype(WIDE)


def gelu_tanh(values):
    return (
        0.5
        * values
        * (
            1.0
            + jnp.tanh(math.sqrt(2.0 / math.pi) * (values + 0.044715 * values * values * values))
        )
    )


def rope_tables(rows):
    place = jnp.arange(rows, dtype=jnp.int32)
    pos = jnp.where(place < PROMPT, place, PROMPT + (place - PROMPT) % CLEN)
    half = ROT // 2
    freq = 10000.0 ** (-2.0 * jnp.arange(half, dtype=WIDE) / ROT)
    angle = pos.astype(WIDE)[:, None] * freq[None, :]
    cosine, sine = jnp.cos(angle), jnp.sin(angle)
    zero, one = jnp.zeros_like(cosine), jnp.ones_like(cosine)
    tabs = ((cosine, cosine, one, one), (zero, sine, zero, zero), (-sine, zero, zero, zero))
    return [jnp.concatenate(tab * (LANES // (4 * half)), axis=1) for tab in tabs]


def shards(
    tokens,
    cotangent,
    block_table,
    ln_gain,
    ln_bias,
    w_qkv,
    b_qkv,
    w_dense,
    b_dense,
    w_fc1,
    b_fc1,
    w_fc2,
    b_fc2,
):
    _, local_rows, width = tokens.shape
    head_dim = width // HEADS
    count = lax.axis_size("ctx")
    me = lax.axis_index("ctx")
    rows = local_rows * count
    local_blocks = local_rows // BLK
    each = w_dense.shape[0]
    hidden = w_fc2.shape[0]
    gain, shift = ln_gain.astype(WIDE), ln_bias.astype(WIDE)

    order, _, _ = ring_of(count)
    places = [0] * count
    for n, device in enumerate(order):
        places[device] = n
    places = jnp.asarray(places, jnp.int32)
    slots = jnp.arange(rows // BLK, dtype=jnp.int32)
    offset = (places[slots // local_blocks] - places[me]) % count
    held_at = ring_rank(offset, count) * local_blocks + slots % local_blocks
    hit = block_table[0][None, :] == slots[:, None]
    where = jnp.sum(jnp.where(hit, held_at[None, :], 0), axis=1).astype(jnp.int32)

    own_tokens = tokens[0].astype(WIDE)
    own_grad = cotangent[0]
    average = jnp.mean(own_tokens, axis=-1, keepdims=True)
    centred = own_tokens - average
    rstd = lax.rsqrt(jnp.mean(centred * centred, axis=-1, keepdims=True) + 1e-05)
    xhat = centred * rstd
    normed_own = (xhat * gain + shift).astype(LOW)

    normed = ring_gather(normed_own, "ctx")
    grads = ring_gather(own_grad, "ctx")

    def gather_rows(shard):
        return lax.all_gather(shard, "fsdp", axis=0, tiled=True)

    qkv_weight = gather_rows(w_qkv.reshape(w_qkv.shape[0], 3 * each))
    fc1_weight = gather_rows(w_fc1)
    dense_turned = gather_rows(w_dense.T)
    fc2_turned = gather_rows(w_fc2.T)

    qkv_bias = lax.dynamic_slice_in_dim(b_qkv.reshape(3, width), me * each, each, 1)
    fc1_bias = lax.dynamic_slice_in_dim(b_fc1, me * hidden, hidden, 0)

    qkv = (dot(normed, qkv_weight, NN) + qkv_bias.reshape(-1).astype(WIDE)).astype(LOW)
    expanded = dot(normed, fc1_weight, NN) + fc1_bias.astype(WIDE)
    activated, gelu_pull = jax.vjp(gelu_tanh, expanded)
    activated = activated.astype(LOW)

    attended_grad = dot(grads, dense_turned, NN).astype(LOW)
    attended, qkv_grad = attention(qkv, attended_grad, where, rope_tables(rows), head_dim)

    out_part = dot(attended, dense_turned, NT) + dot(activated, fc2_turned, NT)
    out_sum = ring_reduce(out_part.astype(LOW), "ctx")
    output = own_tokens + out_sum + b_dense.astype(WIDE) + b_fc2.astype(WIDE)

    expanded_grad = gelu_pull(dot(grads, fc2_turned, NN))[0].astype(LOW)

    def scatter_rows(whole):
        return lax.psum_scatter(
            whole.astype(LOW), "fsdp", scatter_dimension=0, tiled=True
        ).astype(WIDE)

    d_fc2 = scatter_rows(dot(grads, activated, TN)).T
    d_dense = scatter_rows(dot(grads, attended, TN)).T
    d_fc1 = scatter_rows(dot(normed, expanded_grad, TN))
    d_qkv = scatter_rows(dot(normed, qkv_grad, TN))

    normed_grad_part = dot(qkv_grad, qkv_weight, NT) + dot(expanded_grad, fc1_weight, NT)
    normed_grad = ring_reduce(normed_grad_part.astype(LOW), "ctx")

    scaled = normed_grad * gain
    d_tokens = own_grad.astype(WIDE) + rstd * (
        scaled
        - jnp.mean(scaled, axis=-1, keepdims=True)
        - xhat * jnp.mean(scaled * xhat, axis=-1, keepdims=True)
    )

    qkv_bias_part = jnp.sum(qkv_grad.astype(WIDE), axis=0).reshape(3, each)
    fc1_bias_part = jnp.sum(expanded_grad.astype(WIDE), axis=0)
    qkv_bias_wide = lax.dynamic_update_slice_in_dim(
        jnp.zeros((3, width), WIDE), qkv_bias_part, me * each, 1
    ).reshape(-1)
    fc1_bias_wide = lax.dynamic_update_slice_in_dim(
        jnp.zeros((b_fc1.shape[0],), WIDE), fc1_bias_part, me * hidden, 0
    )
    small = jnp.concatenate(
        [
            jnp.sum(normed_grad * xhat, axis=0),
            jnp.sum(normed_grad, axis=0),
            qkv_bias_wide,
            jnp.sum(own_grad.astype(WIDE), axis=0),
            fc1_bias_wide,
        ]
    )
    small = lax.psum(small, ("ctx", "fsdp"))
    cuts = [width, 2 * width, 5 * width, 6 * width]
    d_gain, d_shift, d_b_qkv, d_b_out, d_b_fc1 = jnp.split(small, cuts)
    return (
        output.astype(LOW)[None],
        d_tokens.astype(LOW)[None],
        d_gain,
        d_shift,
        d_qkv.reshape(-1, 3, each),
        d_b_qkv,
        d_dense,
        d_b_out,
        d_fc1,
        d_b_fc1,
        d_fc2,
        d_b_out,
    )


def solution(mesh):
    in_specs = (
        P("fsdp", "ctx", None),
        P("fsdp", "ctx", None),
        P("fsdp", None),
        P(),
        P(),
        P("fsdp", None, "ctx"),
        P(),
        P("ctx", "fsdp"),
        P(),
        P("fsdp", "ctx"),
        P(),
        P("ctx", "fsdp"),
        P(),
    )
    out_specs = (
        P("fsdp", "ctx", None),
        P("fsdp", "ctx", None),
        P(),
        P(),
        P("fsdp", None, "ctx"),
        P(),
        P("ctx", "fsdp"),
        P(),
        P("fsdp", "ctx"),
        P(),
        P("ctx", "fsdp"),
        P(),
    )
    return jax.shard_map(shards, mesh=mesh, in_specs=in_specs, out_specs=out_specs, check_vma=False)
```

```python
import functools
import math

import jax
import jax.numpy as jnp
from jax import lax
from jax.experimental import pallas as pl
from jax.experimental.pallas import tpu as pltpu
from jax.sharding import PartitionSpec as P

HEADS = 32
ROT = 32
PROMPT = 2048
CLEN = 256
BLK = 64
CHUNK = 256
LANES = 128
NT = (((1,), (1,)), ((), ()))
NN = (((1,), (0,)), ((), ()))
TN = (((0,), (0,)), ((), ()))
LOW = jnp.bfloat16
WIDE = jnp.float32
LITTLE = pl.CostEstimate(flops=1000000, bytes_accessed=1000000, transcendentals=0)


def dot(left, right, dims):
    return lax.dot_general(left, right, dims, preferred_element_type=WIDE)


def attention_kernel(where_ref, *refs, chunk, chunks, full_chunks, blk, group, scale):
    per = chunk // blk
    q_in, k_in, v_in, g_in = (refs[n * per : (n + 1) * per] for n in range(4))
    cos_ref, up_ref, down_ref, att_hbm, grad_hbm = refs[4 * per : 4 * per + 5]
    (
        keys,
        values,
        values_t,
        probs,
        key_sum,
        value_sum,
        top_ref,
        total_ref,
        mix_ref,
        back_ref,
        att_stage,
        query_stage,
        key_stage,
        value_stage,
        row_sem,
        col_sem,
    ) = refs[4 * per + 5 :]
    i = pl.program_id(0)
    slot = lax.rem(i, 2)
    half = LANES // 2
    lanes = group * LANES
    heads = 2 * group
    first = lax.broadcasted_iota(jnp.int32, (1, LANES), 1) < half

    def columns(part):
        return pl.ds(part * lanes, lanes)

    def row_copies(which, at):
        stage, target = ((att_stage, att_hbm), (query_stage, grad_hbm))[which]
        return [
            pltpu.make_async_copy(
                stage.at[at, pl.ds(r * blk, blk)],
                target.at[where_ref[i * per + r], :, columns(0)],
                row_sem.at[at, which, r],
            )
            for r in range(per)
        ]

    def col_copies(n):
        block = where_ref[n]
        rows = pl.ds(pl.multiple_of(n * blk, blk), blk)
        return (
            pltpu.make_async_copy(
                key_stage.at[rows], grad_hbm.at[block, :, columns(1)], col_sem.at[0, n]
            ),
            pltpu.make_async_copy(
                value_stage.at[rows], grad_hbm.at[block, :, columns(2)], col_sem.at[1, n]
            ),
        )

    def load(parts):
        return jnp.concatenate([part[0] for part in parts], axis=0)

    def tables(rows):
        return cos_ref[rows], up_ref[rows], down_ref[rows]

    quarter = ROT // 2

    def turned(x, tab, sign):
        return jnp.concatenate(
            [
                y * tab[0]
                + sign
                * (pltpu.roll(y, quarter, 1) * tab[1] + pltpu.roll(y, LANES - quarter, 1) * tab[2])
                for y in (x[:, n * LANES : (n + 1) * LANES] for n in range(group))
            ],
            axis=1,
        )

    def one_head(x, h):
        pair = x[:, (h // 2) * LANES : (h // 2 + 1) * LANES]
        nothing = jnp.zeros_like(pair)
        return jnp.where(first, pair, nothing) if h % 2 == 0 else jnp.where(first, nothing, pair)

    @pl.when(i >= 2)
    def _():
        for which in range(2):
            for copy in row_copies(which, slot):
                copy.wait()

    here = pl.ds(pl.multiple_of(i * chunk, chunk), chunk)
    tab = tables(here)
    query = (turned(load(q_in).astype(WIDE), tab, 1.0) * scale).astype(LOW)
    key_new = turned(load(k_in).astype(WIDE), tab, 1.0)
    value_new = load(v_in)
    grad = load(g_in)
    keys[here] = key_new.astype(LOW)
    values[here] = value_new
    values_t[:, here] = value_new.astype(WIDE).T.astype(LOW)
    key_sum[here] = jnp.zeros((chunk, lanes), WIDE)
    value_sum[here] = jnp.zeros((chunk, lanes), WIDE)
    top_ref[...] = jnp.full(top_ref.shape, -1e30, WIDE)
    total_ref[...] = jnp.zeros(total_ref.shape, WIDE)
    mix_ref[...] = jnp.zeros(mix_ref.shape, WIDE)
    back_ref[...] = jnp.zeros(back_ref.shape, WIDE)
    query_of = [one_head(query, h) for h in range(heads)]
    grad_of = [one_head(grad, h) for h in range(heads)]
    query_pair = [
        jnp.concatenate(query_of[2 * n : 2 * n + 2], axis=0) for n in range(group)
    ]
    grad_pair = [jnp.concatenate(grad_of[2 * n : 2 * n + 2], axis=0) for n in range(group)]
    before = jnp.minimum(i, full_chunks)
    doubles = before // 2
    odd = before - 2 * doubles

    def fold(x, how):
        return how(x.reshape(x.shape[0] // 8, 8, chunk), axis=0)

    def pair_lanes(n):
        return slice(n * LANES, (n + 1) * LANES)

    def head_rows(h):
        return slice(h * half, (h + 1) * half)

    def sweep(tile):
        def double(t, carry):
            start = pl.multiple_of(t * 2 * chunk, 2 * chunk)
            tile(start, start, 2 * chunk, False)
            return carry

        lax.fori_loop(0, doubles, double, 0)
        held = pl.multiple_of(doubles * 2 * chunk, chunk)

        @pl.when(odd == 1)
        def _():
            tile(held, held, 2 * chunk, True)

        @pl.when(odd == 0)
        def _():
            tile(pl.multiple_of(i * chunk, chunk), held, chunk, True)

    def score(start, held, size, masked):
        rows, to = pl.ds(start, size), pl.ds(held, size)
        if masked:
            key_row = lax.broadcasted_iota(jnp.int32, (size, chunk), 0) + start
            query_col = lax.broadcasted_iota(jnp.int32, (size, chunk), 1) + i * chunk
            seen = key_row <= query_col
        for h in range(heads):
            raw = dot(keys[rows, pair_lanes(h // 2)], query_of[h], NT)
            if masked:
                raw = jnp.where(seen, raw, -1e30)
            probs[h, to] = raw
            top_ref[h] = jnp.maximum(top_ref[h], fold(raw, jnp.max))

    sweep(score)
    top = [jnp.max(top_ref[h], axis=0, keepdims=True) for h in range(heads)]

    def mix(start, held, size, masked):
        rows, to = pl.ds(start, size), pl.ds(held, size)
        for h in range(heads):
            weight = jnp.exp(probs[h, to] - top[h])
            probs[h, to] = weight
            total_ref[h] += fold(weight, jnp.sum)
            mix_ref[head_rows(h)] += dot(values_t[head_rows(h), rows], weight.astype(LOW), NN)

    sweep(mix)
    inverse = [1.0 / jnp.sum(total_ref[h], axis=0, keepdims=True) for h in range(heads)]
    attended = jnp.concatenate(
        [mix_ref[head_rows(h)] * inverse[h] for h in range(heads)], axis=0
    )
    shared = grad.astype(WIDE).T * attended
    inner = [jnp.sum(shared[head_rows(h)], axis=0, keepdims=True) for h in range(heads)]
    att_stage[slot] = attended.T.astype(LOW)
    for copy in row_copies(0, slot):
        copy.start()

    def back(start, held, size, masked):
        rows, to = pl.ds(start, size), pl.ds(held, size)
        for n in range(group):
            value = values[rows, pair_lanes(n)]
            weights, grads = [], []
            for h in (2 * n, 2 * n + 1):
                weight = probs[h, to] * inverse[h]
                weight_grad = dot(value, grad_of[h], NT)
                score_grad = (weight * (weight_grad - inner[h])).astype(LOW)
                weights.append(weight.astype(LOW))
                grads.append(score_grad)
            value_sum[rows, pair_lanes(n)] += dot(
                jnp.concatenate(weights, axis=1), grad_pair[n], NN
            )
            key = keys[rows, pair_lanes(n)]
            back_ref[:, pair_lanes(n)] += dot(
                jnp.concatenate(grads, axis=0),
                jnp.concatenate([one_head(key, h) for h in range(2)], axis=0),
                TN,
            )
            key_sum[rows, pair_lanes(n)] += dot(
                jnp.concatenate(grads, axis=1), query_pair[n], NN
            )

    sweep(back)
    query_stage[slot] = turned(back_ref[...] * scale, tab, -1.0).astype(LOW)
    for copy in row_copies(1, slot):
        copy.start()

    @pl.when(i == chunks - 1)
    def _():
        @pl.loop(0, chunks)
        def _(n):
            rows = pl.ds(pl.multiple_of(n * chunk, chunk), chunk)
            key_stage[rows] = turned(key_sum[rows], tables(rows), -1.0).astype(LOW)
            value_stage[rows] = value_sum[rows].astype(LOW)
            for r in range(per):
                for copy in col_copies(n * per + r):
                    copy.start()

        for at in range(2):
            for which in range(2):
                for copy in row_copies(which, at):
                    copy.wait()

        @pl.loop(0, chunks * per)
        def _(n):
            for copy in col_copies(n):
                copy.wait()


def attention(qkv, grad, where, tabs, lanes, which, head_dim):
    rows = grad.shape[0]
    chunk, blk = CHUNK, BLK
    per, chunks, blocks = chunk // blk, rows // chunk, rows // blk
    group = lanes // LANES
    heads = 2 * group
    qkv_blocks = qkv.reshape(blocks, blk, qkv.shape[1])
    grad_blocks = grad.reshape(blocks, blk, grad.shape[1])

    def spec(column, r):
        return pl.BlockSpec((1, blk, lanes), lambda i, at: (at[i * per + r], 0, column))

    in_specs = [spec(3 * which + part, r) for part in range(3) for r in range(per)]
    in_specs += [spec(which, r) for r in range(per)]
    in_specs += [pl.BlockSpec((rows, LANES), lambda i, at: (0, 0), pipeline_mode=pl.Buffered(1))] * 3
    operands = [qkv_blocks] * (3 * per) + [grad_blocks] * per + list(tabs)
    kernel = functools.partial(
        attention_kernel,
        chunk=chunk,
        chunks=chunks,
        full_chunks=PROMPT // chunk,
        blk=blk,
        group=group,
        scale=1.0 / math.sqrt(head_dim),
    )
    attended, grads = pl.pallas_call(
        kernel,
        out_shape=(
            jax.ShapeDtypeStruct((blocks, blk, lanes), LOW),
            jax.ShapeDtypeStruct((blocks, blk, 3 * lanes), LOW),
        ),
        grid_spec=pltpu.PrefetchScalarGridSpec(
            num_scalar_prefetch=1,
            grid=(chunks,),
            in_specs=in_specs,
            out_specs=[pl.BlockSpec(memory_space=pl.ANY)] * 2,
            scratch_shapes=[
                pltpu.VMEM((rows, lanes), LOW),
                pltpu.VMEM((rows, lanes), LOW),
                pltpu.VMEM((lanes, rows), LOW),
                pltpu.VMEM((heads, PROMPT + chunk, chunk), WIDE),
                pltpu.VMEM((rows, lanes), WIDE),
                pltpu.VMEM((rows, lanes), WIDE),
                pltpu.VMEM((heads, 8, chunk), WIDE),
                pltpu.VMEM((heads, 8, chunk), WIDE),
                pltpu.VMEM((lanes, chunk), WIDE),
                pltpu.VMEM((chunk, lanes), WIDE),
                pltpu.VMEM((2, chunk, lanes), LOW),
                pltpu.VMEM((2, chunk, lanes), LOW),
                pltpu.VMEM((rows, lanes), LOW),
                pltpu.VMEM((rows, lanes), LOW),
                pltpu.SemaphoreType.DMA((2, 2, per)),
                pltpu.SemaphoreType.DMA((2, blocks)),
            ],
        ),
        compiler_params=pltpu.CompilerParams(
            dimension_semantics=("arbitrary",), vmem_limit_bytes=56 << 20
        ),
        cost_estimate=LITTLE,
        name="attention",
    )(where, *operands)
    return attended.reshape(rows, lanes), grads.reshape(rows, 3 * lanes)


def after(value, *others):
    return lax.optimization_barrier((value,) + others)[0]


def ring_of(count):
    order = list(range(count // 2)) + list(range(count - 1, count // 2 - 1, -1))
    ahead = [(order[n], order[(n + 1) % count]) for n in range(count)]
    return order, ahead, [(b, a) for a, b in ahead]


def rank_of(offset, count):
    offset %= count
    if offset == 0 or 2 * offset == count:
        return max(2 * offset - 1, 0)
    return 2 * offset if 2 * offset < count else 2 * (count - offset) - 1


def ring_pieces(own, axis, gate=()):
    count = lax.axis_size(axis)
    _, ahead, behind = ring_of(count)
    pieces, half = [own], own.shape[0] // 2
    from_behind = from_ahead = own
    for _ in range(count // 2 - 1):
        from_behind = lax.ppermute(from_behind, axis, ahead)
        from_ahead = lax.ppermute(from_ahead, axis, behind)
        pieces += [from_behind, from_ahead]
    from_behind, from_ahead = after(from_behind[:half], *gate), after(from_ahead[half:], *gate)
    far = [lax.ppermute(from_behind, axis, ahead), lax.ppermute(from_ahead, axis, behind)]
    return pieces + far


def ring_reduce(part, own, axis):
    count = lax.axis_size(axis)
    _, ahead, behind = ring_of(count)
    far = part(count - 1)
    half = far.shape[0] // 2

    def plus(a, b):
        return (a.astype(WIDE) + b.astype(WIDE)).astype(LOW)

    up, down = lax.ppermute(far[:half], axis, ahead), lax.ppermute(far[half:], axis, behind)
    far = early = (up, down)
    if count == 2:
        return own(early).astype(WIDE) + jnp.concatenate(early, axis=0).astype(WIDE), early, early
    for s in range(count // 2 - 1, 0, -1):
        to_ahead, to_behind = part(2 * s), part(2 * s - 1)
        if s == count // 2 - 1:
            free_up = lax.ppermute(to_ahead[half:], axis, ahead)
            free_down = lax.ppermute(to_behind[:half], axis, behind)
            early += (free_up, free_down)
            up = lax.ppermute(plus(to_ahead[:half], up), axis, ahead)
            down = lax.ppermute(plus(to_behind[half:], down), axis, behind)
            late = (up, down)
            up = jnp.concatenate([up, free_up], axis=0)
            down = jnp.concatenate([free_down, down], axis=0)
        else:
            up = lax.ppermute(plus(to_ahead, up), axis, ahead)
            down = lax.ppermute(plus(to_behind, down), axis, behind)
            late = (up, down)
    return own(far).astype(WIDE) + up.astype(WIDE) + down.astype(WIDE), early, late


def ring_exchange(part, axis):
    count = lax.axis_size(axis)
    order, _, _ = ring_of(count)
    got = [None] * count
    got[0] = part(0)
    for offset in range(1, count):
        hops = [(order[n], order[(n + offset) % count]) for n in range(count)]
        got[rank_of(-offset, count)] = lax.ppermute(part(rank_of(offset, count)), axis, hops)
    return got


def sum_everywhere(values, axes):
    for axis in axes:
        count, span = lax.axis_size(axis), 1
        while span < count:
            pairs = [(n, n ^ span) for n in range(count)]
            values = values + lax.ppermute(values, axis, pairs)
            span *= 2
    return values


def gelu_and_slope(h):
    inner_scale = math.sqrt(2.0 / math.pi)
    square = h * h
    t = jnp.tanh(h * (inner_scale + (inner_scale * 0.044715) * square))
    half = 0.5 * h
    rise = 0.5 + 0.5 * t
    bend = inner_scale + (3.0 * inner_scale * 0.044715) * square
    return (h * rise).astype(LOW), (rise + (half - half * t * t) * bend).astype(LOW)


def expand_kernel(x_ref, w_ref, b_ref, act_ref, slope_ref, *, cols):
    x = x_ref[...]
    for n in range(w_ref.shape[1] // cols):
        at = slice(n * cols, (n + 1) * cols)
        act, slope = gelu_and_slope(dot(x, w_ref[:, at], NN) + b_ref[:, at])
        act_ref[:, at] = act
        slope_ref[:, at] = slope


def expand(x, w, b):
    rows, width = x.shape
    hidden = w.shape[1]
    tile = 320
    out = jax.ShapeDtypeStruct((rows, hidden), LOW)
    return pl.pallas_call(
        functools.partial(expand_kernel, cols=min(512, hidden)),
        out_shape=(out, out),
        grid=(rows // tile,),
        in_specs=[
            pl.BlockSpec((tile, width), lambda i: (i, 0)),
            pl.BlockSpec((width, hidden), lambda i: (0, 0), pipeline_mode=pl.Buffered(1)),
            pl.BlockSpec((1, hidden), lambda i: (0, 0)),
        ],
        out_specs=[pl.BlockSpec((tile, hidden), lambda i: (i, 0))] * 2,
        compiler_params=pltpu.CompilerParams(
            dimension_semantics=("arbitrary",), vmem_limit_bytes=48 << 20
        ),
        cost_estimate=LITTLE,
        name="expand",
    )(x, w, b.astype(WIDE)[None])


def input_grad_kernel(*refs, terms):
    grads, weights = refs[:terms], refs[terms : 2 * terms]
    normed_ref, out_ref, sums_ref = refs[2 * terms :]
    total = sum(dot(g[...], w[...], NT) for g, w in zip(grads, weights))
    out_ref[...] = total.astype(LOW)
    sums_ref[0:1] = jnp.sum(total, axis=0, keepdims=True)
    sums_ref[1:2] = jnp.sum(total * normed_ref[...].astype(WIDE), axis=0, keepdims=True)


def input_grad(grads, weights, normed, rank, rows):
    width = normed.shape[1]
    cols = 512
    keep = pl.Buffered(1)
    in_specs = [
        pl.BlockSpec((rows, g.shape[1]), lambda i: (rank, 0), pipeline_mode=keep) for g in grads
    ]
    in_specs += [
        pl.BlockSpec((cols, g.shape[1]), lambda i, at=at: (i, at))
        for g, (_, at) in zip(grads, weights)
    ]
    in_specs.append(pl.BlockSpec((rows, cols), lambda i: (rank, i)))
    return pl.pallas_call(
        functools.partial(input_grad_kernel, terms=len(grads)),
        out_shape=(
            jax.ShapeDtypeStruct((rows, width), LOW),
            jax.ShapeDtypeStruct((2, width), WIDE),
        ),
        grid=(width // cols,),
        in_specs=in_specs,
        out_specs=[
            pl.BlockSpec((rows, cols), lambda i: (0, i)),
            pl.BlockSpec((2, cols), lambda i: (0, i)),
        ],
        compiler_params=pltpu.CompilerParams(
            dimension_semantics=("arbitrary",), vmem_limit_bytes=48 << 20
        ),
        cost_estimate=LITTLE,
        name="input_grad",
    )(*grads, *[w for w, _ in weights], normed)


def pair_grad_kernel(x_ref, y_ref, a_ref, b_ref, out_ref):
    split = a_ref.shape[1]
    out_ref[:, :split] = dot(x_ref[...], a_ref[...], TN).astype(LOW)
    out_ref[:, split:] = dot(y_ref[...], b_ref[...], TN).astype(LOW)


def pair_grad(x, y, a, b):
    rows, width = x.shape
    columns = a.shape[1] + b.shape[1]
    tile = 512
    keep = pl.Buffered(1)
    return pl.pallas_call(
        pair_grad_kernel,
        out_shape=jax.ShapeDtypeStruct((width, columns), LOW),
        grid=(width // tile,),
        in_specs=[
            pl.BlockSpec((rows, tile), lambda i: (0, i)),
            pl.BlockSpec((rows, tile), lambda i: (0, i)),
            pl.BlockSpec(a.shape, lambda i: (0, 0), pipeline_mode=keep),
            pl.BlockSpec(b.shape, lambda i: (0, 0), pipeline_mode=keep),
        ],
        out_specs=pl.BlockSpec((tile, columns), lambda i: (i, 0)),
        compiler_params=pltpu.CompilerParams(
            dimension_semantics=("arbitrary",), vmem_limit_bytes=48 << 20
        ),
        cost_estimate=LITTLE,
        name="pair_grad",
    )(x, y, a, b)


def rope_tables(rows):
    place = jnp.arange(rows, dtype=jnp.int32)
    pos = jnp.where(place < PROMPT, place, PROMPT + (place - PROMPT) % CLEN)
    half = ROT // 2
    freq = 10000.0 ** (-2.0 * jnp.arange(half, dtype=WIDE) / ROT)
    angle = pos.astype(WIDE)[:, None] * freq[None, :]
    cosine, sine = jnp.cos(angle), jnp.sin(angle)
    zero, one = jnp.zeros_like(cosine), jnp.ones_like(cosine)
    tabs = ((cosine, cosine, one, one), (zero, sine, zero, zero), (-sine, zero, zero, zero))
    return [jnp.concatenate(tab * (LANES // (4 * half)), axis=1) for tab in tabs]


def shards(
    tokens,
    cotangent,
    block_table,
    ln_gain,
    ln_bias,
    w_qkv,
    b_qkv,
    w_dense,
    b_dense,
    w_fc1,
    b_fc1,
    w_fc2,
    b_fc2,
):
    _, local_rows, width = tokens.shape
    head_dim = width // HEADS
    count = lax.axis_size("ctx")
    me = lax.axis_index("ctx")
    rows = local_rows * count
    local_blocks = local_rows // BLK
    each = w_dense.shape[0]
    hidden = w_fc2.shape[0]
    gain, shift = ln_gain.astype(WIDE), ln_bias.astype(WIDE)

    def of_rank(whole, rank):
        return whole[rank * local_rows : (rank + 1) * local_rows]

    order, _, _ = ring_of(count)
    places = [0] * count
    for n, device in enumerate(order):
        places[device] = n
    places = jnp.asarray(places, jnp.int32)
    ranks = jnp.asarray([rank_of(n, count) for n in range(count)], jnp.int32)
    slots = jnp.arange(rows // BLK, dtype=jnp.int32)
    offset = (places[slots // local_blocks] - places[me]) % count
    held_at = ranks[offset] * local_blocks + slots % local_blocks
    hit = block_table[0][None, :] == slots[:, None]
    where = jnp.sum(jnp.where(hit, held_at[None, :], 0), axis=1).astype(jnp.int32)

    own_tokens = tokens[0].astype(WIDE)
    own_grad = cotangent[0]
    average = jnp.mean(own_tokens, axis=-1, keepdims=True)
    centred = own_tokens - average
    rstd = lax.rsqrt(jnp.mean(centred * centred, axis=-1, keepdims=True) + 1e-05)
    xhat = centred * rstd
    normed_own = (xhat * gain + shift).astype(LOW)

    def gather_rows(shard):
        return lax.all_gather(shard, "fsdp", axis=0, tiled=True)

    def scatter_rows(whole):
        return lax.psum_scatter(whole, "fsdp", scatter_dimension=0, tiled=True)

    lanes = 2 * LANES if each % (2 * LANES) == 0 else LANES
    groups = each // lanes

    def by_group(values):
        cut = values.reshape(-1, 3, groups, lanes)
        return jnp.swapaxes(cut, 1, 2).reshape(-1, 3 * each)

    normed_pieces = ring_pieces(normed_own, "ctx")
    normed = jnp.concatenate(normed_pieces, axis=0)
    attention_shard = jnp.concatenate([by_group(w_qkv), w_dense.T], axis=1)
    fc1_weight = gather_rows(w_fc1)
    attention_weight = gather_rows(after(attention_shard, *normed_pieces[1:-2]))
    fc2_turned = gather_rows(after(w_fc2.T, *normed_pieces[-2:]))
    qkv_weight, dense_turned = attention_weight[:, : 3 * each], attention_weight[:, 3 * each :]

    fc1_bias = lax.dynamic_slice_in_dim(b_fc1, me * hidden, hidden, 0)
    qkv_bias = lax.dynamic_slice_in_dim(b_qkv.reshape(3, width), me * each, each, 1)
    activated, slope = expand(normed, fc1_weight, fc1_bias)

    sent_grad = after(own_grad, *normed_pieces[-2:])
    grad_pieces = ring_pieces(sent_grad, "ctx", gate=(activated,))
    grads = jnp.concatenate(grad_pieces, axis=0)

    qkv = dot(after(normed, activated), qkv_weight, NN)
    qkv = (qkv + by_group(qkv_bias)[0].astype(WIDE)).astype(LOW)
    attended_grad = dot(after(grads, qkv), dense_turned, NN).astype(LOW)
    d_fc2_part = dot(after(grads, attended_grad), activated, TN).astype(LOW)
    d_fc2 = scatter_rows(d_fc2_part)

    dense_pieces = ring_pieces(dense_turned, "ctx")
    dense_whole = jnp.concatenate(
        dense_pieces[:-2] + [jnp.concatenate(dense_pieces[-2:], axis=0)], axis=1
    )

    def feed_forward(gate, later):
        act = after(activated, *gate)
        ff_part = dot(act, fc2_turned, NT).astype(LOW)
        ff_sum, early, late = ring_reduce(
            lambda rank: of_rank(ff_part, rank), lambda _: of_rank(ff_part, 0), "ctx"
        )
        gated = after(grads, ff_part, *later)
        expanded_grad = (dot(gated, fc2_turned, NN) * slope.astype(WIDE)).astype(LOW)
        d_fc1_part = dot(after(normed, expanded_grad, *early), expanded_grad, TN).astype(LOW)
        return ff_sum, late, expanded_grad, d_fc1_part, scatter_rows(d_fc1_part)

    tabs = rope_tables(rows)
    attended, qkv_grads, d_attention, swapped = [], [], [], []
    ordered = (d_fc2_part,)
    for which in range(groups):
        if which == groups - 1:
            gate = (d_part,) + tuple(dense_pieces) if which else ()
            ff_sum, ff_late, expanded_grad, d_fc1_part, d_fc1 = feed_forward(
                gate, (d_fc2,) if which else ()
            )
            ordered = (d_fc1_part,) + ff_late + tuple(d_attention)
        got, got_grads = attention(
            after(qkv, *ordered), attended_grad, where, tabs, lanes, which, head_dim
        )
        attended.append(got)
        qkv_grads.append(got_grads)
        if which < groups - 1:
            swapped.append(ring_exchange(lambda rank, got=got: of_rank(got, rank), "ctx"))
            d_part = pair_grad(normed, grads, got_grads, got)
            ordered = (d_part,)
            d_attention.append(scatter_rows(d_part))

    weights = [(attention_weight, which) for which in range(groups)] + [(fc1_weight, 0)]
    parts, sums = [None] * count, 0.0
    early_swaps = [piece for pieces in swapped for piece in pieces]
    turn = after(expanded_grad, *early_swaps, *attended)

    def input_part(rank, turn):
        return input_grad(qkv_grads + [turn], weights, normed, rank, local_rows)

    for rank in range(count - 1, 0, -1):
        parts[rank], part_sums = input_part(rank, turn)
        sums = sums + part_sums
        turn = after(turn, parts[rank])

    own_sums = []

    def own_part(arrived):
        gated = after(normed, parts[1], d_fc1, *arrived)
        d_part = pair_grad(gated, grads, qkv_grads[-1], attended[-1])
        d_attention.append(scatter_rows(d_part))
        got = after(attended[-1], *arrived)
        swapped.append(ring_exchange(lambda rank: of_rank(got, rank), "ctx"))
        part, part_sums = input_part(0, after(turn, d_part))
        own_sums.append(part_sums)
        return part

    normed_grad, _, _ = ring_reduce(lambda rank: parts[rank], own_part, "ctx")
    sums = sums + own_sums[0]

    d_qkv = jnp.concatenate(
        [part[:, : 3 * lanes].reshape(-1, 3, lanes) for part in d_attention], axis=2
    ).astype(WIDE)
    d_dense = jnp.concatenate([part[:, 3 * lanes :].T for part in d_attention], axis=0)

    attended_own = jnp.concatenate(
        [swapped[which][rank] for rank in range(count) for which in range(groups)], axis=1
    )
    out_sum = ff_sum + dot(attended_own, dense_whole, NT)
    output = own_tokens + out_sum + b_dense.astype(WIDE) + b_fc2.astype(WIDE)

    scaled = normed_grad * gain
    d_tokens = own_grad.astype(WIDE) + rstd * (
        scaled
        - jnp.mean(scaled, axis=-1, keepdims=True)
        - xhat * jnp.mean(scaled * xhat, axis=-1, keepdims=True)
    )

    qkv_bias_part = jnp.concatenate(
        [jnp.sum(part.astype(WIDE), axis=0).reshape(3, lanes) for part in qkv_grads], axis=1
    )
    fc1_bias_part = jnp.sum(expanded_grad.astype(WIDE), axis=0)
    qkv_bias_wide = lax.dynamic_update_slice_in_dim(
        jnp.zeros((3, width), WIDE), qkv_bias_part, me * each, 1
    ).reshape(-1)
    fc1_bias_wide = lax.dynamic_update_slice_in_dim(
        jnp.zeros((b_fc1.shape[0],), WIDE), fc1_bias_part, me * hidden, 0
    )
    small = sum_everywhere(
        jnp.concatenate(
            [
                sums.reshape(-1),
                qkv_bias_wide,
                jnp.sum(sent_grad.astype(WIDE), axis=0),
                fc1_bias_wide,
            ]
        ),
        ("fsdp", "ctx"),
    )
    d_shift, with_normed, d_b_qkv, d_b_out, d_b_fc1 = jnp.split(
        small, [width, 2 * width, 5 * width, 6 * width]
    )
    d_gain = (with_normed - shift * d_shift) / gain
    return (
        output.astype(LOW)[None],
        d_tokens.astype(LOW)[None],
        d_gain,
        d_shift,
        d_qkv,
        d_b_qkv,
        d_dense.astype(WIDE),
        d_b_out,
        d_fc1.astype(WIDE),
        d_b_fc1,
        d_fc2.T.astype(WIDE),
        d_b_out,
    )


def solution(mesh):
    in_specs = (
        P("fsdp", "ctx", None),
        P("fsdp", "ctx", None),
        P("fsdp", None),
        P(),
        P(),
        P("fsdp", None, "ctx"),
        P(),
        P("ctx", "fsdp"),
        P(),
        P("fsdp", "ctx"),
        P(),
        P("ctx", "fsdp"),
        P(),
    )
    out_specs = (
        P("fsdp", "ctx", None),
        P("fsdp", "ctx", None),
        P(),
        P(),
        P("fsdp", None, "ctx"),
        P(),
        P("ctx", "fsdp"),
        P(),
        P("fsdp", "ctx"),
        P(),
        P("ctx", "fsdp"),
        P(),
    )
    return jax.shard_map(shards, mesh=mesh, in_specs=in_specs, out_specs=out_specs, check_vma=False)
```

```python
import functools
import math

import jax
import jax.numpy as jnp
from jax import lax
from jax.experimental import pallas as pl
from jax.experimental.pallas import tpu as pltpu
from jax.sharding import PartitionSpec as P

HEADS = 32
ROT = 32
PROMPT = 2048
CLEN = 256
BLK = 64
CHUNK = 256
LANES = 128
NT = (((1,), (1,)), ((), ()))
NN = (((1,), (0,)), ((), ()))
TN = (((0,), (0,)), ((), ()))
LOW = jnp.bfloat16
WIDE = jnp.float32
LITTLE = pl.CostEstimate(flops=1000000, bytes_accessed=1000000, transcendentals=0)


def dot(left, right, dims):
    return lax.dot_general(left, right, dims, preferred_element_type=WIDE)


def attention_kernel(where_ref, *refs, chunk, chunks, full_chunks, blk, group, scale):
    per = chunk // blk
    q_in, k_in, v_in, g_in = (refs[n * per : (n + 1) * per] for n in range(4))
    cos_ref, up_ref, down_ref, att_hbm, grad_hbm = refs[4 * per : 4 * per + 5]
    (
        keys,
        values,
        values_t,
        probs,
        key_sum,
        value_sum,
        top_ref,
        total_ref,
        mix_ref,
        back_ref,
        att_stage,
        query_stage,
        key_stage,
        value_stage,
        row_sem,
        col_sem,
    ) = refs[4 * per + 5 :]
    i = pl.program_id(0)
    slot = lax.rem(i, 2)
    half = LANES // 2
    lanes = group * LANES
    heads = 2 * group
    first = lax.broadcasted_iota(jnp.int32, (1, LANES), 1) < half

    def columns(part):
        return pl.ds(part * lanes, lanes)

    def row_copies(which, at):
        stage, target = ((att_stage, att_hbm), (query_stage, grad_hbm))[which]
        return [
            pltpu.make_async_copy(
                stage.at[at, pl.ds(r * blk, blk)],
                target.at[where_ref[i * per + r], :, columns(0)],
                row_sem.at[at, which, r],
            )
            for r in range(per)
        ]

    def col_copies(n):
        block = where_ref[n]
        rows = pl.ds(pl.multiple_of(n * blk, blk), blk)
        return (
            pltpu.make_async_copy(
                key_stage.at[rows], grad_hbm.at[block, :, columns(1)], col_sem.at[0, n]
            ),
            pltpu.make_async_copy(
                value_stage.at[rows], grad_hbm.at[block, :, columns(2)], col_sem.at[1, n]
            ),
        )

    def load(parts):
        return jnp.concatenate([part[0] for part in parts], axis=0)

    def tables(rows):
        return cos_ref[rows], up_ref[rows], down_ref[rows]

    quarter = ROT // 2

    def turned(x, tab, sign):
        return jnp.concatenate(
            [
                y * tab[0]
                + sign
                * (pltpu.roll(y, quarter, 1) * tab[1] + pltpu.roll(y, LANES - quarter, 1) * tab[2])
                for y in (x[:, n * LANES : (n + 1) * LANES] for n in range(group))
            ],
            axis=1,
        )

    def one_head(x, h):
        pair = x[:, (h // 2) * LANES : (h // 2 + 1) * LANES]
        nothing = jnp.zeros_like(pair)
        return jnp.where(first, pair, nothing) if h % 2 == 0 else jnp.where(first, nothing, pair)

    @pl.when(i >= 2)
    def _():
        for which in range(2):
            for copy in row_copies(which, slot):
                copy.wait()

    here = pl.ds(pl.multiple_of(i * chunk, chunk), chunk)
    tab = tables(here)
    query = (turned(load(q_in).astype(WIDE), tab, 1.0) * scale).astype(LOW)
    key_new = turned(load(k_in).astype(WIDE), tab, 1.0)
    value_new = load(v_in)
    grad = load(g_in)
    keys[here] = key_new.astype(LOW)
    values[here] = value_new
    values_t[:, here] = value_new.astype(WIDE).T.astype(LOW)
    key_sum[here] = jnp.zeros((chunk, lanes), WIDE)
    value_sum[here] = jnp.zeros((chunk, lanes), WIDE)
    top_ref[...] = jnp.full(top_ref.shape, -1e30, WIDE)
    total_ref[...] = jnp.zeros(total_ref.shape, WIDE)
    mix_ref[...] = jnp.zeros(mix_ref.shape, WIDE)
    back_ref[...] = jnp.zeros(back_ref.shape, WIDE)
    query_of = [one_head(query, h) for h in range(heads)]
    grad_of = [one_head(grad, h) for h in range(heads)]
    query_pair = [
        jnp.concatenate(query_of[2 * n : 2 * n + 2], axis=0) for n in range(group)
    ]
    grad_pair = [jnp.concatenate(grad_of[2 * n : 2 * n + 2], axis=0) for n in range(group)]
    before = jnp.minimum(i, full_chunks)
    doubles = before // 2
    odd = before - 2 * doubles

    def fold(x, how):
        return how(x.reshape(x.shape[0] // 8, 8, chunk), axis=0)

    def pair_lanes(n):
        return slice(n * LANES, (n + 1) * LANES)

    def head_rows(h):
        return slice(h * half, (h + 1) * half)

    def sweep(tile):
        def double(t, carry):
            start = pl.multiple_of(t * 2 * chunk, 2 * chunk)
            tile(start, start, 2 * chunk, False)
            return carry

        lax.fori_loop(0, doubles, double, 0)
        held = pl.multiple_of(doubles * 2 * chunk, chunk)

        @pl.when(odd == 1)
        def _():
            tile(held, held, 2 * chunk, True)

        @pl.when(odd == 0)
        def _():
            tile(pl.multiple_of(i * chunk, chunk), held, chunk, True)

    def score(start, held, size, masked):
        rows, to = pl.ds(start, size), pl.ds(held, size)
        if masked:
            key_row = lax.broadcasted_iota(jnp.int32, (size, chunk), 0) + start
            query_col = lax.broadcasted_iota(jnp.int32, (size, chunk), 1) + i * chunk
            seen = key_row <= query_col
        for h in range(heads):
            raw = dot(keys[rows, pair_lanes(h // 2)], query_of[h], NT)
            if masked:
                raw = jnp.where(seen, raw, -1e30)
            probs[h, to] = raw
            top_ref[h] = jnp.maximum(top_ref[h], fold(raw, jnp.max))

    sweep(score)
    top = [jnp.max(top_ref[h], axis=0, keepdims=True) for h in range(heads)]

    def mix(start, held, size, masked):
        rows, to = pl.ds(start, size), pl.ds(held, size)
        for h in range(heads):
            weight = jnp.exp(probs[h, to] - top[h])
            probs[h, to] = weight
            total_ref[h] += fold(weight, jnp.sum)
            mix_ref[head_rows(h)] += dot(values_t[head_rows(h), rows], weight.astype(LOW), NN)

    sweep(mix)
    inverse = [1.0 / jnp.sum(total_ref[h], axis=0, keepdims=True) for h in range(heads)]
    attended = jnp.concatenate(
        [mix_ref[head_rows(h)] * inverse[h] for h in range(heads)], axis=0
    )
    shared = grad.astype(WIDE).T * attended
    inner = [jnp.sum(shared[head_rows(h)], axis=0, keepdims=True) for h in range(heads)]
    att_stage[slot] = attended.T.astype(LOW)
    for copy in row_copies(0, slot):
        copy.start()

    def back(start, held, size, masked):
        rows, to = pl.ds(start, size), pl.ds(held, size)
        for n in range(group):
            value = values[rows, pair_lanes(n)]
            weights, grads = [], []
            for h in (2 * n, 2 * n + 1):
                weight = probs[h, to] * inverse[h]
                weight_grad = dot(value, grad_of[h], NT)
                score_grad = (weight * (weight_grad - inner[h])).astype(LOW)
                weights.append(weight.astype(LOW))
                grads.append(score_grad)
            value_sum[rows, pair_lanes(n)] += dot(
                jnp.concatenate(weights, axis=1), grad_pair[n], NN
            )
            key = keys[rows, pair_lanes(n)]
            back_ref[:, pair_lanes(n)] += dot(
                jnp.concatenate(grads, axis=0),
                jnp.concatenate([one_head(key, h) for h in range(2)], axis=0),
                TN,
            )
            key_sum[rows, pair_lanes(n)] += dot(
                jnp.concatenate(grads, axis=1), query_pair[n], NN
            )

    sweep(back)
    query_stage[slot] = turned(back_ref[...] * scale, tab, -1.0).astype(LOW)
    for copy in row_copies(1, slot):
        copy.start()

    @pl.when(i == chunks - 1)
    def _():
        @pl.loop(0, chunks)
        def _(n):
            rows = pl.ds(pl.multiple_of(n * chunk, chunk), chunk)
            key_stage[rows] = turned(key_sum[rows], tables(rows), -1.0).astype(LOW)
            value_stage[rows] = value_sum[rows].astype(LOW)
            for r in range(per):
                for copy in col_copies(n * per + r):
                    copy.start()

        for at in range(2):
            for which in range(2):
                for copy in row_copies(which, at):
                    copy.wait()

        @pl.loop(0, chunks * per)
        def _(n):
            for copy in col_copies(n):
                copy.wait()


def attention(qkv, grad, where, tabs, lanes, which, head_dim):
    rows = grad.shape[0]
    chunk, blk = CHUNK, BLK
    per, chunks, blocks = chunk // blk, rows // chunk, rows // blk
    group = lanes // LANES
    heads = 2 * group
    qkv_blocks = qkv.reshape(blocks, blk, qkv.shape[1])
    grad_blocks = grad.reshape(blocks, blk, grad.shape[1])

    def spec(column, r):
        return pl.BlockSpec((1, blk, lanes), lambda i, at: (at[i * per + r], 0, column))

    in_specs = [spec(3 * which + part, r) for part in range(3) for r in range(per)]
    in_specs += [spec(which, r) for r in range(per)]
    in_specs += [pl.BlockSpec((rows, LANES), lambda i, at: (0, 0), pipeline_mode=pl.Buffered(1))] * 3
    operands = [qkv_blocks] * (3 * per) + [grad_blocks] * per + list(tabs)
    kernel = functools.partial(
        attention_kernel,
        chunk=chunk,
        chunks=chunks,
        full_chunks=PROMPT // chunk,
        blk=blk,
        group=group,
        scale=1.0 / math.sqrt(head_dim),
    )
    attended, grads = pl.pallas_call(
        kernel,
        out_shape=(
            jax.ShapeDtypeStruct((blocks, blk, lanes), LOW),
            jax.ShapeDtypeStruct((blocks, blk, 3 * lanes), LOW),
        ),
        grid_spec=pltpu.PrefetchScalarGridSpec(
            num_scalar_prefetch=1,
            grid=(chunks,),
            in_specs=in_specs,
            out_specs=[pl.BlockSpec(memory_space=pl.ANY)] * 2,
            scratch_shapes=[
                pltpu.VMEM((rows, lanes), LOW),
                pltpu.VMEM((rows, lanes), LOW),
                pltpu.VMEM((lanes, rows), LOW),
                pltpu.VMEM((heads, PROMPT + chunk, chunk), WIDE),
                pltpu.VMEM((rows, lanes), WIDE),
                pltpu.VMEM((rows, lanes), WIDE),
                pltpu.VMEM((heads, 8, chunk), WIDE),
                pltpu.VMEM((heads, 8, chunk), WIDE),
                pltpu.VMEM((lanes, chunk), WIDE),
                pltpu.VMEM((chunk, lanes), WIDE),
                pltpu.VMEM((2, chunk, lanes), LOW),
                pltpu.VMEM((2, chunk, lanes), LOW),
                pltpu.VMEM((rows, lanes), LOW),
                pltpu.VMEM((rows, lanes), LOW),
                pltpu.SemaphoreType.DMA((2, 2, per)),
                pltpu.SemaphoreType.DMA((2, blocks)),
            ],
        ),
        compiler_params=pltpu.CompilerParams(
            dimension_semantics=("arbitrary",), vmem_limit_bytes=56 << 20
        ),
        cost_estimate=LITTLE,
        name="attention",
    )(where, *operands)
    return attended.reshape(rows, lanes), grads.reshape(rows, 3 * lanes)


def after(value, *others):
    return lax.optimization_barrier((value,) + others)[0] if others else value


def ring_of(count):
    order = list(range(count // 2)) + list(range(count - 1, count // 2 - 1, -1))
    ahead = [(order[n], order[(n + 1) % count]) for n in range(count)]
    return order, ahead, [(b, a) for a, b in ahead]


def rank_of(offset, count):
    offset %= count
    if offset == 0 or 2 * offset == count:
        return max(2 * offset - 1, 0)
    return 2 * offset if 2 * offset < count else 2 * (count - offset) - 1


def ring_pieces(own, axis, gate=()):
    count = lax.axis_size(axis)
    _, ahead, behind = ring_of(count)
    pieces, half = [own], own.shape[0] // 2
    from_behind = from_ahead = own
    for _ in range(count // 2 - 1):
        from_behind = lax.ppermute(from_behind, axis, ahead)
        from_ahead = lax.ppermute(from_ahead, axis, behind)
        pieces += [from_behind, from_ahead]
    if gate:
        from_behind, from_ahead = after(from_behind, *gate), after(from_ahead, *gate)
    far = [
        lax.ppermute(from_behind[:half], axis, ahead),
        lax.ppermute(from_ahead[half:], axis, behind),
    ]
    return pieces + far


def ring_reduce(part, own, axis, staged=False):
    count = lax.axis_size(axis)
    _, ahead, behind = ring_of(count)
    far = part(count - 1)
    half = far.shape[0] // 2

    def plus(a, b):
        return (a.astype(WIDE) + b.astype(WIDE)).astype(LOW)

    up, down = lax.ppermute(far[:half], axis, ahead), lax.ppermute(far[half:], axis, behind)
    first = second = last = (up, down)
    if count == 2:
        mine = own(first, second).astype(WIDE)
        return mine + jnp.concatenate(first, axis=0).astype(WIDE), first, second, last
    for s in range(count // 2 - 1, 0, -1):
        to_ahead, to_behind = part(2 * s), part(2 * s - 1)
        if s == count // 2 - 1:
            up = lax.ppermute(plus(to_ahead[:half], up), axis, ahead)
            down = lax.ppermute(plus(to_behind[half:], down), axis, behind)
            second = (up, down)
            gate = second if staged else ()
            free_up = lax.ppermute(after(to_ahead[half:], *gate), axis, ahead)
            free_down = lax.ppermute(after(to_behind[:half], *gate), axis, behind)
            last = (free_up, free_down)
            up = jnp.concatenate([up, free_up], axis=0)
            down = jnp.concatenate([free_down, down], axis=0)
        else:
            up = lax.ppermute(plus(to_ahead, up), axis, ahead)
            down = lax.ppermute(plus(to_behind, down), axis, behind)
            last = (up, down)
    total = own(first, second).astype(WIDE) + up.astype(WIDE) + down.astype(WIDE)
    return total, first, second, last


def ring_exchange(part, axis):
    count = lax.axis_size(axis)
    order, _, _ = ring_of(count)
    got = [None] * count
    got[0] = part(0)
    for offset in range(1, count):
        hops = [(order[n], order[(n + offset) % count]) for n in range(count)]
        got[rank_of(-offset, count)] = lax.ppermute(part(rank_of(offset, count)), axis, hops)
    return got


def sum_everywhere(values, axes):
    for axis in axes:
        count, span = lax.axis_size(axis), 1
        while span < count:
            pairs = [(n, n ^ span) for n in range(count)]
            values = values + lax.ppermute(values, axis, pairs)
            span *= 2
    return values


def gelu_and_slope(h):
    inner_scale = math.sqrt(2.0 / math.pi)
    square = h * h
    t = jnp.tanh(h * (inner_scale + (inner_scale * 0.044715) * square))
    half = 0.5 * h
    rise = 0.5 + 0.5 * t
    bend = inner_scale + (3.0 * inner_scale * 0.044715) * square
    return (h * rise).astype(LOW), (rise + (half - half * t * t) * bend).astype(LOW)


def expand_kernel(x_ref, w_ref, b_ref, act_ref, slope_ref, *, cols):
    x = x_ref[...]
    for n in range(w_ref.shape[1] // cols):
        at = slice(n * cols, (n + 1) * cols)
        act, slope = gelu_and_slope(dot(x, w_ref[:, at], NN) + b_ref[:, at])
        act_ref[:, at] = act
        slope_ref[:, at] = slope


def expand(x, w, b):
    rows, width = x.shape
    hidden = w.shape[1]
    tile = 320
    out = jax.ShapeDtypeStruct((rows, hidden), LOW)
    return pl.pallas_call(
        functools.partial(expand_kernel, cols=min(512, hidden)),
        out_shape=(out, out),
        grid=(rows // tile,),
        in_specs=[
            pl.BlockSpec((tile, width), lambda i: (i, 0)),
            pl.BlockSpec((width, hidden), lambda i: (0, 0), pipeline_mode=pl.Buffered(1)),
            pl.BlockSpec((1, hidden), lambda i: (0, 0)),
        ],
        out_specs=[pl.BlockSpec((tile, hidden), lambda i: (i, 0))] * 2,
        compiler_params=pltpu.CompilerParams(
            dimension_semantics=("arbitrary",), vmem_limit_bytes=48 << 20
        ),
        cost_estimate=pl.CostEstimate(
            flops=2 * rows * width * hidden,
            bytes_accessed=2 * (rows * width + width * hidden + 2 * rows * hidden),
            transcendentals=rows * hidden,
        ),
        name="expand",
    )(x, w, b.astype(WIDE)[None])


def input_grad_kernel(*refs, terms):
    grads, weights = refs[:terms], refs[terms : 2 * terms]
    normed_ref, out_ref, sums_ref = refs[2 * terms :]
    total = sum(dot(g[...], w[...], NT) for g, w in zip(grads, weights))
    out_ref[...] = total.astype(LOW)
    sums_ref[0:1] = jnp.sum(total, axis=0, keepdims=True)
    sums_ref[1:2] = jnp.sum(total * normed_ref[...].astype(WIDE), axis=0, keepdims=True)


def input_grad(grads, weights, normed, rank, rows):
    width = normed.shape[1]
    cols = 512
    keep = pl.Buffered(1)
    in_specs = [
        pl.BlockSpec((rows, g.shape[1]), lambda i: (rank, 0), pipeline_mode=keep) for g in grads
    ]
    in_specs += [
        pl.BlockSpec((cols, g.shape[1]), lambda i, at=at: (i, at))
        for g, (_, at) in zip(grads, weights)
    ]
    in_specs.append(pl.BlockSpec((rows, cols), lambda i: (rank, i)))
    return pl.pallas_call(
        functools.partial(input_grad_kernel, terms=len(grads)),
        out_shape=(
            jax.ShapeDtypeStruct((rows, width), LOW),
            jax.ShapeDtypeStruct((2, width), WIDE),
        ),
        grid=(width // cols,),
        in_specs=in_specs,
        out_specs=[
            pl.BlockSpec((rows, cols), lambda i: (0, i)),
            pl.BlockSpec((2, cols), lambda i: (0, i)),
        ],
        compiler_params=pltpu.CompilerParams(
            dimension_semantics=("arbitrary",), vmem_limit_bytes=48 << 20
        ),
        cost_estimate=LITTLE,
        name="input_grad",
    )(*grads, *[w for w, _ in weights], normed)


def pair_grad_kernel(x_ref, y_ref, a_ref, b_ref, out_ref):
    split = a_ref.shape[1]
    out_ref[:, :split] = dot(x_ref[...], a_ref[...], TN).astype(LOW)
    out_ref[:, split:] = dot(y_ref[...], b_ref[...], TN).astype(LOW)


def pair_grad(x, y, a, b):
    rows, width = x.shape
    columns = a.shape[1] + b.shape[1]
    tile = 512
    keep = pl.Buffered(1)
    return pl.pallas_call(
        pair_grad_kernel,
        out_shape=jax.ShapeDtypeStruct((width, columns), LOW),
        grid=(width // tile,),
        in_specs=[
            pl.BlockSpec((rows, tile), lambda i: (0, i)),
            pl.BlockSpec((rows, tile), lambda i: (0, i)),
            pl.BlockSpec(a.shape, lambda i: (0, 0), pipeline_mode=keep),
            pl.BlockSpec(b.shape, lambda i: (0, 0), pipeline_mode=keep),
        ],
        out_specs=pl.BlockSpec((tile, columns), lambda i: (i, 0)),
        compiler_params=pltpu.CompilerParams(
            dimension_semantics=("arbitrary",), vmem_limit_bytes=48 << 20
        ),
        cost_estimate=LITTLE,
        name="pair_grad",
    )(x, y, a, b)


def rope_tables(rows):
    place = jnp.arange(rows, dtype=jnp.int32)
    pos = jnp.where(place < PROMPT, place, PROMPT + (place - PROMPT) % CLEN)
    half = ROT // 2
    freq = 10000.0 ** (-2.0 * jnp.arange(half, dtype=WIDE) / ROT)
    angle = pos.astype(WIDE)[:, None] * freq[None, :]
    cosine, sine = jnp.cos(angle), jnp.sin(angle)
    zero, one = jnp.zeros_like(cosine), jnp.ones_like(cosine)
    tabs = ((cosine, cosine, one, one), (zero, sine, zero, zero), (-sine, zero, zero, zero))
    return [jnp.concatenate(tab * (LANES // (4 * half)), axis=1) for tab in tabs]


def shards(
    tokens,
    cotangent,
    block_table,
    ln_gain,
    ln_bias,
    w_qkv,
    b_qkv,
    w_dense,
    b_dense,
    w_fc1,
    b_fc1,
    w_fc2,
    b_fc2,
):
    _, local_rows, width = tokens.shape
    head_dim = width // HEADS
    count = lax.axis_size("ctx")
    me = lax.axis_index("ctx")
    rows = local_rows * count
    local_blocks = local_rows // BLK
    each = w_dense.shape[0]
    hidden = w_fc2.shape[0]
    gain, shift = ln_gain.astype(WIDE), ln_bias.astype(WIDE)

    def of_rank(whole, rank):
        return whole[rank * local_rows : (rank + 1) * local_rows]

    order, _, _ = ring_of(count)
    places = [0] * count
    for n, device in enumerate(order):
        places[device] = n
    places = jnp.asarray(places, jnp.int32)
    ranks = jnp.asarray([rank_of(n, count) for n in range(count)], jnp.int32)
    slots = jnp.arange(rows // BLK, dtype=jnp.int32)
    offset = (places[slots // local_blocks] - places[me]) % count
    held_at = ranks[offset] * local_blocks + slots % local_blocks
    hit = block_table[0][None, :] == slots[:, None]
    where = jnp.sum(jnp.where(hit, held_at[None, :], 0), axis=1).astype(jnp.int32)

    own_tokens = tokens[0].astype(WIDE)
    own_grad = cotangent[0]
    average = jnp.mean(own_tokens, axis=-1, keepdims=True)
    centred = own_tokens - average
    rstd = lax.rsqrt(jnp.mean(centred * centred, axis=-1, keepdims=True) + 1e-05)
    xhat = centred * rstd
    normed_own = (xhat * gain + shift).astype(LOW)

    def gather_rows(shard):
        return lax.all_gather(shard, "fsdp", axis=0, tiled=True)

    def scatter_rows(whole):
        return lax.psum_scatter(whole, "fsdp", scatter_dimension=0, tiled=True)

    lanes = 2 * LANES if each % (2 * LANES) == 0 else LANES
    groups = each // lanes

    def by_group(values):
        cut = values.reshape(-1, 3, groups, lanes)
        return jnp.swapaxes(cut, 1, 2).reshape(-1, 3 * each)

    normed_pieces = ring_pieces(normed_own, "ctx")
    normed = jnp.concatenate(normed_pieces, axis=0)
    attention_shard = jnp.concatenate([by_group(w_qkv), w_dense.T], axis=1)
    fc1_weight = gather_rows(w_fc1)
    fc2_turned = gather_rows(after(w_fc2.T, *normed_pieces[1:-2]))
    attention_weight = gather_rows(after(attention_shard, *normed_pieces[-2:]))
    qkv_weight, dense_turned = attention_weight[:, : 3 * each], attention_weight[:, 3 * each :]

    fc1_bias = lax.dynamic_slice_in_dim(b_fc1, me * hidden, hidden, 0)
    qkv_bias = lax.dynamic_slice_in_dim(b_qkv.reshape(3, width), me * each, each, 1)
    activated, slope = expand(normed, fc1_weight, fc1_bias)

    sent_grad = after(own_grad, *normed_pieces[-2:])
    grad_pieces = ring_pieces(sent_grad, "ctx", gate=(activated,))
    ff_part = dot(activated, fc2_turned, NT).astype(LOW)
    grads = jnp.concatenate([after(piece, ff_part) for piece in grad_pieces], axis=0)
    ff_sum, first, second, last = ring_reduce(
        lambda rank: of_rank(ff_part, rank), lambda *_: of_rank(ff_part, 0), "ctx", staged=True
    )

    gated = after(grads, ff_part)
    expanded_grad = (dot(gated, fc2_turned, NN) * slope.astype(WIDE)).astype(LOW)
    d_fc2_part = dot(after(grads, expanded_grad, *first), activated, TN).astype(LOW)
    d_fc2 = scatter_rows(d_fc2_part)
    qkv = dot(after(normed, d_fc2_part), qkv_weight, NN)
    qkv = (qkv + by_group(qkv_bias)[0].astype(WIDE)).astype(LOW)
    attended_grad = dot(after(grads, qkv), dense_turned, NN).astype(LOW)
    gated = after(normed, attended_grad, *second)
    d_fc1_part = dot(gated, expanded_grad, TN).astype(LOW)
    d_fc1 = scatter_rows(d_fc1_part)

    dense_pieces = ring_pieces(after(dense_turned, *second), "ctx")
    dense_whole = jnp.concatenate(
        dense_pieces[:-2] + [jnp.concatenate(dense_pieces[-2:], axis=0)], axis=1
    )

    tabs = rope_tables(rows)
    attended, qkv_grads, d_attention, swapped = [], [], [], []
    ordered = (d_fc1_part,)
    for which in range(groups):
        got, got_grads = attention(
            after(qkv, *ordered), attended_grad, where, tabs, lanes, which, head_dim
        )
        attended.append(got)
        qkv_grads.append(got_grads)
        if which < groups - 1:
            swapped.append(ring_exchange(lambda rank, got=got: of_rank(got, rank), "ctx"))
            gated = after(normed, d_fc2, *last, *dense_pieces[1:-2]) if which == 0 else normed
            d_part = pair_grad(gated, grads, got_grads, got)
            ordered = (d_part,)
            d_attention.append(scatter_rows(d_part))

    weights = [(attention_weight, which) for which in range(groups)] + [(fc1_weight, 0)]
    parts, sums = [None] * count, 0.0
    early_swaps = [piece for pieces in swapped for piece in pieces]
    turn = after(expanded_grad, d_fc1, *dense_pieces[-2:], *early_swaps, *attended)
    swapped.append(ring_exchange(lambda rank: of_rank(attended[-1], rank), "ctx"))

    def input_part(rank, turn):
        return input_grad(qkv_grads + [turn], weights, normed, rank, local_rows)

    for rank in range(count - 1, 0, -1):
        if rank == 1:
            turn = after(turn, *swapped[-1])
        parts[rank], part_sums = input_part(rank, turn)
        sums = sums + part_sums
        turn = after(turn, parts[rank])
        if rank == count - 1:
            gated = after(normed, parts[rank], *d_attention)
            d_part = pair_grad(gated, grads, qkv_grads[-1], attended[-1])
            d_attention.append(scatter_rows(d_part))
            turn = after(turn, d_part)

    own_sums = []

    def own_part(first, second):
        part, part_sums = input_part(0, after(turn, *first))
        own_sums.append(part_sums)
        return part

    normed_grad, *_ = ring_reduce(lambda rank: parts[rank], own_part, "ctx")
    sums = sums + own_sums[0]

    d_qkv = jnp.concatenate(
        [part[:, : 3 * lanes].reshape(-1, 3, lanes) for part in d_attention], axis=2
    ).astype(WIDE)
    d_dense = jnp.concatenate([part[:, 3 * lanes :].T for part in d_attention], axis=0)

    attended_own = jnp.concatenate(
        [swapped[which][rank] for rank in range(count) for which in range(groups)], axis=1
    )
    out_sum = ff_sum + dot(attended_own, dense_whole, NT)
    output = own_tokens + out_sum + b_dense.astype(WIDE) + b_fc2.astype(WIDE)

    scaled = normed_grad * gain
    d_tokens = own_grad.astype(WIDE) + rstd * (
        scaled
        - jnp.mean(scaled, axis=-1, keepdims=True)
        - xhat * jnp.mean(scaled * xhat, axis=-1, keepdims=True)
    )

    qkv_bias_part = jnp.concatenate(
        [jnp.sum(part.astype(WIDE), axis=0).reshape(3, lanes) for part in qkv_grads], axis=1
    )
    fc1_bias_part = jnp.sum(expanded_grad.astype(WIDE), axis=0)
    qkv_bias_wide = lax.dynamic_update_slice_in_dim(
        jnp.zeros((3, width), WIDE), qkv_bias_part, me * each, 1
    ).reshape(-1)
    fc1_bias_wide = lax.dynamic_update_slice_in_dim(
        jnp.zeros((b_fc1.shape[0],), WIDE), fc1_bias_part, me * hidden, 0
    )
    small = sum_everywhere(
        jnp.concatenate(
            [
                sums.reshape(-1),
                qkv_bias_wide,
                jnp.sum(sent_grad.astype(WIDE), axis=0),
                fc1_bias_wide,
            ]
        ),
        ("fsdp", "ctx"),
    )
    d_shift, with_normed, d_b_qkv, d_b_out, d_b_fc1 = jnp.split(
        small, [width, 2 * width, 5 * width, 6 * width]
    )
    d_gain = (with_normed - shift * d_shift) / gain
    return (
        output.astype(LOW)[None],
        d_tokens.astype(LOW)[None],
        d_gain,
        d_shift,
        d_qkv,
        d_b_qkv,
        d_dense.astype(WIDE),
        d_b_out,
        d_fc1.astype(WIDE),
        d_b_fc1,
        d_fc2.T.astype(WIDE),
        d_b_out,
    )


def solution(mesh):
    in_specs = (
        P("fsdp", "ctx", None),
        P("fsdp", "ctx", None),
        P("fsdp", None),
        P(),
        P(),
        P("fsdp", None, "ctx"),
        P(),
        P("ctx", "fsdp"),
        P(),
        P("fsdp", "ctx"),
        P(),
        P("ctx", "fsdp"),
        P(),
    )
    out_specs = (
        P("fsdp", "ctx", None),
        P("fsdp", "ctx", None),
        P(),
        P(),
        P("fsdp", None, "ctx"),
        P(),
        P("ctx", "fsdp"),
        P(),
        P("fsdp", "ctx"),
        P(),
        P("ctx", "fsdp"),
        P(),
    )
    return jax.shard_map(shards, mesh=mesh, in_specs=in_specs, out_specs=out_specs, check_vma=False)
```

```python
import functools
import math

import jax
import jax.numpy as jnp
from jax import lax
from jax.experimental import pallas as pl
from jax.experimental.pallas import tpu as pltpu
from jax.sharding import PartitionSpec as P

HEADS = 32
ROT = 32
PROMPT = 2048
CLEN = 256
BLK = 64
CHUNK = 256
LANES = 128
NT = (((1,), (1,)), ((), ()))
NN = (((1,), (0,)), ((), ()))
TN = (((0,), (0,)), ((), ()))
LOW = jnp.bfloat16
WIDE = jnp.float32
LITTLE = pl.CostEstimate(flops=1000000, bytes_accessed=1000000, transcendentals=0)


def dot(left, right, dims):
    return lax.dot_general(left, right, dims, preferred_element_type=WIDE)


def attention_kernel(where_ref, *refs, chunk, chunks, full_chunks, blk, group, scale):
    per = chunk // blk
    q_in, k_in, v_in, g_in = (refs[n * per : (n + 1) * per] for n in range(4))
    cos_ref, up_ref, down_ref, att_hbm, grad_hbm = refs[4 * per : 4 * per + 5]
    (
        keys,
        values,
        values_t,
        probs,
        key_sum,
        value_sum,
        top_ref,
        total_ref,
        mix_ref,
        back_ref,
        att_stage,
        query_stage,
        key_stage,
        value_stage,
        row_sem,
        col_sem,
    ) = refs[4 * per + 5 :]
    i = pl.program_id(0)
    slot = lax.rem(i, 2)
    half = LANES // 2
    lanes = group * LANES
    heads = 2 * group
    first = lax.broadcasted_iota(jnp.int32, (1, LANES), 1) < half

    def columns(part):
        return pl.ds(part * lanes, lanes)

    def row_copies(which, at):
        stage, target = ((att_stage, att_hbm), (query_stage, grad_hbm))[which]
        return [
            pltpu.make_async_copy(
                stage.at[at, pl.ds(r * blk, blk)],
                target.at[where_ref[i * per + r], :, columns(0)],
                row_sem.at[at, which, r],
            )
            for r in range(per)
        ]

    def col_copies(n):
        block = where_ref[n]
        rows = pl.ds(pl.multiple_of(n * blk, blk), blk)
        return (
            pltpu.make_async_copy(
                key_stage.at[rows], grad_hbm.at[block, :, columns(1)], col_sem.at[0, n]
            ),
            pltpu.make_async_copy(
                value_stage.at[rows], grad_hbm.at[block, :, columns(2)], col_sem.at[1, n]
            ),
        )

    def load(parts):
        return jnp.concatenate([part[0] for part in parts], axis=0)

    def tables(rows):
        return cos_ref[rows], up_ref[rows], down_ref[rows]

    quarter = ROT // 2

    def turned(x, tab, sign):
        return jnp.concatenate(
            [
                y * tab[0]
                + sign
                * (pltpu.roll(y, quarter, 1) * tab[1] + pltpu.roll(y, LANES - quarter, 1) * tab[2])
                for y in (x[:, n * LANES : (n + 1) * LANES] for n in range(group))
            ],
            axis=1,
        )

    def one_head(x, h):
        pair = x[:, (h // 2) * LANES : (h // 2 + 1) * LANES]
        nothing = jnp.zeros_like(pair)
        return jnp.where(first, pair, nothing) if h % 2 == 0 else jnp.where(first, nothing, pair)

    @pl.when(i >= 2)
    def _():
        for which in range(2):
            for copy in row_copies(which, slot):
                copy.wait()

    here = pl.ds(pl.multiple_of(i * chunk, chunk), chunk)
    tab = tables(here)
    query = (turned(load(q_in).astype(WIDE), tab, 1.0) * scale).astype(LOW)
    key_new = turned(load(k_in).astype(WIDE), tab, 1.0)
    value_new = load(v_in)
    grad = load(g_in)
    keys[here] = key_new.astype(LOW)
    values[here] = value_new
    values_t[:, here] = value_new.astype(WIDE).T.astype(LOW)
    key_sum[here] = jnp.zeros((chunk, lanes), WIDE)
    value_sum[here] = jnp.zeros((chunk, lanes), WIDE)
    top_ref[...] = jnp.full(top_ref.shape, -1e30, WIDE)
    total_ref[...] = jnp.zeros(total_ref.shape, WIDE)
    mix_ref[...] = jnp.zeros(mix_ref.shape, WIDE)
    back_ref[...] = jnp.zeros(back_ref.shape, WIDE)
    query_of = [one_head(query, h) for h in range(heads)]
    grad_of = [one_head(grad, h) for h in range(heads)]
    query_pair = [
        jnp.concatenate(query_of[2 * n : 2 * n + 2], axis=0) for n in range(group)
    ]
    grad_pair = [jnp.concatenate(grad_of[2 * n : 2 * n + 2], axis=0) for n in range(group)]
    before = jnp.minimum(i, full_chunks)
    doubles = before // 2
    odd = before - 2 * doubles

    def fold(x, how):
        return how(x.reshape(x.shape[0] // 8, 8, chunk), axis=0)

    def pair_lanes(n):
        return slice(n * LANES, (n + 1) * LANES)

    def head_rows(h):
        return slice(h * half, (h + 1) * half)

    def sweep(tile):
        def double(t, carry):
            start = pl.multiple_of(t * 2 * chunk, 2 * chunk)
            tile(start, start, 2 * chunk, False)
            return carry

        lax.fori_loop(0, doubles, double, 0)
        held = pl.multiple_of(doubles * 2 * chunk, chunk)

        @pl.when(odd == 1)
        def _():
            tile(held, held, 2 * chunk, True)

        @pl.when(odd == 0)
        def _():
            tile(pl.multiple_of(i * chunk, chunk), held, chunk, True)

    def score(start, held, size, masked):
        rows, to = pl.ds(start, size), pl.ds(held, size)
        if masked:
            key_row = lax.broadcasted_iota(jnp.int32, (size, chunk), 0) + start
            query_col = lax.broadcasted_iota(jnp.int32, (size, chunk), 1) + i * chunk
            seen = key_row <= query_col
        for h in range(heads):
            raw = dot(keys[rows, pair_lanes(h // 2)], query_of[h], NT)
            if masked:
                raw = jnp.where(seen, raw, -1e30)
            probs[h, to] = raw
            top_ref[h] = jnp.maximum(top_ref[h], fold(raw, jnp.max))

    sweep(score)
    top = [jnp.max(top_ref[h], axis=0, keepdims=True) for h in range(heads)]

    def mix(start, held, size, masked):
        rows, to = pl.ds(start, size), pl.ds(held, size)
        for h in range(heads):
            weight = jnp.exp(probs[h, to] - top[h])
            probs[h, to] = weight
            total_ref[h] += fold(weight, jnp.sum)
            mix_ref[head_rows(h)] += dot(values_t[head_rows(h), rows], weight.astype(LOW), NN)

    sweep(mix)
    inverse = [1.0 / jnp.sum(total_ref[h], axis=0, keepdims=True) for h in range(heads)]
    attended = jnp.concatenate(
        [mix_ref[head_rows(h)] * inverse[h] for h in range(heads)], axis=0
    )
    shared = grad.astype(WIDE).T * attended
    inner = [jnp.sum(shared[head_rows(h)], axis=0, keepdims=True) for h in range(heads)]
    att_stage[slot] = attended.T.astype(LOW)
    for copy in row_copies(0, slot):
        copy.start()

    def back(start, held, size, masked):
        rows, to = pl.ds(start, size), pl.ds(held, size)
        for n in range(group):
            value = values[rows, pair_lanes(n)]
            weights, grads = [], []
            for h in (2 * n, 2 * n + 1):
                weight = probs[h, to] * inverse[h]
                weight_grad = dot(value, grad_of[h], NT)
                score_grad = (weight * (weight_grad - inner[h])).astype(LOW)
                weights.append(weight.astype(LOW))
                grads.append(score_grad)
            value_sum[rows, pair_lanes(n)] += dot(
                jnp.concatenate(weights, axis=1), grad_pair[n], NN
            )
            key = keys[rows, pair_lanes(n)]
            back_ref[:, pair_lanes(n)] += dot(
                jnp.concatenate(grads, axis=0),
                jnp.concatenate([one_head(key, h) for h in range(2)], axis=0),
                TN,
            )
            key_sum[rows, pair_lanes(n)] += dot(
                jnp.concatenate(grads, axis=1), query_pair[n], NN
            )

    sweep(back)
    query_stage[slot] = turned(back_ref[...] * scale, tab, -1.0).astype(LOW)
    for copy in row_copies(1, slot):
        copy.start()

    @pl.when(i == chunks - 1)
    def _():
        @pl.loop(0, chunks)
        def _(n):
            rows = pl.ds(pl.multiple_of(n * chunk, chunk), chunk)
            key_stage[rows] = turned(key_sum[rows], tables(rows), -1.0).astype(LOW)
            value_stage[rows] = value_sum[rows].astype(LOW)
            for r in range(per):
                for copy in col_copies(n * per + r):
                    copy.start()

        for at in range(2):
            for which in range(2):
                for copy in row_copies(which, at):
                    copy.wait()

        @pl.loop(0, chunks * per)
        def _(n):
            for copy in col_copies(n):
                copy.wait()


def attention(qkv, grad, where, tabs, lanes, which, head_dim):
    rows = grad.shape[0]
    chunk, blk = CHUNK, BLK
    per, chunks, blocks = chunk // blk, rows // chunk, rows // blk
    group = lanes // LANES
    heads = 2 * group
    qkv_blocks = qkv.reshape(blocks, blk, qkv.shape[1])
    grad_blocks = grad.reshape(blocks, blk, grad.shape[1])

    def spec(column, r):
        return pl.BlockSpec((1, blk, lanes), lambda i, at: (at[i * per + r], 0, column))

    in_specs = [spec(3 * which + part, r) for part in range(3) for r in range(per)]
    in_specs += [spec(which, r) for r in range(per)]
    in_specs += [pl.BlockSpec((rows, LANES), lambda i, at: (0, 0), pipeline_mode=pl.Buffered(1))] * 3
    operands = [qkv_blocks] * (3 * per) + [grad_blocks] * per + list(tabs)
    kernel = functools.partial(
        attention_kernel,
        chunk=chunk,
        chunks=chunks,
        full_chunks=PROMPT // chunk,
        blk=blk,
        group=group,
        scale=1.0 / math.sqrt(head_dim),
    )
    attended, grads = pl.pallas_call(
        kernel,
        out_shape=(
            jax.ShapeDtypeStruct((blocks, blk, lanes), LOW),
            jax.ShapeDtypeStruct((blocks, blk, 3 * lanes), LOW),
        ),
        grid_spec=pltpu.PrefetchScalarGridSpec(
            num_scalar_prefetch=1,
            grid=(chunks,),
            in_specs=in_specs,
            out_specs=[pl.BlockSpec(memory_space=pl.ANY)] * 2,
            scratch_shapes=[
                pltpu.VMEM((rows, lanes), LOW),
                pltpu.VMEM((rows, lanes), LOW),
                pltpu.VMEM((lanes, rows), LOW),
                pltpu.VMEM((heads, PROMPT + chunk, chunk), WIDE),
                pltpu.VMEM((rows, lanes), WIDE),
                pltpu.VMEM((rows, lanes), WIDE),
                pltpu.VMEM((heads, 8, chunk), WIDE),
                pltpu.VMEM((heads, 8, chunk), WIDE),
                pltpu.VMEM((lanes, chunk), WIDE),
                pltpu.VMEM((chunk, lanes), WIDE),
                pltpu.VMEM((2, chunk, lanes), LOW),
                pltpu.VMEM((2, chunk, lanes), LOW),
                pltpu.VMEM((rows, lanes), LOW),
                pltpu.VMEM((rows, lanes), LOW),
                pltpu.SemaphoreType.DMA((2, 2, per)),
                pltpu.SemaphoreType.DMA((2, blocks)),
            ],
        ),
        compiler_params=pltpu.CompilerParams(
            dimension_semantics=("arbitrary",), vmem_limit_bytes=56 << 20
        ),
        cost_estimate=LITTLE,
        name="attention",
    )(where, *operands)
    return attended.reshape(rows, lanes), grads.reshape(rows, 3 * lanes)


def after(value, *others):
    return lax.optimization_barrier((value,) + others)[0] if others else value


def ring_of(count):
    order = list(range(count // 2)) + list(range(count - 1, count // 2 - 1, -1))
    ahead = [(order[n], order[(n + 1) % count]) for n in range(count)]
    return order, ahead, [(b, a) for a, b in ahead]


def rank_of(offset, count):
    offset %= count
    if offset == 0 or 2 * offset == count:
        return max(2 * offset - 1, 0)
    return 2 * offset if 2 * offset < count else 2 * (count - offset) - 1


def ring_pieces(own, axis, gate=()):
    count = lax.axis_size(axis)
    _, ahead, behind = ring_of(count)
    pieces, half = [own], own.shape[0] // 2
    from_behind = from_ahead = own
    for _ in range(count // 2 - 1):
        from_behind = lax.ppermute(from_behind, axis, ahead)
        from_ahead = lax.ppermute(from_ahead, axis, behind)
        pieces += [from_behind, from_ahead]
    if gate:
        from_behind, from_ahead = after(from_behind, *gate), after(from_ahead, *gate)
    far = [
        lax.ppermute(from_behind[:half], axis, ahead),
        lax.ppermute(from_ahead[half:], axis, behind),
    ]
    return pieces + far


def ring_reduce(part, axis, cuts=1, staged=False):
    count = lax.axis_size(axis)
    _, ahead, behind = ring_of(count)
    far = part(count - 1)
    half = far.shape[0] // 2

    def plus(a, b):
        return (a.astype(WIDE) + b.astype(WIDE)).astype(LOW)

    up, down = lax.ppermute(far[:half], axis, ahead), lax.ppermute(far[half:], axis, behind)
    hops = [(up, down)]
    if count == 2:
        return [(0, up), (half, down)], hops
    cut = half // cuts
    to_ahead, to_behind = part(count - 2), part(count - 3)
    got_up, got_down = {}, {}

    def loose():
        for n in range(cuts):
            at = half + n * cut
            gate = hops[-1] if staged else ()
            got_up[at] = lax.ppermute(after(to_ahead[at : at + cut], *gate), axis, ahead)
            at = n * cut
            got_down[at] = lax.ppermute(after(to_behind[at : at + cut], *gate), axis, behind)
            hops.append((got_up[half + at], got_down[at]))

    def summed():
        for n in range(cuts):
            at, span = n * cut, slice(n * cut, (n + 1) * cut)
            got_up[at] = lax.ppermute(plus(to_ahead[span], up[span]), axis, ahead)
            there = slice(half + at, half + at + cut)
            got_down[half + at] = lax.ppermute(plus(to_behind[there], down[span]), axis, behind)
            hops.append((got_up[at], got_down[half + at]))

    for send in (summed, loose) if staged else (loose, summed):
        send()
    if count == 4:
        return sorted(got_up.items()) + sorted(got_down.items()), hops
    up = jnp.concatenate([piece for _, piece in sorted(got_up.items())], axis=0)
    down = jnp.concatenate([piece for _, piece in sorted(got_down.items())], axis=0)
    for s in range(count // 2 - 2, 0, -1):
        up = lax.ppermute(plus(part(2 * s), up), axis, ahead)
        down = lax.ppermute(plus(part(2 * s - 1), down), axis, behind)
        hops.append((up, down))
    return [(0, up), (0, down)], hops


def ring_exchange(part, axis):
    count = lax.axis_size(axis)
    order, _, _ = ring_of(count)
    got = [None] * count
    got[0] = part(0)
    for offset in range(1, count):
        hops = [(order[n], order[(n + offset) % count]) for n in range(count)]
        got[rank_of(-offset, count)] = lax.ppermute(part(rank_of(offset, count)), axis, hops)
    return got


def sum_everywhere(values, axes):
    for axis in axes:
        count, span = lax.axis_size(axis), 1
        while span < count:
            pairs = [(n, n ^ span) for n in range(count)]
            values = values + lax.ppermute(values, axis, pairs)
            span *= 2
    return values


def gelu_and_slope(h):
    inner_scale = math.sqrt(2.0 / math.pi)
    square = h * h
    t = jnp.tanh(h * (inner_scale + (inner_scale * 0.044715) * square))
    half = 0.5 * h
    rise = 0.5 + 0.5 * t
    bend = inner_scale + (3.0 * inner_scale * 0.044715) * square
    return (h * rise).astype(LOW), (rise + (half - half * t * t) * bend).astype(LOW)


def expand_kernel(x_ref, w_ref, b_ref, act_ref, slope_ref, *, cols):
    x = x_ref[...]
    for n in range(w_ref.shape[1] // cols):
        at = slice(n * cols, (n + 1) * cols)
        act, slope = gelu_and_slope(dot(x, w_ref[:, at], NN) + b_ref[:, at])
        act_ref[:, at] = act
        slope_ref[:, at] = slope


def expand(x, w, b):
    rows, width = x.shape
    hidden = w.shape[1]
    tile = 320
    out = jax.ShapeDtypeStruct((rows, hidden), LOW)
    return pl.pallas_call(
        functools.partial(expand_kernel, cols=min(512, hidden)),
        out_shape=(out, out),
        grid=(rows // tile,),
        in_specs=[
            pl.BlockSpec((tile, width), lambda i: (i, 0)),
            pl.BlockSpec((width, hidden), lambda i: (0, 0), pipeline_mode=pl.Buffered(1)),
            pl.BlockSpec((1, hidden), lambda i: (0, 0)),
        ],
        out_specs=[pl.BlockSpec((tile, hidden), lambda i: (i, 0))] * 2,
        compiler_params=pltpu.CompilerParams(
            dimension_semantics=("arbitrary",), vmem_limit_bytes=48 << 20
        ),
        cost_estimate=pl.CostEstimate(
            flops=2 * rows * width * hidden,
            bytes_accessed=2 * (rows * width + width * hidden + 2 * rows * hidden),
            transcendentals=rows * hidden,
        ),
        name="expand",
    )(x, w, b.astype(WIDE)[None])


def input_grad_kernel(*refs, terms, ranks):
    grads, weights = refs[: terms * ranks], refs[terms * ranks : terms * ranks + terms]
    rest = refs[terms * (ranks + 1) :]
    normed_refs, out_refs, sums_ref = rest[:ranks], rest[ranks : 2 * ranks], rest[2 * ranks]
    plain = weighted = 0.0
    for n in range(ranks):
        mine = grads[n * terms : (n + 1) * terms]
        total = sum(dot(g[...], w[...], NT) for g, w in zip(mine, weights))
        out_refs[n][...] = total.astype(LOW)
        plain += jnp.sum(total, axis=0, keepdims=True)
        weighted += jnp.sum(total * normed_refs[n][...].astype(WIDE), axis=0, keepdims=True)
    sums_ref[0:1] = plain
    sums_ref[1:2] = weighted


def input_grad(grads, weights, normed, ranks, rows):
    width = normed.shape[1]
    cols = 512
    keep = pl.Buffered(1)
    in_specs = [
        pl.BlockSpec((rows, g.shape[1]), lambda i, rank=rank: (rank, 0), pipeline_mode=keep)
        for rank in ranks
        for g in grads
    ]
    in_specs += [
        pl.BlockSpec((cols, g.shape[1]), lambda i, at=at: (i, at))
        for g, (_, at) in zip(grads, weights)
    ]
    in_specs += [pl.BlockSpec((rows, cols), lambda i, rank=rank: (rank, i)) for rank in ranks]
    *parts, sums = pl.pallas_call(
        functools.partial(input_grad_kernel, terms=len(grads), ranks=len(ranks)),
        out_shape=[jax.ShapeDtypeStruct((rows, width), LOW)] * len(ranks)
        + [jax.ShapeDtypeStruct((2, width), WIDE)],
        grid=(width // cols,),
        in_specs=in_specs,
        out_specs=[pl.BlockSpec((rows, cols), lambda i: (0, i))] * len(ranks)
        + [pl.BlockSpec((2, cols), lambda i: (0, i))],
        compiler_params=pltpu.CompilerParams(
            dimension_semantics=("arbitrary",), vmem_limit_bytes=56 << 20
        ),
        cost_estimate=LITTLE,
        name="input_grad",
    )(*grads * len(ranks), *[w for w, _ in weights], *[normed] * len(ranks))
    return parts, sums


def place_kernel(*refs, starts, count, groups):
    pieces = refs[: count * groups]
    dense = refs[count * groups : count * groups + count + 1]
    rest = refs[count * (groups + 1) + 1 :]
    token_ref, bias_ref, own_ref = rest[:3]
    terms, out_ref, acc = rest[3:-2], rest[-2], rest[-1]
    acc[...] = token_ref[...].astype(WIDE) + bias_ref[...] + own_ref[...].astype(WIDE)
    for start, term in zip(starts, terms):
        acc[start : start + term.shape[0]] += term[...].astype(WIDE)
    lanes = pieces[0].shape[1]
    steps = pl.num_programs(0)
    low_half = pl.program_id(0) * 2 < steps
    far = jnp.where(low_half, dense[count - 1][...], dense[count][...])
    total = acc[...]
    for rank in range(count):
        weight = dense[rank][...] if rank < count - 1 else far
        for n in range(groups):
            part = weight[:, n * lanes : (n + 1) * lanes]
            total += dot(pieces[rank * groups + n][...], part, NT)
    out_ref[...] = total.astype(LOW)


def place_output(pieces, dense_pieces, tokens, bias, own, terms, count, groups):
    rows, width = tokens.shape
    cols = 512
    half = width // cols // 2
    whole = lambda a: pl.BlockSpec(a.shape, lambda i: (0, 0), pipeline_mode=pl.Buffered(1))
    in_specs = [whole(piece) for piece in pieces]
    depth = dense_pieces[0].shape[1]
    in_specs += [pl.BlockSpec((cols, depth), lambda i: (i, 0)) for _ in range(count - 1)]
    in_specs.append(pl.BlockSpec((cols, depth), lambda i: (jnp.minimum(i, half - 1), 0)))
    in_specs.append(pl.BlockSpec((cols, depth), lambda i: (jnp.maximum(i - half, 0), 0)))
    by_column = lambda n: pl.BlockSpec((n, cols), lambda i: (0, i))
    in_specs += [by_column(rows), by_column(1), by_column(rows)]
    in_specs += [by_column(term.shape[0]) for _, term in terms]
    return pl.pallas_call(
        functools.partial(
            place_kernel, starts=tuple(start for start, _ in terms), count=count, groups=groups
        ),
        out_shape=jax.ShapeDtypeStruct((rows, width), LOW),
        grid=(width // cols,),
        in_specs=in_specs,
        out_specs=by_column(rows),
        scratch_shapes=[pltpu.VMEM((rows, cols), WIDE)],
        compiler_params=pltpu.CompilerParams(
            dimension_semantics=("arbitrary",), vmem_limit_bytes=48 << 20
        ),
        cost_estimate=LITTLE,
        name="place_output",
    )(*pieces, *dense_pieces, tokens, bias, own, *[term for _, term in terms])


def token_grad_kernel(token_ref, grad_ref, own_ref, gain_ref, *refs, starts, tile):
    terms, out_ref, total = refs[:-2], refs[-2], refs[-1]
    first = pl.program_id(0) * tile
    total[...] = own_ref[...].astype(WIDE)
    for start, term in zip(starts, terms):
        size = min(tile, term.shape[0])
        for at in range(0, term.shape[0], size):

            @pl.when(first == (start + at) // tile * tile)
            def _(start=start, term=term, at=at, size=size):
                to = (start + at) % tile
                total[to : to + size] += term[at : at + size].astype(WIDE)

    x = token_ref[...].astype(WIDE)
    centred = x - jnp.mean(x, axis=-1, keepdims=True)
    rstd = lax.rsqrt(jnp.mean(centred * centred, axis=-1, keepdims=True) + 1e-05)
    xhat = centred * rstd
    scaled = total[...] * gain_ref[...]
    mean = jnp.mean(scaled, axis=-1, keepdims=True)
    along = jnp.mean(scaled * xhat, axis=-1, keepdims=True)
    out_ref[...] = (grad_ref[...].astype(WIDE) + rstd * (scaled - mean - xhat * along)).astype(LOW)


def token_grad(tokens, grad, own, gain, terms, tile):
    rows, width = tokens.shape
    by_row = pl.BlockSpec((tile, width), lambda i: (i, 0))
    whole = lambda a: pl.BlockSpec(a.shape, lambda i: (0, 0), pipeline_mode=pl.Buffered(1))
    return pl.pallas_call(
        functools.partial(
            token_grad_kernel, starts=tuple(start for start, _ in terms), tile=tile
        ),
        out_shape=jax.ShapeDtypeStruct((rows, width), LOW),
        grid=(rows // tile,),
        in_specs=[by_row, by_row, by_row, pl.BlockSpec((1, width), lambda i: (0, 0))]
        + [whole(term) for _, term in terms],
        out_specs=by_row,
        scratch_shapes=[pltpu.VMEM((tile, width), WIDE)],
        compiler_params=pltpu.CompilerParams(
            dimension_semantics=("arbitrary",), vmem_limit_bytes=48 << 20
        ),
        cost_estimate=LITTLE,
        name="token_grad",
    )(tokens, grad, own, gain[None], *[term for _, term in terms])


def pair_grad_kernel(x_ref, y_ref, a_ref, b_ref, out_ref):
    split = a_ref.shape[1]
    out_ref[:, :split] = dot(x_ref[...], a_ref[...], TN).astype(LOW)
    out_ref[:, split:] = dot(y_ref[...], b_ref[...], TN).astype(LOW)


def pair_grad(x, y, a, b):
    rows, width = x.shape
    columns = a.shape[1] + b.shape[1]
    tile = 512
    keep = pl.Buffered(1)
    return pl.pallas_call(
        pair_grad_kernel,
        out_shape=jax.ShapeDtypeStruct((width, columns), LOW),
        grid=(width // tile,),
        in_specs=[
            pl.BlockSpec((rows, tile), lambda i: (0, i)),
            pl.BlockSpec((rows, tile), lambda i: (0, i)),
            pl.BlockSpec(a.shape, lambda i: (0, 0), pipeline_mode=keep),
            pl.BlockSpec(b.shape, lambda i: (0, 0), pipeline_mode=keep),
        ],
        out_specs=pl.BlockSpec((tile, columns), lambda i: (i, 0)),
        compiler_params=pltpu.CompilerParams(
            dimension_semantics=("arbitrary",), vmem_limit_bytes=48 << 20
        ),
        cost_estimate=LITTLE,
        name="pair_grad",
    )(x, y, a, b)


def rope_tables(rows):
    place = jnp.arange(rows, dtype=jnp.int32)
    pos = jnp.where(place < PROMPT, place, PROMPT + (place - PROMPT) % CLEN)
    half = ROT // 2
    freq = 10000.0 ** (-2.0 * jnp.arange(half, dtype=WIDE) / ROT)
    angle = pos.astype(WIDE)[:, None] * freq[None, :]
    cosine, sine = jnp.cos(angle), jnp.sin(angle)
    zero, one = jnp.zeros_like(cosine), jnp.ones_like(cosine)
    tabs = ((cosine, cosine, one, one), (zero, sine, zero, zero), (-sine, zero, zero, zero))
    return [jnp.concatenate(tab * (LANES // (4 * half)), axis=1) for tab in tabs]


def shards(
    tokens,
    cotangent,
    block_table,
    ln_gain,
    ln_bias,
    w_qkv,
    b_qkv,
    w_dense,
    b_dense,
    w_fc1,
    b_fc1,
    w_fc2,
    b_fc2,
):
    _, local_rows, width = tokens.shape
    head_dim = width // HEADS
    count = lax.axis_size("ctx")
    me = lax.axis_index("ctx")
    rows = local_rows * count
    local_blocks = local_rows // BLK
    each = w_dense.shape[0]
    hidden = w_fc2.shape[0]
    gain, shift = ln_gain.astype(WIDE), ln_bias.astype(WIDE)

    def of_rank(whole, rank):
        return whole[rank * local_rows : (rank + 1) * local_rows]

    order, _, _ = ring_of(count)
    places = [0] * count
    for n, device in enumerate(order):
        places[device] = n
    places = jnp.asarray(places, jnp.int32)
    ranks = jnp.asarray([rank_of(n, count) for n in range(count)], jnp.int32)
    slots = jnp.arange(rows // BLK, dtype=jnp.int32)
    offset = (places[slots // local_blocks] - places[me]) % count
    held_at = ranks[offset] * local_blocks + slots % local_blocks
    hit = block_table[0][None, :] == slots[:, None]
    where = jnp.sum(jnp.where(hit, held_at[None, :], 0), axis=1).astype(jnp.int32)

    own_tokens = tokens[0].astype(WIDE)
    own_grad = cotangent[0]
    average = jnp.mean(own_tokens, axis=-1, keepdims=True)
    centred = own_tokens - average
    rstd = lax.rsqrt(jnp.mean(centred * centred, axis=-1, keepdims=True) + 1e-05)
    xhat = centred * rstd
    normed_own = (xhat * gain + shift).astype(LOW)

    def gather_rows(shard):
        return lax.all_gather(shard, "fsdp", axis=0, tiled=True)

    def scatter_rows(whole):
        return lax.psum_scatter(whole, "fsdp", scatter_dimension=0, tiled=True)

    lanes = 2 * LANES if each % (2 * LANES) == 0 else LANES
    groups = each // lanes

    def by_group(values):
        cut = values.reshape(-1, 3, groups, lanes)
        return jnp.swapaxes(cut, 1, 2).reshape(-1, 3 * each)

    normed_pieces = ring_pieces(normed_own, "ctx")
    normed = jnp.concatenate(normed_pieces, axis=0)
    attention_shard = jnp.concatenate([by_group(w_qkv), w_dense.T], axis=1)
    fc1_weight = gather_rows(w_fc1)
    fc2_turned = gather_rows(after(w_fc2.T, *normed_pieces[1:-2]))
    attention_weight = gather_rows(after(attention_shard, *normed_pieces[-2:]))
    qkv_weight, dense_turned = attention_weight[:, : 3 * each], attention_weight[:, 3 * each :]

    tabs = rope_tables(rows)
    normed = after(normed, where, *tabs)

    fc1_bias = lax.dynamic_slice_in_dim(b_fc1, me * hidden, hidden, 0)
    qkv_bias = lax.dynamic_slice_in_dim(b_qkv.reshape(3, width), me * each, each, 1)
    activated, slope = expand(normed, fc1_weight, fc1_bias)

    sent_grad = after(own_grad, *normed_pieces[-2:])
    grad_pieces = ring_pieces(sent_grad, "ctx", gate=(activated,))
    ff_part = dot(activated, fc2_turned, NT).astype(LOW)
    grads = jnp.concatenate([after(piece, ff_part) for piece in grad_pieces], axis=0)
    ff_terms, ff_hops = ring_reduce(lambda rank: of_rank(ff_part, rank), "ctx", staged=True)
    first, second, last = ff_hops[0], ff_hops[min(1, len(ff_hops) - 1)], ff_hops[-1]

    gated = after(grads, ff_part)
    expanded_grad = (dot(gated, fc2_turned, NN) * slope.astype(WIDE)).astype(LOW)
    d_fc2_part = dot(after(grads, expanded_grad, *first), activated, TN).astype(LOW)
    d_fc2 = scatter_rows(d_fc2_part)
    qkv = dot(after(normed, d_fc2_part), qkv_weight, NN)
    qkv = (qkv + by_group(qkv_bias)[0].astype(WIDE)).astype(LOW)
    attended_grad = dot(after(grads, qkv), dense_turned, NN).astype(LOW)
    gated = after(normed, attended_grad, *second)
    d_fc1_part = dot(gated, expanded_grad, TN).astype(LOW)
    d_fc1 = scatter_rows(d_fc1_part)

    dense_pieces = ring_pieces(after(dense_turned, *second), "ctx")

    attended, qkv_grads, d_attention, swapped = [], [], [], []
    ordered = (d_fc1_part,)
    for which in range(groups):
        got, got_grads = attention(
            after(qkv, *ordered), attended_grad, where, tabs, lanes, which, head_dim
        )
        attended.append(got)
        qkv_grads.append(got_grads)
        if which < groups - 1:
            swapped.append(ring_exchange(lambda rank, got=got: of_rank(got, rank), "ctx"))
            gated = after(normed, d_fc2, *last, *dense_pieces[1:-2]) if which == 0 else normed
            d_part = pair_grad(gated, grads, got_grads, got)
            ordered = (d_part,)
            d_attention.append(scatter_rows(d_part))

    weights = [(attention_weight, which) for which in range(groups)] + [(fc1_weight, 0)]
    early_swaps = [piece for pieces in swapped for piece in pieces]
    turn = after(expanded_grad, d_fc1, *dense_pieces[-2:], *early_swaps, *attended)
    swapped.append(ring_exchange(lambda rank: of_rank(attended[-1], rank), "ctx"))
    far_part, far_sums = input_grad(qkv_grads + [turn], weights, normed, [count - 1], local_rows)
    middle = list(range(count - 2, 0, -1))
    middle_sums, parts = 0.0, {count - 1: far_part[0]}
    turn = after(turn, *far_part)
    for n in range(0, len(middle), 2):
        some, some_sums = input_grad(
            qkv_grads + [turn], weights, normed, middle[n : n + 2], local_rows
        )
        turn = after(turn, *some)
        middle_sums = middle_sums + some_sums
        parts.update(zip(middle[n : n + 2], some))

    grad_terms, hops = ring_reduce(lambda rank: parts[rank], "ctx", cuts=2)
    covers = hops[1:] if len(hops) == 5 else [()] * 4
    gated = after(normed, turn, *hops[0], *swapped[-1], *d_attention)
    d_part = pair_grad(gated, grads, qkv_grads[-1], attended[-1])
    d_attention.append(scatter_rows(d_part))
    own_part, own_sums = input_grad(
        qkv_grads + [after(turn, d_part, *covers[0])], weights, normed, [0], local_rows
    )
    attended_own = [swapped[which][rank] for rank in range(count) for which in range(groups)]
    output = place_output(
        attended_own,
        dense_pieces,
        after(tokens[0], *own_part, *covers[1]),
        (b_dense.astype(WIDE) + b_fc2.astype(WIDE))[None],
        ff_part,
        ff_terms,
        count,
        groups,
    )
    sums = after(far_sums + middle_sums + own_sums, output, *covers[2])
    d_tokens = token_grad(tokens[0], own_grad, own_part[0], gain, grad_terms, local_rows // 4)

    d_qkv = jnp.concatenate(
        [part[:, : 3 * lanes].reshape(-1, 3, lanes) for part in d_attention], axis=2
    ).astype(WIDE)
    d_dense = jnp.concatenate([part[:, 3 * lanes :].T for part in d_attention], axis=0)

    qkv_bias_part = jnp.concatenate(
        [jnp.sum(part.astype(WIDE), axis=0).reshape(3, lanes) for part in qkv_grads], axis=1
    )
    fc1_bias_part = jnp.sum(expanded_grad.astype(WIDE), axis=0)
    qkv_bias_wide = lax.dynamic_update_slice_in_dim(
        jnp.zeros((3, width), WIDE), qkv_bias_part, me * each, 1
    ).reshape(-1)
    fc1_bias_wide = lax.dynamic_update_slice_in_dim(
        jnp.zeros((b_fc1.shape[0],), WIDE), fc1_bias_part, me * hidden, 0
    )
    small = sum_everywhere(
        jnp.concatenate(
            [
                sums.reshape(-1),
                qkv_bias_wide,
                jnp.sum(sent_grad.astype(WIDE), axis=0),
                fc1_bias_wide,
            ]
        ),
        ("fsdp",),
    )
    small = sum_everywhere(after(small, *covers[3]), ("ctx",))
    d_shift, with_normed, d_b_qkv, d_b_out, d_b_fc1 = jnp.split(
        small, [width, 2 * width, 5 * width, 6 * width]
    )
    d_gain = (with_normed - shift * d_shift) / gain
    return (
        output[None],
        d_tokens[None],
        d_gain,
        d_shift,
        d_qkv,
        d_b_qkv,
        d_dense.astype(WIDE),
        d_b_out,
        d_fc1.astype(WIDE),
        d_b_fc1,
        d_fc2.T.astype(WIDE),
        d_b_out,
    )


def solution(mesh):
    in_specs = (
        P("fsdp", "ctx", None),
        P("fsdp", "ctx", None),
        P("fsdp", None),
        P(),
        P(),
        P("fsdp", None, "ctx"),
        P(),
        P("ctx", "fsdp"),
        P(),
        P("fsdp", "ctx"),
        P(),
        P("ctx", "fsdp"),
        P(),
    )
    out_specs = (
        P("fsdp", "ctx", None),
        P("fsdp", "ctx", None),
        P(),
        P(),
        P("fsdp", None, "ctx"),
        P(),
        P("ctx", "fsdp"),
        P(),
        P("fsdp", "ctx"),
        P(),
        P("ctx", "fsdp"),
        P(),
    )
    return jax.shard_map(shards, mesh=mesh, in_specs=in_specs, out_specs=out_specs, check_vma=False)
```

```python
import functools
import math

import jax
import jax.numpy as jnp
from jax import lax
from jax.experimental import pallas as pl
from jax.experimental.pallas import tpu as pltpu
from jax.sharding import PartitionSpec as P

HEADS = 32
ROT = 32
PROMPT = 2048
CLEN = 256
BLK = 64
CHUNK = 256
LANES = 128
NT = (((1,), (1,)), ((), ()))
NN = (((1,), (0,)), ((), ()))
TN = (((0,), (0,)), ((), ()))
LOW = jnp.bfloat16
WIDE = jnp.float32
LITTLE = pl.CostEstimate(flops=1000000, bytes_accessed=1000000, transcendentals=0)
MUCH = pl.CostEstimate(flops=100000000000, bytes_accessed=1000000, transcendentals=0)


def dot(left, right, dims):
    return lax.dot_general(left, right, dims, preferred_element_type=WIDE)


def attention_kernel(where_ref, *refs, chunk, chunks, full_chunks, blk, group, scale):
    per = chunk // blk
    q_in, k_in, v_in, g_in = (refs[n * per : (n + 1) * per] for n in range(4))
    cos_ref, up_ref, down_ref, att_hbm, grad_hbm = refs[4 * per : 4 * per + 5]
    (
        keys,
        values,
        values_t,
        probs,
        key_sum,
        value_sum,
        top_ref,
        total_ref,
        mix_ref,
        back_ref,
        att_stage,
        query_stage,
        key_stage,
        value_stage,
        row_sem,
        col_sem,
    ) = refs[4 * per + 5 :]
    i = pl.program_id(0)
    slot = lax.rem(i, 2)
    half = LANES // 2
    lanes = group * LANES
    heads = 2 * group
    first = lax.broadcasted_iota(jnp.int32, (1, LANES), 1) < half

    def columns(part):
        return pl.ds(part * lanes, lanes)

    def row_copies(which, at):
        stage, target = ((att_stage, att_hbm), (query_stage, grad_hbm))[which]
        return [
            pltpu.make_async_copy(
                stage.at[at, pl.ds(r * blk, blk)],
                target.at[where_ref[i * per + r], :, columns(0)],
                row_sem.at[at, which, r],
            )
            for r in range(per)
        ]

    def col_copies(n):
        block = where_ref[n]
        rows = pl.ds(pl.multiple_of(n * blk, blk), blk)
        return (
            pltpu.make_async_copy(
                key_stage.at[rows], grad_hbm.at[block, :, columns(1)], col_sem.at[0, n]
            ),
            pltpu.make_async_copy(
                value_stage.at[rows], grad_hbm.at[block, :, columns(2)], col_sem.at[1, n]
            ),
        )

    def load(parts):
        return jnp.concatenate([part[0] for part in parts], axis=0)

    def tables(rows):
        return cos_ref[rows], up_ref[rows], down_ref[rows]

    quarter = ROT // 2

    def turned(x, tab, sign):
        return jnp.concatenate(
            [
                y * tab[0]
                + sign
                * (pltpu.roll(y, quarter, 1) * tab[1] + pltpu.roll(y, LANES - quarter, 1) * tab[2])
                for y in (x[:, n * LANES : (n + 1) * LANES] for n in range(group))
            ],
            axis=1,
        )

    def one_head(x, h):
        pair = x[:, (h // 2) * LANES : (h // 2 + 1) * LANES]
        nothing = jnp.zeros_like(pair)
        return jnp.where(first, pair, nothing) if h % 2 == 0 else jnp.where(first, nothing, pair)

    @pl.when(i >= 2)
    def _():
        for which in range(2):
            for copy in row_copies(which, slot):
                copy.wait()

    here = pl.ds(pl.multiple_of(i * chunk, chunk), chunk)
    tab = tables(here)
    query = (turned(load(q_in).astype(WIDE), tab, 1.0) * scale).astype(LOW)
    key_new = turned(load(k_in).astype(WIDE), tab, 1.0)
    value_new = load(v_in)
    grad = load(g_in)
    keys[here] = key_new.astype(LOW)
    values[here] = value_new
    values_t[:, here] = value_new.astype(WIDE).T.astype(LOW)
    key_sum[here] = jnp.zeros((chunk, lanes), WIDE)
    value_sum[here] = jnp.zeros((chunk, lanes), WIDE)
    top_ref[...] = jnp.full(top_ref.shape, -1e30, WIDE)
    total_ref[...] = jnp.zeros(total_ref.shape, WIDE)
    mix_ref[...] = jnp.zeros(mix_ref.shape, WIDE)
    back_ref[...] = jnp.zeros(back_ref.shape, WIDE)
    query_of = [one_head(query, h) for h in range(heads)]
    grad_of = [one_head(grad, h) for h in range(heads)]
    query_pair = [
        jnp.concatenate(query_of[2 * n : 2 * n + 2], axis=0) for n in range(group)
    ]
    grad_pair = [jnp.concatenate(grad_of[2 * n : 2 * n + 2], axis=0) for n in range(group)]
    before = jnp.minimum(i, full_chunks)
    doubles = before // 2
    odd = before - 2 * doubles

    def fold(x, how):
        return how(x.reshape(x.shape[0] // 8, 8, chunk), axis=0)

    def pair_lanes(n):
        return slice(n * LANES, (n + 1) * LANES)

    def head_rows(h):
        return slice(h * half, (h + 1) * half)

    def sweep(tile):
        def quad(t, carry):
            start = pl.multiple_of(t * 4 * chunk, 4 * chunk)
            tile(start, start, 4 * chunk, False)
            return carry

        lax.fori_loop(0, doubles // 2, quad, 0)

        @pl.when(doubles % 2 == 1)
        def _():
            start = pl.multiple_of((doubles - 1) * 2 * chunk, 2 * chunk)
            tile(start, start, 2 * chunk, False)

        held = pl.multiple_of(doubles * 2 * chunk, chunk)

        @pl.when(odd == 1)
        def _():
            tile(held, held, 2 * chunk, True)

        @pl.when(odd == 0)
        def _():
            tile(pl.multiple_of(i * chunk, chunk), held, chunk, True)

    def score(start, held, size, masked):
        rows, to = pl.ds(start, size), pl.ds(held, size)
        if masked:
            key_row = lax.broadcasted_iota(jnp.int32, (size, chunk), 0) + start
            query_col = lax.broadcasted_iota(jnp.int32, (size, chunk), 1) + i * chunk
            seen = key_row <= query_col
        for h in range(heads):
            raw = dot(keys[rows, pair_lanes(h // 2)], query_of[h], NT)
            if masked:
                raw = jnp.where(seen, raw, -1e30)
            probs[h, to] = raw
            top_ref[h] = jnp.maximum(top_ref[h], fold(raw, jnp.max))

    sweep(score)
    top = [jnp.max(top_ref[h], axis=0, keepdims=True) for h in range(heads)]

    def mix(start, held, size, masked):
        rows, to = pl.ds(start, size), pl.ds(held, size)
        for h in range(heads):
            weight = jnp.exp(probs[h, to] - top[h])
            probs[h, to] = weight
            total_ref[h] += fold(weight, jnp.sum)
            mix_ref[head_rows(h)] += dot(values_t[head_rows(h), rows], weight.astype(LOW), NN)

    sweep(mix)
    inverse = [1.0 / jnp.sum(total_ref[h], axis=0, keepdims=True) for h in range(heads)]
    attended = jnp.concatenate(
        [mix_ref[head_rows(h)] * inverse[h] for h in range(heads)], axis=0
    )
    shared = grad.astype(WIDE).T * attended
    inner = [jnp.sum(shared[head_rows(h)], axis=0, keepdims=True) for h in range(heads)]
    att_stage[slot] = attended.T.astype(LOW)
    for copy in row_copies(0, slot):
        copy.start()

    def back(start, held, size, masked):
        rows, to = pl.ds(start, size), pl.ds(held, size)
        for n in range(group):
            value = values[rows, pair_lanes(n)]
            weights, grads = [], []
            for h in (2 * n, 2 * n + 1):
                weight = probs[h, to] * inverse[h]
                weight_grad = dot(value, grad_of[h], NT)
                score_grad = (weight * (weight_grad - inner[h])).astype(LOW)
                weights.append(weight.astype(LOW))
                grads.append(score_grad)
            value_sum[rows, pair_lanes(n)] += dot(
                jnp.concatenate(weights, axis=1), grad_pair[n], NN
            )
            key = keys[rows, pair_lanes(n)]
            back_ref[:, pair_lanes(n)] += dot(
                jnp.concatenate(grads, axis=0),
                jnp.concatenate([one_head(key, h) for h in range(2)], axis=0),
                TN,
            )
            key_sum[rows, pair_lanes(n)] += dot(
                jnp.concatenate(grads, axis=1), query_pair[n], NN
            )

    sweep(back)
    query_stage[slot] = turned(back_ref[...] * scale, tab, -1.0).astype(LOW)
    for copy in row_copies(1, slot):
        copy.start()

    @pl.when(i == chunks - 1)
    def _():
        @pl.loop(0, chunks)
        def _(n):
            rows = pl.ds(pl.multiple_of(n * chunk, chunk), chunk)
            key_stage[rows] = turned(key_sum[rows], tables(rows), -1.0).astype(LOW)
            value_stage[rows] = value_sum[rows].astype(LOW)
            for r in range(per):
                for copy in col_copies(n * per + r):
                    copy.start()

        for at in range(2):
            for which in range(2):
                for copy in row_copies(which, at):
                    copy.wait()

        @pl.loop(0, chunks * per)
        def _(n):
            for copy in col_copies(n):
                copy.wait()


def attention(qkv, grad, where, tabs, lanes, which, head_dim):
    rows = grad.shape[0]
    chunk, blk = CHUNK, BLK
    per, chunks, blocks = chunk // blk, rows // chunk, rows // blk
    group = lanes // LANES
    heads = 2 * group
    qkv_blocks = qkv.reshape(blocks, blk, qkv.shape[1])
    grad_blocks = grad.reshape(blocks, blk, grad.shape[1])

    def spec(column, r):
        return pl.BlockSpec((1, blk, lanes), lambda i, at: (at[i * per + r], 0, column))

    in_specs = [spec(3 * which + part, r) for part in range(3) for r in range(per)]
    in_specs += [spec(which, r) for r in range(per)]
    in_specs += [pl.BlockSpec((rows, LANES), lambda i, at: (0, 0), pipeline_mode=pl.Buffered(1))] * 3
    operands = [qkv_blocks] * (3 * per) + [grad_blocks] * per + list(tabs)
    kernel = functools.partial(
        attention_kernel,
        chunk=chunk,
        chunks=chunks,
        full_chunks=PROMPT // chunk,
        blk=blk,
        group=group,
        scale=1.0 / math.sqrt(head_dim),
    )
    attended, grads = pl.pallas_call(
        kernel,
        out_shape=(
            jax.ShapeDtypeStruct((blocks, blk, lanes), LOW),
            jax.ShapeDtypeStruct((blocks, blk, 3 * lanes), LOW),
        ),
        grid_spec=pltpu.PrefetchScalarGridSpec(
            num_scalar_prefetch=1,
            grid=(chunks,),
            in_specs=in_specs,
            out_specs=[pl.BlockSpec(memory_space=pl.ANY)] * 2,
            scratch_shapes=[
                pltpu.VMEM((rows, lanes), LOW),
                pltpu.VMEM((rows, lanes), LOW),
                pltpu.VMEM((lanes, rows), LOW),
                pltpu.VMEM((heads, PROMPT + chunk, chunk), WIDE),
                pltpu.VMEM((rows, lanes), WIDE),
                pltpu.VMEM((rows, lanes), WIDE),
                pltpu.VMEM((heads, 8, chunk), WIDE),
                pltpu.VMEM((heads, 8, chunk), WIDE),
                pltpu.VMEM((lanes, chunk), WIDE),
                pltpu.VMEM((chunk, lanes), WIDE),
                pltpu.VMEM((2, chunk, lanes), LOW),
                pltpu.VMEM((2, chunk, lanes), LOW),
                pltpu.VMEM((rows, lanes), LOW),
                pltpu.VMEM((rows, lanes), LOW),
                pltpu.SemaphoreType.DMA((2, 2, per)),
                pltpu.SemaphoreType.DMA((2, blocks)),
            ],
        ),
        compiler_params=pltpu.CompilerParams(
            dimension_semantics=("arbitrary",), vmem_limit_bytes=56 << 20
        ),
        cost_estimate=LITTLE,
        name="attention",
    )(where, *operands)
    return attended.reshape(rows, lanes), grads.reshape(rows, 3 * lanes)


def after(value, *others):
    return lax.optimization_barrier((value,) + others)[0] if others else value


def ring_of(count):
    order = list(range(count // 2)) + list(range(count - 1, count // 2 - 1, -1))
    ahead = [(order[n], order[(n + 1) % count]) for n in range(count)]
    return order, ahead, [(b, a) for a, b in ahead]


def rank_of(offset, count):
    offset %= count
    if offset == 0 or 2 * offset == count:
        return max(2 * offset - 1, 0)
    return 2 * offset if 2 * offset < count else 2 * (count - offset) - 1


def ring_pieces(own, axis, gate=()):
    count = lax.axis_size(axis)
    _, ahead, behind = ring_of(count)
    pieces, half = [own], own.shape[0] // 2
    from_behind = from_ahead = own
    for _ in range(count // 2 - 1):
        from_behind = lax.ppermute(from_behind, axis, ahead)
        from_ahead = lax.ppermute(from_ahead, axis, behind)
        pieces += [from_behind, from_ahead]
    if gate:
        from_behind, from_ahead = after(from_behind, *gate), after(from_ahead, *gate)
    far = [
        lax.ppermute(from_behind[:half], axis, ahead),
        lax.ppermute(from_ahead[half:], axis, behind),
    ]
    return pieces + far


def ring_reduce(part, axis, cuts=1, chained=False):
    count = lax.axis_size(axis)
    _, ahead, behind = ring_of(count)
    far = part(count - 1)
    half = far.shape[0] // 2

    def plus(a, b):
        return (a.astype(WIDE) + b.astype(WIDE)).astype(LOW)

    up, down = lax.ppermute(far[:half], axis, ahead), lax.ppermute(far[half:], axis, behind)
    hops = [(up, down)]
    if count == 2:
        return [(0, up), (half, down)], hops
    to_ahead, to_behind = part(count - 2), part(count - 3)
    got_up, got_down = {}, {}

    got_up[0] = lax.ppermute(plus(to_ahead[:half], up), axis, ahead)
    got_down[half] = lax.ppermute(plus(to_behind[half:], down), axis, behind)
    hops.append((got_up[0], got_down[half]))
    for at in range(0, half, half // cuts):
        span, there = slice(at, at + half // cuts), slice(half + at, half + at + half // cuts)
        gate = hops[-1] if chained else ()
        got_up[half + at] = lax.ppermute(after(to_ahead[there], *gate), axis, ahead)
        got_down[at] = lax.ppermute(after(to_behind[span], *gate), axis, behind)
        hops.append((got_up[half + at], got_down[at]))
    if count == 4:
        return sorted(got_up.items()) + sorted(got_down.items()), hops
    up = jnp.concatenate([piece for _, piece in sorted(got_up.items())], axis=0)
    down = jnp.concatenate([piece for _, piece in sorted(got_down.items())], axis=0)
    for s in range(count // 2 - 2, 0, -1):
        up = lax.ppermute(plus(part(2 * s), up), axis, ahead)
        down = lax.ppermute(plus(part(2 * s - 1), down), axis, behind)
        hops.append((up, down))
    return [(0, up), (0, down)], hops


def ring_exchange(part, axis):
    count = lax.axis_size(axis)
    order, _, _ = ring_of(count)
    got = [None] * count
    got[0] = part(0)
    for offset in range(1, count):
        hops = [(order[n], order[(n + offset) % count]) for n in range(count)]
        got[rank_of(-offset, count)] = lax.ppermute(part(rank_of(offset, count)), axis, hops)
    return got


def sum_everywhere(values, axes):
    for axis in axes:
        count, span = lax.axis_size(axis), 1
        while span < count:
            pairs = [(n, n ^ span) for n in range(count)]
            values = values + lax.ppermute(values, axis, pairs)
            span *= 2
    return values


def gelu_and_slope(h):
    inner_scale = math.sqrt(2.0 / math.pi)
    square = h * h
    t = jnp.tanh(h * (inner_scale + (inner_scale * 0.044715) * square))
    half = 0.5 * h
    rise = 0.5 + 0.5 * t
    bend = inner_scale + (3.0 * inner_scale * 0.044715) * square
    return (h * rise).astype(LOW), (rise + (half - half * t * t) * bend).astype(LOW)


def expand_kernel(x_ref, w_ref, b_ref, act_ref, slope_ref, *, cols):
    x = x_ref[...]
    for n in range(w_ref.shape[1] // cols):
        at = slice(n * cols, (n + 1) * cols)
        act, slope = gelu_and_slope(dot(x, w_ref[:, at], NN) + b_ref[:, at])
        act_ref[:, at] = act
        slope_ref[:, at] = slope


def expand(x, w, b):
    rows, width = x.shape
    hidden = w.shape[1]
    tile = 320
    out = jax.ShapeDtypeStruct((rows, hidden), LOW)
    return pl.pallas_call(
        functools.partial(expand_kernel, cols=min(512, hidden)),
        out_shape=(out, out),
        grid=(rows // tile,),
        in_specs=[
            pl.BlockSpec((tile, width), lambda i: (i, 0)),
            pl.BlockSpec((width, hidden), lambda i: (0, 0), pipeline_mode=pl.Buffered(1)),
            pl.BlockSpec((1, hidden), lambda i: (0, 0)),
        ],
        out_specs=[pl.BlockSpec((tile, hidden), lambda i: (i, 0))] * 2,
        compiler_params=pltpu.CompilerParams(
            dimension_semantics=("arbitrary",), vmem_limit_bytes=48 << 20
        ),
        cost_estimate=pl.CostEstimate(
            flops=2 * rows * width * hidden,
            bytes_accessed=2 * (rows * width + width * hidden + 2 * rows * hidden),
            transcendentals=rows * hidden,
        ),
        name="expand",
    )(x, w, b.astype(WIDE)[None])


def input_grad_kernel(*refs, terms, ranks):
    grads, weights = refs[: terms * ranks], refs[terms * ranks : terms * ranks + terms]
    rest = refs[terms * (ranks + 1) :]
    normed_refs, out_refs, sums_ref = rest[:ranks], rest[ranks : 2 * ranks], rest[2 * ranks]
    plain = weighted = 0.0
    for n in range(ranks):
        mine = grads[n * terms : (n + 1) * terms]
        total = sum(dot(g[...], w[...], NT) for g, w in zip(mine, weights))
        out_refs[n][...] = total.astype(LOW)
        plain += jnp.sum(total, axis=0, keepdims=True)
        weighted += jnp.sum(total * normed_refs[n][...].astype(WIDE), axis=0, keepdims=True)
    sums_ref[0:1] = plain
    sums_ref[1:2] = weighted


def input_grad(grads, weights, normed, ranks, rows):
    width = normed.shape[1]
    cols = 512
    keep = pl.Buffered(1)
    in_specs = [
        pl.BlockSpec((rows, g.shape[1]), lambda i, rank=rank: (rank, 0), pipeline_mode=keep)
        for rank in ranks
        for g in grads
    ]
    in_specs += [
        pl.BlockSpec((cols, g.shape[1]), lambda i, at=at: (i, at))
        for g, (_, at) in zip(grads, weights)
    ]
    in_specs += [pl.BlockSpec((rows, cols), lambda i, rank=rank: (rank, i)) for rank in ranks]
    *parts, sums = pl.pallas_call(
        functools.partial(input_grad_kernel, terms=len(grads), ranks=len(ranks)),
        out_shape=[jax.ShapeDtypeStruct((rows, width), LOW)] * len(ranks)
        + [jax.ShapeDtypeStruct((2, width), WIDE)],
        grid=(width // cols,),
        in_specs=in_specs,
        out_specs=[pl.BlockSpec((rows, cols), lambda i: (0, i))] * len(ranks)
        + [pl.BlockSpec((2, cols), lambda i: (0, i))],
        compiler_params=pltpu.CompilerParams(
            dimension_semantics=("arbitrary",), vmem_limit_bytes=58 << 20
        ),
        cost_estimate=LITTLE,
        name="input_grad",
    )(*grads * len(ranks), *[w for w, _ in weights], *[normed] * len(ranks))
    return parts, sums


def place_kernel(*refs, starts, count, groups):
    pieces = refs[: count * groups]
    dense = refs[count * groups : count * groups + count + 1]
    rest = refs[count * (groups + 1) + 1 :]
    token_ref, bias_ref, own_ref = rest[:3]
    terms, out_ref, acc = rest[3:-2], rest[-2], rest[-1]
    acc[...] = token_ref[...].astype(WIDE) + bias_ref[...] + own_ref[...].astype(WIDE)
    for start, term in zip(starts, terms):
        acc[start : start + term.shape[0]] += term[...].astype(WIDE)
    lanes = pieces[0].shape[1]
    steps = pl.num_programs(0)
    low_half = pl.program_id(0) * 2 < steps
    far = jnp.where(low_half, dense[count - 1][...], dense[count][...])
    total = acc[...]
    for rank in range(count):
        weight = dense[rank][...] if rank < count - 1 else far
        for n in range(groups):
            part = weight[:, n * lanes : (n + 1) * lanes]
            total += dot(pieces[rank * groups + n][...], part, NT)
    out_ref[...] = total.astype(LOW)


def place_output(pieces, dense_pieces, tokens, bias, own, terms, count, groups):
    rows, width = tokens.shape
    cols = 512
    half = width // cols // 2
    whole = lambda a: pl.BlockSpec(a.shape, lambda i: (0, 0), pipeline_mode=pl.Buffered(1))
    in_specs = [whole(piece) for piece in pieces]
    depth = dense_pieces[0].shape[1]
    in_specs += [pl.BlockSpec((cols, depth), lambda i: (i, 0)) for _ in range(count - 1)]
    in_specs.append(pl.BlockSpec((cols, depth), lambda i: (jnp.minimum(i, half - 1), 0)))
    in_specs.append(pl.BlockSpec((cols, depth), lambda i: (jnp.maximum(i - half, 0), 0)))
    by_column = lambda n: pl.BlockSpec((n, cols), lambda i: (0, i))
    in_specs += [by_column(rows), by_column(1), by_column(rows)]
    in_specs += [by_column(term.shape[0]) for _, term in terms]
    return pl.pallas_call(
        functools.partial(
            place_kernel, starts=tuple(start for start, _ in terms), count=count, groups=groups
        ),
        out_shape=jax.ShapeDtypeStruct((rows, width), LOW),
        grid=(width // cols,),
        in_specs=in_specs,
        out_specs=by_column(rows),
        scratch_shapes=[pltpu.VMEM((rows, cols), WIDE)],
        compiler_params=pltpu.CompilerParams(
            dimension_semantics=("arbitrary",), vmem_limit_bytes=48 << 20
        ),
        cost_estimate=MUCH,
        name="place_output",
    )(*pieces, *dense_pieces, tokens, bias, own, *[term for _, term in terms])


def token_grad_kernel(token_ref, grad_ref, own_ref, gain_ref, *refs, starts, tile):
    terms, out_ref, total = refs[:-2], refs[-2], refs[-1]
    first = pl.program_id(0) * tile
    total[...] = own_ref[...].astype(WIDE)
    for start, term in zip(starts, terms):
        size = min(tile, term.shape[0])
        for at in range(0, term.shape[0], size):

            @pl.when(first == (start + at) // tile * tile)
            def _(start=start, term=term, at=at, size=size):
                to = (start + at) % tile
                total[to : to + size] += term[at : at + size].astype(WIDE)

    x = token_ref[...].astype(WIDE)
    centred = x - jnp.mean(x, axis=-1, keepdims=True)
    rstd = lax.rsqrt(jnp.mean(centred * centred, axis=-1, keepdims=True) + 1e-05)
    xhat = centred * rstd
    scaled = total[...] * gain_ref[...]
    mean = jnp.mean(scaled, axis=-1, keepdims=True)
    along = jnp.mean(scaled * xhat, axis=-1, keepdims=True)
    out_ref[...] = (grad_ref[...].astype(WIDE) + rstd * (scaled - mean - xhat * along)).astype(LOW)


def token_grad(tokens, grad, own, gain, terms, tile):
    rows, width = tokens.shape
    by_row = pl.BlockSpec((tile, width), lambda i: (i, 0))
    whole = lambda a: pl.BlockSpec(a.shape, lambda i: (0, 0), pipeline_mode=pl.Buffered(1))
    return pl.pallas_call(
        functools.partial(
            token_grad_kernel, starts=tuple(start for start, _ in terms), tile=tile
        ),
        out_shape=jax.ShapeDtypeStruct((rows, width), LOW),
        grid=(rows // tile,),
        in_specs=[by_row, by_row, by_row, pl.BlockSpec((1, width), lambda i: (0, 0))]
        + [whole(term) for _, term in terms],
        out_specs=by_row,
        scratch_shapes=[pltpu.VMEM((tile, width), WIDE)],
        compiler_params=pltpu.CompilerParams(
            dimension_semantics=("arbitrary",), vmem_limit_bytes=48 << 20
        ),
        cost_estimate=MUCH,
        name="token_grad",
    )(tokens, grad, own, gain[None], *[term for _, term in terms])


def pair_grad_kernel(x_ref, y_ref, a_ref, b_ref, out_ref):
    split = a_ref.shape[1]
    out_ref[:, :split] = dot(x_ref[...], a_ref[...], TN).astype(LOW)
    out_ref[:, split:] = dot(y_ref[...], b_ref[...], TN).astype(LOW)


def pair_grad(x, y, a, b):
    rows, width = x.shape
    columns = a.shape[1] + b.shape[1]
    tile = 512
    keep = pl.Buffered(1)
    return pl.pallas_call(
        pair_grad_kernel,
        out_shape=jax.ShapeDtypeStruct((width, columns), LOW),
        grid=(width // tile,),
        in_specs=[
            pl.BlockSpec((rows, tile), lambda i: (0, i)),
            pl.BlockSpec((rows, tile), lambda i: (0, i)),
            pl.BlockSpec(a.shape, lambda i: (0, 0), pipeline_mode=keep),
            pl.BlockSpec(b.shape, lambda i: (0, 0), pipeline_mode=keep),
        ],
        out_specs=pl.BlockSpec((tile, columns), lambda i: (i, 0)),
        compiler_params=pltpu.CompilerParams(
            dimension_semantics=("arbitrary",), vmem_limit_bytes=58 << 20
        ),
        cost_estimate=LITTLE,
        name="pair_grad",
    )(x, y, a, b)


def rope_tables(rows):
    place = jnp.arange(rows, dtype=jnp.int32)
    pos = jnp.where(place < PROMPT, place, PROMPT + (place - PROMPT) % CLEN)
    half = ROT // 2
    freq = 10000.0 ** (-2.0 * jnp.arange(half, dtype=WIDE) / ROT)
    angle = pos.astype(WIDE)[:, None] * freq[None, :]
    cosine, sine = jnp.cos(angle), jnp.sin(angle)
    zero, one = jnp.zeros_like(cosine), jnp.ones_like(cosine)
    tabs = ((cosine, cosine, one, one), (zero, sine, zero, zero), (-sine, zero, zero, zero))
    return [jnp.concatenate(tab * (LANES // (4 * half)), axis=1) for tab in tabs]


def shards(
    tokens,
    cotangent,
    block_table,
    ln_gain,
    ln_bias,
    w_qkv,
    b_qkv,
    w_dense,
    b_dense,
    w_fc1,
    b_fc1,
    w_fc2,
    b_fc2,
):
    _, local_rows, width = tokens.shape
    head_dim = width // HEADS
    count = lax.axis_size("ctx")
    me = lax.axis_index("ctx")
    rows = local_rows * count
    local_blocks = local_rows // BLK
    each = w_dense.shape[0]
    hidden = w_fc2.shape[0]
    gain, shift = ln_gain.astype(WIDE), ln_bias.astype(WIDE)

    def of_rank(whole, rank):
        return whole[rank * local_rows : (rank + 1) * local_rows]

    order, _, _ = ring_of(count)
    places = [0] * count
    for n, device in enumerate(order):
        places[device] = n
    places = jnp.asarray(places, jnp.int32)
    ranks = jnp.asarray([rank_of(n, count) for n in range(count)], jnp.int32)
    slots = jnp.arange(rows // BLK, dtype=jnp.int32)
    offset = (places[slots // local_blocks] - places[me]) % count
    held_at = ranks[offset] * local_blocks + slots % local_blocks
    hit = block_table[0][None, :] == slots[:, None]
    where = jnp.sum(jnp.where(hit, held_at[None, :], 0), axis=1).astype(jnp.int32)

    own_tokens = tokens[0].astype(WIDE)
    own_grad = cotangent[0]
    average = jnp.mean(own_tokens, axis=-1, keepdims=True)
    centred = own_tokens - average
    rstd = lax.rsqrt(jnp.mean(centred * centred, axis=-1, keepdims=True) + 1e-05)
    xhat = centred * rstd
    normed_own = (xhat * gain + shift).astype(LOW)

    def gather_rows(shard):
        return lax.all_gather(shard, "fsdp", axis=0, tiled=True)

    def scatter_rows(whole):
        return lax.psum_scatter(whole, "fsdp", scatter_dimension=0, tiled=True)

    lanes = 2 * LANES if each % (2 * LANES) == 0 else LANES
    groups = each // lanes

    def by_group(values):
        cut = values.reshape(-1, 3, groups, lanes)
        return jnp.swapaxes(cut, 1, 2).reshape(-1, 3 * each)

    normed_pieces = ring_pieces(normed_own, "ctx")
    normed = jnp.concatenate(normed_pieces, axis=0)
    attention_shard = jnp.concatenate([by_group(w_qkv), w_dense.T], axis=1)
    fc1_weight = gather_rows(w_fc1)
    fc2_turned = gather_rows(after(w_fc2.T, *normed_pieces[1:-2]))
    attention_weight = gather_rows(after(attention_shard, *normed_pieces[-2:]))
    qkv_weight, dense_turned = attention_weight[:, : 3 * each], attention_weight[:, 3 * each :]

    tabs = rope_tables(rows)
    own_grad_sum = jnp.sum(own_grad.astype(WIDE), axis=0)
    normed = after(normed, where, own_grad_sum, *tabs)

    fc1_bias = lax.dynamic_slice_in_dim(b_fc1, me * hidden, hidden, 0)
    qkv_bias = lax.dynamic_slice_in_dim(b_qkv.reshape(3, width), me * each, each, 1)
    activated, slope = expand(normed, fc1_weight, fc1_bias)

    sent_grad = after(own_grad, *normed_pieces[-2:])
    grad_pieces = ring_pieces(sent_grad, "ctx", gate=(activated,))
    ff_part = dot(activated, fc2_turned, NT).astype(LOW)
    grads = jnp.concatenate([after(piece, ff_part) for piece in grad_pieces], axis=0)
    ff_terms, ff_hops = ring_reduce(lambda rank: of_rank(ff_part, rank), "ctx", chained=True)
    first, second, last = ff_hops[0], ff_hops[min(1, len(ff_hops) - 1)], ff_hops[-1]

    gated = after(grads, ff_part)
    expanded_grad = (dot(gated, fc2_turned, NN) * slope.astype(WIDE)).astype(LOW)
    d_fc2_part = dot(after(grads, expanded_grad, *first), activated, TN).astype(LOW)
    d_fc2 = scatter_rows(d_fc2_part)
    qkv = dot(after(normed, d_fc2_part), qkv_weight, NN)
    qkv = (qkv + by_group(qkv_bias)[0].astype(WIDE)).astype(LOW)
    attended_grad = dot(after(grads, qkv, *second), dense_turned, NN).astype(LOW)
    gated = after(normed, attended_grad)
    d_fc1_part = dot(gated, expanded_grad, TN).astype(LOW)
    d_fc1 = scatter_rows(d_fc1_part)

    dense_pieces = ring_pieces(after(dense_turned, *second), "ctx")

    attended, qkv_grads, d_attention, swapped = [], [], [], []
    ordered = (d_fc1_part,)
    for which in range(groups):
        got, got_grads = attention(
            after(qkv, *ordered), attended_grad, where, tabs, lanes, which, head_dim
        )
        attended.append(got)
        qkv_grads.append(got_grads)
        if which < groups - 1:
            swapped.append(ring_exchange(lambda rank, got=got: of_rank(got, rank), "ctx"))
            gated = after(normed, d_fc2, *last, *dense_pieces[1:-2]) if which == 0 else normed
            d_part = pair_grad(gated, grads, got_grads, got)
            ordered = (d_part,)
            d_attention.append(scatter_rows(d_part))

    weights = [(attention_weight, which) for which in range(groups)] + [(fc1_weight, 0)]
    early_swaps = [piece for pieces in swapped for piece in pieces]
    turn = after(expanded_grad, d_fc1, *dense_pieces[-2:], *early_swaps, *attended)
    swapped.append(ring_exchange(lambda rank: of_rank(attended[-1], rank), "ctx"))
    far_part, far_sums = input_grad(qkv_grads + [turn], weights, normed, [count - 1], local_rows)
    middle = list(range(count - 2, 0, -1))
    middle_sums, parts = 0.0, {count - 1: far_part[0]}
    turn = after(turn, *far_part)
    for n in range(0, len(middle), 2):
        some, some_sums = input_grad(
            qkv_grads + [turn], weights, normed, middle[n : n + 2], local_rows
        )
        turn = after(turn, *some)
        middle_sums = middle_sums + some_sums
        parts.update(zip(middle[n : n + 2], some))

    grad_terms, hops = ring_reduce(lambda rank: parts[rank], "ctx", cuts=2)
    covers = hops[1:] if len(hops) == 4 else [()] * 3
    gated = after(normed, turn, *hops[0], *swapped[-1], *d_attention)
    d_part = pair_grad(gated, grads, qkv_grads[-1], attended[-1])
    d_attention.append(scatter_rows(d_part))
    own_part, own_sums = input_grad(
        qkv_grads + [after(turn, d_part)], weights, normed, [0], local_rows
    )
    attended_own = [swapped[which][rank] for rank in range(count) for which in range(groups)]
    output = place_output(
        attended_own,
        dense_pieces,
        after(tokens[0], *own_part, *covers[0]),
        (b_dense.astype(WIDE) + b_fc2.astype(WIDE))[None],
        ff_part,
        ff_terms,
        count,
        groups,
    )
    sums = after(far_sums + middle_sums + own_sums, output, *covers[1])
    d_tokens = token_grad(tokens[0], own_grad, own_part[0], gain, grad_terms, local_rows // 4)

    d_qkv = jnp.concatenate(
        [part[:, : 3 * lanes].reshape(-1, 3, lanes) for part in d_attention], axis=2
    ).astype(WIDE)
    d_dense = jnp.concatenate([part[:, 3 * lanes :].T for part in d_attention], axis=0)
    d_fc1, d_fc2 = d_fc1.astype(WIDE), d_fc2.T.astype(WIDE)

    qkv_bias_part = jnp.concatenate(
        [jnp.sum(part.astype(WIDE), axis=0).reshape(3, lanes) for part in qkv_grads], axis=1
    )
    fc1_bias_part = jnp.sum(expanded_grad.astype(WIDE), axis=0)
    qkv_bias_wide = lax.dynamic_update_slice_in_dim(
        jnp.zeros((3, width), WIDE), qkv_bias_part, me * each, 1
    ).reshape(-1)
    fc1_bias_wide = lax.dynamic_update_slice_in_dim(
        jnp.zeros((b_fc1.shape[0],), WIDE), fc1_bias_part, me * hidden, 0
    )
    small = sum_everywhere(
        jnp.concatenate(
            [
                sums.reshape(-1),
                qkv_bias_wide,
                own_grad_sum,
                fc1_bias_wide,
            ]
        ),
        ("fsdp",),
    )
    small = sum_everywhere(after(small, d_fc1, d_fc2, *covers[2]), ("ctx",))
    d_shift, with_normed, d_b_qkv, d_b_out, d_b_fc1 = jnp.split(
        small, [width, 2 * width, 5 * width, 6 * width]
    )
    d_gain = (with_normed - shift * d_shift) / gain
    return (
        output[None],
        d_tokens[None],
        d_gain,
        d_shift,
        d_qkv,
        d_b_qkv,
        d_dense.astype(WIDE),
        d_b_out,
        d_fc1,
        d_b_fc1,
        d_fc2,
        d_b_out,
    )


def solution(mesh):
    in_specs = (
        P("fsdp", "ctx", None),
        P("fsdp", "ctx", None),
        P("fsdp", None),
        P(),
        P(),
        P("fsdp", None, "ctx"),
        P(),
        P("ctx", "fsdp"),
        P(),
        P("fsdp", "ctx"),
        P(),
        P("ctx", "fsdp"),
        P(),
    )
    out_specs = (
        P("fsdp", "ctx", None),
        P("fsdp", "ctx", None),
        P(),
        P(),
        P("fsdp", None, "ctx"),
        P(),
        P("ctx", "fsdp"),
        P(),
        P("fsdp", "ctx"),
        P(),
        P("ctx", "fsdp"),
        P(),
    )
    return jax.shard_map(shards, mesh=mesh, in_specs=in_specs, out_specs=out_specs, check_vma=False)
```

```python
import functools
import math

import jax
import jax.numpy as jnp
from jax import lax
from jax.experimental import pallas as pl
from jax.experimental.pallas import tpu as pltpu
from jax.sharding import PartitionSpec as P

HEADS = 32
ROT = 32
PROMPT = 2048
CLEN = 256
BLK = 64
CHUNK = 256
LANES = 128
NT = (((1,), (1,)), ((), ()))
NN = (((1,), (0,)), ((), ()))
TN = (((0,), (0,)), ((), ()))
LOW = jnp.bfloat16
WIDE = jnp.float32
LITTLE = pl.CostEstimate(flops=1000000, bytes_accessed=1000000, transcendentals=0)
MUCH = pl.CostEstimate(flops=100000000000, bytes_accessed=1000000, transcendentals=0)


def dot(left, right, dims):
    return lax.dot_general(left, right, dims, preferred_element_type=WIDE)


def attention_kernel(where_ref, *refs, chunk, chunks, full_chunks, blk, group, scale):
    per = chunk // blk
    qkv_in, g_in = refs[:per], refs[per : 2 * per]
    cos_ref, up_ref, down_ref, att_hbm, grad_hbm = refs[2 * per : 2 * per + 5]
    (
        keys,
        values,
        values_t,
        probs,
        key_sum,
        value_sum,
        top_ref,
        total_ref,
        mix_ref,
        back_ref,
        att_stage,
        query_stage,
        key_stage,
        value_stage,
        row_sem,
        col_sem,
    ) = refs[2 * per + 5 :]
    i = pl.program_id(0)
    slot = lax.rem(i, 2)
    half = LANES // 2
    lanes = group * LANES
    heads = 2 * group
    first = lax.broadcasted_iota(jnp.int32, (1, LANES), 1) < half

    def columns(part):
        return pl.ds(part * lanes, lanes)

    def row_copies(which, at):
        stage, target = ((att_stage, att_hbm), (query_stage, grad_hbm))[which]
        return [
            pltpu.make_async_copy(
                stage.at[at, pl.ds(r * blk, blk)],
                target.at[where_ref[i * per + r], :, columns(0)],
                row_sem.at[at, which, r],
            )
            for r in range(per)
        ]

    def col_copies(n):
        block = where_ref[n]
        rows = pl.ds(pl.multiple_of(n * blk, blk), blk)
        return (
            pltpu.make_async_copy(
                key_stage.at[rows], grad_hbm.at[block, :, columns(1)], col_sem.at[0, n]
            ),
            pltpu.make_async_copy(
                value_stage.at[rows], grad_hbm.at[block, :, columns(2)], col_sem.at[1, n]
            ),
        )

    def load(parts):
        return jnp.concatenate([part[0] for part in parts], axis=0)

    def tables(rows):
        return cos_ref[rows], up_ref[rows], down_ref[rows]

    quarter = ROT // 2

    def turned(x, tab, sign):
        return jnp.concatenate(
            [
                y * tab[0]
                + sign
                * (pltpu.roll(y, quarter, 1) * tab[1] + pltpu.roll(y, LANES - quarter, 1) * tab[2])
                for y in (x[:, n * LANES : (n + 1) * LANES] for n in range(group))
            ],
            axis=1,
        )

    def one_head(x, h):
        pair = x[:, (h // 2) * LANES : (h // 2 + 1) * LANES]
        nothing = jnp.zeros_like(pair)
        return jnp.where(first, pair, nothing) if h % 2 == 0 else jnp.where(first, nothing, pair)

    @pl.when(i >= 2)
    def _():
        for which in range(2):
            for copy in row_copies(which, slot):
                copy.wait()

    here = pl.ds(pl.multiple_of(i * chunk, chunk), chunk)
    tab = tables(here)
    qkv = load(qkv_in)
    query = (turned(qkv[:, :lanes].astype(WIDE), tab, 1.0) * scale).astype(LOW)
    key_new = turned(qkv[:, lanes : 2 * lanes].astype(WIDE), tab, 1.0)
    value_new = qkv[:, 2 * lanes :]
    grad = load(g_in)
    keys[here] = key_new.astype(LOW)
    values[here] = value_new
    values_t[:, here] = value_new.T
    key_sum[here] = jnp.zeros((chunk, lanes), WIDE)
    value_sum[here] = jnp.zeros((chunk, lanes), WIDE)
    top_ref[...] = jnp.full(top_ref.shape, -1e30, WIDE)
    total_ref[...] = jnp.zeros(total_ref.shape, WIDE)
    mix_ref[...] = jnp.zeros(mix_ref.shape, WIDE)
    back_ref[...] = jnp.zeros(back_ref.shape, WIDE)
    query_of = [one_head(query, h) for h in range(heads)]
    grad_of = [one_head(grad, h) for h in range(heads)]
    query_pair = [
        jnp.concatenate(query_of[2 * n : 2 * n + 2], axis=0) for n in range(group)
    ]
    grad_pair = [jnp.concatenate(grad_of[2 * n : 2 * n + 2], axis=0) for n in range(group)]
    before = jnp.minimum(i, full_chunks)
    doubles = before // 2
    odd = before - 2 * doubles

    def fold(x, how):
        return how(x.reshape(x.shape[0] // 8, 8, chunk), axis=0)

    def pair_lanes(n):
        return slice(n * LANES, (n + 1) * LANES)

    def head_rows(h):
        return slice(h * half, (h + 1) * half)

    def sweep(tile):
        def quad(t, carry):
            start = pl.multiple_of(t * 4 * chunk, 4 * chunk)
            tile(start, start, 4 * chunk, False)
            return carry

        lax.fori_loop(0, doubles // 2, quad, 0)

        @pl.when(doubles % 2 == 1)
        def _():
            start = pl.multiple_of((doubles - 1) * 2 * chunk, 2 * chunk)
            tile(start, start, 2 * chunk, False)

        held = pl.multiple_of(doubles * 2 * chunk, chunk)

        @pl.when(odd == 1)
        def _():
            tile(held, held, 2 * chunk, True)

        @pl.when(odd == 0)
        def _():
            tile(pl.multiple_of(i * chunk, chunk), held, chunk, True)

    def score(start, held, size, masked):
        rows, to = pl.ds(start, size), pl.ds(held, size)
        if masked:
            key_row = lax.broadcasted_iota(jnp.int32, (size, chunk), 0) + start
            query_col = lax.broadcasted_iota(jnp.int32, (size, chunk), 1) + i * chunk
            seen = key_row <= query_col
        for h in range(heads):
            raw = dot(keys[rows, pair_lanes(h // 2)], query_of[h], NT)
            if masked:
                raw = jnp.where(seen, raw, -1e30)
            probs[h, to] = raw
            top_ref[h] = jnp.maximum(top_ref[h], fold(raw, jnp.max))

    sweep(score)
    top = [jnp.max(top_ref[h], axis=0, keepdims=True) for h in range(heads)]

    def mix(start, held, size, masked):
        rows, to = pl.ds(start, size), pl.ds(held, size)
        for h in range(heads):
            weight = jnp.exp(probs[h, to] - top[h])
            probs[h, to] = weight
            total_ref[h] += fold(weight, jnp.sum)
            mix_ref[head_rows(h)] += dot(values_t[head_rows(h), rows], weight.astype(LOW), NN)

    sweep(mix)
    inverse = [1.0 / jnp.sum(total_ref[h], axis=0, keepdims=True) for h in range(heads)]
    attended = jnp.concatenate(
        [mix_ref[head_rows(h)] * inverse[h] for h in range(heads)], axis=0
    )
    shared = grad.T.astype(WIDE) * attended
    inner = [jnp.sum(shared[head_rows(h)], axis=0, keepdims=True) for h in range(heads)]
    att_stage[slot] = attended.astype(LOW).T
    for copy in row_copies(0, slot):
        copy.start()

    def back(start, held, size, masked):
        rows, to = pl.ds(start, size), pl.ds(held, size)
        for n in range(group):
            value = values[rows, pair_lanes(n)]
            weights, grads = [], []
            for h in (2 * n, 2 * n + 1):
                weight = probs[h, to] * inverse[h]
                weight_grad = dot(value, grad_of[h], NT)
                score_grad = (weight * (weight_grad - inner[h])).astype(LOW)
                weights.append(weight.astype(LOW))
                grads.append(score_grad)
            value_sum[rows, pair_lanes(n)] += dot(
                jnp.concatenate(weights, axis=1), grad_pair[n], NN
            )
            key = keys[rows, pair_lanes(n)]
            back_ref[:, pair_lanes(n)] += dot(
                jnp.concatenate(grads, axis=0),
                jnp.concatenate([one_head(key, h) for h in range(2)], axis=0),
                TN,
            )
            key_sum[rows, pair_lanes(n)] += dot(
                jnp.concatenate(grads, axis=1), query_pair[n], NN
            )

    sweep(back)
    query_stage[slot] = turned(back_ref[...] * scale, tab, -1.0).astype(LOW)
    for copy in row_copies(1, slot):
        copy.start()

    @pl.when(i == chunks - 1)
    def _():
        @pl.loop(0, chunks)
        def _(n):
            rows = pl.ds(pl.multiple_of(n * chunk, chunk), chunk)
            key_stage[rows] = turned(key_sum[rows], tables(rows), -1.0).astype(LOW)
            value_stage[rows] = value_sum[rows].astype(LOW)
            for r in range(per):
                for copy in col_copies(n * per + r):
                    copy.start()

        for at in range(2):
            for which in range(2):
                for copy in row_copies(which, at):
                    copy.wait()

        @pl.loop(0, chunks * per)
        def _(n):
            for copy in col_copies(n):
                copy.wait()


def attention(qkv, grad, where, tabs, lanes, which, head_dim):
    rows = grad.shape[0]
    chunk, blk = CHUNK, BLK
    per, chunks, blocks = chunk // blk, rows // chunk, rows // blk
    group = lanes // LANES
    heads = 2 * group
    qkv_blocks = qkv.reshape(blocks, blk, qkv.shape[1])
    grad_blocks = grad.reshape(blocks, blk, grad.shape[1])

    def spec(columns, r):
        return pl.BlockSpec((1, blk, columns), lambda i, at: (at[i * per + r], 0, which))

    in_specs = [spec(3 * lanes, r) for r in range(per)] + [spec(lanes, r) for r in range(per)]
    in_specs += [pl.BlockSpec((rows, LANES), lambda i, at: (0, 0), pipeline_mode=pl.Buffered(1))] * 3
    operands = [qkv_blocks] * per + [grad_blocks] * per + list(tabs)
    kernel = functools.partial(
        attention_kernel,
        chunk=chunk,
        chunks=chunks,
        full_chunks=PROMPT // chunk,
        blk=blk,
        group=group,
        scale=1.0 / math.sqrt(head_dim),
    )
    attended, grads = pl.pallas_call(
        kernel,
        out_shape=(
            jax.ShapeDtypeStruct((blocks, blk, lanes), LOW),
            jax.ShapeDtypeStruct((blocks, blk, 3 * lanes), LOW),
        ),
        grid_spec=pltpu.PrefetchScalarGridSpec(
            num_scalar_prefetch=1,
            grid=(chunks,),
            in_specs=in_specs,
            out_specs=[pl.BlockSpec(memory_space=pl.ANY)] * 2,
            scratch_shapes=[
                pltpu.VMEM((rows, lanes), LOW),
                pltpu.VMEM((rows, lanes), LOW),
                pltpu.VMEM((lanes, rows), LOW),
                pltpu.VMEM((heads, PROMPT + chunk, chunk), WIDE),
                pltpu.VMEM((rows, lanes), WIDE),
                pltpu.VMEM((rows, lanes), WIDE),
                pltpu.VMEM((heads, 8, chunk), WIDE),
                pltpu.VMEM((heads, 8, chunk), WIDE),
                pltpu.VMEM((lanes, chunk), WIDE),
                pltpu.VMEM((chunk, lanes), WIDE),
                pltpu.VMEM((2, chunk, lanes), LOW),
                pltpu.VMEM((2, chunk, lanes), LOW),
                pltpu.VMEM((rows, lanes), LOW),
                pltpu.VMEM((rows, lanes), LOW),
                pltpu.SemaphoreType.DMA((2, 2, per)),
                pltpu.SemaphoreType.DMA((2, blocks)),
            ],
        ),
        compiler_params=pltpu.CompilerParams(
            dimension_semantics=("arbitrary",), vmem_limit_bytes=56 << 20
        ),
        cost_estimate=LITTLE,
        name="attention",
    )(where, *operands)
    return attended.reshape(rows, lanes), grads.reshape(rows, 3 * lanes)


def after(value, *others):
    return lax.optimization_barrier((value,) + others)[0] if others else value


def ring_of(count):
    order = list(range(count // 2)) + list(range(count - 1, count // 2 - 1, -1))
    ahead = [(order[n], order[(n + 1) % count]) for n in range(count)]
    return order, ahead, [(b, a) for a, b in ahead]


def rank_of(offset, count):
    offset %= count
    if offset == 0 or 2 * offset == count:
        return max(2 * offset - 1, 0)
    return 2 * offset if 2 * offset < count else 2 * (count - offset) - 1


def ring_pieces(own, axis, gate=()):
    count = lax.axis_size(axis)
    _, ahead, behind = ring_of(count)
    pieces, half = [own], own.shape[0] // 2
    from_behind = from_ahead = own
    for _ in range(count // 2 - 1):
        from_behind = lax.ppermute(from_behind, axis, ahead)
        from_ahead = lax.ppermute(from_ahead, axis, behind)
        pieces += [from_behind, from_ahead]
    if gate:
        from_behind, from_ahead = after(from_behind, *gate), after(from_ahead, *gate)
    far = [
        lax.ppermute(from_behind[:half], axis, ahead),
        lax.ppermute(from_ahead[half:], axis, behind),
    ]
    return pieces + far


def ring_reduce(part, axis, cuts=1, chained=False):
    count = lax.axis_size(axis)
    _, ahead, behind = ring_of(count)

    def plus(a, b):
        return (a.astype(WIDE) + b.astype(WIDE)).astype(LOW)

    def cut_rows(term, sizes):
        if isinstance(term, (list, tuple)):
            return term
        ends = [sum(sizes[: n + 1]) for n in range(len(sizes))]
        return [term[end - size : end] for end, size in zip(ends, sizes)]

    far = part(count - 1)
    half = sum(a.shape[0] for a in far) // 2 if isinstance(far, (list, tuple)) else far.shape[0] // 2
    far = cut_rows(far, [half, half])
    up, down = lax.ppermute(far[0], axis, ahead), lax.ppermute(far[1], axis, behind)
    hops = [(up, down)]
    if count == 2:
        return [(0, up), (half, down)], hops
    pieces = [half // cuts] * cuts
    to_ahead = cut_rows(part(count - 2), [half] + pieces)
    to_behind = cut_rows(part(count - 3), pieces + [half])
    got_up, got_down = {}, {}
    got_up[0] = lax.ppermute(plus(to_ahead[0], up), axis, ahead)
    got_down[half] = lax.ppermute(plus(to_behind[-1], down), axis, behind)
    hops.append((got_up[0], got_down[half]))
    for n in range(cuts):
        gate = hops[-1] if chained else ()
        at = n * (half // cuts)
        got_up[half + at] = lax.ppermute(after(to_ahead[1 + n], *gate), axis, ahead)
        got_down[at] = lax.ppermute(after(to_behind[n], *gate), axis, behind)
        hops.append((got_up[half + at], got_down[at]))
    if count == 4:
        return sorted(got_up.items()) + sorted(got_down.items()), hops
    up = jnp.concatenate([piece for _, piece in sorted(got_up.items())], axis=0)
    down = jnp.concatenate([piece for _, piece in sorted(got_down.items())], axis=0)
    for s in range(count // 2 - 2, 0, -1):
        up = lax.ppermute(plus(part(2 * s), up), axis, ahead)
        down = lax.ppermute(plus(part(2 * s - 1), down), axis, behind)
        hops.append((up, down))
    return [(0, up), (0, down)], hops


def ring_exchange(part, axis):
    count = lax.axis_size(axis)
    order, _, _ = ring_of(count)
    got = [None] * count
    got[0] = part(0)
    for offset in range(1, count):
        hops = [(order[n], order[(n + offset) % count]) for n in range(count)]
        got[rank_of(-offset, count)] = lax.ppermute(part(rank_of(offset, count)), axis, hops)
    return got


def sum_everywhere(values, axes):
    for axis in axes:
        count, span = lax.axis_size(axis), 1
        while span < count:
            pairs = [(n, n ^ span) for n in range(count)]
            values = values + lax.ppermute(values, axis, pairs)
            span *= 2
    return values


def gelu_and_slope(h):
    inner_scale = math.sqrt(2.0 / math.pi)
    square = h * h
    t = jnp.tanh(h * (inner_scale + (inner_scale * 0.044715) * square))
    half = 0.5 * h
    rise = 0.5 + 0.5 * t
    bend = inner_scale + (3.0 * inner_scale * 0.044715) * square
    return (h * rise).astype(LOW), (rise + (half - half * t * t) * bend).astype(LOW)


def expand_kernel(x_ref, w_ref, b_ref, act_ref, slope_ref, *, cols):
    x = x_ref[...]
    for n in range(w_ref.shape[1] // cols):
        at = slice(n * cols, (n + 1) * cols)
        act, slope = gelu_and_slope(dot(x, w_ref[:, at], NN) + b_ref[:, at])
        act_ref[:, at] = act
        slope_ref[:, at] = slope


def expand(x, w, b):
    rows, width = x.shape
    hidden = w.shape[1]
    tile = 320
    out = jax.ShapeDtypeStruct((rows, hidden), LOW)
    return pl.pallas_call(
        functools.partial(expand_kernel, cols=min(512, hidden)),
        out_shape=(out, out),
        grid=(rows // tile,),
        in_specs=[
            pl.BlockSpec((tile, width), lambda i: (i, 0)),
            pl.BlockSpec((width, hidden), lambda i: (0, 0), pipeline_mode=pl.Buffered(1)),
            pl.BlockSpec((1, hidden), lambda i: (0, 0)),
        ],
        out_specs=[pl.BlockSpec((tile, hidden), lambda i: (i, 0))] * 2,
        compiler_params=pltpu.CompilerParams(
            dimension_semantics=("arbitrary",), vmem_limit_bytes=48 << 20
        ),
        cost_estimate=pl.CostEstimate(
            flops=2 * rows * width * hidden,
            bytes_accessed=2 * (rows * width + width * hidden + 2 * rows * hidden),
            transcendentals=rows * hidden,
        ),
        name="expand",
    )(x, w, b.astype(WIDE)[None])


def input_grad_kernel(*refs, terms, ranks):
    grads, weights = refs[: terms * ranks], refs[terms * ranks : terms * ranks + terms]
    rest = refs[terms * (ranks + 1) :]
    normed_refs, out_refs, sums_ref = rest[:ranks], list(rest[ranks:-1]), rest[-1]
    plain = weighted = 0.0
    for n in range(ranks):
        mine = grads[n * terms : (n + 1) * terms]
        total = sum(dot(g[...], w[...], NT) for g, w in zip(mine, weights))
        at = 0
        while at < total.shape[0]:
            out_ref = out_refs.pop(0)
            out_ref[...] = total[at : at + out_ref.shape[0]].astype(LOW)
            at += out_ref.shape[0]
        plain += jnp.sum(total, axis=0, keepdims=True)
        weighted += jnp.sum(total * normed_refs[n][...].astype(WIDE), axis=0, keepdims=True)
    sums_ref[0:1] = plain
    sums_ref[1:2] = weighted


def input_grad(grads, weights, normed, ranks, rows, cuts, cost):
    width = normed.shape[1]
    cols = 512
    keep = pl.Buffered(1)
    in_specs = [
        pl.BlockSpec((rows, g.shape[1]), lambda i, rank=rank: (rank, 0), pipeline_mode=keep)
        for rank in ranks
        for g in grads
    ]
    in_specs += [
        pl.BlockSpec((cols, g.shape[1]), lambda i, at=at: (i, at))
        for g, (_, at) in zip(grads, weights)
    ]
    in_specs += [pl.BlockSpec((rows, cols), lambda i, rank=rank: (rank, i)) for rank in ranks]
    sizes = [size for cut in cuts for size in cut]
    *parts, sums = pl.pallas_call(
        functools.partial(input_grad_kernel, terms=len(grads), ranks=len(ranks)),
        out_shape=[jax.ShapeDtypeStruct((size, width), LOW) for size in sizes]
        + [jax.ShapeDtypeStruct((2, width), WIDE)],
        grid=(width // cols,),
        in_specs=in_specs,
        out_specs=[pl.BlockSpec((size, cols), lambda i: (0, i)) for size in sizes]
        + [pl.BlockSpec((2, cols), lambda i: (0, i))],
        compiler_params=pltpu.CompilerParams(
            dimension_semantics=("arbitrary",), vmem_limit_bytes=58 << 20
        ),
        cost_estimate=cost,
        name="input_grad",
    )(*grads * len(ranks), *[w for w, _ in weights], *[normed] * len(ranks))
    return [[parts.pop(0) for _ in cut] for cut in cuts], sums


def place_kernel(*refs, starts, count, groups):
    pieces = refs[: count * groups]
    dense = refs[count * groups : count * groups + count + 1]
    rest = refs[count * (groups + 1) + 1 :]
    token_ref, bias_ref, own_ref = rest[:3]
    terms, out_ref, acc = rest[3:-2], rest[-2], rest[-1]
    acc[...] = token_ref[...].astype(WIDE) + bias_ref[...] + own_ref[...].astype(WIDE)
    for start, term in zip(starts, terms):
        acc[start : start + term.shape[0]] += term[...].astype(WIDE)
    lanes = pieces[0].shape[1]
    steps = pl.num_programs(0)
    low_half = pl.program_id(0) * 2 < steps
    far = jnp.where(low_half, dense[count - 1][...], dense[count][...])
    total = acc[...]
    for rank in range(count):
        weight = dense[rank][...] if rank < count - 1 else far
        for n in range(groups):
            part = weight[:, n * lanes : (n + 1) * lanes]
            total += dot(pieces[rank * groups + n][...], part, NT)
    out_ref[...] = total.astype(LOW)


def place_output(pieces, dense_pieces, tokens, bias, own, terms, count, groups):
    rows, width = tokens.shape
    cols = 512
    half = width // cols // 2
    whole = lambda a: pl.BlockSpec(a.shape, lambda i: (0, 0), pipeline_mode=pl.Buffered(1))
    in_specs = [whole(piece) for piece in pieces]
    depth = dense_pieces[0].shape[1]
    in_specs += [pl.BlockSpec((cols, depth), lambda i: (i, 0)) for _ in range(count - 1)]
    in_specs.append(pl.BlockSpec((cols, depth), lambda i: (jnp.minimum(i, half - 1), 0)))
    in_specs.append(pl.BlockSpec((cols, depth), lambda i: (jnp.maximum(i - half, 0), 0)))
    by_column = lambda n: pl.BlockSpec((n, cols), lambda i: (0, i))
    in_specs += [by_column(rows), by_column(1), by_column(rows)]
    in_specs += [by_column(term.shape[0]) for _, term in terms]
    return pl.pallas_call(
        functools.partial(
            place_kernel, starts=tuple(start for start, _ in terms), count=count, groups=groups
        ),
        out_shape=jax.ShapeDtypeStruct((rows, width), LOW),
        grid=(width // cols,),
        in_specs=in_specs,
        out_specs=by_column(rows),
        scratch_shapes=[pltpu.VMEM((rows, cols), WIDE)],
        compiler_params=pltpu.CompilerParams(
            dimension_semantics=("arbitrary",), vmem_limit_bytes=48 << 20
        ),
        cost_estimate=LITTLE,
        name="place_output",
    )(*pieces, *dense_pieces, tokens, bias, own, *[term for _, term in terms])


def token_grad_kernel(token_ref, grad_ref, own_ref, gain_ref, *refs, starts, tile):
    terms, out_ref, total = refs[:-2], refs[-2], refs[-1]
    first = pl.program_id(0) * tile
    total[...] = own_ref[...].astype(WIDE)
    for start, term in zip(starts, terms):
        size = min(tile, term.shape[0])
        for at in range(0, term.shape[0], size):

            @pl.when(first == (start + at) // tile * tile)
            def _(start=start, term=term, at=at, size=size):
                to = (start + at) % tile
                total[to : to + size] += term[at : at + size].astype(WIDE)

    x = token_ref[...].astype(WIDE)
    centred = x - jnp.mean(x, axis=-1, keepdims=True)
    rstd = lax.rsqrt(jnp.mean(centred * centred, axis=-1, keepdims=True) + 1e-05)
    xhat = centred * rstd
    scaled = total[...] * gain_ref[...]
    mean = jnp.mean(scaled, axis=-1, keepdims=True)
    along = jnp.mean(scaled * xhat, axis=-1, keepdims=True)
    out_ref[...] = (grad_ref[...].astype(WIDE) + rstd * (scaled - mean - xhat * along)).astype(LOW)


def token_grad(tokens, grad, own, gain, terms, tile):
    rows, width = tokens.shape
    by_row = pl.BlockSpec((tile, width), lambda i: (i, 0))
    whole = lambda a: pl.BlockSpec(a.shape, lambda i: (0, 0), pipeline_mode=pl.Buffered(1))
    return pl.pallas_call(
        functools.partial(
            token_grad_kernel, starts=tuple(start for start, _ in terms), tile=tile
        ),
        out_shape=jax.ShapeDtypeStruct((rows, width), LOW),
        grid=(rows // tile,),
        in_specs=[by_row, by_row, by_row, pl.BlockSpec((1, width), lambda i: (0, 0))]
        + [whole(term) for _, term in terms],
        out_specs=by_row,
        scratch_shapes=[pltpu.VMEM((tile, width), WIDE)],
        compiler_params=pltpu.CompilerParams(
            dimension_semantics=("arbitrary",), vmem_limit_bytes=48 << 20
        ),
        cost_estimate=LITTLE,
        name="token_grad",
    )(tokens, grad, own, gain[None], *[term for _, term in terms])


def pair_grad_kernel(x_ref, y_ref, a_ref, b_ref, out_ref):
    split = a_ref.shape[1]
    out_ref[:, :split] = dot(x_ref[...], a_ref[...], TN).astype(LOW)
    out_ref[:, split:] = dot(y_ref[...], b_ref[...], TN).astype(LOW)


def pair_grad(x, y, a, b):
    rows, width = x.shape
    columns = a.shape[1] + b.shape[1]
    tile = 512
    keep = pl.Buffered(1)
    return pl.pallas_call(
        pair_grad_kernel,
        out_shape=jax.ShapeDtypeStruct((width, columns), LOW),
        grid=(width // tile,),
        in_specs=[
            pl.BlockSpec((rows, tile), lambda i: (0, i)),
            pl.BlockSpec((rows, tile), lambda i: (0, i)),
            pl.BlockSpec(a.shape, lambda i: (0, 0), pipeline_mode=keep),
            pl.BlockSpec(b.shape, lambda i: (0, 0), pipeline_mode=keep),
        ],
        out_specs=pl.BlockSpec((tile, columns), lambda i: (i, 0)),
        compiler_params=pltpu.CompilerParams(
            dimension_semantics=("arbitrary",), vmem_limit_bytes=58 << 20
        ),
        cost_estimate=LITTLE,
        name="pair_grad",
    )(x, y, a, b)


def rope_tables(rows):
    place = jnp.arange(rows, dtype=jnp.int32)
    pos = jnp.where(place < PROMPT, place, PROMPT + (place - PROMPT) % CLEN)
    half = ROT // 2
    freq = 10000.0 ** (-2.0 * jnp.arange(half, dtype=WIDE) / ROT)
    angle = pos.astype(WIDE)[:, None] * freq[None, :]
    cosine, sine = jnp.cos(angle), jnp.sin(angle)
    zero, one = jnp.zeros_like(cosine), jnp.ones_like(cosine)
    tabs = ((cosine, cosine, one, one), (zero, sine, zero, zero), (-sine, zero, zero, zero))
    return [jnp.concatenate(tab * (LANES // (4 * half)), axis=1) for tab in tabs]


def shards(
    tokens,
    cotangent,
    block_table,
    ln_gain,
    ln_bias,
    w_qkv,
    b_qkv,
    w_dense,
    b_dense,
    w_fc1,
    b_fc1,
    w_fc2,
    b_fc2,
):
    _, local_rows, width = tokens.shape
    head_dim = width // HEADS
    count = lax.axis_size("ctx")
    me = lax.axis_index("ctx")
    rows = local_rows * count
    local_blocks = local_rows // BLK
    each = w_dense.shape[0]
    hidden = w_fc2.shape[0]
    gain, shift = ln_gain.astype(WIDE), ln_bias.astype(WIDE)

    def of_rank(whole, rank):
        return whole[rank * local_rows : (rank + 1) * local_rows]

    order, _, _ = ring_of(count)
    places = [0] * count
    for n, device in enumerate(order):
        places[device] = n
    places = jnp.asarray(places, jnp.int32)
    ranks = jnp.asarray([rank_of(n, count) for n in range(count)], jnp.int32)
    slots = jnp.arange(rows // BLK, dtype=jnp.int32)
    offset = (places[slots // local_blocks] - places[me]) % count
    held_at = ranks[offset] * local_blocks + slots % local_blocks
    hit = block_table[0][None, :] == slots[:, None]
    where = jnp.sum(jnp.where(hit, held_at[None, :], 0), axis=1).astype(jnp.int32)

    own_tokens = tokens[0].astype(WIDE)
    own_grad = cotangent[0]
    average = jnp.mean(own_tokens, axis=-1, keepdims=True)
    centred = own_tokens - average
    rstd = lax.rsqrt(jnp.mean(centred * centred, axis=-1, keepdims=True) + 1e-05)
    xhat = centred * rstd
    normed_own = (xhat * gain + shift).astype(LOW)

    def gather_rows(shard):
        return lax.all_gather(shard, "fsdp", axis=0, tiled=True)

    def scatter_rows(whole):
        return lax.psum_scatter(whole, "fsdp", scatter_dimension=0, tiled=True)

    lanes = 2 * LANES if each % (2 * LANES) == 0 else LANES
    groups = each // lanes

    def by_group(values):
        cut = values.reshape(-1, 3, groups, lanes)
        return jnp.swapaxes(cut, 1, 2).reshape(-1, 3 * each)

    normed_pieces = ring_pieces(normed_own, "ctx")
    normed = jnp.concatenate(normed_pieces, axis=0)
    attention_shard = jnp.concatenate([by_group(w_qkv), w_dense.T], axis=1)
    fc1_weight = gather_rows(w_fc1)
    fc2_turned = gather_rows(after(w_fc2.T, *normed_pieces[1:-2]))
    attention_weight = gather_rows(after(attention_shard, *normed_pieces[-2:]))
    qkv_weight, dense_turned = attention_weight[:, : 3 * each], attention_weight[:, 3 * each :]

    tabs = rope_tables(rows)
    own_grad_sum = jnp.sum(own_grad.astype(WIDE), axis=0)
    normed = after(normed, where, own_grad_sum, *tabs)

    fc1_bias = lax.dynamic_slice_in_dim(b_fc1, me * hidden, hidden, 0)
    qkv_bias = lax.dynamic_slice_in_dim(b_qkv.reshape(3, width), me * each, each, 1)
    activated, slope = expand(normed, fc1_weight, fc1_bias)

    sent_grad = after(own_grad, *normed_pieces[-2:])
    grad_pieces = ring_pieces(sent_grad, "ctx", gate=(activated,))
    ff_part = dot(activated, fc2_turned, NT).astype(LOW)
    grads = jnp.concatenate([after(piece, ff_part) for piece in grad_pieces], axis=0)
    ff_terms, ff_hops = ring_reduce(lambda rank: of_rank(ff_part, rank), "ctx", chained=True)
    first, second, last = ff_hops[0], ff_hops[min(1, len(ff_hops) - 1)], ff_hops[-1]

    gated = after(grads, ff_part)
    expanded_grad = (dot(gated, fc2_turned, NN) * slope.astype(WIDE)).astype(LOW)
    d_fc2_part = dot(after(grads, expanded_grad, *first), activated, TN).astype(LOW)
    d_fc2 = scatter_rows(d_fc2_part)
    qkv = dot(after(normed, d_fc2_part), qkv_weight, NN)
    qkv = (qkv + by_group(qkv_bias)[0].astype(WIDE)).astype(LOW)
    attended_grad = dot(after(grads, qkv, *second), dense_turned, NN).astype(LOW)
    gated = after(normed, attended_grad)
    d_fc1_part = dot(gated, expanded_grad, TN).astype(LOW)
    d_fc1 = scatter_rows(d_fc1_part)

    dense_pieces = ring_pieces(after(dense_turned, *second), "ctx")

    attended, qkv_grads, d_attention, swapped = [], [], [], []
    ordered = (d_fc1_part,)
    for which in range(groups):
        got, got_grads = attention(
            after(qkv, *ordered), attended_grad, where, tabs, lanes, which, head_dim
        )
        attended.append(got)
        qkv_grads.append(got_grads)
        if which < groups - 1:
            swapped.append(ring_exchange(lambda rank, got=got: of_rank(got, rank), "ctx"))
            gated = after(normed, d_fc2, *last, *dense_pieces[1:-2]) if which == 0 else normed
            d_part = pair_grad(gated, grads, got_grads, got)
            ordered = (d_part,)
            d_attention.append(scatter_rows(d_part))

    weights = [(attention_weight, which) for which in range(groups)] + [(fc1_weight, 0)]
    early_swaps = [piece for pieces in swapped for piece in pieces]
    turn = after(expanded_grad, d_fc1, *dense_pieces[-2:], *early_swaps, *attended)
    swapped.append(ring_exchange(lambda rank: of_rank(attended[-1], rank), "ctx"))
    half = local_rows // 2
    whole, far_cut, ahead_cut, behind_cut = [local_rows], [half, half], [half], [half]
    if count > 2:
        ahead_cut, behind_cut = [half, half // 2, half // 2], [half // 2, half // 2, half]
    cut_of = {0: whole, count - 2: ahead_cut, count - 3: behind_cut, count - 1: far_cut}

    def some_ranks(ranks, turn, cost=LITTLE):
        cuts = [cut_of.get(rank, whole) for rank in ranks]
        return input_grad(qkv_grads + [turn], weights, normed, ranks, local_rows, cuts, cost)

    far_part, far_sums = some_ranks([count - 1], turn)
    middle = list(range(count - 2, 0, -1))
    middle_sums, parts = 0.0, {count - 1: far_part[0]}
    turn = after(turn, *far_part[0])
    for n in range(0, len(middle), 2):
        some, some_sums = some_ranks(middle[n : n + 2], turn)
        turn = after(turn, *[piece for pieces in some for piece in pieces])
        middle_sums = middle_sums + some_sums
        parts.update(zip(middle[n : n + 2], some))
    for rank, pieces in parts.items():
        if len(pieces) == 1:
            parts[rank] = pieces[0]

    grad_terms, hops = ring_reduce(lambda rank: parts[rank], "ctx", cuts=2)
    covers = hops[1:] if len(hops) == 4 else [()] * 3
    gated = after(normed, turn, *hops[0], *swapped[-1], *d_attention)
    d_part = pair_grad(gated, grads, qkv_grads[-1], attended[-1])
    d_attention.append(scatter_rows(d_part))
    [own_part], own_sums = some_ranks([0], after(turn, d_part), MUCH)
    attended_own = [swapped[which][rank] for rank in range(count) for which in range(groups)]
    output = place_output(
        attended_own,
        dense_pieces,
        after(tokens[0], *own_part, *covers[0]),
        (b_dense.astype(WIDE) + b_fc2.astype(WIDE))[None],
        ff_part,
        ff_terms,
        count,
        groups,
    )
    sums = after(far_sums + middle_sums + own_sums, output, *covers[1])
    d_tokens = token_grad(tokens[0], own_grad, own_part[0], gain, grad_terms, local_rows // 4)

    d_qkv = jnp.concatenate(
        [part[:, : 3 * lanes].reshape(-1, 3, lanes) for part in d_attention], axis=2
    ).astype(WIDE)
    d_dense = jnp.concatenate([part[:, 3 * lanes :].T for part in d_attention], axis=0)
    d_fc1, d_fc2 = d_fc1.astype(WIDE), d_fc2.T.astype(WIDE)

    qkv_bias_part = jnp.concatenate(
        [jnp.sum(part.astype(WIDE), axis=0).reshape(3, lanes) for part in qkv_grads], axis=1
    )
    fc1_bias_part = jnp.sum(expanded_grad.astype(WIDE), axis=0)
    qkv_bias_wide = lax.dynamic_update_slice_in_dim(
        jnp.zeros((3, width), WIDE), qkv_bias_part, me * each, 1
    ).reshape(-1)
    fc1_bias_wide = lax.dynamic_update_slice_in_dim(
        jnp.zeros((b_fc1.shape[0],), WIDE), fc1_bias_part, me * hidden, 0
    )
    small = sum_everywhere(
        jnp.concatenate(
            [
                sums.reshape(-1),
                qkv_bias_wide,
                own_grad_sum,
                fc1_bias_wide,
            ]
        ),
        ("fsdp",),
    )
    small = sum_everywhere(after(small, d_fc1, d_fc2, *covers[2]), ("ctx",))
    d_shift, with_normed, d_b_qkv, d_b_out, d_b_fc1 = jnp.split(
        small, [width, 2 * width, 5 * width, 6 * width]
    )
    d_gain = (with_normed - shift * d_shift) / gain
    return (
        output[None],
        d_tokens[None],
        d_gain,
        d_shift,
        d_qkv,
        d_b_qkv,
        d_dense.astype(WIDE),
        d_b_out,
        d_fc1,
        d_b_fc1,
        d_fc2,
        d_b_out,
    )


def solution(mesh):
    in_specs = (
        P("fsdp", "ctx", None),
        P("fsdp", "ctx", None),
        P("fsdp", None),
        P(),
        P(),
        P("fsdp", None, "ctx"),
        P(),
        P("ctx", "fsdp"),
        P(),
        P("fsdp", "ctx"),
        P(),
        P("ctx", "fsdp"),
        P(),
    )
    out_specs = (
        P("fsdp", "ctx", None),
        P("fsdp", "ctx", None),
        P(),
        P(),
        P("fsdp", None, "ctx"),
        P(),
        P("ctx", "fsdp"),
        P(),
        P("fsdp", "ctx"),
        P(),
        P("ctx", "fsdp"),
        P(),
    )
    return jax.shard_map(shards, mesh=mesh, in_specs=in_specs, out_specs=out_specs, check_vma=False)
```

```python
import functools
import math

import jax
import jax.numpy as jnp
from jax import lax
from jax.experimental import pallas as pl
from jax.experimental.pallas import tpu as pltpu
from jax.sharding import PartitionSpec as P

HEADS = 32
ROT = 32
PROMPT = 2048
CLEN = 256
BLK = 64
CHUNK = 256
LANES = 128
NT = (((1,), (1,)), ((), ()))
NN = (((1,), (0,)), ((), ()))
TN = (((0,), (0,)), ((), ()))
LOW = jnp.bfloat16
WIDE = jnp.float32
LITTLE = pl.CostEstimate(flops=1000000, bytes_accessed=1000000, transcendentals=0)
MUCH = pl.CostEstimate(flops=100000000000, bytes_accessed=1000000, transcendentals=0)


def dot(left, right, dims):
    return lax.dot_general(left, right, dims, preferred_element_type=WIDE)


def attention_kernel(where_ref, *refs, chunk, chunks, full_chunks, blk, group, scale):
    per = chunk // blk
    qkv_in, g_in = refs[:per], refs[per : 2 * per]
    cos_ref, up_ref, down_ref, att_hbm, grad_hbm, sums_ref = refs[2 * per : 2 * per + 6]
    (
        keys,
        values,
        values_t,
        probs,
        key_sum,
        value_sum,
        top_ref,
        total_ref,
        mix_ref,
        back_ref,
        att_stage,
        query_stage,
        key_stage,
        value_stage,
        row_sem,
        col_sem,
    ) = refs[2 * per + 6 :]
    i = pl.program_id(0)
    slot = lax.rem(i, 2)
    half = LANES // 2
    lanes = group * LANES
    heads = 2 * group
    first = lax.broadcasted_iota(jnp.int32, (1, LANES), 1) < half

    def columns(part):
        return pl.ds(part * lanes, lanes)

    def row_copies(which, at):
        stage, target = ((att_stage, att_hbm), (query_stage, grad_hbm))[which]
        return [
            pltpu.make_async_copy(
                stage.at[at, pl.ds(r * blk, blk)],
                target.at[where_ref[i * per + r], :, columns(0)],
                row_sem.at[at, which, r],
            )
            for r in range(per)
        ]

    def col_copies(n):
        block = where_ref[n]
        rows = pl.ds(pl.multiple_of(n * blk, blk), blk)
        return (
            pltpu.make_async_copy(
                key_stage.at[rows], grad_hbm.at[block, :, columns(1)], col_sem.at[0, n]
            ),
            pltpu.make_async_copy(
                value_stage.at[rows], grad_hbm.at[block, :, columns(2)], col_sem.at[1, n]
            ),
        )

    def load(parts):
        return jnp.concatenate([part[0] for part in parts], axis=0)

    def tables(rows):
        return cos_ref[rows], up_ref[rows], down_ref[rows]

    quarter = ROT // 2

    def turned(x, tab, sign):
        return jnp.concatenate(
            [
                y * tab[0]
                + sign
                * (pltpu.roll(y, quarter, 1) * tab[1] + pltpu.roll(y, LANES - quarter, 1) * tab[2])
                for y in (x[:, n * LANES : (n + 1) * LANES] for n in range(group))
            ],
            axis=1,
        )

    def one_head(x, h):
        pair = x[:, (h // 2) * LANES : (h // 2 + 1) * LANES]
        nothing = jnp.zeros_like(pair)
        return jnp.where(first, pair, nothing) if h % 2 == 0 else jnp.where(first, nothing, pair)

    @pl.when(i >= 2)
    def _():
        for which in range(2):
            for copy in row_copies(which, slot):
                copy.wait()

    here = pl.ds(pl.multiple_of(i * chunk, chunk), chunk)
    tab = tables(here)
    qkv = load(qkv_in)
    query = (turned(qkv[:, :lanes].astype(WIDE), tab, 1.0) * scale).astype(LOW)
    key_new = turned(qkv[:, lanes : 2 * lanes].astype(WIDE), tab, 1.0)
    value_new = qkv[:, 2 * lanes :]
    grad = load(g_in)
    keys[here] = key_new.astype(LOW)
    values[here] = value_new
    values_t[:, here] = value_new.T
    key_sum[here] = jnp.zeros((chunk, lanes), WIDE)
    value_sum[here] = jnp.zeros((chunk, lanes), WIDE)
    top_ref[...] = jnp.full(top_ref.shape, -1e30, WIDE)
    total_ref[...] = jnp.zeros(total_ref.shape, WIDE)
    mix_ref[...] = jnp.zeros(mix_ref.shape, WIDE)
    back_ref[...] = jnp.zeros(back_ref.shape, WIDE)
    query_of = [one_head(query, h) for h in range(heads)]
    grad_of = [one_head(grad, h) for h in range(heads)]
    query_pair = [
        jnp.concatenate(query_of[2 * n : 2 * n + 2], axis=0) for n in range(group)
    ]
    grad_pair = [jnp.concatenate(grad_of[2 * n : 2 * n + 2], axis=0) for n in range(group)]
    before = jnp.minimum(i, full_chunks)
    doubles = before // 2
    odd = before - 2 * doubles

    def fold(x, how):
        return how(x.reshape(x.shape[0] // 8, 8, chunk), axis=0)

    def pair_lanes(n):
        return slice(n * LANES, (n + 1) * LANES)

    def head_rows(h):
        return slice(h * half, (h + 1) * half)

    def sweep(tile):
        def quad(t, carry):
            start = pl.multiple_of(t * 4 * chunk, 4 * chunk)
            tile(start, start, 4 * chunk, False)
            return carry

        lax.fori_loop(0, doubles // 2, quad, 0)

        @pl.when(doubles % 2 == 1)
        def _():
            start = pl.multiple_of((doubles - 1) * 2 * chunk, 2 * chunk)
            tile(start, start, 2 * chunk, False)

        held = pl.multiple_of(doubles * 2 * chunk, chunk)

        @pl.when(odd == 1)
        def _():
            tile(held, held, 2 * chunk, True)

        @pl.when(odd == 0)
        def _():
            tile(pl.multiple_of(i * chunk, chunk), held, chunk, True)

    def score(start, held, size, masked):
        rows, to = pl.ds(start, size), pl.ds(held, size)
        if masked:
            key_row = lax.broadcasted_iota(jnp.int32, (size, chunk), 0) + start
            query_col = lax.broadcasted_iota(jnp.int32, (size, chunk), 1) + i * chunk
            seen = key_row <= query_col
        for h in range(heads):
            raw = dot(keys[rows, pair_lanes(h // 2)], query_of[h], NT)
            if masked:
                raw = jnp.where(seen, raw, -1e30)
            probs[h, to] = raw
            top_ref[h] = jnp.maximum(top_ref[h], fold(raw, jnp.max))

    sweep(score)
    top = [jnp.max(top_ref[h], axis=0, keepdims=True) for h in range(heads)]

    def mix(start, held, size, masked):
        rows, to = pl.ds(start, size), pl.ds(held, size)
        for h in range(heads):
            weight = jnp.exp(probs[h, to] - top[h])
            probs[h, to] = weight
            total_ref[h] += fold(weight, jnp.sum)
            mix_ref[head_rows(h)] += dot(values_t[head_rows(h), rows], weight.astype(LOW), NN)

    sweep(mix)
    inverse = [1.0 / jnp.sum(total_ref[h], axis=0, keepdims=True) for h in range(heads)]
    attended = jnp.concatenate(
        [mix_ref[head_rows(h)] * inverse[h] for h in range(heads)], axis=0
    )
    shared = grad.T.astype(WIDE) * attended
    inner = [jnp.sum(shared[head_rows(h)], axis=0, keepdims=True) for h in range(heads)]
    att_stage[slot] = attended.astype(LOW).T
    for copy in row_copies(0, slot):
        copy.start()

    def back(start, held, size, masked):
        rows, to = pl.ds(start, size), pl.ds(held, size)
        for n in range(group):
            value = values[rows, pair_lanes(n)]
            weights, grads = [], []
            for h in (2 * n, 2 * n + 1):
                weight = probs[h, to] * inverse[h]
                weight_grad = dot(value, grad_of[h], NT)
                score_grad = (weight * (weight_grad - inner[h])).astype(LOW)
                weights.append(weight.astype(LOW))
                grads.append(score_grad)
            value_sum[rows, pair_lanes(n)] += dot(
                jnp.concatenate(weights, axis=1), grad_pair[n], NN
            )
            key = keys[rows, pair_lanes(n)]
            back_ref[:, pair_lanes(n)] += dot(
                jnp.concatenate(grads, axis=0),
                jnp.concatenate([one_head(key, h) for h in range(2)], axis=0),
                TN,
            )
            key_sum[rows, pair_lanes(n)] += dot(
                jnp.concatenate(grads, axis=1), query_pair[n], NN
            )

    sweep(back)
    query_grad = turned(back_ref[...] * scale, tab, -1.0)
    query_stage[slot] = query_grad.astype(LOW)

    def column_sums(x):
        return jnp.sum(x.reshape(chunk // 8, 8, lanes), axis=0)

    @pl.when(i == 0)
    def _():
        sums_ref[...] = jnp.zeros(sums_ref.shape, WIDE)

    sums_ref[:, :lanes] += column_sums(query_grad)
    for copy in row_copies(1, slot):
        copy.start()

    @pl.when(i == chunks - 1)
    def _():
        @pl.loop(0, chunks)
        def _(n):
            rows = pl.ds(pl.multiple_of(n * chunk, chunk), chunk)
            key_grad = turned(key_sum[rows], tables(rows), -1.0)
            key_stage[rows] = key_grad.astype(LOW)
            value_stage[rows] = value_sum[rows].astype(LOW)
            sums_ref[:, lanes : 2 * lanes] += column_sums(key_grad)
            sums_ref[:, 2 * lanes :] += column_sums(value_sum[rows])
            for r in range(per):
                for copy in col_copies(n * per + r):
                    copy.start()

        for at in range(2):
            for which in range(2):
                for copy in row_copies(which, at):
                    copy.wait()

        @pl.loop(0, chunks * per)
        def _(n):
            for copy in col_copies(n):
                copy.wait()


def attention(qkv, grad, where, tabs, lanes, which, head_dim):
    rows = grad.shape[0]
    chunk, blk = CHUNK, BLK
    per, chunks, blocks = chunk // blk, rows // chunk, rows // blk
    group = lanes // LANES
    heads = 2 * group
    qkv_blocks = qkv.reshape(blocks, blk, qkv.shape[1])
    grad_blocks = grad.reshape(blocks, blk, grad.shape[1])

    def spec(columns, r):
        return pl.BlockSpec((1, blk, columns), lambda i, at: (at[i * per + r], 0, which))

    in_specs = [spec(3 * lanes, r) for r in range(per)] + [spec(lanes, r) for r in range(per)]
    in_specs += [pl.BlockSpec((rows, LANES), lambda i, at: (0, 0), pipeline_mode=pl.Buffered(1))] * 3
    operands = [qkv_blocks] * per + [grad_blocks] * per + list(tabs)
    kernel = functools.partial(
        attention_kernel,
        chunk=chunk,
        chunks=chunks,
        full_chunks=PROMPT // chunk,
        blk=blk,
        group=group,
        scale=1.0 / math.sqrt(head_dim),
    )
    attended, grads, sums = pl.pallas_call(
        kernel,
        out_shape=(
            jax.ShapeDtypeStruct((blocks, blk, lanes), LOW),
            jax.ShapeDtypeStruct((blocks, blk, 3 * lanes), LOW),
            jax.ShapeDtypeStruct((8, 3 * lanes), WIDE),
        ),
        grid_spec=pltpu.PrefetchScalarGridSpec(
            num_scalar_prefetch=1,
            grid=(chunks,),
            in_specs=in_specs,
            out_specs=[pl.BlockSpec(memory_space=pl.ANY)] * 2
            + [pl.BlockSpec((8, 3 * lanes), lambda i, at: (0, 0))],
            scratch_shapes=[
                pltpu.VMEM((rows, lanes), LOW),
                pltpu.VMEM((rows, lanes), LOW),
                pltpu.VMEM((lanes, rows), LOW),
                pltpu.VMEM((heads, PROMPT + chunk, chunk), WIDE),
                pltpu.VMEM((rows, lanes), WIDE),
                pltpu.VMEM((rows, lanes), WIDE),
                pltpu.VMEM((heads, 8, chunk), WIDE),
                pltpu.VMEM((heads, 8, chunk), WIDE),
                pltpu.VMEM((lanes, chunk), WIDE),
                pltpu.VMEM((chunk, lanes), WIDE),
                pltpu.VMEM((2, chunk, lanes), LOW),
                pltpu.VMEM((2, chunk, lanes), LOW),
                pltpu.VMEM((rows, lanes), LOW),
                pltpu.VMEM((rows, lanes), LOW),
                pltpu.SemaphoreType.DMA((2, 2, per)),
                pltpu.SemaphoreType.DMA((2, blocks)),
            ],
        ),
        compiler_params=pltpu.CompilerParams(
            dimension_semantics=("arbitrary",), vmem_limit_bytes=56 << 20
        ),
        cost_estimate=LITTLE,
        name="attention",
    )(where, *operands)
    return attended.reshape(rows, lanes), grads.reshape(rows, 3 * lanes), jnp.sum(sums, axis=0)


def after(value, *others):
    return lax.optimization_barrier((value,) + others)[0] if others else value


def ring_of(count):
    order = list(range(count // 2)) + list(range(count - 1, count // 2 - 1, -1))
    ahead = [(order[n], order[(n + 1) % count]) for n in range(count)]
    return order, ahead, [(b, a) for a, b in ahead]


def rank_of(offset, count):
    offset %= count
    if offset == 0 or 2 * offset == count:
        return max(2 * offset - 1, 0)
    return 2 * offset if 2 * offset < count else 2 * (count - offset) - 1


def ring_pieces(own, axis, gate=()):
    count = lax.axis_size(axis)
    _, ahead, behind = ring_of(count)
    pieces, half = [own], own.shape[0] // 2
    from_behind = from_ahead = own
    for _ in range(count // 2 - 1):
        from_behind = lax.ppermute(from_behind, axis, ahead)
        from_ahead = lax.ppermute(from_ahead, axis, behind)
        pieces += [from_behind, from_ahead]
    if gate:
        from_behind, from_ahead = after(from_behind, *gate), after(from_ahead, *gate)
    far = [
        lax.ppermute(from_behind[:half], axis, ahead),
        lax.ppermute(from_ahead[half:], axis, behind),
    ]
    return pieces + far


def ring_reduce(part, axis, cuts=1, chained=False):
    count = lax.axis_size(axis)
    _, ahead, behind = ring_of(count)

    def plus(a, b):
        return (a.astype(WIDE) + b.astype(WIDE)).astype(LOW)

    def cut_rows(term, sizes):
        if isinstance(term, (list, tuple)):
            return term
        ends = [sum(sizes[: n + 1]) for n in range(len(sizes))]
        return [term[end - size : end] for end, size in zip(ends, sizes)]

    far = part(count - 1)
    half = sum(a.shape[0] for a in far) // 2 if isinstance(far, (list, tuple)) else far.shape[0] // 2
    far = cut_rows(far, [half, half])
    up, down = lax.ppermute(far[0], axis, ahead), lax.ppermute(far[1], axis, behind)
    hops = [(up, down)]
    if count == 2:
        return [(0, up), (half, down)], hops
    pieces = [half // cuts] * cuts
    to_ahead = cut_rows(part(count - 2), [half] + pieces)
    to_behind = cut_rows(part(count - 3), pieces + [half])
    got_up, got_down = {}, {}
    got_up[0] = lax.ppermute(plus(to_ahead[0], up), axis, ahead)
    got_down[half] = lax.ppermute(plus(to_behind[-1], down), axis, behind)
    hops.append((got_up[0], got_down[half]))
    for n in range(cuts):
        gate = hops[-1] if chained else ()
        at = n * (half // cuts)
        got_up[half + at] = lax.ppermute(after(to_ahead[1 + n], *gate), axis, ahead)
        got_down[at] = lax.ppermute(after(to_behind[n], *gate), axis, behind)
        hops.append((got_up[half + at], got_down[at]))
    if count == 4:
        return sorted(got_up.items()) + sorted(got_down.items()), hops
    up = jnp.concatenate([piece for _, piece in sorted(got_up.items())], axis=0)
    down = jnp.concatenate([piece for _, piece in sorted(got_down.items())], axis=0)
    for s in range(count // 2 - 2, 0, -1):
        up = lax.ppermute(plus(part(2 * s), up), axis, ahead)
        down = lax.ppermute(plus(part(2 * s - 1), down), axis, behind)
        hops.append((up, down))
    return [(0, up), (0, down)], hops


def ring_exchange(part, axis):
    count = lax.axis_size(axis)
    order, _, _ = ring_of(count)
    got = [None] * count
    got[0] = part(0)
    for offset in range(1, count):
        hops = [(order[n], order[(n + offset) % count]) for n in range(count)]
        got[rank_of(-offset, count)] = lax.ppermute(part(rank_of(offset, count)), axis, hops)
    return got


def sum_everywhere(values, axes, gate=()):
    for axis in axes:
        count, span = lax.axis_size(axis), 1
        while span < count:
            pairs = [(n, n ^ span) for n in range(count)]
            if axis == axes[-1] and 2 * span >= count:
                values = after(values, *gate)
            values = values + lax.ppermute(values, axis, pairs)
            span *= 2
    return values


def gelu_and_slope(h):
    inner_scale = math.sqrt(2.0 / math.pi)
    square = h * h
    t = jnp.tanh(h * (inner_scale + (inner_scale * 0.044715) * square))
    half = 0.5 * h
    rise = 0.5 + 0.5 * t
    bend = inner_scale + (3.0 * inner_scale * 0.044715) * square
    return (h * rise).astype(LOW), (rise + (half - half * t * t) * bend).astype(LOW)


def expand_kernel(x_ref, w_ref, b_ref, act_ref, slope_ref, *, cols):
    x = x_ref[...]
    for n in range(w_ref.shape[1] // cols):
        at = slice(n * cols, (n + 1) * cols)
        act, slope = gelu_and_slope(dot(x, w_ref[:, at], NN) + b_ref[:, at])
        act_ref[:, at] = act
        slope_ref[:, at] = slope


def expand(x, w, b):
    rows, width = x.shape
    hidden = w.shape[1]
    tile = 320
    out = jax.ShapeDtypeStruct((rows, hidden), LOW)
    return pl.pallas_call(
        functools.partial(expand_kernel, cols=min(512, hidden)),
        out_shape=(out, out),
        grid=(rows // tile,),
        in_specs=[
            pl.BlockSpec((tile, width), lambda i: (i, 0)),
            pl.BlockSpec((width, hidden), lambda i: (0, 0), pipeline_mode=pl.Buffered(1)),
            pl.BlockSpec((1, hidden), lambda i: (0, 0)),
        ],
        out_specs=[pl.BlockSpec((tile, hidden), lambda i: (i, 0))] * 2,
        compiler_params=pltpu.CompilerParams(
            dimension_semantics=("arbitrary",), vmem_limit_bytes=48 << 20
        ),
        cost_estimate=pl.CostEstimate(
            flops=2 * rows * width * hidden,
            bytes_accessed=2 * (rows * width + width * hidden + 2 * rows * hidden),
            transcendentals=rows * hidden,
        ),
        name="expand",
    )(x, w, b[None])


def input_grad_kernel(*refs, terms, ranks):
    grads, weights = refs[: terms * ranks], refs[terms * ranks : terms * ranks + terms]
    rest = refs[terms * (ranks + 1) :]
    normed_refs, out_refs, sums_ref = rest[:ranks], list(rest[ranks:-1]), rest[-1]
    plain = weighted = 0.0
    for n in range(ranks):
        mine = grads[n * terms : (n + 1) * terms]
        total = sum(dot(g[...], w[...], NT) for g, w in zip(mine, weights))
        at = 0
        while at < total.shape[0]:
            out_ref = out_refs.pop(0)
            out_ref[...] = total[at : at + out_ref.shape[0]].astype(LOW)
            at += out_ref.shape[0]
        plain += jnp.sum(total, axis=0, keepdims=True)
        weighted += jnp.sum(total * normed_refs[n][...].astype(WIDE), axis=0, keepdims=True)
    sums_ref[0:1] = plain
    sums_ref[1:2] = weighted


def input_grad(grads, weights, normed, ranks, rows, cuts, cost):
    width = normed.shape[1]
    cols = 512
    keep = pl.Buffered(1)
    in_specs = [
        pl.BlockSpec((rows, g.shape[1]), lambda i, rank=rank: (rank, 0), pipeline_mode=keep)
        for rank in ranks
        for g in grads
    ]
    in_specs += [
        pl.BlockSpec((cols, g.shape[1]), lambda i, at=at: (i, at))
        for g, (_, at) in zip(grads, weights)
    ]
    in_specs += [pl.BlockSpec((rows, cols), lambda i, rank=rank: (rank, i)) for rank in ranks]
    sizes = [size for cut in cuts for size in cut]
    *parts, sums = pl.pallas_call(
        functools.partial(input_grad_kernel, terms=len(grads), ranks=len(ranks)),
        out_shape=[jax.ShapeDtypeStruct((size, width), LOW) for size in sizes]
        + [jax.ShapeDtypeStruct((2, width), WIDE)],
        grid=(width // cols,),
        in_specs=in_specs,
        out_specs=[pl.BlockSpec((size, cols), lambda i: (0, i)) for size in sizes]
        + [pl.BlockSpec((2, cols), lambda i: (0, i))],
        compiler_params=pltpu.CompilerParams(
            dimension_semantics=("arbitrary",), vmem_limit_bytes=58 << 20
        ),
        cost_estimate=cost,
        name="input_grad",
    )(*grads * len(ranks), *[w for w, _ in weights], *[normed] * len(ranks))
    return [[parts.pop(0) for _ in cut] for cut in cuts], sums


def place_kernel(*refs, starts, count, groups):
    pieces = refs[: count * groups]
    dense = refs[count * groups : count * groups + count + 1]
    rest = refs[count * (groups + 1) + 1 :]
    token_ref, bias_ref, own_ref = rest[:3]
    terms, out_ref, acc = rest[3:-2], rest[-2], rest[-1]
    acc[...] = token_ref[...].astype(WIDE) + bias_ref[...] + own_ref[...].astype(WIDE)
    for start, term in zip(starts, terms):
        acc[start : start + term.shape[0]] += term[...].astype(WIDE)
    lanes = pieces[0].shape[1]
    steps = pl.num_programs(0)
    low_half = pl.program_id(0) * 2 < steps
    far = jnp.where(low_half, dense[count - 1][...], dense[count][...])
    total = acc[...]
    for rank in range(count):
        weight = dense[rank][...] if rank < count - 1 else far
        for n in range(groups):
            part = weight[:, n * lanes : (n + 1) * lanes]
            total += dot(pieces[rank * groups + n][...], part, NT)
    out_ref[...] = total.astype(LOW)


def place_output(pieces, dense_pieces, tokens, bias, own, terms, count, groups):
    rows, width = tokens.shape
    cols = 512
    half = width // cols // 2
    whole = lambda a: pl.BlockSpec(a.shape, lambda i: (0, 0), pipeline_mode=pl.Buffered(1))
    in_specs = [whole(piece) for piece in pieces]
    depth = dense_pieces[0].shape[1]
    in_specs += [pl.BlockSpec((cols, depth), lambda i: (i, 0)) for _ in range(count - 1)]
    in_specs.append(pl.BlockSpec((cols, depth), lambda i: (jnp.minimum(i, half - 1), 0)))
    in_specs.append(pl.BlockSpec((cols, depth), lambda i: (jnp.maximum(i - half, 0), 0)))
    by_column = lambda n: pl.BlockSpec((n, cols), lambda i: (0, i))
    in_specs += [by_column(rows), by_column(1), by_column(rows)]
    in_specs += [by_column(term.shape[0]) for _, term in terms]
    return pl.pallas_call(
        functools.partial(
            place_kernel, starts=tuple(start for start, _ in terms), count=count, groups=groups
        ),
        out_shape=jax.ShapeDtypeStruct((rows, width), LOW),
        grid=(width // cols,),
        in_specs=in_specs,
        out_specs=by_column(rows),
        scratch_shapes=[pltpu.VMEM((rows, cols), WIDE)],
        compiler_params=pltpu.CompilerParams(
            dimension_semantics=("arbitrary",), vmem_limit_bytes=58 << 20
        ),
        cost_estimate=LITTLE,
        name="place_output",
    )(*pieces, *dense_pieces, tokens, bias, own, *[term for _, term in terms])


def token_grad_kernel(token_ref, grad_ref, own_ref, gain_ref, *refs, starts, tile):
    terms, out_ref, total = refs[:-2], refs[-2], refs[-1]
    first = pl.program_id(0) * tile
    total[...] = own_ref[...].astype(WIDE)
    for start, term in zip(starts, terms):
        size = min(tile, term.shape[0])
        for at in range(0, term.shape[0], size):

            @pl.when(first == (start + at) // tile * tile)
            def _(start=start, term=term, at=at, size=size):
                to = (start + at) % tile
                total[to : to + size] += term[at : at + size].astype(WIDE)

    x = token_ref[...].astype(WIDE)
    centred = x - jnp.mean(x, axis=-1, keepdims=True)
    rstd = lax.rsqrt(jnp.mean(centred * centred, axis=-1, keepdims=True) + 1e-05)
    xhat = centred * rstd
    scaled = total[...] * gain_ref[...]
    mean = jnp.mean(scaled, axis=-1, keepdims=True)
    along = jnp.mean(scaled * xhat, axis=-1, keepdims=True)
    out_ref[...] = (grad_ref[...].astype(WIDE) + rstd * (scaled - mean - xhat * along)).astype(LOW)


def token_grad(tokens, grad, own, gain, terms, tile):
    rows, width = tokens.shape
    by_row = pl.BlockSpec((tile, width), lambda i: (i, 0))
    whole = lambda a: pl.BlockSpec(a.shape, lambda i: (0, 0), pipeline_mode=pl.Buffered(1))
    return pl.pallas_call(
        functools.partial(
            token_grad_kernel, starts=tuple(start for start, _ in terms), tile=tile
        ),
        out_shape=jax.ShapeDtypeStruct((rows, width), LOW),
        grid=(rows // tile,),
        in_specs=[by_row, by_row, by_row, pl.BlockSpec((1, width), lambda i: (0, 0))]
        + [whole(term) for _, term in terms],
        out_specs=by_row,
        scratch_shapes=[pltpu.VMEM((tile, width), WIDE)],
        compiler_params=pltpu.CompilerParams(
            dimension_semantics=("arbitrary",), vmem_limit_bytes=48 << 20
        ),
        cost_estimate=LITTLE,
        name="token_grad",
    )(tokens, grad, own, gain[None], *[term for _, term in terms])


def pair_grad_kernel(x_ref, y_ref, a_ref, b_ref, out_ref):
    split = a_ref.shape[1]
    out_ref[:, :split] = dot(x_ref[...], a_ref[...], TN).astype(LOW)
    out_ref[:, split:] = dot(y_ref[...], b_ref[...], TN).astype(LOW)


def pair_grad(x, y, a, b):
    rows, width = x.shape
    columns = a.shape[1] + b.shape[1]
    tile = 512
    keep = pl.Buffered(1)
    return pl.pallas_call(
        pair_grad_kernel,
        out_shape=jax.ShapeDtypeStruct((width, columns), LOW),
        grid=(width // tile,),
        in_specs=[
            pl.BlockSpec((rows, tile), lambda i: (0, i)),
            pl.BlockSpec((rows, tile), lambda i: (0, i)),
            pl.BlockSpec(a.shape, lambda i: (0, 0), pipeline_mode=keep),
            pl.BlockSpec(b.shape, lambda i: (0, 0), pipeline_mode=keep),
        ],
        out_specs=pl.BlockSpec((tile, columns), lambda i: (i, 0)),
        compiler_params=pltpu.CompilerParams(
            dimension_semantics=("arbitrary",), vmem_limit_bytes=58 << 20
        ),
        cost_estimate=LITTLE,
        name="pair_grad",
    )(x, y, a, b)


def rope_tables(rows):
    place = lax.broadcasted_iota(jnp.int32, (rows, LANES), 0)
    lane = lax.broadcasted_iota(jnp.int32, (rows, LANES), 1)
    pos = jnp.where(place < PROMPT, place, PROMPT + (place - PROMPT) % CLEN)
    half = ROT // 2
    freq = 10000.0 ** (-2.0 * jnp.arange(half, dtype=WIDE) / ROT)
    angle = pos.astype(WIDE) * jnp.tile(freq, LANES // half)[None, :]
    dim = lane % (LANES // 2)
    cosine, sine = jnp.cos(angle), jnp.sin(angle)
    return [
        jnp.where(dim < ROT, cosine, 1.0),
        jnp.where((dim >= half) & (dim < ROT), sine, 0.0),
        jnp.where(dim < half, -sine, 0.0),
    ]


def shards(
    tokens,
    cotangent,
    block_table,
    ln_gain,
    ln_bias,
    w_qkv,
    b_qkv,
    w_dense,
    b_dense,
    w_fc1,
    b_fc1,
    w_fc2,
    b_fc2,
):
    _, local_rows, width = tokens.shape
    head_dim = width // HEADS
    count = lax.axis_size("ctx")
    me = lax.axis_index("ctx")
    rows = local_rows * count
    local_blocks = local_rows // BLK
    each = w_dense.shape[0]
    hidden = w_fc2.shape[0]
    gain, shift = ln_gain.astype(WIDE), ln_bias.astype(WIDE)

    def of_rank(whole, rank):
        return whole[rank * local_rows : (rank + 1) * local_rows]

    order, _, _ = ring_of(count)
    places = [0] * count
    for n, device in enumerate(order):
        places[device] = n
    places = jnp.asarray(places, jnp.int32)
    ranks = jnp.asarray([rank_of(n, count) for n in range(count)], jnp.int32)
    slots = jnp.arange(rows // BLK, dtype=jnp.int32)
    offset = (places[slots // local_blocks] - places[me]) % count
    held_at = ranks[offset] * local_blocks + slots % local_blocks
    hit = block_table[0][None, :] == slots[:, None]
    where = jnp.sum(jnp.where(hit, held_at[None, :], 0), axis=1).astype(jnp.int32)

    own_tokens = tokens[0].astype(WIDE)
    own_grad = cotangent[0]
    average = jnp.mean(own_tokens, axis=-1, keepdims=True)
    centred = own_tokens - average
    rstd = lax.rsqrt(jnp.mean(centred * centred, axis=-1, keepdims=True) + 1e-05)
    xhat = centred * rstd
    normed_own = (xhat * gain + shift).astype(LOW)

    def gather_rows(shard):
        return lax.all_gather(shard, "fsdp", axis=0, tiled=True)

    def scatter_rows(whole):
        return lax.psum_scatter(whole, "fsdp", scatter_dimension=0, tiled=True)

    lanes = 2 * LANES if each % (2 * LANES) == 0 else LANES
    groups = each // lanes

    def by_group(values):
        cut = values.reshape(-1, 3, groups, lanes)
        return jnp.swapaxes(cut, 1, 2).reshape(-1, 3 * each)

    tabs = rope_tables(rows)
    own_grad_sum = jnp.sum(own_grad.astype(WIDE), axis=0)
    fc1_bias = lax.dynamic_slice_in_dim(b_fc1, me * hidden, hidden, 0).astype(WIDE)
    early = (where, own_grad_sum, fc1_bias, *tabs)
    normed_pieces = ring_pieces(normed_own, "ctx")
    normed = after(jnp.concatenate(normed_pieces, axis=0), *early)
    attention_shard = jnp.concatenate([by_group(w_qkv), w_dense.T], axis=1)
    fc1_weight = gather_rows(w_fc1)
    fc2_turned = gather_rows(after(w_fc2.T, *normed_pieces[1:-2]))
    attention_weight = gather_rows(after(attention_shard, *normed_pieces[-2:]))
    qkv_weight, dense_turned = attention_weight[:, : 3 * each], attention_weight[:, 3 * each :]

    qkv_bias = lax.dynamic_slice_in_dim(b_qkv.reshape(3, width), me * each, each, 1)
    activated, slope = expand(normed, fc1_weight, fc1_bias)

    sent_grad = after(own_grad, *normed_pieces[-2:])
    grad_pieces = ring_pieces(sent_grad, "ctx", gate=(activated,))
    ff_part = dot(activated, fc2_turned, NT).astype(LOW)
    grads = jnp.concatenate([after(piece, ff_part) for piece in grad_pieces], axis=0)
    ff_terms, ff_hops = ring_reduce(lambda rank: of_rank(ff_part, rank), "ctx", chained=True)
    first, second, last = ff_hops[0], ff_hops[min(1, len(ff_hops) - 1)], ff_hops[-1]

    gated = after(grads, ff_part)
    expanded_grad = (dot(gated, fc2_turned, NN) * slope.astype(WIDE)).astype(LOW)
    d_fc2_part = dot(after(grads, expanded_grad, *first), activated, TN).astype(LOW)
    d_fc2 = scatter_rows(d_fc2_part)
    qkv = dot(after(normed, d_fc2_part), qkv_weight, NN)
    qkv = (qkv + by_group(qkv_bias)[0].astype(WIDE)).astype(LOW)
    attended_grad = dot(after(grads, qkv, *second), dense_turned, NN).astype(LOW)
    gated = after(normed, attended_grad)
    d_fc1_part = dot(gated, expanded_grad, TN).astype(LOW)
    d_fc1 = scatter_rows(d_fc1_part)

    dense_pieces = ring_pieces(after(dense_turned, *second), "ctx")

    attended, qkv_grads, qkv_sums, d_attention, swapped = [], [], [], [], []
    ordered = (d_fc1_part,)
    for which in range(groups):
        got, got_grads, got_sums = attention(
            after(qkv, *ordered), attended_grad, where, tabs, lanes, which, head_dim
        )
        attended.append(got)
        qkv_grads.append(got_grads)
        qkv_sums.append(got_sums)
        if which < groups - 1:
            swapped.append(ring_exchange(lambda rank, got=got: of_rank(got, rank), "ctx"))
            gated = after(normed, d_fc2, *last, *dense_pieces[1:-2]) if which == 0 else normed
            d_part = pair_grad(gated, grads, got_grads, got)
            ordered = (d_part,)
            d_attention.append(scatter_rows(d_part))

    weights = [(attention_weight, which) for which in range(groups)] + [(fc1_weight, 0)]
    early_swaps = [piece for pieces in swapped for piece in pieces]
    turn = after(expanded_grad, d_fc1, *dense_pieces[-2:], *early_swaps, *attended)
    swapped.append(ring_exchange(lambda rank: of_rank(attended[-1], rank), "ctx"))
    half = local_rows // 2
    whole, far_cut, ahead_cut, behind_cut = [local_rows], [half, half], [half], [half]
    if count > 2:
        ahead_cut, behind_cut = [half, half // 2, half // 2], [half // 2, half // 2, half]
    cut_of = {0: whole, count - 2: ahead_cut, count - 3: behind_cut, count - 1: far_cut}

    def some_ranks(ranks, turn, cost=LITTLE):
        cuts = [cut_of.get(rank, whole) for rank in ranks]
        return input_grad(qkv_grads + [turn], weights, normed, ranks, local_rows, cuts, cost)

    far_part, far_sums = some_ranks([count - 1], turn)
    middle = list(range(count - 2, 0, -1))
    middle_sums, parts = 0.0, {count - 1: far_part[0]}
    turn = after(turn, *far_part[0])
    for n in range(0, len(middle), 2):
        some, some_sums = some_ranks(middle[n : n + 2], turn)
        turn = after(turn, *[piece for pieces in some for piece in pieces])
        middle_sums = middle_sums + some_sums
        parts.update(zip(middle[n : n + 2], some))
    for rank, pieces in parts.items():
        if len(pieces) == 1:
            parts[rank] = pieces[0]

    grad_terms, hops = ring_reduce(lambda rank: parts[rank], "ctx", cuts=2)
    covers = hops[1:] if len(hops) == 4 else [()] * 3
    gated = after(normed, turn, *hops[0], *swapped[-1], *d_attention)
    d_part = pair_grad(gated, grads, qkv_grads[-1], attended[-1])
    d_attention.append(scatter_rows(d_part))
    [own_part], own_sums = some_ranks([0], after(turn, d_part), MUCH)
    attended_own = [swapped[which][rank] for rank in range(count) for which in range(groups)]
    output = place_output(
        attended_own,
        dense_pieces,
        after(tokens[0], *own_part, *covers[0]),
        (b_dense.astype(WIDE) + b_fc2.astype(WIDE))[None],
        ff_part,
        ff_terms,
        count,
        groups,
    )
    sums = after(far_sums + middle_sums + own_sums, output, *covers[1])

    d_qkv = jnp.concatenate(
        [part[:, : 3 * lanes].reshape(-1, 3, lanes) for part in d_attention], axis=2
    ).astype(WIDE)
    d_dense = jnp.concatenate([part[:, 3 * lanes :].T for part in d_attention], axis=0)
    d_dense = d_dense.astype(WIDE)
    d_fc1, d_fc2 = d_fc1.astype(WIDE), d_fc2.T.astype(WIDE)

    qkv_bias_part = jnp.concatenate(
        [part.reshape(3, lanes) for part in qkv_sums], axis=1
    )
    fc1_bias_part = jnp.sum(expanded_grad.astype(WIDE), axis=0)
    qkv_bias_wide = lax.dynamic_update_slice_in_dim(
        jnp.zeros((3, width), WIDE), qkv_bias_part, me * each, 1
    ).reshape(-1)
    fc1_bias_wide = lax.dynamic_update_slice_in_dim(
        jnp.zeros((b_fc1.shape[0],), WIDE), fc1_bias_part, me * hidden, 0
    )
    small = sum_everywhere(
        jnp.concatenate(
            [
                sums.reshape(-1),
                qkv_bias_wide,
                own_grad_sum,
                fc1_bias_wide,
            ]
        ),
        ("fsdp",),
    )
    small = after(small, d_fc1, d_fc2)
    d_tokens = token_grad(
        after(tokens[0], small), own_grad, own_part[0], gain, grad_terms, local_rows // 4
    )
    small = sum_everywhere(small, ("ctx",), gate=(d_tokens,))
    small = after(small, d_qkv, d_dense)
    d_shift, with_normed, d_b_qkv, d_b_out, d_b_fc1 = jnp.split(
        small, [width, 2 * width, 5 * width, 6 * width]
    )
    d_gain = (with_normed - shift * d_shift) / gain
    return (
        output[None],
        d_tokens[None],
        d_gain,
        d_shift,
        d_qkv,
        d_b_qkv,
        d_dense,
        d_b_out,
        d_fc1,
        d_b_fc1,
        d_fc2,
        d_b_out,
    )


def solution(mesh):
    in_specs = (
        P("fsdp", "ctx", None),
        P("fsdp", "ctx", None),
        P("fsdp", None),
        P(),
        P(),
        P("fsdp", None, "ctx"),
        P(),
        P("ctx", "fsdp"),
        P(),
        P("fsdp", "ctx"),
        P(),
        P("ctx", "fsdp"),
        P(),
    )
    out_specs = (
        P("fsdp", "ctx", None),
        P("fsdp", "ctx", None),
        P(),
        P(),
        P("fsdp", None, "ctx"),
        P(),
        P("ctx", "fsdp"),
        P(),
        P("fsdp", "ctx"),
        P(),
        P("ctx", "fsdp"),
        P(),
    )
    return jax.shard_map(shards, mesh=mesh, in_specs=in_specs, out_specs=out_specs, check_vma=False)
```

```python
import functools
import math

import jax
import jax.numpy as jnp
from jax import lax
from jax.experimental import pallas as pl
from jax.experimental.pallas import tpu as pltpu
from jax.sharding import PartitionSpec as P

HEADS = 32
ROT = 32
PROMPT = 2048
CLEN = 256
BLK = 64
CHUNK = 256
LANES = 128
NT = (((1,), (1,)), ((), ()))
NN = (((1,), (0,)), ((), ()))
TN = (((0,), (0,)), ((), ()))
LOW = jnp.bfloat16
WIDE = jnp.float32
LITTLE = pl.CostEstimate(flops=1000000, bytes_accessed=1000000, transcendentals=0)
MUCH = pl.CostEstimate(flops=100000000000, bytes_accessed=1000000, transcendentals=0)


def dot(left, right, dims):
    return lax.dot_general(left, right, dims, preferred_element_type=WIDE)


def attention_kernel(where_ref, *refs, chunk, chunks, full_chunks, blk, group, scale):
    per = chunk // blk
    qkv_in, g_in = refs[:per], refs[per : 2 * per]
    cos_ref, up_ref, down_ref, att_hbm, grad_hbm, sums_ref = refs[2 * per : 2 * per + 6]
    (
        keys,
        values,
        values_t,
        probs,
        key_sum,
        value_sum,
        top_ref,
        total_ref,
        mix_ref,
        back_ref,
        att_stage,
        query_stage,
        key_stage,
        value_stage,
        row_sem,
        col_sem,
    ) = refs[2 * per + 6 :]
    i = pl.program_id(0)
    slot = lax.rem(i, 2)
    half = LANES // 2
    lanes = group * LANES
    heads = 2 * group
    first = lax.broadcasted_iota(jnp.int32, (1, LANES), 1) < half

    def columns(part):
        return pl.ds(part * lanes, lanes)

    def row_copies(which, at):
        stage, target = ((att_stage, att_hbm), (query_stage, grad_hbm))[which]
        return [
            pltpu.make_async_copy(
                stage.at[at, pl.ds(r * blk, blk)],
                target.at[where_ref[i * per + r], :, columns(0)],
                row_sem.at[at, which, r],
            )
            for r in range(per)
        ]

    def col_copies(n):
        block = where_ref[n]
        rows = pl.ds(pl.multiple_of(n * blk, blk), blk)
        return (
            pltpu.make_async_copy(
                key_stage.at[rows], grad_hbm.at[block, :, columns(1)], col_sem.at[0, n]
            ),
            pltpu.make_async_copy(
                value_stage.at[rows], grad_hbm.at[block, :, columns(2)], col_sem.at[1, n]
            ),
        )

    def load(parts):
        return jnp.concatenate([part[0] for part in parts], axis=0)

    def tables(rows):
        return cos_ref[rows], up_ref[rows], down_ref[rows]

    quarter = ROT // 2

    def turned(x, tab, sign):
        return jnp.concatenate(
            [
                y * tab[0]
                + sign
                * (pltpu.roll(y, quarter, 1) * tab[1] + pltpu.roll(y, LANES - quarter, 1) * tab[2])
                for y in (x[:, n * LANES : (n + 1) * LANES] for n in range(group))
            ],
            axis=1,
        )

    def one_head(x, h):
        pair = x[:, (h // 2) * LANES : (h // 2 + 1) * LANES]
        nothing = jnp.zeros_like(pair)
        return jnp.where(first, pair, nothing) if h % 2 == 0 else jnp.where(first, nothing, pair)

    @pl.when(i >= 2)
    def _():
        for which in range(2):
            for copy in row_copies(which, slot):
                copy.wait()

    here = pl.ds(pl.multiple_of(i * chunk, chunk), chunk)
    tab = tables(here)
    qkv = load(qkv_in)
    query = (turned(qkv[:, :lanes].astype(WIDE), tab, 1.0) * scale).astype(LOW)
    key_new = turned(qkv[:, lanes : 2 * lanes].astype(WIDE), tab, 1.0)
    value_new = qkv[:, 2 * lanes :]
    grad = load(g_in)
    keys[here] = key_new.astype(LOW)
    values[here] = value_new
    values_t[:, here] = value_new.T
    key_sum[here] = jnp.zeros((chunk, lanes), WIDE)
    value_sum[here] = jnp.zeros((chunk, lanes), WIDE)
    top_ref[...] = jnp.full(top_ref.shape, -1e30, WIDE)
    total_ref[...] = jnp.zeros(total_ref.shape, WIDE)
    mix_ref[...] = jnp.zeros(mix_ref.shape, WIDE)
    back_ref[...] = jnp.zeros(back_ref.shape, WIDE)
    query_of = [one_head(query, h) for h in range(heads)]
    grad_of = [one_head(grad, h) for h in range(heads)]
    query_pair = [
        jnp.concatenate(query_of[2 * n : 2 * n + 2], axis=0) for n in range(group)
    ]
    grad_pair = [jnp.concatenate(grad_of[2 * n : 2 * n + 2], axis=0) for n in range(group)]
    before = jnp.minimum(i, full_chunks)
    doubles = before // 2
    odd = before - 2 * doubles

    def fold(x, how):
        return how(x.reshape(x.shape[0] // 8, 8, chunk), axis=0)

    def pair_lanes(n):
        return slice(n * LANES, (n + 1) * LANES)

    def head_rows(h):
        return slice(h * half, (h + 1) * half)

    def sweep(tile):
        def quad(t, carry):
            start = pl.multiple_of(t * 4 * chunk, 4 * chunk)
            tile(start, start, 4 * chunk, False)
            return carry

        lax.fori_loop(0, doubles // 2, quad, 0)

        @pl.when(doubles % 2 == 1)
        def _():
            start = pl.multiple_of((doubles - 1) * 2 * chunk, 2 * chunk)
            tile(start, start, 2 * chunk, False)

        held = pl.multiple_of(doubles * 2 * chunk, chunk)

        @pl.when(odd == 1)
        def _():
            tile(held, held, 2 * chunk, True)

        @pl.when(odd == 0)
        def _():
            tile(pl.multiple_of(i * chunk, chunk), held, chunk, True)

    def score(start, held, size, masked):
        rows, to = pl.ds(start, size), pl.ds(held, size)
        if masked:
            key_row = lax.broadcasted_iota(jnp.int32, (size, chunk), 0) + start
            query_col = lax.broadcasted_iota(jnp.int32, (size, chunk), 1) + i * chunk
            seen = key_row <= query_col
        for h in range(heads):
            raw = dot(keys[rows, pair_lanes(h // 2)], query_of[h], NT)
            if masked:
                raw = jnp.where(seen, raw, -1e30)
            probs[h, to] = raw
            top_ref[h] = jnp.maximum(top_ref[h], fold(raw, jnp.max))

    sweep(score)
    top = [jnp.max(top_ref[h], axis=0, keepdims=True) for h in range(heads)]

    def mix(start, held, size, masked):
        rows, to = pl.ds(start, size), pl.ds(held, size)
        for h in range(heads):
            weight = jnp.exp(probs[h, to] - top[h])
            probs[h, to] = weight
            total_ref[h] += fold(weight, jnp.sum)
            mix_ref[head_rows(h)] += dot(values_t[head_rows(h), rows], weight.astype(LOW), NN)

    sweep(mix)
    inverse = [1.0 / jnp.sum(total_ref[h], axis=0, keepdims=True) for h in range(heads)]
    attended = jnp.concatenate(
        [mix_ref[head_rows(h)] * inverse[h] for h in range(heads)], axis=0
    )
    shared = grad.T.astype(WIDE) * attended
    inner = [jnp.sum(shared[head_rows(h)], axis=0, keepdims=True) for h in range(heads)]
    att_stage[slot] = attended.astype(LOW).T
    for copy in row_copies(0, slot):
        copy.start()

    def back(start, held, size, masked):
        rows, to = pl.ds(start, size), pl.ds(held, size)
        for n in range(group):
            value = values[rows, pair_lanes(n)]
            weights, grads = [], []
            for h in (2 * n, 2 * n + 1):
                weight = probs[h, to] * inverse[h]
                weight_grad = dot(value, grad_of[h], NT)
                score_grad = (weight * (weight_grad - inner[h])).astype(LOW)
                weights.append(weight.astype(LOW))
                grads.append(score_grad)
            value_sum[rows, pair_lanes(n)] += dot(
                jnp.concatenate(weights, axis=1), grad_pair[n], NN
            )
            key = keys[rows, pair_lanes(n)]
            back_ref[:, pair_lanes(n)] += dot(
                jnp.concatenate(grads, axis=0),
                jnp.concatenate([one_head(key, h) for h in range(2)], axis=0),
                TN,
            )
            key_sum[rows, pair_lanes(n)] += dot(
                jnp.concatenate(grads, axis=1), query_pair[n], NN
            )

    sweep(back)
    query_grad = turned(back_ref[...] * scale, tab, -1.0)
    query_stage[slot] = query_grad.astype(LOW)

    def column_sums(x):
        return jnp.sum(x.reshape(chunk // 8, 8, lanes), axis=0)

    @pl.when(i == 0)
    def _():
        sums_ref[...] = jnp.zeros(sums_ref.shape, WIDE)

    sums_ref[:, :lanes] += column_sums(query_grad)
    for copy in row_copies(1, slot):
        copy.start()

    @pl.when(i == chunks - 1)
    def _():
        @pl.loop(0, chunks)
        def _(n):
            rows = pl.ds(pl.multiple_of(n * chunk, chunk), chunk)
            key_grad = turned(key_sum[rows], tables(rows), -1.0)
            key_stage[rows] = key_grad.astype(LOW)
            value_stage[rows] = value_sum[rows].astype(LOW)
            sums_ref[:, lanes : 2 * lanes] += column_sums(key_grad)
            sums_ref[:, 2 * lanes :] += column_sums(value_sum[rows])
            for r in range(per):
                for copy in col_copies(n * per + r):
                    copy.start()

        for at in range(2):
            for which in range(2):
                for copy in row_copies(which, at):
                    copy.wait()

        @pl.loop(0, chunks * per)
        def _(n):
            for copy in col_copies(n):
                copy.wait()


def attention(qkv, grad, where, tabs, lanes, which, head_dim):
    rows = grad.shape[0]
    chunk, blk = CHUNK, BLK
    per, chunks, blocks = chunk // blk, rows // chunk, rows // blk
    group = lanes // LANES
    heads = 2 * group
    qkv_blocks = qkv.reshape(blocks, blk, qkv.shape[1])
    grad_blocks = grad.reshape(blocks, blk, grad.shape[1])

    def spec(columns, r):
        return pl.BlockSpec((1, blk, columns), lambda i, at: (at[i * per + r], 0, which))

    in_specs = [spec(3 * lanes, r) for r in range(per)] + [spec(lanes, r) for r in range(per)]
    in_specs += [pl.BlockSpec((rows, LANES), lambda i, at: (0, 0), pipeline_mode=pl.Buffered(1))] * 3
    operands = [qkv_blocks] * per + [grad_blocks] * per + list(tabs)
    kernel = functools.partial(
        attention_kernel,
        chunk=chunk,
        chunks=chunks,
        full_chunks=PROMPT // chunk,
        blk=blk,
        group=group,
        scale=1.0 / math.sqrt(head_dim),
    )
    attended, grads, sums = pl.pallas_call(
        kernel,
        out_shape=(
            jax.ShapeDtypeStruct((blocks, blk, lanes), LOW),
            jax.ShapeDtypeStruct((blocks, blk, 3 * lanes), LOW),
            jax.ShapeDtypeStruct((8, 3 * lanes), WIDE),
        ),
        grid_spec=pltpu.PrefetchScalarGridSpec(
            num_scalar_prefetch=1,
            grid=(chunks,),
            in_specs=in_specs,
            out_specs=[pl.BlockSpec(memory_space=pl.ANY)] * 2
            + [pl.BlockSpec((8, 3 * lanes), lambda i, at: (0, 0))],
            scratch_shapes=[
                pltpu.VMEM((rows, lanes), LOW),
                pltpu.VMEM((rows, lanes), LOW),
                pltpu.VMEM((lanes, rows), LOW),
                pltpu.VMEM((heads, PROMPT + chunk, chunk), WIDE),
                pltpu.VMEM((rows, lanes), WIDE),
                pltpu.VMEM((rows, lanes), WIDE),
                pltpu.VMEM((heads, 8, chunk), WIDE),
                pltpu.VMEM((heads, 8, chunk), WIDE),
                pltpu.VMEM((lanes, chunk), WIDE),
                pltpu.VMEM((chunk, lanes), WIDE),
                pltpu.VMEM((2, chunk, lanes), LOW),
                pltpu.VMEM((2, chunk, lanes), LOW),
                pltpu.VMEM((rows, lanes), LOW),
                pltpu.VMEM((rows, lanes), LOW),
                pltpu.SemaphoreType.DMA((2, 2, per)),
                pltpu.SemaphoreType.DMA((2, blocks)),
            ],
        ),
        compiler_params=pltpu.CompilerParams(
            dimension_semantics=("arbitrary",), vmem_limit_bytes=56 << 20
        ),
        cost_estimate=LITTLE,
        name="attention",
    )(where, *operands)
    return attended.reshape(rows, lanes), grads.reshape(rows, 3 * lanes), jnp.sum(sums, axis=0)


def after(value, *others):
    return lax.optimization_barrier((value,) + others)[0] if others else value


def ring_of(count):
    order = list(range(count // 2)) + list(range(count - 1, count // 2 - 1, -1))
    ahead = [(order[n], order[(n + 1) % count]) for n in range(count)]
    return order, ahead, [(b, a) for a, b in ahead]


def rank_of(offset, count):
    offset %= count
    if offset == 0 or 2 * offset == count:
        return max(2 * offset - 1, 0)
    return 2 * offset if 2 * offset < count else 2 * (count - offset) - 1


def ring_pieces(own, axis, gate=()):
    count = lax.axis_size(axis)
    _, ahead, behind = ring_of(count)
    pieces, half = [own], own.shape[0] // 2
    from_behind = from_ahead = own
    for _ in range(count // 2 - 1):
        from_behind = lax.ppermute(from_behind, axis, ahead)
        from_ahead = lax.ppermute(from_ahead, axis, behind)
        pieces += [from_behind, from_ahead]
    if gate:
        from_behind, from_ahead = after(from_behind, *gate), after(from_ahead, *gate)
    far = [
        lax.ppermute(from_behind[:half], axis, ahead),
        lax.ppermute(from_ahead[half:], axis, behind),
    ]
    return pieces + far


def ring_reduce(part, axis, cuts=1, chained=False):
    count = lax.axis_size(axis)
    _, ahead, behind = ring_of(count)

    def plus(a, b):
        return (a.astype(WIDE) + b.astype(WIDE)).astype(LOW)

    def cut_rows(term, sizes):
        if isinstance(term, (list, tuple)):
            return term
        ends = [sum(sizes[: n + 1]) for n in range(len(sizes))]
        return [term[end - size : end] for end, size in zip(ends, sizes)]

    far = part(count - 1)
    half = sum(a.shape[0] for a in far) // 2 if isinstance(far, (list, tuple)) else far.shape[0] // 2
    far = cut_rows(far, [half, half])
    up, down = lax.ppermute(far[0], axis, ahead), lax.ppermute(far[1], axis, behind)
    hops = [(up, down)]
    if count == 2:
        return [(0, up), (half, down)], hops
    pieces = [half // cuts] * cuts
    to_ahead = cut_rows(part(count - 2), [half] + pieces)
    to_behind = cut_rows(part(count - 3), pieces + [half])
    got_up, got_down = {}, {}
    got_up[0] = lax.ppermute(plus(to_ahead[0], up), axis, ahead)
    got_down[half] = lax.ppermute(plus(to_behind[-1], down), axis, behind)
    hops.append((got_up[0], got_down[half]))
    for n in range(cuts):
        gate = hops[-1] if chained else ()
        at = n * (half // cuts)
        got_up[half + at] = lax.ppermute(after(to_ahead[1 + n], *gate), axis, ahead)
        got_down[at] = lax.ppermute(after(to_behind[n], *gate), axis, behind)
        hops.append((got_up[half + at], got_down[at]))
    if count == 4:
        return sorted(got_up.items()) + sorted(got_down.items()), hops
    up = jnp.concatenate([piece for _, piece in sorted(got_up.items())], axis=0)
    down = jnp.concatenate([piece for _, piece in sorted(got_down.items())], axis=0)
    for s in range(count // 2 - 2, 0, -1):
        up = lax.ppermute(plus(part(2 * s), up), axis, ahead)
        down = lax.ppermute(plus(part(2 * s - 1), down), axis, behind)
        hops.append((up, down))
    return [(0, up), (0, down)], hops


def ring_exchange(part, axis):
    count = lax.axis_size(axis)
    order, _, _ = ring_of(count)
    got = [None] * count
    got[0] = part(0)
    for offset in range(1, count):
        hops = [(order[n], order[(n + offset) % count]) for n in range(count)]
        got[rank_of(-offset, count)] = lax.ppermute(part(rank_of(offset, count)), axis, hops)
    return got


def sum_everywhere(values, axes, gates=()):
    gates = list(gates)
    for axis in axes:
        count, span = lax.axis_size(axis), 1
        while span < count:
            pairs = [(n, n ^ span) for n in range(count)]
            values = after(values, *(gates.pop(0) if gates else ()))
            values = values + lax.ppermute(values, axis, pairs)
            span *= 2
    return values


def gelu_and_slope(h):
    inner_scale = math.sqrt(2.0 / math.pi)
    square = h * h
    t = jnp.tanh(h * (inner_scale + (inner_scale * 0.044715) * square))
    half = 0.5 * h
    rise = 0.5 + 0.5 * t
    bend = inner_scale + (3.0 * inner_scale * 0.044715) * square
    return (h * rise).astype(LOW), (rise + (half - half * t * t) * bend).astype(LOW)


def expand_kernel(x_ref, w_ref, b_ref, act_ref, slope_ref, *, cols):
    x = x_ref[...]
    for n in range(w_ref.shape[1] // cols):
        at = slice(n * cols, (n + 1) * cols)
        act, slope = gelu_and_slope(dot(x, w_ref[:, at], NN) + b_ref[:, at])
        act_ref[:, at] = act
        slope_ref[:, at] = slope


def expand(x, w, b):
    rows, width = x.shape
    hidden = w.shape[1]
    tile = 320
    out = jax.ShapeDtypeStruct((rows, hidden), LOW)
    return pl.pallas_call(
        functools.partial(expand_kernel, cols=min(512, hidden)),
        out_shape=(out, out),
        grid=(rows // tile,),
        in_specs=[
            pl.BlockSpec((tile, width), lambda i: (i, 0)),
            pl.BlockSpec((width, hidden), lambda i: (0, 0), pipeline_mode=pl.Buffered(1)),
            pl.BlockSpec((1, hidden), lambda i: (0, 0)),
        ],
        out_specs=[pl.BlockSpec((tile, hidden), lambda i: (i, 0))] * 2,
        compiler_params=pltpu.CompilerParams(
            dimension_semantics=("arbitrary",), vmem_limit_bytes=48 << 20
        ),
        cost_estimate=pl.CostEstimate(
            flops=2 * rows * width * hidden,
            bytes_accessed=2 * (rows * width + width * hidden + 2 * rows * hidden),
            transcendentals=rows * hidden,
        ),
        name="expand",
    )(x, w, b[None])


def slope_grad_kernel(*refs, spans, cols):
    pieces = refs[: len(spans)]
    w_ref, slope_ref, out_ref, whole_ref, sums_ref = refs[len(spans) :]
    i = pl.program_id(0)
    for (first, span), piece in zip(spans, pieces):

        @pl.when((i >= first) & (i < first + span))
        def _(piece=piece):
            whole_ref[...] = piece[...]

    @pl.when(i == 0)
    def _():
        sums_ref[...] = jnp.zeros(sums_ref.shape, WIDE)

    x = whole_ref[...]
    for n in range(w_ref.shape[1] // cols):
        at = slice(n * cols, (n + 1) * cols)
        value = dot(x, w_ref[:, at], NN) * slope_ref[:, at].astype(WIDE)
        out_ref[:, at] = value.astype(LOW)
        sums_ref[:, at] += jnp.sum(value.reshape(value.shape[0] // 8, 8, cols), axis=0)


def slope_grad(pieces, w, slope):
    width, hidden = w.shape
    tile = pieces[-1].shape[0]
    spans, first = [], 0
    for piece in pieces:
        spans.append((first, piece.shape[0] // tile))
        first += piece.shape[0] // tile
    by_row = pl.BlockSpec((tile, hidden), lambda i: (i, 0))

    def piece_spec(first, span):
        return pl.BlockSpec((tile, width), lambda i: (jnp.clip(i - first, 0, span - 1), 0))

    grad, whole, sums = pl.pallas_call(
        functools.partial(slope_grad_kernel, spans=tuple(spans), cols=min(512, hidden)),
        out_shape=(
            jax.ShapeDtypeStruct((first * tile, hidden), LOW),
            jax.ShapeDtypeStruct((first * tile, width), LOW),
            jax.ShapeDtypeStruct((8, hidden), WIDE),
        ),
        grid=(first,),
        in_specs=[piece_spec(*span) for span in spans]
        + [
            pl.BlockSpec((width, hidden), lambda i: (0, 0), pipeline_mode=pl.Buffered(1)),
            by_row,
        ],
        out_specs=[
            by_row,
            pl.BlockSpec((tile, width), lambda i: (i, 0)),
            pl.BlockSpec((8, hidden), lambda i: (0, 0)),
        ],
        compiler_params=pltpu.CompilerParams(
            dimension_semantics=("arbitrary",), vmem_limit_bytes=48 << 20
        ),
        cost_estimate=pl.CostEstimate(
            flops=2 * first * tile * width * hidden,
            bytes_accessed=2 * first * tile * (2 * width + 2 * hidden),
            transcendentals=0,
        ),
        name="slope_grad",
    )(*pieces, w, slope)
    return grad, whole, jnp.sum(sums, axis=0)


def input_grad_kernel(*refs, terms, ranks):
    grads, weights = refs[: terms * ranks], refs[terms * ranks : terms * ranks + terms]
    rest = refs[terms * (ranks + 1) :]
    normed_refs, out_refs, sums_ref = rest[:ranks], list(rest[ranks:-1]), rest[-1]
    plain = weighted = 0.0
    for n in range(ranks):
        mine = grads[n * terms : (n + 1) * terms]
        total = sum(dot(g[...], w[...], NT) for g, w in zip(mine, weights))
        at = 0
        while at < total.shape[0]:
            out_ref = out_refs.pop(0)
            out_ref[...] = total[at : at + out_ref.shape[0]].astype(LOW)
            at += out_ref.shape[0]
        plain += jnp.sum(total, axis=0, keepdims=True)
        weighted += jnp.sum(total * normed_refs[n][...].astype(WIDE), axis=0, keepdims=True)
    sums_ref[0:1] = plain
    sums_ref[1:2] = weighted


def input_grad(grads, weights, normed, ranks, rows, cuts, cost):
    width = normed.shape[1]
    cols = 512
    keep = pl.Buffered(1)
    in_specs = [
        pl.BlockSpec((rows, g.shape[1]), lambda i, rank=rank: (rank, 0), pipeline_mode=keep)
        for rank in ranks
        for g in grads
    ]
    in_specs += [
        pl.BlockSpec((cols, g.shape[1]), lambda i, at=at: (i, at))
        for g, (_, at) in zip(grads, weights)
    ]
    in_specs += [pl.BlockSpec((rows, cols), lambda i, rank=rank: (rank, i)) for rank in ranks]
    sizes = [size for cut in cuts for size in cut]
    *parts, sums = pl.pallas_call(
        functools.partial(input_grad_kernel, terms=len(grads), ranks=len(ranks)),
        out_shape=[jax.ShapeDtypeStruct((size, width), LOW) for size in sizes]
        + [jax.ShapeDtypeStruct((2, width), WIDE)],
        grid=(width // cols,),
        in_specs=in_specs,
        out_specs=[pl.BlockSpec((size, cols), lambda i: (0, i)) for size in sizes]
        + [pl.BlockSpec((2, cols), lambda i: (0, i))],
        compiler_params=pltpu.CompilerParams(
            dimension_semantics=("arbitrary",), vmem_limit_bytes=58 << 20
        ),
        cost_estimate=cost,
        name="input_grad",
    )(*grads * len(ranks), *[w for w, _ in weights], *[normed] * len(ranks))
    return [[parts.pop(0) for _ in cut] for cut in cuts], sums


def place_kernel(*refs, starts, count, groups):
    pieces = refs[: count * groups]
    dense = refs[count * groups : count * groups + count + 1]
    rest = refs[count * (groups + 1) + 1 :]
    token_ref, bias_ref, own_ref = rest[:3]
    terms, out_ref, acc = rest[3:-2], rest[-2], rest[-1]
    acc[...] = token_ref[...].astype(WIDE) + bias_ref[...] + own_ref[...].astype(WIDE)
    for start, term in zip(starts, terms):
        acc[start : start + term.shape[0]] += term[...].astype(WIDE)
    lanes = pieces[0].shape[1]
    steps = pl.num_programs(0)
    low_half = pl.program_id(0) * 2 < steps
    far = jnp.where(low_half, dense[count - 1][...], dense[count][...])
    total = acc[...]
    for rank in range(count):
        weight = dense[rank][...] if rank < count - 1 else far
        for n in range(groups):
            part = weight[:, n * lanes : (n + 1) * lanes]
            total += dot(pieces[rank * groups + n][...], part, NT)
    out_ref[...] = total.astype(LOW)


def place_output(pieces, dense_pieces, tokens, bias, own, terms, count, groups):
    rows, width = tokens.shape
    cols = 512
    half = width // cols // 2
    whole = lambda a: pl.BlockSpec(a.shape, lambda i: (0, 0), pipeline_mode=pl.Buffered(1))
    in_specs = [whole(piece) for piece in pieces]
    depth = dense_pieces[0].shape[1]
    in_specs += [pl.BlockSpec((cols, depth), lambda i: (i, 0)) for _ in range(count - 1)]
    in_specs.append(pl.BlockSpec((cols, depth), lambda i: (jnp.minimum(i, half - 1), 0)))
    in_specs.append(pl.BlockSpec((cols, depth), lambda i: (jnp.maximum(i - half, 0), 0)))
    by_column = lambda n: pl.BlockSpec((n, cols), lambda i: (0, i))
    in_specs += [by_column(rows), by_column(1), by_column(rows)]
    in_specs += [by_column(term.shape[0]) for _, term in terms]
    return pl.pallas_call(
        functools.partial(
            place_kernel, starts=tuple(start for start, _ in terms), count=count, groups=groups
        ),
        out_shape=jax.ShapeDtypeStruct((rows, width), LOW),
        grid=(width // cols,),
        in_specs=in_specs,
        out_specs=by_column(rows),
        scratch_shapes=[pltpu.VMEM((rows, cols), WIDE)],
        compiler_params=pltpu.CompilerParams(
            dimension_semantics=("arbitrary",), vmem_limit_bytes=58 << 20
        ),
        cost_estimate=LITTLE,
        name="place_output",
    )(*pieces, *dense_pieces, tokens, bias, own, *[term for _, term in terms])


def token_grad_kernel(token_ref, grad_ref, own_ref, gain_ref, *refs, starts, tile):
    terms, out_ref, total = refs[:-2], refs[-2], refs[-1]
    first = pl.program_id(0) * tile
    total[...] = own_ref[...].astype(WIDE)
    for start, term in zip(starts, terms):
        size = min(tile, term.shape[0])
        for at in range(0, term.shape[0], size):

            @pl.when(first == (start + at) // tile * tile)
            def _(start=start, term=term, at=at, size=size):
                to = (start + at) % tile
                total[to : to + size] += term[at : at + size].astype(WIDE)

    x = token_ref[...].astype(WIDE)
    centred = x - jnp.mean(x, axis=-1, keepdims=True)
    rstd = lax.rsqrt(jnp.mean(centred * centred, axis=-1, keepdims=True) + 1e-05)
    xhat = centred * rstd
    scaled = total[...] * gain_ref[...]
    mean = jnp.mean(scaled, axis=-1, keepdims=True)
    along = jnp.mean(scaled * xhat, axis=-1, keepdims=True)
    out_ref[...] = (grad_ref[...].astype(WIDE) + rstd * (scaled - mean - xhat * along)).astype(LOW)


def token_grad(tokens, grad, own, gain, terms, tile):
    rows, width = tokens.shape
    by_row = pl.BlockSpec((tile, width), lambda i: (i, 0))
    whole = lambda a: pl.BlockSpec(a.shape, lambda i: (0, 0), pipeline_mode=pl.Buffered(1))
    return pl.pallas_call(
        functools.partial(
            token_grad_kernel, starts=tuple(start for start, _ in terms), tile=tile
        ),
        out_shape=jax.ShapeDtypeStruct((rows, width), LOW),
        grid=(rows // tile,),
        in_specs=[by_row, by_row, by_row, pl.BlockSpec((1, width), lambda i: (0, 0))]
        + [whole(term) for _, term in terms],
        out_specs=by_row,
        scratch_shapes=[pltpu.VMEM((tile, width), WIDE)],
        compiler_params=pltpu.CompilerParams(
            dimension_semantics=("arbitrary",), vmem_limit_bytes=48 << 20
        ),
        cost_estimate=LITTLE,
        name="token_grad",
    )(tokens, grad, own, gain[None], *[term for _, term in terms])


def pair_grad_kernel(x_ref, y_ref, a_ref, b_ref, out_ref):
    split = a_ref.shape[1]
    out_ref[:, :split] = dot(x_ref[...], a_ref[...], TN).astype(LOW)
    out_ref[:, split:] = dot(y_ref[...], b_ref[...], TN).astype(LOW)


def pair_grad(x, y, a, b):
    rows, width = x.shape
    columns = a.shape[1] + b.shape[1]
    tile = 512
    keep = pl.Buffered(1)
    return pl.pallas_call(
        pair_grad_kernel,
        out_shape=jax.ShapeDtypeStruct((width, columns), LOW),
        grid=(width // tile,),
        in_specs=[
            pl.BlockSpec((rows, tile), lambda i: (0, i)),
            pl.BlockSpec((rows, tile), lambda i: (0, i)),
            pl.BlockSpec(a.shape, lambda i: (0, 0), pipeline_mode=keep),
            pl.BlockSpec(b.shape, lambda i: (0, 0), pipeline_mode=keep),
        ],
        out_specs=pl.BlockSpec((tile, columns), lambda i: (i, 0)),
        compiler_params=pltpu.CompilerParams(
            dimension_semantics=("arbitrary",), vmem_limit_bytes=58 << 20
        ),
        cost_estimate=LITTLE,
        name="pair_grad",
    )(x, y, a, b)


def rope_tables(rows):
    place = lax.broadcasted_iota(jnp.int32, (rows, LANES), 0)
    lane = lax.broadcasted_iota(jnp.int32, (rows, LANES), 1)
    pos = jnp.where(place < PROMPT, place, PROMPT + (place - PROMPT) % CLEN)
    half = ROT // 2
    freq = 10000.0 ** (-2.0 * jnp.arange(half, dtype=WIDE) / ROT)
    angle = pos.astype(WIDE) * jnp.tile(freq, LANES // half)[None, :]
    dim = lane % (LANES // 2)
    cosine, sine = jnp.cos(angle), jnp.sin(angle)
    return [
        jnp.where(dim < ROT, cosine, 1.0),
        jnp.where((dim >= half) & (dim < ROT), sine, 0.0),
        jnp.where(dim < half, -sine, 0.0),
    ]


def shards(
    tokens,
    cotangent,
    block_table,
    ln_gain,
    ln_bias,
    w_qkv,
    b_qkv,
    w_dense,
    b_dense,
    w_fc1,
    b_fc1,
    w_fc2,
    b_fc2,
):
    _, local_rows, width = tokens.shape
    head_dim = width // HEADS
    count = lax.axis_size("ctx")
    me = lax.axis_index("ctx")
    rows = local_rows * count
    local_blocks = local_rows // BLK
    each = w_dense.shape[0]
    hidden = w_fc2.shape[0]
    gain, shift = ln_gain.astype(WIDE), ln_bias.astype(WIDE)

    def of_rank(whole, rank):
        return whole[rank * local_rows : (rank + 1) * local_rows]

    order, _, _ = ring_of(count)
    places = [0] * count
    for n, device in enumerate(order):
        places[device] = n
    places = jnp.asarray(places, jnp.int32)
    ranks = jnp.asarray([rank_of(n, count) for n in range(count)], jnp.int32)
    slots = jnp.arange(rows // BLK, dtype=jnp.int32)
    offset = (places[slots // local_blocks] - places[me]) % count
    held_at = ranks[offset] * local_blocks + slots % local_blocks
    hit = block_table[0][None, :] == slots[:, None]
    where = jnp.sum(jnp.where(hit, held_at[None, :], 0), axis=1).astype(jnp.int32)

    own_tokens = tokens[0].astype(WIDE)
    own_grad = cotangent[0]
    average = jnp.mean(own_tokens, axis=-1, keepdims=True)
    centred = own_tokens - average
    rstd = lax.rsqrt(jnp.mean(centred * centred, axis=-1, keepdims=True) + 1e-05)
    xhat = centred * rstd
    normed_own = (xhat * gain + shift).astype(LOW)

    def gather_rows(shard):
        return lax.all_gather(shard, "fsdp", axis=0, tiled=True)

    def scatter_rows(whole):
        return lax.psum_scatter(whole, "fsdp", scatter_dimension=0, tiled=True)

    lanes = 2 * LANES if each % (2 * LANES) == 0 else LANES
    groups = each // lanes

    def by_group(values):
        cut = values.reshape(-1, 3, groups, lanes)
        return jnp.swapaxes(cut, 1, 2).reshape(-1, 3 * each)

    tabs = rope_tables(rows)
    own_grad_sum = jnp.sum(own_grad.astype(WIDE), axis=0)
    fc1_bias = lax.dynamic_slice_in_dim(b_fc1, me * hidden, hidden, 0).astype(WIDE)
    early = (where, own_grad_sum, fc1_bias, *tabs)
    normed_pieces = ring_pieces(normed_own, "ctx")
    normed = after(jnp.concatenate(normed_pieces, axis=0), *early)
    attention_shard = jnp.concatenate([by_group(w_qkv), w_dense.T], axis=1)
    fc1_weight = gather_rows(w_fc1)
    fc2_turned = gather_rows(after(w_fc2.T, *normed_pieces[1:-2]))
    attention_weight = gather_rows(after(attention_shard, *normed_pieces[-2:]))
    qkv_weight, dense_turned = attention_weight[:, : 3 * each], attention_weight[:, 3 * each :]

    qkv_bias = lax.dynamic_slice_in_dim(b_qkv.reshape(3, width), me * each, each, 1)
    activated, slope = expand(normed, fc1_weight, fc1_bias)

    sent_grad = after(own_grad, *normed_pieces[-2:])
    grad_pieces = ring_pieces(sent_grad, "ctx", gate=(activated,))
    ff_part = dot(activated, fc2_turned, NT).astype(LOW)
    ff_terms, ff_hops = ring_reduce(lambda rank: of_rank(ff_part, rank), "ctx", chained=True)
    first, second, last = ff_hops[0], ff_hops[min(1, len(ff_hops) - 1)], ff_hops[-1]

    gated = [after(piece, ff_part) for piece in grad_pieces]
    expanded_grad, grads, fc1_bias_part = slope_grad(gated, fc2_turned, slope)
    d_fc2_part = dot(after(grads, expanded_grad, *first), activated, TN).astype(LOW)
    d_fc2 = scatter_rows(d_fc2_part)
    qkv = dot(after(normed, d_fc2_part), qkv_weight, NN)
    qkv = (qkv + by_group(qkv_bias)[0].astype(WIDE)).astype(LOW)
    attended_grad = dot(after(grads, qkv, *second), dense_turned, NN).astype(LOW)
    gated = after(normed, attended_grad)
    d_fc1_part = dot(gated, expanded_grad, TN).astype(LOW)
    d_fc1 = scatter_rows(d_fc1_part)

    dense_pieces = ring_pieces(after(dense_turned, *second), "ctx")

    attended, qkv_grads, qkv_sums, d_attention, swapped = [], [], [], [], []
    ordered = (d_fc1_part,)
    for which in range(groups):
        got, got_grads, got_sums = attention(
            after(qkv, *ordered), attended_grad, where, tabs, lanes, which, head_dim
        )
        attended.append(got)
        qkv_grads.append(got_grads)
        qkv_sums.append(got_sums)
        if which < groups - 1:
            swapped.append(ring_exchange(lambda rank, got=got: of_rank(got, rank), "ctx"))
            gated = after(normed, d_fc2, *last, *dense_pieces[1:-2]) if which == 0 else normed
            d_part = pair_grad(gated, grads, got_grads, got)
            ordered = (d_part,)
            d_attention.append(scatter_rows(d_part))

    weights = [(attention_weight, which) for which in range(groups)] + [(fc1_weight, 0)]
    early_swaps = [piece for pieces in swapped for piece in pieces]
    turn = after(expanded_grad, d_fc1, *dense_pieces[-2:], *early_swaps, *attended)
    swapped.append(ring_exchange(lambda rank: of_rank(attended[-1], rank), "ctx"))
    half = local_rows // 2
    whole, far_cut, ahead_cut, behind_cut = [local_rows], [half, half], [half], [half]
    if count > 2:
        ahead_cut, behind_cut = [half, half], [half, half]
    cut_of = {0: whole, count - 2: ahead_cut, count - 3: behind_cut, count - 1: far_cut}

    def some_ranks(ranks, turn, cost=LITTLE):
        cuts = [cut_of.get(rank, whole) for rank in ranks]
        return input_grad(qkv_grads + [turn], weights, normed, ranks, local_rows, cuts, cost)

    far_part, far_sums = some_ranks([count - 1], turn)
    middle = list(range(count - 2, 0, -1))
    middle_sums, parts = 0.0, {count - 1: far_part[0]}
    turn = after(turn, *far_part[0])
    for n in range(0, len(middle), 2):
        some, some_sums = some_ranks(middle[n : n + 2], turn)
        turn = after(turn, *[piece for pieces in some for piece in pieces])
        middle_sums = middle_sums + some_sums
        parts.update(zip(middle[n : n + 2], some))
    for rank, pieces in parts.items():
        if len(pieces) == 1:
            parts[rank] = pieces[0]

    grad_terms, hops = ring_reduce(lambda rank: parts[rank], "ctx")
    last_hops = [piece for hop in hops[1:3] for piece in hop]
    gated = after(normed, turn, *hops[0], *swapped[-1], *d_attention)
    d_part = pair_grad(gated, grads, qkv_grads[-1], attended[-1])
    d_attention.append(scatter_rows(d_part))
    [own_part], own_sums = some_ranks([0], after(turn, d_part), MUCH)
    attended_own = [swapped[which][rank] for rank in range(count) for which in range(groups)]
    output = place_output(
        attended_own,
        dense_pieces,
        after(tokens[0], *own_part),
        (b_dense.astype(WIDE) + b_fc2.astype(WIDE))[None],
        ff_part,
        ff_terms,
        count,
        groups,
    )
    sums = after(far_sums + middle_sums + own_sums, output, *last_hops)

    d_qkv = jnp.concatenate(
        [part[:, : 3 * lanes].reshape(-1, 3, lanes) for part in d_attention], axis=2
    ).astype(WIDE)
    d_dense = jnp.concatenate([part[:, 3 * lanes :].T for part in d_attention], axis=0)
    d_dense = d_dense.astype(WIDE)
    d_fc1, d_fc2 = d_fc1.astype(WIDE), d_fc2.T.astype(WIDE)

    qkv_bias_part = jnp.concatenate(
        [part.reshape(3, lanes) for part in qkv_sums], axis=1
    )
    qkv_bias_wide = lax.dynamic_update_slice_in_dim(
        jnp.zeros((3, width), WIDE), qkv_bias_part, me * each, 1
    ).reshape(-1)
    fc1_bias_wide = lax.dynamic_update_slice_in_dim(
        jnp.zeros((b_fc1.shape[0],), WIDE), fc1_bias_part, me * hidden, 0
    )
    small = (
        jnp.concatenate(
            [
                sums.reshape(-1),
                qkv_bias_wide,
                own_grad_sum,
                fc1_bias_wide,
            ]
        )
    )
    d_tokens = token_grad(
        after(tokens[0], small), own_grad, own_part[0], gain, grad_terms, local_rows // 4
    )
    gates = [(), (d_tokens,), (d_fc1, d_fc2), (), (d_qkv, d_dense)]
    small = sum_everywhere(small, ("fsdp", "ctx"), gates)
    d_shift, with_normed, d_b_qkv, d_b_out, d_b_fc1 = jnp.split(
        small, [width, 2 * width, 5 * width, 6 * width]
    )
    d_gain = (with_normed - shift * d_shift) / gain
    return (
        output[None],
        d_tokens[None],
        d_gain,
        d_shift,
        d_qkv,
        d_b_qkv,
        d_dense,
        d_b_out,
        d_fc1,
        d_b_fc1,
        d_fc2,
        d_b_out,
    )


def solution(mesh):
    in_specs = (
        P("fsdp", "ctx", None),
        P("fsdp", "ctx", None),
        P("fsdp", None),
        P(),
        P(),
        P("fsdp", None, "ctx"),
        P(),
        P("ctx", "fsdp"),
        P(),
        P("fsdp", "ctx"),
        P(),
        P("ctx", "fsdp"),
        P(),
    )
    out_specs = (
        P("fsdp", "ctx", None),
        P("fsdp", "ctx", None),
        P(),
        P(),
        P("fsdp", None, "ctx"),
        P(),
        P("ctx", "fsdp"),
        P(),
        P("fsdp", "ctx"),
        P(),
        P("ctx", "fsdp"),
        P(),
    )
    return jax.shard_map(shards, mesh=mesh, in_specs=in_specs, out_specs=out_specs, check_vma=False)
```

```python
import functools
import math

import jax
import jax.numpy as jnp
from jax import lax
from jax.experimental import pallas as pl
from jax.experimental.pallas import tpu as pltpu
from jax.sharding import PartitionSpec as P

HEADS = 32
ROT = 32
PROMPT = 2048
CLEN = 256
BLK = 64
CHUNK = 256
LANES = 128
NT = (((1,), (1,)), ((), ()))
NN = (((1,), (0,)), ((), ()))
TN = (((0,), (0,)), ((), ()))
LOW = jnp.bfloat16
WIDE = jnp.float32
LITTLE = pl.CostEstimate(flops=1000000, bytes_accessed=1000000, transcendentals=0)
MUCH = pl.CostEstimate(flops=100000000000, bytes_accessed=1000000, transcendentals=0)


def dot(left, right, dims):
    return lax.dot_general(left, right, dims, preferred_element_type=WIDE)


def attention_kernel(where_ref, *refs, chunk, chunks, full_chunks, blk, group, scale):
    per = chunk // blk
    qkv_in, g_in = refs[:per], refs[per : 2 * per]
    cos_ref, up_ref, down_ref, att_hbm, grad_hbm, sums_ref = refs[2 * per : 2 * per + 6]
    (
        keys,
        values,
        values_t,
        probs,
        key_sum,
        value_sum,
        top_ref,
        total_ref,
        mix_ref,
        back_ref,
        att_stage,
        query_stage,
        key_stage,
        value_stage,
        row_sem,
        col_sem,
    ) = refs[2 * per + 6 :]
    i = pl.program_id(0)
    slot = lax.rem(i, 2)
    half = LANES // 2
    lanes = group * LANES
    heads = 2 * group
    first = lax.broadcasted_iota(jnp.int32, (1, LANES), 1) < half

    def columns(part):
        return pl.ds(part * lanes, lanes)

    def row_copies(which, at):
        stage, target = ((att_stage, att_hbm), (query_stage, grad_hbm))[which]
        return [
            pltpu.make_async_copy(
                stage.at[at, pl.ds(r * blk, blk)],
                target.at[where_ref[i * per + r], :, columns(0)],
                row_sem.at[at, which, r],
            )
            for r in range(per)
        ]

    def col_copies(n):
        block = where_ref[n]
        rows = pl.ds(pl.multiple_of(n * blk, blk), blk)
        return (
            pltpu.make_async_copy(
                key_stage.at[rows], grad_hbm.at[block, :, columns(1)], col_sem.at[0, n]
            ),
            pltpu.make_async_copy(
                value_stage.at[rows], grad_hbm.at[block, :, columns(2)], col_sem.at[1, n]
            ),
        )

    def load(parts):
        return jnp.concatenate([part[0] for part in parts], axis=0)

    def tables(rows):
        return cos_ref[rows], up_ref[rows], down_ref[rows]

    quarter = ROT // 2

    def turned(x, tab, sign):
        return jnp.concatenate(
            [
                y * tab[0]
                + sign
                * (pltpu.roll(y, quarter, 1) * tab[1] + pltpu.roll(y, LANES - quarter, 1) * tab[2])
                for y in (x[:, n * LANES : (n + 1) * LANES] for n in range(group))
            ],
            axis=1,
        )

    def one_head(x, h):
        pair = x[:, (h // 2) * LANES : (h // 2 + 1) * LANES]
        nothing = jnp.zeros_like(pair)
        return jnp.where(first, pair, nothing) if h % 2 == 0 else jnp.where(first, nothing, pair)

    @pl.when(i >= 2)
    def _():
        for which in range(2):
            for copy in row_copies(which, slot):
                copy.wait()

    here = pl.ds(pl.multiple_of(i * chunk, chunk), chunk)
    tab = tables(here)
    qkv = load(qkv_in)
    query = (turned(qkv[:, :lanes].astype(WIDE), tab, 1.0) * scale).astype(LOW)
    key_new = turned(qkv[:, lanes : 2 * lanes].astype(WIDE), tab, 1.0)
    value_new = qkv[:, 2 * lanes :]
    grad = load(g_in)
    keys[here] = key_new.astype(LOW)
    values[here] = value_new
    values_t[:, here] = value_new.T
    key_sum[here] = jnp.zeros((chunk, lanes), WIDE)
    value_sum[here] = jnp.zeros((chunk, lanes), WIDE)
    top_ref[...] = jnp.full(top_ref.shape, -1e30, WIDE)
    total_ref[...] = jnp.zeros(total_ref.shape, WIDE)
    mix_ref[...] = jnp.zeros(mix_ref.shape, WIDE)
    back_ref[...] = jnp.zeros(back_ref.shape, WIDE)
    query_of = [one_head(query, h) for h in range(heads)]
    grad_of = [one_head(grad, h) for h in range(heads)]
    query_pair = [
        jnp.concatenate(query_of[2 * n : 2 * n + 2], axis=0) for n in range(group)
    ]
    grad_pair = [jnp.concatenate(grad_of[2 * n : 2 * n + 2], axis=0) for n in range(group)]
    before = jnp.minimum(i, full_chunks)
    doubles = before // 2
    odd = before - 2 * doubles

    def fold(x, how):
        return how(x.reshape(x.shape[0] // 8, 8, chunk), axis=0)

    def pair_lanes(n):
        return slice(n * LANES, (n + 1) * LANES)

    def head_rows(h):
        return slice(h * half, (h + 1) * half)

    def sweep(tile):
        def quad(t, carry):
            start = pl.multiple_of(t * 4 * chunk, 4 * chunk)
            tile(start, start, 4 * chunk, False)
            return carry

        lax.fori_loop(0, doubles // 2, quad, 0)

        @pl.when(doubles % 2 == 1)
        def _():
            start = pl.multiple_of((doubles - 1) * 2 * chunk, 2 * chunk)
            tile(start, start, 2 * chunk, False)

        held = pl.multiple_of(doubles * 2 * chunk, chunk)

        @pl.when(odd == 1)
        def _():
            tile(held, held, 2 * chunk, True)

        @pl.when(odd == 0)
        def _():
            tile(pl.multiple_of(i * chunk, chunk), held, chunk, True)

    def score(start, held, size, masked):
        rows, to = pl.ds(start, size), pl.ds(held, size)
        if masked:
            key_row = lax.broadcasted_iota(jnp.int32, (size, chunk), 0) + start
            query_col = lax.broadcasted_iota(jnp.int32, (size, chunk), 1) + i * chunk
            seen = key_row <= query_col
        for h in range(heads):
            raw = dot(keys[rows, pair_lanes(h // 2)], query_of[h], NT)
            if masked:
                raw = jnp.where(seen, raw, -1e30)
            probs[h, to] = raw
            top_ref[h] = jnp.maximum(top_ref[h], fold(raw, jnp.max))

    sweep(score)
    top = [jnp.max(top_ref[h], axis=0, keepdims=True) for h in range(heads)]

    def mix(start, held, size, masked):
        rows, to = pl.ds(start, size), pl.ds(held, size)
        for h in range(heads):
            weight = jnp.exp(probs[h, to] - top[h])
            probs[h, to] = weight
            total_ref[h] += fold(weight, jnp.sum)
            mix_ref[head_rows(h)] += dot(values_t[head_rows(h), rows], weight.astype(LOW), NN)

    sweep(mix)
    inverse = [1.0 / jnp.sum(total_ref[h], axis=0, keepdims=True) for h in range(heads)]
    attended = jnp.concatenate(
        [mix_ref[head_rows(h)] * inverse[h] for h in range(heads)], axis=0
    )
    shared = grad.T.astype(WIDE) * attended
    inner = [jnp.sum(shared[head_rows(h)], axis=0, keepdims=True) for h in range(heads)]
    att_stage[slot] = attended.astype(LOW).T
    for copy in row_copies(0, slot):
        copy.start()

    def back(start, held, size, masked):
        rows, to = pl.ds(start, size), pl.ds(held, size)
        for n in range(group):
            value = values[rows, pair_lanes(n)]
            weights, grads = [], []
            for h in (2 * n, 2 * n + 1):
                weight = probs[h, to] * inverse[h]
                weight_grad = dot(value, grad_of[h], NT)
                score_grad = (weight * (weight_grad - inner[h])).astype(LOW)
                weights.append(weight.astype(LOW))
                grads.append(score_grad)
            value_sum[rows, pair_lanes(n)] += dot(
                jnp.concatenate(weights, axis=1), grad_pair[n], NN
            )
            key = keys[rows, pair_lanes(n)]
            back_ref[:, pair_lanes(n)] += dot(
                jnp.concatenate(grads, axis=0),
                jnp.concatenate([one_head(key, h) for h in range(2)], axis=0),
                TN,
            )
            key_sum[rows, pair_lanes(n)] += dot(
                jnp.concatenate(grads, axis=1), query_pair[n], NN
            )

    sweep(back)
    query_grad = turned(back_ref[...] * scale, tab, -1.0)
    query_stage[slot] = query_grad.astype(LOW)

    def column_sums(x):
        return jnp.sum(x.reshape(chunk // 8, 8, lanes), axis=0)

    @pl.when(i == 0)
    def _():
        sums_ref[...] = jnp.zeros(sums_ref.shape, WIDE)

    sums_ref[:, :lanes] += column_sums(query_grad)
    for copy in row_copies(1, slot):
        copy.start()

    @pl.when(i == chunks - 1)
    def _():
        @pl.loop(0, chunks)
        def _(n):
            rows = pl.ds(pl.multiple_of(n * chunk, chunk), chunk)
            key_grad = turned(key_sum[rows], tables(rows), -1.0)
            key_stage[rows] = key_grad.astype(LOW)
            value_stage[rows] = value_sum[rows].astype(LOW)
            sums_ref[:, lanes : 2 * lanes] += column_sums(key_grad)
            sums_ref[:, 2 * lanes :] += column_sums(value_sum[rows])
            for r in range(per):
                for copy in col_copies(n * per + r):
                    copy.start()

        for at in range(2):
            for which in range(2):
                for copy in row_copies(which, at):
                    copy.wait()

        @pl.loop(0, chunks * per)
        def _(n):
            for copy in col_copies(n):
                copy.wait()


def attention(qkv, grad, where, tabs, lanes, which, head_dim):
    rows = grad.shape[0]
    chunk, blk = CHUNK, BLK
    per, chunks, blocks = chunk // blk, rows // chunk, rows // blk
    group = lanes // LANES
    heads = 2 * group
    qkv_blocks = qkv.reshape(blocks, blk, qkv.shape[1])
    grad_blocks = grad.reshape(blocks, blk, grad.shape[1])

    def spec(columns, r):
        return pl.BlockSpec((1, blk, columns), lambda i, at: (at[i * per + r], 0, which))

    in_specs = [spec(3 * lanes, r) for r in range(per)] + [spec(lanes, r) for r in range(per)]
    in_specs += [pl.BlockSpec((rows, LANES), lambda i, at: (0, 0), pipeline_mode=pl.Buffered(1))] * 3
    operands = [qkv_blocks] * per + [grad_blocks] * per + list(tabs)
    kernel = functools.partial(
        attention_kernel,
        chunk=chunk,
        chunks=chunks,
        full_chunks=PROMPT // chunk,
        blk=blk,
        group=group,
        scale=1.0 / math.sqrt(head_dim),
    )
    attended, grads, sums = pl.pallas_call(
        kernel,
        out_shape=(
            jax.ShapeDtypeStruct((blocks, blk, lanes), LOW),
            jax.ShapeDtypeStruct((blocks, blk, 3 * lanes), LOW),
            jax.ShapeDtypeStruct((8, 3 * lanes), WIDE),
        ),
        grid_spec=pltpu.PrefetchScalarGridSpec(
            num_scalar_prefetch=1,
            grid=(chunks,),
            in_specs=in_specs,
            out_specs=[pl.BlockSpec(memory_space=pl.ANY)] * 2
            + [pl.BlockSpec((8, 3 * lanes), lambda i, at: (0, 0))],
            scratch_shapes=[
                pltpu.VMEM((rows, lanes), LOW),
                pltpu.VMEM((rows, lanes), LOW),
                pltpu.VMEM((lanes, rows), LOW),
                pltpu.VMEM((heads, PROMPT + chunk, chunk), WIDE),
                pltpu.VMEM((rows, lanes), WIDE),
                pltpu.VMEM((rows, lanes), WIDE),
                pltpu.VMEM((heads, 8, chunk), WIDE),
                pltpu.VMEM((heads, 8, chunk), WIDE),
                pltpu.VMEM((lanes, chunk), WIDE),
                pltpu.VMEM((chunk, lanes), WIDE),
                pltpu.VMEM((2, chunk, lanes), LOW),
                pltpu.VMEM((2, chunk, lanes), LOW),
                pltpu.VMEM((rows, lanes), LOW),
                pltpu.VMEM((rows, lanes), LOW),
                pltpu.SemaphoreType.DMA((2, 2, per)),
                pltpu.SemaphoreType.DMA((2, blocks)),
            ],
        ),
        compiler_params=pltpu.CompilerParams(
            dimension_semantics=("arbitrary",), vmem_limit_bytes=56 << 20
        ),
        cost_estimate=LITTLE,
        name="attention",
    )(where, *operands)
    return attended.reshape(rows, lanes), grads.reshape(rows, 3 * lanes), jnp.sum(sums, axis=0)


def after(value, *others):
    return lax.optimization_barrier((value,) + others)[0] if others else value


def ring_of(count):
    order = list(range(count // 2)) + list(range(count - 1, count // 2 - 1, -1))
    ahead = [(order[n], order[(n + 1) % count]) for n in range(count)]
    return order, ahead, [(b, a) for a, b in ahead]


def rank_of(offset, count):
    offset %= count
    if offset == 0 or 2 * offset == count:
        return max(2 * offset - 1, 0)
    return 2 * offset if 2 * offset < count else 2 * (count - offset) - 1


def ring_pieces(own, axis, gate=()):
    count = lax.axis_size(axis)
    _, ahead, behind = ring_of(count)
    pieces, half = [own], own.shape[0] // 2
    from_behind = from_ahead = own
    for _ in range(count // 2 - 1):
        from_behind = lax.ppermute(from_behind, axis, ahead)
        from_ahead = lax.ppermute(from_ahead, axis, behind)
        pieces += [from_behind, from_ahead]
    if gate:
        from_behind, from_ahead = after(from_behind, *gate), after(from_ahead, *gate)
        if count > 2:
            pieces[-2:] = [from_behind, from_ahead]
    far = [
        lax.ppermute(from_behind[:half], axis, ahead),
        lax.ppermute(from_ahead[half:], axis, behind),
    ]
    return pieces + far


def ring_reduce(part, axis, cuts=1, chained=False):
    count = lax.axis_size(axis)
    _, ahead, behind = ring_of(count)

    def plus(a, b):
        return (a.astype(WIDE) + b.astype(WIDE)).astype(LOW)

    def cut_rows(term, sizes):
        if isinstance(term, (list, tuple)):
            return term
        ends = [sum(sizes[: n + 1]) for n in range(len(sizes))]
        return [term[end - size : end] for end, size in zip(ends, sizes)]

    far = part(count - 1)
    half = sum(a.shape[0] for a in far) // 2 if isinstance(far, (list, tuple)) else far.shape[0] // 2
    far = cut_rows(far, [half, half])
    up, down = lax.ppermute(far[0], axis, ahead), lax.ppermute(far[1], axis, behind)
    hops = [(up, down)]
    if count == 2:
        return [(0, up), (half, down)], hops
    pieces = [half // cuts] * cuts
    to_ahead = cut_rows(part(count - 2), [half] + pieces)
    to_behind = cut_rows(part(count - 3), pieces + [half])
    got_up, got_down = {}, {}
    got_up[0] = lax.ppermute(plus(to_ahead[0], up), axis, ahead)
    got_down[half] = lax.ppermute(plus(to_behind[-1], down), axis, behind)
    hops.append((got_up[0], got_down[half]))
    for n in range(cuts):
        gate = hops[-1] if chained else ()
        at = n * (half // cuts)
        got_up[half + at] = lax.ppermute(after(to_ahead[1 + n], *gate), axis, ahead)
        got_down[at] = lax.ppermute(after(to_behind[n], *gate), axis, behind)
        hops.append((got_up[half + at], got_down[at]))
    if count == 4:
        return sorted(got_up.items()) + sorted(got_down.items()), hops
    up = jnp.concatenate([piece for _, piece in sorted(got_up.items())], axis=0)
    down = jnp.concatenate([piece for _, piece in sorted(got_down.items())], axis=0)
    for s in range(count // 2 - 2, 0, -1):
        up = lax.ppermute(plus(part(2 * s), up), axis, ahead)
        down = lax.ppermute(plus(part(2 * s - 1), down), axis, behind)
        hops.append((up, down))
    return [(0, up), (0, down)], hops


def ring_exchange(part, axis):
    count = lax.axis_size(axis)
    order, _, _ = ring_of(count)
    got = [None] * count
    got[0] = part(0)
    for offset in range(1, count):
        hops = [(order[n], order[(n + offset) % count]) for n in range(count)]
        got[rank_of(-offset, count)] = lax.ppermute(part(rank_of(offset, count)), axis, hops)
    return got


def exchange_steps(axes):
    steps = []
    for axis in axes:
        count, span = lax.axis_size(axis), 1
        while span < count:
            steps.append((axis, [(n, n ^ span) for n in range(count)]))
            span *= 2
    return steps


def exchange(values, steps):
    for axis, pairs in steps:
        values = values + lax.ppermute(values, axis, pairs)
    return values


def gelu_and_slope(h):
    inner_scale = math.sqrt(2.0 / math.pi)
    square = h * h
    t = jnp.tanh(h * (inner_scale + (inner_scale * 0.044715) * square))
    half = 0.5 * h
    rise = 0.5 + 0.5 * t
    bend = inner_scale + (3.0 * inner_scale * 0.044715) * square
    return (h * rise).astype(LOW), (rise + (half - half * t * t) * bend).astype(LOW)


def join_piece(pieces, spans, whole_ref):
    i = pl.program_id(0)
    for (first, span), piece in zip(spans, pieces):

        @pl.when((i >= first) & (i < first + span))
        def _(piece=piece):
            whole_ref[...] = piece[...]


def piece_blocks(pieces):
    tile, width = pieces[-1].shape
    spans, first = [], 0
    for piece in pieces:
        spans.append((first, piece.shape[0] // tile))
        first += piece.shape[0] // tile

    def spec(first, span):
        return pl.BlockSpec((tile, width), lambda i: (jnp.clip(i - first, 0, span - 1), 0))

    return tile, tuple(spans), [spec(*span) for span in spans]


def expand_kernel(*refs, spans, cols):
    w_ref, b_ref, act_ref, slope_ref, whole_ref = refs[len(spans) :]
    join_piece(refs[: len(spans)], spans, whole_ref)
    x = whole_ref[...]
    for n in range(w_ref.shape[1] // cols):
        at = slice(n * cols, (n + 1) * cols)
        act, slope = gelu_and_slope(dot(x, w_ref[:, at], NN) + b_ref[:, at])
        act_ref[:, at] = act
        slope_ref[:, at] = slope


def expand(pieces, w, b):
    width, hidden = w.shape
    tile, spans, specs = piece_blocks(pieces)
    rows = sum(piece.shape[0] for piece in pieces)
    by_row = pl.BlockSpec((tile, hidden), lambda i: (i, 0))
    out = jax.ShapeDtypeStruct((rows, hidden), LOW)
    return pl.pallas_call(
        functools.partial(expand_kernel, spans=spans, cols=min(512, hidden)),
        out_shape=(out, out, jax.ShapeDtypeStruct((rows, width), LOW)),
        grid=(rows // tile,),
        in_specs=specs
        + [
            pl.BlockSpec((width, hidden), lambda i: (0, 0), pipeline_mode=pl.Buffered(1)),
            pl.BlockSpec((1, hidden), lambda i: (0, 0)),
        ],
        out_specs=[by_row, by_row, pl.BlockSpec((tile, width), lambda i: (i, 0))],
        compiler_params=pltpu.CompilerParams(
            dimension_semantics=("arbitrary",), vmem_limit_bytes=48 << 20
        ),
        cost_estimate=pl.CostEstimate(
            flops=2 * rows * width * hidden,
            bytes_accessed=2 * rows * (2 * width + 2 * hidden),
            transcendentals=rows * hidden,
        ),
        name="expand",
    )(*pieces, w, b[None])


def slope_grad_kernel(*refs, spans, cols):
    pieces = refs[: len(spans)]
    w_ref, slope_ref, out_ref, whole_ref, sums_ref = refs[len(spans) :]
    join_piece(pieces, spans, whole_ref)

    @pl.when(pl.program_id(0) == 0)
    def _():
        sums_ref[...] = jnp.zeros(sums_ref.shape, WIDE)

    x = whole_ref[...]
    for n in range(w_ref.shape[1] // cols):
        at = slice(n * cols, (n + 1) * cols)
        value = dot(x, w_ref[:, at], NN) * slope_ref[:, at].astype(WIDE)
        out_ref[:, at] = value.astype(LOW)
        sums_ref[:, at] += jnp.sum(value.reshape(value.shape[0] // 8, 8, cols), axis=0)


def slope_grad(pieces, w, slope):
    width, hidden = w.shape
    tile, spans, specs = piece_blocks(pieces)
    first = sum(span for _, span in spans)
    by_row = pl.BlockSpec((tile, hidden), lambda i: (i, 0))
    grad, whole, sums = pl.pallas_call(
        functools.partial(slope_grad_kernel, spans=spans, cols=min(512, hidden)),
        out_shape=(
            jax.ShapeDtypeStruct((first * tile, hidden), LOW),
            jax.ShapeDtypeStruct((first * tile, width), LOW),
            jax.ShapeDtypeStruct((8, hidden), WIDE),
        ),
        grid=(first,),
        in_specs=specs
        + [
            pl.BlockSpec((width, hidden), lambda i: (0, 0), pipeline_mode=pl.Buffered(1)),
            by_row,
        ],
        out_specs=[
            by_row,
            pl.BlockSpec((tile, width), lambda i: (i, 0)),
            pl.BlockSpec((8, hidden), lambda i: (0, 0)),
        ],
        compiler_params=pltpu.CompilerParams(
            dimension_semantics=("arbitrary",), vmem_limit_bytes=48 << 20
        ),
        cost_estimate=pl.CostEstimate(
            flops=2 * first * tile * width * hidden,
            bytes_accessed=2 * first * tile * (2 * width + 2 * hidden),
            transcendentals=0,
        ),
        name="slope_grad",
    )(*pieces, w, slope)
    return grad, whole, jnp.sum(sums, axis=0)


def input_grad_kernel(*refs, terms, ranks):
    grads, weights = refs[: terms * ranks], refs[terms * ranks : terms * ranks + terms]
    rest = refs[terms * (ranks + 1) :]
    normed_refs, out_refs, sums_ref = rest[:ranks], list(rest[ranks:-1]), rest[-1]
    plain = weighted = 0.0
    for n in range(ranks):
        mine = grads[n * terms : (n + 1) * terms]
        total = sum(dot(g[...], w[...], NT) for g, w in zip(mine, weights))
        at = 0
        while at < total.shape[0]:
            out_ref = out_refs.pop(0)
            out_ref[...] = total[at : at + out_ref.shape[0]].astype(LOW)
            at += out_ref.shape[0]
        plain += jnp.sum(total, axis=0, keepdims=True)
        weighted += jnp.sum(total * normed_refs[n][...].astype(WIDE), axis=0, keepdims=True)
    sums_ref[0:1] = plain
    sums_ref[1:2] = weighted


def input_grad(grads, weights, normed, ranks, rows, cuts, cost):
    width = normed.shape[1]
    cols = 512
    keep = pl.Buffered(1)
    in_specs = [
        pl.BlockSpec((rows, g.shape[1]), lambda i, rank=rank: (rank, 0), pipeline_mode=keep)
        for rank in ranks
        for g in grads
    ]
    in_specs += [
        pl.BlockSpec((cols, g.shape[1]), lambda i, at=at: (i, at))
        for g, (_, at) in zip(grads, weights)
    ]
    in_specs += [pl.BlockSpec((rows, cols), lambda i, rank=rank: (rank, i)) for rank in ranks]
    sizes = [size for cut in cuts for size in cut]
    *parts, sums = pl.pallas_call(
        functools.partial(input_grad_kernel, terms=len(grads), ranks=len(ranks)),
        out_shape=[jax.ShapeDtypeStruct((size, width), LOW) for size in sizes]
        + [jax.ShapeDtypeStruct((2, width), WIDE)],
        grid=(width // cols,),
        in_specs=in_specs,
        out_specs=[pl.BlockSpec((size, cols), lambda i: (0, i)) for size in sizes]
        + [pl.BlockSpec((2, cols), lambda i: (0, i))],
        compiler_params=pltpu.CompilerParams(
            dimension_semantics=("arbitrary",), vmem_limit_bytes=58 << 20
        ),
        cost_estimate=cost,
        name="input_grad",
    )(*grads * len(ranks), *[w for w, _ in weights], *[normed] * len(ranks))
    return [[parts.pop(0) for _ in cut] for cut in cuts], sums


def place_kernel(*refs, starts, count, groups):
    pieces = refs[: count * groups]
    dense = refs[count * groups : count * groups + count + 1]
    rest = refs[count * (groups + 1) + 1 :]
    token_ref, bias_ref, own_ref = rest[:3]
    terms, out_ref, acc = rest[3:-2], rest[-2], rest[-1]
    acc[...] = token_ref[...].astype(WIDE) + bias_ref[...] + own_ref[...].astype(WIDE)
    for start, term in zip(starts, terms):
        acc[start : start + term.shape[0]] += term[...].astype(WIDE)
    steps = pl.num_programs(0)
    low_half = pl.program_id(0) * 2 < steps
    far = jnp.where(low_half, dense[count - 1][...], dense[count][...])
    total = acc[...]
    for rank in range(count):
        weight = dense[rank][...] if rank < count - 1 else far
        mine = [piece[...] for piece in pieces[rank * groups : (rank + 1) * groups]]
        total += dot(jnp.concatenate(mine, axis=1), weight, NT)
    out_ref[...] = total.astype(LOW)


def place_output(pieces, dense_pieces, tokens, bias, own, terms, count, groups):
    rows, width = tokens.shape
    cols = 512
    half = width // cols // 2
    whole = lambda a: pl.BlockSpec(a.shape, lambda i: (0, 0), pipeline_mode=pl.Buffered(1))
    in_specs = [whole(piece) for piece in pieces]
    depth = dense_pieces[0].shape[1]
    in_specs += [pl.BlockSpec((cols, depth), lambda i: (i, 0)) for _ in range(count - 1)]
    in_specs.append(pl.BlockSpec((cols, depth), lambda i: (jnp.minimum(i, half - 1), 0)))
    in_specs.append(pl.BlockSpec((cols, depth), lambda i: (jnp.maximum(i - half, 0), 0)))
    by_column = lambda n: pl.BlockSpec((n, cols), lambda i: (0, i))
    in_specs += [by_column(rows), by_column(1), by_column(rows)]
    in_specs += [by_column(term.shape[0]) for _, term in terms]
    return pl.pallas_call(
        functools.partial(
            place_kernel, starts=tuple(start for start, _ in terms), count=count, groups=groups
        ),
        out_shape=jax.ShapeDtypeStruct((rows, width), LOW),
        grid=(width // cols,),
        in_specs=in_specs,
        out_specs=by_column(rows),
        scratch_shapes=[pltpu.VMEM((rows, cols), WIDE)],
        compiler_params=pltpu.CompilerParams(
            dimension_semantics=("arbitrary",), vmem_limit_bytes=58 << 20
        ),
        cost_estimate=LITTLE,
        name="place_output",
    )(*pieces, *dense_pieces, tokens, bias, own, *[term for _, term in terms])


def token_grad_kernel(token_ref, grad_ref, own_ref, gain_ref, *refs, starts, tile):
    terms, out_ref, total = refs[:-2], refs[-2], refs[-1]
    first = pl.program_id(0) * tile
    total[...] = own_ref[...].astype(WIDE)
    for start, term in zip(starts, terms):
        size = min(tile, term.shape[0])
        for at in range(0, term.shape[0], size):

            @pl.when(first == (start + at) // tile * tile)
            def _(start=start, term=term, at=at, size=size):
                to = (start + at) % tile
                total[to : to + size] += term[at : at + size].astype(WIDE)

    x = token_ref[...].astype(WIDE)
    centred = x - jnp.mean(x, axis=-1, keepdims=True)
    rstd = lax.rsqrt(jnp.mean(centred * centred, axis=-1, keepdims=True) + 1e-05)
    xhat = centred * rstd
    scaled = total[...] * gain_ref[...]
    mean = jnp.mean(scaled, axis=-1, keepdims=True)
    along = jnp.mean(scaled * xhat, axis=-1, keepdims=True)
    out_ref[...] = (grad_ref[...].astype(WIDE) + rstd * (scaled - mean - xhat * along)).astype(LOW)


def token_grad(tokens, grad, own, gain, terms, tile):
    rows, width = tokens.shape
    by_row = pl.BlockSpec((tile, width), lambda i: (i, 0))
    whole = lambda a: pl.BlockSpec(a.shape, lambda i: (0, 0), pipeline_mode=pl.Buffered(1))
    return pl.pallas_call(
        functools.partial(
            token_grad_kernel, starts=tuple(start for start, _ in terms), tile=tile
        ),
        out_shape=jax.ShapeDtypeStruct((rows, width), LOW),
        grid=(rows // tile,),
        in_specs=[by_row, by_row, by_row, pl.BlockSpec((1, width), lambda i: (0, 0))]
        + [whole(term) for _, term in terms],
        out_specs=by_row,
        scratch_shapes=[pltpu.VMEM((tile, width), WIDE)],
        compiler_params=pltpu.CompilerParams(
            dimension_semantics=("arbitrary",), vmem_limit_bytes=48 << 20
        ),
        cost_estimate=LITTLE,
        name="token_grad",
    )(tokens, grad, own, gain[None], *[term for _, term in terms])


def pair_grad_kernel(x_ref, y_ref, a_ref, b_ref, out_ref):
    split = a_ref.shape[1]
    out_ref[:, :split] = dot(x_ref[...], a_ref[...], TN).astype(LOW)
    out_ref[:, split:] = dot(y_ref[...], b_ref[...], TN).astype(LOW)


def pair_grad(x, y, a, b):
    rows, width = x.shape
    columns = a.shape[1] + b.shape[1]
    tile = 512
    keep = pl.Buffered(1)
    return pl.pallas_call(
        pair_grad_kernel,
        out_shape=jax.ShapeDtypeStruct((width, columns), LOW),
        grid=(width // tile,),
        in_specs=[
            pl.BlockSpec((rows, tile), lambda i: (0, i)),
            pl.BlockSpec((rows, tile), lambda i: (0, i)),
            pl.BlockSpec(a.shape, lambda i: (0, 0), pipeline_mode=keep),
            pl.BlockSpec(b.shape, lambda i: (0, 0), pipeline_mode=keep),
        ],
        out_specs=pl.BlockSpec((tile, columns), lambda i: (i, 0)),
        compiler_params=pltpu.CompilerParams(
            dimension_semantics=("arbitrary",), vmem_limit_bytes=58 << 20
        ),
        cost_estimate=LITTLE,
        name="pair_grad",
    )(x, y, a, b)


def rope_tables(rows):
    place = lax.broadcasted_iota(jnp.int32, (rows, LANES), 0)
    lane = lax.broadcasted_iota(jnp.int32, (rows, LANES), 1)
    pos = jnp.where(place < PROMPT, place, PROMPT + (place - PROMPT) % CLEN)
    half = ROT // 2
    freq = 10000.0 ** (-2.0 * jnp.arange(half, dtype=WIDE) / ROT)
    angle = pos.astype(WIDE) * jnp.tile(freq, LANES // half)[None, :]
    dim = lane % (LANES // 2)
    cosine, sine = jnp.cos(angle), jnp.sin(angle)
    return [
        jnp.where(dim < ROT, cosine, 1.0),
        jnp.where((dim >= half) & (dim < ROT), sine, 0.0),
        jnp.where(dim < half, -sine, 0.0),
    ]


def shards(
    tokens,
    cotangent,
    block_table,
    ln_gain,
    ln_bias,
    w_qkv,
    b_qkv,
    w_dense,
    b_dense,
    w_fc1,
    b_fc1,
    w_fc2,
    b_fc2,
):
    _, local_rows, width = tokens.shape
    head_dim = width // HEADS
    count = lax.axis_size("ctx")
    me = lax.axis_index("ctx")
    rows = local_rows * count
    local_blocks = local_rows // BLK
    each = w_dense.shape[0]
    hidden = w_fc2.shape[0]
    gain, shift = ln_gain.astype(WIDE), ln_bias.astype(WIDE)

    def of_rank(whole, rank):
        return whole[rank * local_rows : (rank + 1) * local_rows]

    order, _, _ = ring_of(count)
    places = [0] * count
    for n, device in enumerate(order):
        places[device] = n
    places = jnp.asarray(places, jnp.int32)
    ranks = jnp.asarray([rank_of(n, count) for n in range(count)], jnp.int32)
    slots = jnp.arange(rows // BLK, dtype=jnp.int32)
    offset = (places[slots // local_blocks] - places[me]) % count
    held_at = ranks[offset] * local_blocks + slots % local_blocks
    hit = block_table[0][None, :] == slots[:, None]
    where = jnp.sum(jnp.where(hit, held_at[None, :], 0), axis=1).astype(jnp.int32)

    own_tokens = tokens[0].astype(WIDE)
    own_grad = cotangent[0]
    average = jnp.mean(own_tokens, axis=-1, keepdims=True)
    centred = own_tokens - average
    rstd = lax.rsqrt(jnp.mean(centred * centred, axis=-1, keepdims=True) + 1e-05)
    xhat = centred * rstd
    normed_own = (xhat * gain + shift).astype(LOW)

    def gather_rows(shard):
        return lax.all_gather(shard, "fsdp", axis=0, tiled=True)

    def scatter_rows(whole):
        return lax.psum_scatter(whole, "fsdp", scatter_dimension=0, tiled=True)

    lanes = 2 * LANES if each % (2 * LANES) == 0 else LANES
    groups = each // lanes

    def by_group(values):
        cut = values.reshape(-1, 3, groups, lanes)
        return jnp.swapaxes(cut, 1, 2).reshape(-1, 3 * each)

    tabs = rope_tables(rows)
    own_grad_sum = jnp.sum(own_grad.astype(WIDE), axis=0)
    fc1_bias = lax.dynamic_slice_in_dim(b_fc1, me * hidden, hidden, 0).astype(WIDE)
    early = (where, own_grad_sum, fc1_bias, *tabs)
    normed_pieces = ring_pieces(normed_own, "ctx", gate=early)
    attention_shard = jnp.concatenate([by_group(w_qkv), w_dense.T], axis=1)
    fc1_weight = gather_rows(w_fc1)
    fc2_turned = gather_rows(after(w_fc2.T, *normed_pieces[1:-2]))
    attention_weight = gather_rows(after(attention_shard, *normed_pieces[-2:]))
    qkv_weight, dense_turned = attention_weight[:, : 3 * each], attention_weight[:, 3 * each :]

    qkv_bias = lax.dynamic_slice_in_dim(b_qkv.reshape(3, width), me * each, each, 1)
    activated, slope, normed = expand(normed_pieces, fc1_weight, fc1_bias)

    sent_grad = after(own_grad, *normed_pieces[-2:])
    grad_pieces = ring_pieces(sent_grad, "ctx", gate=(activated,))
    ff_part = dot(activated, fc2_turned, NT).astype(LOW)
    ff_terms, ff_hops = ring_reduce(lambda rank: of_rank(ff_part, rank), "ctx", chained=True)
    first, second, last = ff_hops[0], ff_hops[min(1, len(ff_hops) - 1)], ff_hops[-1]

    gated = [after(piece, ff_part) for piece in grad_pieces]
    expanded_grad, grads, fc1_bias_part = slope_grad(gated, fc2_turned, slope)
    d_fc2_part = dot(after(grads, expanded_grad, *first), activated, TN).astype(LOW)
    d_fc2 = scatter_rows(d_fc2_part)
    qkv = dot(after(normed, d_fc2_part), qkv_weight, NN)
    qkv = (qkv + by_group(qkv_bias)[0].astype(WIDE)).astype(LOW)
    attended_grad = dot(after(grads, qkv, *second), dense_turned, NN).astype(LOW)
    gated = after(normed, attended_grad)
    d_fc1_part = dot(gated, expanded_grad, TN).astype(LOW)
    d_fc1 = scatter_rows(d_fc1_part)

    dense_pieces = ring_pieces(after(dense_turned, *second), "ctx")

    attended, qkv_grads, qkv_sums, d_attention, swapped = [], [], [], [], []
    ordered = (d_fc1_part,)
    for which in range(groups):
        got, got_grads, got_sums = attention(
            after(qkv, *ordered), attended_grad, where, tabs, lanes, which, head_dim
        )
        attended.append(got)
        qkv_grads.append(got_grads)
        qkv_sums.append(got_sums)
        if which < groups - 1:
            swapped.append(ring_exchange(lambda rank, got=got: of_rank(got, rank), "ctx"))
            gated = after(normed, d_fc2, *last, *dense_pieces[1:-2]) if which == 0 else normed
            d_part = pair_grad(gated, grads, got_grads, got)
            ordered = (d_part,)
            d_attention.append(scatter_rows(d_part))

    weights = [(attention_weight, which) for which in range(groups)] + [(fc1_weight, 0)]
    early_swaps = [piece for pieces in swapped for piece in pieces]
    turn = after(expanded_grad, d_fc1, *dense_pieces[-2:], *early_swaps, *attended)
    swapped.append(ring_exchange(lambda rank: of_rank(attended[-1], rank), "ctx"))
    half = local_rows // 2
    whole, far_cut, ahead_cut, behind_cut = [local_rows], [half, half], [half], [half]
    if count > 2:
        ahead_cut, behind_cut = [half, half], [half, half]
    cut_of = {0: whole, count - 2: ahead_cut, count - 3: behind_cut, count - 1: far_cut}

    def some_ranks(ranks, turn, cost=LITTLE):
        cuts = [cut_of.get(rank, whole) for rank in ranks]
        return input_grad(qkv_grads + [turn], weights, normed, ranks, local_rows, cuts, cost)

    far_part, far_sums = some_ranks([count - 1], turn)
    middle = list(range(count - 2, 0, -1))
    middle_sums, parts = 0.0, {count - 1: far_part[0]}
    turn = after(turn, *far_part[0])
    for n in range(0, len(middle), 2):
        some, some_sums = some_ranks(middle[n : n + 2], turn)
        turn = after(turn, *[piece for pieces in some for piece in pieces])
        middle_sums = middle_sums + some_sums
        parts.update(zip(middle[n : n + 2], some))
    for rank, pieces in parts.items():
        if len(pieces) == 1:
            parts[rank] = pieces[0]

    grad_terms, hops = ring_reduce(lambda rank: parts[rank], "ctx")
    last_hops = [piece for hop in hops[1:3] for piece in hop]
    gated = after(normed, turn, *hops[0], *swapped[-1], *d_attention)
    d_part = pair_grad(gated, grads, qkv_grads[-1], attended[-1])
    d_attention.append(scatter_rows(d_part))
    [own_part], own_sums = some_ranks([0], after(turn, d_part), MUCH)
    d_qkv = jnp.concatenate(
        [part[:, : 3 * lanes].reshape(-1, 3, lanes) for part in d_attention], axis=2
    ).astype(WIDE)
    d_dense = jnp.concatenate([part[:, 3 * lanes :].T for part in d_attention], axis=0)
    d_dense = d_dense.astype(WIDE)

    qkv_bias_part = jnp.concatenate(
        [part.reshape(3, lanes) for part in qkv_sums], axis=1
    )
    qkv_bias_wide = lax.dynamic_update_slice_in_dim(
        jnp.zeros((3, width), WIDE), qkv_bias_part, me * each, 1
    ).reshape(-1)
    fc1_bias_wide = lax.dynamic_update_slice_in_dim(
        jnp.zeros((b_fc1.shape[0],), WIDE), fc1_bias_part, me * hidden, 0
    )
    small = jnp.concatenate(
        [
            (far_sums + middle_sums + own_sums).reshape(-1),
            qkv_bias_wide,
            own_grad_sum,
            fc1_bias_wide,
        ]
    )
    steps = exchange_steps(("fsdp", "ctx"))
    small = exchange(small, steps[:1])
    small = exchange(after(small, *last_hops), steps[1:2])
    d_fc1, d_fc2 = d_fc1.astype(WIDE), d_fc2.T.astype(WIDE)
    output = place_output(
        [swapped[which][rank] for rank in range(count) for which in range(groups)],
        dense_pieces,
        after(tokens[0], small, d_fc1, d_fc2, *own_part),
        (b_dense.astype(WIDE) + b_fc2.astype(WIDE))[None],
        ff_part,
        ff_terms,
        count,
        groups,
    )
    small = exchange(small, steps[2:-2])
    d_tokens = token_grad(
        after(tokens[0], output), own_grad, own_part[0], gain, grad_terms, local_rows // 4
    )
    small = exchange(after(small, output), steps[-2:-1])
    small = exchange(after(small, d_tokens), steps[-1:])
    small = after(small, d_qkv, d_dense)
    d_shift, with_normed, d_b_qkv, d_b_out, d_b_fc1 = jnp.split(
        small, [width, 2 * width, 5 * width, 6 * width]
    )
    d_gain = (with_normed - shift * d_shift) / gain
    return (
        output[None],
        d_tokens[None],
        d_gain,
        d_shift,
        d_qkv,
        d_b_qkv,
        d_dense,
        d_b_out,
        d_fc1,
        d_b_fc1,
        d_fc2,
        d_b_out,
    )


def solution(mesh):
    in_specs = (
        P("fsdp", "ctx", None),
        P("fsdp", "ctx", None),
        P("fsdp", None),
        P(),
        P(),
        P("fsdp", None, "ctx"),
        P(),
        P("ctx", "fsdp"),
        P(),
        P("fsdp", "ctx"),
        P(),
        P("ctx", "fsdp"),
        P(),
    )
    out_specs = (
        P("fsdp", "ctx", None),
        P("fsdp", "ctx", None),
        P(),
        P(),
        P("fsdp", None, "ctx"),
        P(),
        P("ctx", "fsdp"),
        P(),
        P("fsdp", "ctx"),
        P(),
        P("ctx", "fsdp"),
        P(),
    )
    return jax.shard_map(shards, mesh=mesh, in_specs=in_specs, out_specs=out_specs, check_vma=False)
```

```python
import functools
import math

import jax
import jax.numpy as jnp
from jax import lax
from jax.experimental import pallas as pl
from jax.experimental.pallas import tpu as pltpu
from jax.sharding import PartitionSpec as P

HEADS = 32
ROT = 32
PROMPT = 2048
CLEN = 256
BLK = 64
CHUNK = 256
LANES = 128
NT = (((1,), (1,)), ((), ()))
NN = (((1,), (0,)), ((), ()))
TN = (((0,), (0,)), ((), ()))
LOW = jnp.bfloat16
WIDE = jnp.float32
LITTLE = pl.CostEstimate(flops=1000000, bytes_accessed=1000000, transcendentals=0)
MUCH = pl.CostEstimate(flops=100000000000, bytes_accessed=1000000, transcendentals=0)


def dot(left, right, dims):
    return lax.dot_general(left, right, dims, preferred_element_type=WIDE)


def attention_kernel(where_ref, *refs, chunk, chunks, full_chunks, blk, group, scale):
    per = chunk // blk
    qkv_in, g_in = refs[:per], refs[per : 2 * per]
    cos_ref, up_ref, down_ref, att_hbm, grad_hbm, sums_ref = refs[2 * per : 2 * per + 6]
    (
        keys,
        values,
        values_t,
        probs,
        key_sum,
        value_sum,
        top_ref,
        total_ref,
        mix_ref,
        back_ref,
        att_stage,
        query_stage,
        key_stage,
        value_stage,
        row_sem,
        col_sem,
    ) = refs[2 * per + 6 :]
    i = pl.program_id(0)
    slot = lax.rem(i, 2)
    half = LANES // 2
    lanes = group * LANES
    heads = 2 * group
    first = lax.broadcasted_iota(jnp.int32, (1, LANES), 1) < half

    def columns(part):
        return pl.ds(part * lanes, lanes)

    def row_copies(which, at):
        stage, target = ((att_stage, att_hbm), (query_stage, grad_hbm))[which]
        return [
            pltpu.make_async_copy(
                stage.at[at, pl.ds(r * blk, blk)],
                target.at[where_ref[i * per + r], :, columns(0)],
                row_sem.at[at, which, r],
            )
            for r in range(per)
        ]

    def col_copies(n):
        block = where_ref[n]
        rows = pl.ds(pl.multiple_of(n * blk, blk), blk)
        return (
            pltpu.make_async_copy(
                key_stage.at[rows], grad_hbm.at[block, :, columns(1)], col_sem.at[0, n]
            ),
            pltpu.make_async_copy(
                value_stage.at[rows], grad_hbm.at[block, :, columns(2)], col_sem.at[1, n]
            ),
        )

    def load(parts):
        return jnp.concatenate([part[0] for part in parts], axis=0)

    def tables(rows):
        return cos_ref[rows], up_ref[rows], down_ref[rows]

    quarter = ROT // 2

    def turned(x, tab, sign):
        return jnp.concatenate(
            [
                y * tab[0]
                + sign
                * (pltpu.roll(y, quarter, 1) * tab[1] + pltpu.roll(y, LANES - quarter, 1) * tab[2])
                for y in (x[:, n * LANES : (n + 1) * LANES] for n in range(group))
            ],
            axis=1,
        )

    def one_head(x, h):
        pair = x[:, (h // 2) * LANES : (h // 2 + 1) * LANES]
        nothing = jnp.zeros_like(pair)
        return jnp.where(first, pair, nothing) if h % 2 == 0 else jnp.where(first, nothing, pair)

    @pl.when(i >= 2)
    def _():
        for which in range(2):
            for copy in row_copies(which, slot):
                copy.wait()

    here = pl.ds(pl.multiple_of(i * chunk, chunk), chunk)
    tab = tables(here)
    qkv = load(qkv_in)
    query = (turned(qkv[:, :lanes].astype(WIDE), tab, 1.0) * scale).astype(LOW)
    key_new = turned(qkv[:, lanes : 2 * lanes].astype(WIDE), tab, 1.0)
    value_new = qkv[:, 2 * lanes :]
    grad = load(g_in)
    keys[here] = key_new.astype(LOW)
    values[here] = value_new
    values_t[:, here] = value_new.T
    key_sum[here] = jnp.zeros((chunk, lanes), WIDE)
    value_sum[here] = jnp.zeros((chunk, lanes), WIDE)
    top_ref[...] = jnp.full(top_ref.shape, -1e30, WIDE)
    total_ref[...] = jnp.zeros(total_ref.shape, WIDE)
    mix_ref[...] = jnp.zeros(mix_ref.shape, WIDE)
    back_ref[...] = jnp.zeros(back_ref.shape, WIDE)
    query_of = [one_head(query, h) for h in range(heads)]
    grad_of = [one_head(grad, h) for h in range(heads)]
    query_pair = [
        jnp.concatenate(query_of[2 * n : 2 * n + 2], axis=0) for n in range(group)
    ]
    grad_pair = [jnp.concatenate(grad_of[2 * n : 2 * n + 2], axis=0) for n in range(group)]
    before = jnp.minimum(i, full_chunks)
    doubles = before // 2
    odd = before - 2 * doubles

    def fold(x, how):
        return how(x.reshape(x.shape[0] // 8, 8, chunk), axis=0)

    def pair_lanes(n):
        return slice(n * LANES, (n + 1) * LANES)

    def head_rows(h):
        return slice(h * half, (h + 1) * half)

    def sweep(tile):
        def quad(t, carry):
            start = pl.multiple_of(t * 4 * chunk, 4 * chunk)
            tile(start, start, 4 * chunk, False)
            return carry

        lax.fori_loop(0, doubles // 2, quad, 0)

        @pl.when(doubles % 2 == 1)
        def _():
            start = pl.multiple_of((doubles - 1) * 2 * chunk, 2 * chunk)
            tile(start, start, 2 * chunk, False)

        held = pl.multiple_of(doubles * 2 * chunk, chunk)

        @pl.when(odd == 1)
        def _():
            tile(held, held, 2 * chunk, True)

        @pl.when(odd == 0)
        def _():
            tile(pl.multiple_of(i * chunk, chunk), held, chunk, True)

    def score(start, held, size, masked):
        rows, to = pl.ds(start, size), pl.ds(held, size)
        if masked:
            key_row = lax.broadcasted_iota(jnp.int32, (size, chunk), 0) + start
            query_col = lax.broadcasted_iota(jnp.int32, (size, chunk), 1) + i * chunk
            seen = key_row <= query_col
        for h in range(heads):
            raw = dot(keys[rows, pair_lanes(h // 2)], query_of[h], NT)
            if masked:
                raw = jnp.where(seen, raw, -1e30)
            probs[h, to] = raw
            top_ref[h] = jnp.maximum(top_ref[h], fold(raw, jnp.max))

    sweep(score)
    top = [jnp.max(top_ref[h], axis=0, keepdims=True) for h in range(heads)]

    def mix(start, held, size, masked):
        rows, to = pl.ds(start, size), pl.ds(held, size)
        for h in range(heads):
            weight = jnp.exp(probs[h, to] - top[h])
            probs[h, to] = weight
            total_ref[h] += fold(weight, jnp.sum)
            mix_ref[head_rows(h)] += dot(values_t[head_rows(h), rows], weight.astype(LOW), NN)

    sweep(mix)
    inverse = [1.0 / jnp.sum(total_ref[h], axis=0, keepdims=True) for h in range(heads)]
    attended = jnp.concatenate(
        [mix_ref[head_rows(h)] * inverse[h] for h in range(heads)], axis=0
    )
    shared = grad.T.astype(WIDE) * attended
    inner = [jnp.sum(shared[head_rows(h)], axis=0, keepdims=True) for h in range(heads)]
    att_stage[slot] = attended.astype(LOW).T
    for copy in row_copies(0, slot):
        copy.start()

    def back(start, held, size, masked):
        rows, to = pl.ds(start, size), pl.ds(held, size)
        for n in range(group):
            value = values[rows, pair_lanes(n)]
            weights, grads = [], []
            for h in (2 * n, 2 * n + 1):
                weight = probs[h, to] * inverse[h]
                weight_grad = dot(value, grad_of[h], NT)
                score_grad = (weight * (weight_grad - inner[h])).astype(LOW)
                weights.append(weight.astype(LOW))
                grads.append(score_grad)
            value_sum[rows, pair_lanes(n)] += dot(
                jnp.concatenate(weights, axis=1), grad_pair[n], NN
            )
            key = keys[rows, pair_lanes(n)]
            back_ref[:, pair_lanes(n)] += dot(
                jnp.concatenate(grads, axis=0),
                jnp.concatenate([one_head(key, h) for h in range(2)], axis=0),
                TN,
            )
            key_sum[rows, pair_lanes(n)] += dot(
                jnp.concatenate(grads, axis=1), query_pair[n], NN
            )

    sweep(back)
    query_grad = turned(back_ref[...] * scale, tab, -1.0)
    query_stage[slot] = query_grad.astype(LOW)

    def column_sums(x):
        return jnp.sum(x.reshape(chunk // 8, 8, lanes), axis=0)

    @pl.when(i == 0)
    def _():
        sums_ref[...] = jnp.zeros(sums_ref.shape, WIDE)

    sums_ref[:, :lanes] += column_sums(query_grad)
    for copy in row_copies(1, slot):
        copy.start()

    @pl.when(i == chunks - 1)
    def _():
        @pl.loop(0, chunks)
        def _(n):
            rows = pl.ds(pl.multiple_of(n * chunk, chunk), chunk)
            key_grad = turned(key_sum[rows], tables(rows), -1.0)
            key_stage[rows] = key_grad.astype(LOW)
            value_stage[rows] = value_sum[rows].astype(LOW)
            sums_ref[:, lanes : 2 * lanes] += column_sums(key_grad)
            sums_ref[:, 2 * lanes :] += column_sums(value_sum[rows])
            for r in range(per):
                for copy in col_copies(n * per + r):
                    copy.start()

        for at in range(2):
            for which in range(2):
                for copy in row_copies(which, at):
                    copy.wait()

        @pl.loop(0, chunks * per)
        def _(n):
            for copy in col_copies(n):
                copy.wait()


def attention(qkv, grad, where, tabs, lanes, which, head_dim):
    rows = grad.shape[0]
    chunk, blk = CHUNK, BLK
    per, chunks, blocks = chunk // blk, rows // chunk, rows // blk
    group = lanes // LANES
    heads = 2 * group
    qkv_blocks = qkv.reshape(blocks, blk, qkv.shape[1])
    grad_blocks = grad.reshape(blocks, blk, grad.shape[1])

    def spec(columns, r):
        return pl.BlockSpec((1, blk, columns), lambda i, at: (at[i * per + r], 0, which))

    in_specs = [spec(3 * lanes, r) for r in range(per)] + [spec(lanes, r) for r in range(per)]
    in_specs += [pl.BlockSpec((rows, LANES), lambda i, at: (0, 0), pipeline_mode=pl.Buffered(1))] * 3
    operands = [qkv_blocks] * per + [grad_blocks] * per + list(tabs)
    kernel = functools.partial(
        attention_kernel,
        chunk=chunk,
        chunks=chunks,
        full_chunks=PROMPT // chunk,
        blk=blk,
        group=group,
        scale=1.0 / math.sqrt(head_dim),
    )
    attended, grads, sums = pl.pallas_call(
        kernel,
        out_shape=(
            jax.ShapeDtypeStruct((blocks, blk, lanes), LOW),
            jax.ShapeDtypeStruct((blocks, blk, 3 * lanes), LOW),
            jax.ShapeDtypeStruct((8, 3 * lanes), WIDE),
        ),
        grid_spec=pltpu.PrefetchScalarGridSpec(
            num_scalar_prefetch=1,
            grid=(chunks,),
            in_specs=in_specs,
            out_specs=[pl.BlockSpec(memory_space=pl.ANY)] * 2
            + [pl.BlockSpec((8, 3 * lanes), lambda i, at: (0, 0))],
            scratch_shapes=[
                pltpu.VMEM((rows, lanes), LOW),
                pltpu.VMEM((rows, lanes), LOW),
                pltpu.VMEM((lanes, rows), LOW),
                pltpu.VMEM((heads, PROMPT + chunk, chunk), WIDE),
                pltpu.VMEM((rows, lanes), WIDE),
                pltpu.VMEM((rows, lanes), WIDE),
                pltpu.VMEM((heads, 8, chunk), WIDE),
                pltpu.VMEM((heads, 8, chunk), WIDE),
                pltpu.VMEM((lanes, chunk), WIDE),
                pltpu.VMEM((chunk, lanes), WIDE),
                pltpu.VMEM((2, chunk, lanes), LOW),
                pltpu.VMEM((2, chunk, lanes), LOW),
                pltpu.VMEM((rows, lanes), LOW),
                pltpu.VMEM((rows, lanes), LOW),
                pltpu.SemaphoreType.DMA((2, 2, per)),
                pltpu.SemaphoreType.DMA((2, blocks)),
            ],
        ),
        compiler_params=pltpu.CompilerParams(
            dimension_semantics=("arbitrary",), vmem_limit_bytes=56 << 20
        ),
        cost_estimate=LITTLE,
        name="attention",
    )(where, *operands)
    return attended.reshape(rows, lanes), grads.reshape(rows, 3 * lanes), jnp.sum(sums, axis=0)


def after(value, *others):
    return lax.optimization_barrier((value,) + others)[0] if others else value


def ring_of(count):
    order = list(range(count // 2)) + list(range(count - 1, count // 2 - 1, -1))
    ahead = [(order[n], order[(n + 1) % count]) for n in range(count)]
    return order, ahead, [(b, a) for a, b in ahead]


def rank_of(offset, count):
    offset %= count
    if offset == 0 or 2 * offset == count:
        return max(2 * offset - 1, 0)
    return 2 * offset if 2 * offset < count else 2 * (count - offset) - 1


def ring_pieces(own, axis, gate=()):
    count = lax.axis_size(axis)
    _, ahead, behind = ring_of(count)
    pieces, half = [own], own.shape[0] // 2
    from_behind = from_ahead = own
    for _ in range(count // 2 - 1):
        from_behind = lax.ppermute(from_behind, axis, ahead)
        from_ahead = lax.ppermute(from_ahead, axis, behind)
        pieces += [from_behind, from_ahead]
    if gate:
        from_behind, from_ahead = after(from_behind, *gate), after(from_ahead, *gate)
        if count > 2:
            pieces[-2:] = [from_behind, from_ahead]
    far = [
        lax.ppermute(from_behind[:half], axis, ahead),
        lax.ppermute(from_ahead[half:], axis, behind),
    ]
    return pieces + far


def ring_reduce(part, axis, cuts=1, chained=False):
    count = lax.axis_size(axis)
    _, ahead, behind = ring_of(count)

    def plus(a, b):
        return (a.astype(WIDE) + b.astype(WIDE)).astype(LOW)

    def cut_rows(term, sizes):
        if isinstance(term, (list, tuple)):
            return term
        ends = [sum(sizes[: n + 1]) for n in range(len(sizes))]
        return [term[end - size : end] for end, size in zip(ends, sizes)]

    far = part(count - 1)
    half = sum(a.shape[0] for a in far) // 2 if isinstance(far, (list, tuple)) else far.shape[0] // 2
    far = cut_rows(far, [half, half])
    up, down = lax.ppermute(far[0], axis, ahead), lax.ppermute(far[1], axis, behind)
    hops = [(up, down)]
    if count == 2:
        return [(0, up), (half, down)], hops
    pieces = [half // cuts] * cuts
    to_ahead = cut_rows(part(count - 2), [half] + pieces)
    to_behind = cut_rows(part(count - 3), pieces + [half])
    got_up, got_down = {}, {}
    got_up[0] = lax.ppermute(plus(to_ahead[0], up), axis, ahead)
    got_down[half] = lax.ppermute(plus(to_behind[-1], down), axis, behind)
    hops.append((got_up[0], got_down[half]))
    for n in range(cuts):
        gate = hops[-1] if chained else ()
        at = n * (half // cuts)
        got_up[half + at] = lax.ppermute(after(to_ahead[1 + n], *gate), axis, ahead)
        got_down[at] = lax.ppermute(after(to_behind[n], *gate), axis, behind)
        hops.append((got_up[half + at], got_down[at]))
    if count == 4:
        return sorted(got_up.items()) + sorted(got_down.items()), hops
    up = jnp.concatenate([piece for _, piece in sorted(got_up.items())], axis=0)
    down = jnp.concatenate([piece for _, piece in sorted(got_down.items())], axis=0)
    for s in range(count // 2 - 2, 0, -1):
        up = lax.ppermute(plus(part(2 * s), up), axis, ahead)
        down = lax.ppermute(plus(part(2 * s - 1), down), axis, behind)
        hops.append((up, down))
    return [(0, up), (0, down)], hops


def ring_exchange(part, axis):
    count = lax.axis_size(axis)
    order, _, _ = ring_of(count)
    got = [None] * count
    got[0] = part(0)
    for offset in range(1, count):
        hops = [(order[n], order[(n + offset) % count]) for n in range(count)]
        got[rank_of(-offset, count)] = lax.ppermute(part(rank_of(offset, count)), axis, hops)
    return got


def exchange_steps(axes):
    steps = []
    for axis in axes:
        count, span = lax.axis_size(axis), 1
        while span < count:
            steps.append((axis, [(n, n ^ span) for n in range(count)]))
            span *= 2
    return steps


def exchange(values, steps):
    for axis, pairs in steps:
        values = values + lax.ppermute(values, axis, pairs)
    return values


def gelu_and_slope(h):
    inner_scale = math.sqrt(2.0 / math.pi)
    square = h * h
    t = jnp.tanh(h * (inner_scale + (inner_scale * 0.044715) * square))
    half = 0.5 * h
    rise = 0.5 + 0.5 * t
    bend = inner_scale + (3.0 * inner_scale * 0.044715) * square
    return (h * rise).astype(LOW), (rise + (half - half * t * t) * bend).astype(LOW)


def join_piece(pieces, spans, whole_ref):
    i = pl.program_id(0)
    for (first, span), piece in zip(spans, pieces):

        @pl.when((i >= first) & (i < first + span))
        def _(piece=piece):
            whole_ref[...] = piece[...]


def piece_blocks(pieces):
    tile, width = pieces[-1].shape
    spans, first = [], 0
    for piece in pieces:
        spans.append((first, piece.shape[0] // tile))
        first += piece.shape[0] // tile

    def spec(first, span):
        return pl.BlockSpec((tile, width), lambda i: (jnp.clip(i - first, 0, span - 1), 0))

    return tile, tuple(spans), [spec(*span) for span in spans]


def expand_kernel(*refs, spans, cols):
    w_ref, b_ref, act_ref, slope_ref, whole_ref = refs[len(spans) :]
    join_piece(refs[: len(spans)], spans, whole_ref)
    x = whole_ref[...]
    for n in range(w_ref.shape[1] // cols):
        at = slice(n * cols, (n + 1) * cols)
        act, slope = gelu_and_slope(dot(x, w_ref[:, at], NN) + b_ref[:, at])
        act_ref[:, at] = act
        slope_ref[:, at] = slope


def expand(pieces, w, b):
    width, hidden = w.shape
    tile, spans, specs = piece_blocks(pieces)
    rows = sum(piece.shape[0] for piece in pieces)
    by_row = pl.BlockSpec((tile, hidden), lambda i: (i, 0))
    out = jax.ShapeDtypeStruct((rows, hidden), LOW)
    return pl.pallas_call(
        functools.partial(expand_kernel, spans=spans, cols=min(512, hidden)),
        out_shape=(out, out, jax.ShapeDtypeStruct((rows, width), LOW)),
        grid=(rows // tile,),
        in_specs=specs
        + [
            pl.BlockSpec((width, hidden), lambda i: (0, 0), pipeline_mode=pl.Buffered(1)),
            pl.BlockSpec((1, hidden), lambda i: (0, 0)),
        ],
        out_specs=[by_row, by_row, pl.BlockSpec((tile, width), lambda i: (i, 0))],
        compiler_params=pltpu.CompilerParams(
            dimension_semantics=("arbitrary",), vmem_limit_bytes=48 << 20
        ),
        cost_estimate=pl.CostEstimate(
            flops=2 * rows * width * hidden,
            bytes_accessed=2 * rows * (2 * width + 2 * hidden),
            transcendentals=rows * hidden,
        ),
        name="expand",
    )(*pieces, w, b[None])


def slope_grad_kernel(*refs, spans, cols):
    pieces = refs[: len(spans)]
    w_ref, slope_ref, out_ref, whole_ref, sums_ref = refs[len(spans) :]
    join_piece(pieces, spans, whole_ref)

    @pl.when(pl.program_id(0) == 0)
    def _():
        sums_ref[...] = jnp.zeros(sums_ref.shape, WIDE)

    x = whole_ref[...]
    for n in range(w_ref.shape[1] // cols):
        at = slice(n * cols, (n + 1) * cols)
        value = dot(x, w_ref[:, at], NN) * slope_ref[:, at].astype(WIDE)
        out_ref[:, at] = value.astype(LOW)
        sums_ref[:, at] += jnp.sum(value.reshape(value.shape[0] // 8, 8, cols), axis=0)


def slope_grad(pieces, w, slope):
    width, hidden = w.shape
    tile, spans, specs = piece_blocks(pieces)
    first = sum(span for _, span in spans)
    by_row = pl.BlockSpec((tile, hidden), lambda i: (i, 0))
    grad, whole, sums = pl.pallas_call(
        functools.partial(slope_grad_kernel, spans=spans, cols=min(512, hidden)),
        out_shape=(
            jax.ShapeDtypeStruct((first * tile, hidden), LOW),
            jax.ShapeDtypeStruct((first * tile, width), LOW),
            jax.ShapeDtypeStruct((8, hidden), WIDE),
        ),
        grid=(first,),
        in_specs=specs
        + [
            pl.BlockSpec((width, hidden), lambda i: (0, 0), pipeline_mode=pl.Buffered(1)),
            by_row,
        ],
        out_specs=[
            by_row,
            pl.BlockSpec((tile, width), lambda i: (i, 0)),
            pl.BlockSpec((8, hidden), lambda i: (0, 0)),
        ],
        compiler_params=pltpu.CompilerParams(
            dimension_semantics=("arbitrary",), vmem_limit_bytes=48 << 20
        ),
        cost_estimate=pl.CostEstimate(
            flops=2 * first * tile * width * hidden,
            bytes_accessed=2 * first * tile * (2 * width + 2 * hidden),
            transcendentals=0,
        ),
        name="slope_grad",
    )(*pieces, w, slope)
    return grad, whole, jnp.sum(sums, axis=0)


def input_grad_kernel(*refs, terms, ranks):
    grads, weights = refs[: terms * ranks], refs[terms * ranks : terms * ranks + terms]
    rest = refs[terms * (ranks + 1) :]
    normed_refs, out_refs, sums_ref = rest[:ranks], list(rest[ranks:-1]), rest[-1]
    plain = weighted = 0.0
    for n in range(ranks):
        mine = grads[n * terms : (n + 1) * terms]
        total = sum(dot(g[...], w[...], NT) for g, w in zip(mine, weights))
        at = 0
        while at < total.shape[0]:
            out_ref = out_refs.pop(0)
            out_ref[...] = total[at : at + out_ref.shape[0]].astype(LOW)
            at += out_ref.shape[0]
        plain += jnp.sum(total, axis=0, keepdims=True)
        weighted += jnp.sum(total * normed_refs[n][...].astype(WIDE), axis=0, keepdims=True)
    sums_ref[0:1] = plain
    sums_ref[1:2] = weighted


def input_grad(grads, weights, normed, ranks, rows, cuts, cost):
    width = normed.shape[1]
    cols = 512
    keep = pl.Buffered(1)
    in_specs = [
        pl.BlockSpec((rows, g.shape[1]), lambda i, rank=rank: (rank, 0), pipeline_mode=keep)
        for rank in ranks
        for g in grads
    ]
    in_specs += [
        pl.BlockSpec((cols, g.shape[1]), lambda i, at=at: (i, at))
        for g, (_, at) in zip(grads, weights)
    ]
    in_specs += [pl.BlockSpec((rows, cols), lambda i, rank=rank: (rank, i)) for rank in ranks]
    sizes = [size for cut in cuts for size in cut]
    *parts, sums = pl.pallas_call(
        functools.partial(input_grad_kernel, terms=len(grads), ranks=len(ranks)),
        out_shape=[jax.ShapeDtypeStruct((size, width), LOW) for size in sizes]
        + [jax.ShapeDtypeStruct((2, width), WIDE)],
        grid=(width // cols,),
        in_specs=in_specs,
        out_specs=[pl.BlockSpec((size, cols), lambda i: (0, i)) for size in sizes]
        + [pl.BlockSpec((2, cols), lambda i: (0, i))],
        compiler_params=pltpu.CompilerParams(
            dimension_semantics=("arbitrary",), vmem_limit_bytes=58 << 20
        ),
        cost_estimate=cost,
        name="input_grad",
    )(*grads * len(ranks), *[w for w, _ in weights], *[normed] * len(ranks))
    return [[parts.pop(0) for _ in cut] for cut in cuts], sums


def place_kernel(*refs, starts, count, groups):
    pieces = refs[: count * groups]
    dense = refs[count * groups : count * groups + count + 1]
    rest = refs[count * (groups + 1) + 1 :]
    token_ref, bias_ref, own_ref = rest[:3]
    terms, out_ref, acc = rest[3:-2], rest[-2], rest[-1]
    acc[...] = token_ref[...].astype(WIDE) + bias_ref[...] + own_ref[...].astype(WIDE)
    for start, term in zip(starts, terms):
        acc[start : start + term.shape[0]] += term[...].astype(WIDE)
    steps = pl.num_programs(0)
    low_half = pl.program_id(0) * 2 < steps
    far = jnp.where(low_half, dense[count - 1][...], dense[count][...])
    total = acc[...]
    for rank in range(count):
        weight = dense[rank][...] if rank < count - 1 else far
        mine = [piece[...] for piece in pieces[rank * groups : (rank + 1) * groups]]
        total += dot(jnp.concatenate(mine, axis=1), weight, NT)
    out_ref[...] = total.astype(LOW)


def place_output(pieces, dense_pieces, tokens, bias, own, terms, count, groups):
    rows, width = tokens.shape
    cols = 512
    half = width // cols // 2
    whole = lambda a: pl.BlockSpec(a.shape, lambda i: (0, 0), pipeline_mode=pl.Buffered(1))
    in_specs = [whole(piece) for piece in pieces]
    depth = dense_pieces[0].shape[1]
    in_specs += [pl.BlockSpec((cols, depth), lambda i: (i, 0)) for _ in range(count - 1)]
    in_specs.append(pl.BlockSpec((cols, depth), lambda i: (jnp.minimum(i, half - 1), 0)))
    in_specs.append(pl.BlockSpec((cols, depth), lambda i: (jnp.maximum(i - half, 0), 0)))
    by_column = lambda n: pl.BlockSpec((n, cols), lambda i: (0, i))
    in_specs += [by_column(rows), by_column(1), by_column(rows)]
    in_specs += [by_column(term.shape[0]) for _, term in terms]
    return pl.pallas_call(
        functools.partial(
            place_kernel, starts=tuple(start for start, _ in terms), count=count, groups=groups
        ),
        out_shape=jax.ShapeDtypeStruct((rows, width), LOW),
        grid=(width // cols,),
        in_specs=in_specs,
        out_specs=by_column(rows),
        scratch_shapes=[pltpu.VMEM((rows, cols), WIDE)],
        compiler_params=pltpu.CompilerParams(
            dimension_semantics=("arbitrary",), vmem_limit_bytes=58 << 20
        ),
        cost_estimate=LITTLE,
        name="place_output",
    )(*pieces, *dense_pieces, tokens, bias, own, *[term for _, term in terms])


def token_grad_kernel(token_ref, grad_ref, own_ref, gain_ref, *refs, starts, tile):
    terms, out_ref, total = refs[:-2], refs[-2], refs[-1]
    first = pl.program_id(0) * tile
    total[...] = own_ref[...].astype(WIDE)
    for start, term in zip(starts, terms):
        size = min(tile, term.shape[0])
        for at in range(0, term.shape[0], size):

            @pl.when(first == (start + at) // tile * tile)
            def _(start=start, term=term, at=at, size=size):
                to = (start + at) % tile
                total[to : to + size] += term[at : at + size].astype(WIDE)

    x = token_ref[...].astype(WIDE)
    centred = x - jnp.mean(x, axis=-1, keepdims=True)
    rstd = lax.rsqrt(jnp.mean(centred * centred, axis=-1, keepdims=True) + 1e-05)
    xhat = centred * rstd
    scaled = total[...] * gain_ref[...]
    mean = jnp.mean(scaled, axis=-1, keepdims=True)
    along = jnp.mean(scaled * xhat, axis=-1, keepdims=True)
    out_ref[...] = (grad_ref[...].astype(WIDE) + rstd * (scaled - mean - xhat * along)).astype(LOW)


def token_grad(tokens, grad, own, gain, terms, tile):
    rows, width = tokens.shape
    by_row = pl.BlockSpec((tile, width), lambda i: (i, 0))
    whole = lambda a: pl.BlockSpec(a.shape, lambda i: (0, 0), pipeline_mode=pl.Buffered(1))
    return pl.pallas_call(
        functools.partial(
            token_grad_kernel, starts=tuple(start for start, _ in terms), tile=tile
        ),
        out_shape=jax.ShapeDtypeStruct((rows, width), LOW),
        grid=(rows // tile,),
        in_specs=[by_row, by_row, by_row, pl.BlockSpec((1, width), lambda i: (0, 0))]
        + [whole(term) for _, term in terms],
        out_specs=by_row,
        scratch_shapes=[pltpu.VMEM((tile, width), WIDE)],
        compiler_params=pltpu.CompilerParams(
            dimension_semantics=("arbitrary",), vmem_limit_bytes=48 << 20
        ),
        cost_estimate=LITTLE,
        name="token_grad",
    )(tokens, grad, own, gain[None], *[term for _, term in terms])


def pair_grad_kernel(x_ref, y_ref, a_ref, b_ref, out_ref):
    split = a_ref.shape[1]
    out_ref[:, :split] = dot(x_ref[...], a_ref[...], TN).astype(LOW)
    out_ref[:, split:] = dot(y_ref[...], b_ref[...], TN).astype(LOW)


def pair_grad(x, y, a, b):
    rows, width = x.shape
    columns = a.shape[1] + b.shape[1]
    tile = 512
    keep = pl.Buffered(1)
    return pl.pallas_call(
        pair_grad_kernel,
        out_shape=jax.ShapeDtypeStruct((width, columns), LOW),
        grid=(width // tile,),
        in_specs=[
            pl.BlockSpec((rows, tile), lambda i: (0, i)),
            pl.BlockSpec((rows, tile), lambda i: (0, i)),
            pl.BlockSpec(a.shape, lambda i: (0, 0), pipeline_mode=keep),
            pl.BlockSpec(b.shape, lambda i: (0, 0), pipeline_mode=keep),
        ],
        out_specs=pl.BlockSpec((tile, columns), lambda i: (i, 0)),
        compiler_params=pltpu.CompilerParams(
            dimension_semantics=("arbitrary",), vmem_limit_bytes=58 << 20
        ),
        cost_estimate=LITTLE,
        name="pair_grad",
    )(x, y, a, b)


def rope_tables(rows):
    place = lax.broadcasted_iota(jnp.int32, (rows, LANES), 0)
    lane = lax.broadcasted_iota(jnp.int32, (rows, LANES), 1)
    pos = jnp.where(place < PROMPT, place, PROMPT + (place - PROMPT) % CLEN)
    half = ROT // 2
    freq = 10000.0 ** (-2.0 * jnp.arange(half, dtype=WIDE) / ROT)
    angle = pos.astype(WIDE) * jnp.tile(freq, LANES // half)[None, :]
    dim = lane % (LANES // 2)
    cosine, sine = jnp.cos(angle), jnp.sin(angle)
    return [
        jnp.where(dim < ROT, cosine, 1.0),
        jnp.where((dim >= half) & (dim < ROT), sine, 0.0),
        jnp.where(dim < half, -sine, 0.0),
    ]


def shards(
    tokens,
    cotangent,
    block_table,
    ln_gain,
    ln_bias,
    w_qkv,
    b_qkv,
    w_dense,
    b_dense,
    w_fc1,
    b_fc1,
    w_fc2,
    b_fc2,
):
    _, local_rows, width = tokens.shape
    head_dim = width // HEADS
    count = lax.axis_size("ctx")
    me = lax.axis_index("ctx")
    rows = local_rows * count
    local_blocks = local_rows // BLK
    each = w_dense.shape[0]
    hidden = w_fc2.shape[0]
    gain, shift = ln_gain.astype(WIDE), ln_bias.astype(WIDE)

    def of_rank(whole, rank):
        return whole[rank * local_rows : (rank + 1) * local_rows]

    order, _, _ = ring_of(count)
    places = [0] * count
    for n, device in enumerate(order):
        places[device] = n
    places = jnp.asarray(places, jnp.int32)
    ranks = jnp.asarray([rank_of(n, count) for n in range(count)], jnp.int32)
    slots = jnp.arange(rows // BLK, dtype=jnp.int32)
    offset = (places[slots // local_blocks] - places[me]) % count
    held_at = ranks[offset] * local_blocks + slots % local_blocks
    hit = block_table[0][None, :] == slots[:, None]
    where = jnp.sum(jnp.where(hit, held_at[None, :], 0), axis=1).astype(jnp.int32)

    own_tokens = tokens[0].astype(WIDE)
    own_grad = cotangent[0]
    average = jnp.mean(own_tokens, axis=-1, keepdims=True)
    centred = own_tokens - average
    rstd = lax.rsqrt(jnp.mean(centred * centred, axis=-1, keepdims=True) + 1e-05)
    xhat = centred * rstd
    normed_own = (xhat * gain + shift).astype(LOW)

    def gather_rows(shard):
        return lax.all_gather(shard, "fsdp", axis=0, tiled=True)

    def scatter_rows(whole):
        return lax.psum_scatter(whole, "fsdp", scatter_dimension=0, tiled=True)

    lanes = 2 * LANES if each % (2 * LANES) == 0 else LANES
    groups = each // lanes

    def by_group(values):
        cut = values.reshape(-1, 3, groups, lanes)
        return jnp.swapaxes(cut, 1, 2).reshape(-1, 3 * each)

    tabs = rope_tables(rows)
    own_grad_sum = jnp.sum(own_grad.astype(WIDE), axis=0)
    fc1_bias = lax.dynamic_slice_in_dim(b_fc1, me * hidden, hidden, 0).astype(WIDE)
    early = (where, own_grad_sum, fc1_bias, *tabs)
    normed_pieces = ring_pieces(normed_own, "ctx", gate=early)
    attention_shard = jnp.concatenate([by_group(w_qkv), w_dense.T], axis=1)
    fc1_weight = gather_rows(w_fc1)
    fc2_turned = gather_rows(after(w_fc2.T, *normed_pieces[1:-2]))
    attention_weight = gather_rows(after(attention_shard, *normed_pieces[-2:]))
    qkv_weight, dense_turned = attention_weight[:, : 3 * each], attention_weight[:, 3 * each :]

    qkv_bias = lax.dynamic_slice_in_dim(b_qkv.reshape(3, width), me * each, each, 1)
    activated, slope, normed = expand(normed_pieces, fc1_weight, fc1_bias)

    sent_grad = after(own_grad, *normed_pieces[-2:])
    grad_pieces = ring_pieces(sent_grad, "ctx", gate=(activated,))
    ff_part = dot(activated, fc2_turned, NT).astype(LOW)
    ff_terms, ff_hops = ring_reduce(lambda rank: of_rank(ff_part, rank), "ctx", chained=True)
    first, second, last = ff_hops[0], ff_hops[min(1, len(ff_hops) - 1)], ff_hops[-1]

    gated = [after(piece, ff_part) for piece in grad_pieces]
    expanded_grad, grads, fc1_bias_part = slope_grad(gated, fc2_turned, slope)
    d_fc2_part = dot(after(grads, expanded_grad, *first), activated, TN).astype(LOW)
    d_fc2 = scatter_rows(d_fc2_part)
    qkv = dot(after(normed, d_fc2_part), qkv_weight, NN)
    qkv = (qkv + by_group(qkv_bias)[0].astype(WIDE)).astype(LOW)
    attended_grad = dot(after(grads, qkv, *second), dense_turned, NN).astype(LOW)
    gated = after(normed, attended_grad)
    d_fc1_part = dot(gated, expanded_grad, TN).astype(LOW)
    d_fc1 = scatter_rows(d_fc1_part)

    dense_pieces = ring_pieces(after(dense_turned, *second), "ctx")

    attended, qkv_grads, qkv_sums, d_attention, swapped = [], [], [], [], []
    ordered = (d_fc1_part,)
    for which in range(groups):
        got, got_grads, got_sums = attention(
            after(qkv, *ordered), attended_grad, where, tabs, lanes, which, head_dim
        )
        attended.append(got)
        qkv_grads.append(got_grads)
        qkv_sums.append(got_sums)
        if which < groups - 1:
            swapped.append(ring_exchange(lambda rank, got=got: of_rank(got, rank), "ctx"))
            gated = after(normed, d_fc2, *last, *dense_pieces[1:-2]) if which == 0 else normed
            d_part = pair_grad(gated, grads, got_grads, got)
            ordered = (d_part,)
            d_attention.append(scatter_rows(d_part))

    weights = [(attention_weight, which) for which in range(groups)] + [(fc1_weight, 0)]
    early_swaps = [piece for pieces in swapped for piece in pieces]
    turn = after(expanded_grad, d_fc1, *dense_pieces[-2:], *early_swaps, *attended)
    swapped.append(ring_exchange(lambda rank: of_rank(attended[-1], rank), "ctx"))
    half = local_rows // 2
    whole, far_cut, ahead_cut, behind_cut = [local_rows], [half, half], [half], [half]
    if count > 2:
        ahead_cut, behind_cut = [half, half], [half, half]
    cut_of = {0: whole, count - 2: ahead_cut, count - 3: behind_cut, count - 1: far_cut}

    def some_ranks(ranks, turn, cost=LITTLE):
        cuts = [cut_of.get(rank, whole) for rank in ranks]
        return input_grad(qkv_grads + [turn], weights, normed, ranks, local_rows, cuts, cost)

    far_part, far_sums = some_ranks([count - 1], turn)
    middle = list(range(count - 2, 0, -1))
    middle_sums, parts = 0.0, {count - 1: far_part[0]}
    turn = after(turn, *far_part[0])
    for n in range(0, len(middle), 2):
        some, some_sums = some_ranks(middle[n : n + 2], turn)
        turn = after(turn, *[piece for pieces in some for piece in pieces])
        middle_sums = middle_sums + some_sums
        parts.update(zip(middle[n : n + 2], some))
    for rank, pieces in parts.items():
        if len(pieces) == 1:
            parts[rank] = pieces[0]

    grad_terms, hops = ring_reduce(lambda rank: parts[rank], "ctx")
    last_hops = [piece for hop in hops[1:3] for piece in hop]
    gated = after(normed, turn, *hops[0], *swapped[-1], *d_attention)
    d_part = pair_grad(gated, grads, qkv_grads[-1], attended[-1])
    d_attention.append(scatter_rows(d_part))
    [own_part], own_sums = some_ranks([0], after(turn, d_part), MUCH)
    d_qkv = jnp.concatenate(
        [part[:, : 3 * lanes].reshape(-1, 3, lanes) for part in d_attention], axis=2
    ).astype(WIDE)
    d_dense = jnp.concatenate([part[:, 3 * lanes :].T for part in d_attention], axis=0)
    d_dense = d_dense.astype(WIDE)

    qkv_bias_part = jnp.concatenate(
        [part.reshape(3, lanes) for part in qkv_sums], axis=1
    )
    qkv_bias_wide = lax.dynamic_update_slice_in_dim(
        jnp.zeros((3, width), WIDE), qkv_bias_part, me * each, 1
    ).reshape(-1)
    fc1_bias_wide = lax.dynamic_update_slice_in_dim(
        jnp.zeros((b_fc1.shape[0],), WIDE), fc1_bias_part, me * hidden, 0
    )
    small = jnp.concatenate(
        [
            (far_sums + middle_sums + own_sums).reshape(-1),
            qkv_bias_wide,
            own_grad_sum,
            fc1_bias_wide,
        ]
    )
    steps = exchange_steps(("fsdp", "ctx"))
    small = exchange(small, steps[:1])
    d_fc1, d_fc2 = d_fc1.astype(WIDE), d_fc2.T.astype(WIDE)
    output = place_output(
        [swapped[which][rank] for rank in range(count) for which in range(groups)],
        dense_pieces,
        after(tokens[0], *own_part),
        (b_dense.astype(WIDE) + b_fc2.astype(WIDE))[None],
        ff_part,
        ff_terms,
        count,
        groups,
    )
    small = exchange(after(small, output, *last_hops), steps[1:2])
    d_tokens = token_grad(
        after(tokens[0], output), own_grad, own_part[0], gain, grad_terms, local_rows // 4
    )
    small = exchange(after(small, d_tokens), steps[2:-1])
    small = exchange(after(small, d_fc1, d_fc2), steps[-1:])
    small = after(small, d_qkv, d_dense)
    d_shift, with_normed, d_b_qkv, d_b_out, d_b_fc1 = jnp.split(
        small, [width, 2 * width, 5 * width, 6 * width]
    )
    d_gain = (with_normed - shift * d_shift) / gain
    return (
        output[None],
        d_tokens[None],
        d_gain,
        d_shift,
        d_qkv,
        d_b_qkv,
        d_dense,
        d_b_out,
        d_fc1,
        d_b_fc1,
        d_fc2,
        d_b_out,
    )


def solution(mesh):
    in_specs = (
        P("fsdp", "ctx", None),
        P("fsdp", "ctx", None),
        P("fsdp", None),
        P(),
        P(),
        P("fsdp", None, "ctx"),
        P(),
        P("ctx", "fsdp"),
        P(),
        P("fsdp", "ctx"),
        P(),
        P("ctx", "fsdp"),
        P(),
    )
    out_specs = (
        P("fsdp", "ctx", None),
        P("fsdp", "ctx", None),
        P(),
        P(),
        P("fsdp", None, "ctx"),
        P(),
        P("ctx", "fsdp"),
        P(),
        P("fsdp", "ctx"),
        P(),
        P("ctx", "fsdp"),
        P(),
    )
    return jax.shard_map(shards, mesh=mesh, in_specs=in_specs, out_specs=out_specs, check_vma=False)
```

```python
import functools
import math

import jax
import jax.numpy as jnp
from jax import lax
from jax.experimental import pallas as pl
from jax.experimental.pallas import tpu as pltpu
from jax.sharding import PartitionSpec as P

HEADS = 32
ROT = 32
PROMPT = 2048
CLEN = 256
BLK = 64
CHUNK = 256
LANES = 128
NT = (((1,), (1,)), ((), ()))
NN = (((1,), (0,)), ((), ()))
TN = (((0,), (0,)), ((), ()))
LOW = jnp.bfloat16
WIDE = jnp.float32
LITTLE = pl.CostEstimate(flops=1000000, bytes_accessed=1000000, transcendentals=0)
MUCH = pl.CostEstimate(flops=100000000000, bytes_accessed=1000000, transcendentals=0)


def dot(left, right, dims):
    return lax.dot_general(left, right, dims, preferred_element_type=WIDE)


def attention_kernel(where_ref, *refs, chunk, chunks, full_chunks, blk, group, scale):
    per = chunk // blk
    qkv_in, g_in = refs[:per], refs[per : 2 * per]
    cos_ref, up_ref, down_ref, att_hbm, grad_hbm, sums_ref = refs[2 * per : 2 * per + 6]
    (
        keys,
        values,
        values_t,
        probs,
        key_sum,
        value_sum,
        top_ref,
        total_ref,
        mix_ref,
        back_ref,
        att_stage,
        query_stage,
        key_stage,
        value_stage,
        row_sem,
        col_sem,
    ) = refs[2 * per + 6 :]
    i = pl.program_id(0)
    slot = lax.rem(i, 2)
    half = LANES // 2
    lanes = group * LANES
    heads = 2 * group
    first = lax.broadcasted_iota(jnp.int32, (1, LANES), 1) < half

    def columns(part):
        return pl.ds(part * lanes, lanes)

    def row_copies(which, at):
        stage, target = ((att_stage, att_hbm), (query_stage, grad_hbm))[which]
        return [
            pltpu.make_async_copy(
                stage.at[at, pl.ds(r * blk, blk)],
                target.at[where_ref[i * per + r], :, columns(0)],
                row_sem.at[at, which, r],
            )
            for r in range(per)
        ]

    def col_copies(n):
        block = where_ref[n]
        rows = pl.ds(pl.multiple_of(n * blk, blk), blk)
        return (
            pltpu.make_async_copy(
                key_stage.at[rows], grad_hbm.at[block, :, columns(1)], col_sem.at[0, n]
            ),
            pltpu.make_async_copy(
                value_stage.at[rows], grad_hbm.at[block, :, columns(2)], col_sem.at[1, n]
            ),
        )

    def load(parts):
        return jnp.concatenate([part[0] for part in parts], axis=0)

    def tables(rows):
        return cos_ref[rows], up_ref[rows], down_ref[rows]

    quarter = ROT // 2

    def turned(x, tab, sign):
        return jnp.concatenate(
            [
                y * tab[0]
                + sign
                * (pltpu.roll(y, quarter, 1) * tab[1] + pltpu.roll(y, LANES - quarter, 1) * tab[2])
                for y in (x[:, n * LANES : (n + 1) * LANES] for n in range(group))
            ],
            axis=1,
        )

    def one_head(x, h):
        pair = x[:, (h // 2) * LANES : (h // 2 + 1) * LANES]
        nothing = jnp.zeros_like(pair)
        return jnp.where(first, pair, nothing) if h % 2 == 0 else jnp.where(first, nothing, pair)

    @pl.when(i >= 2)
    def _():
        for which in range(2):
            for copy in row_copies(which, slot):
                copy.wait()

    here = pl.ds(pl.multiple_of(i * chunk, chunk), chunk)
    tab = tables(here)
    qkv = load(qkv_in)
    query = (turned(qkv[:, :lanes].astype(WIDE), tab, 1.0) * scale).astype(LOW)
    key_new = turned(qkv[:, lanes : 2 * lanes].astype(WIDE), tab, 1.0)
    value_new = qkv[:, 2 * lanes :]
    grad = load(g_in)
    keys[here] = key_new.astype(LOW)
    values[here] = value_new
    values_t[:, here] = value_new.T
    key_sum[here] = jnp.zeros((chunk, lanes), WIDE)
    value_sum[here] = jnp.zeros((chunk, lanes), WIDE)
    top_ref[...] = jnp.full(top_ref.shape, -1e30, WIDE)
    total_ref[...] = jnp.zeros(total_ref.shape, WIDE)
    mix_ref[...] = jnp.zeros(mix_ref.shape, WIDE)
    back_ref[...] = jnp.zeros(back_ref.shape, WIDE)
    query_of = [one_head(query, h) for h in range(heads)]
    grad_of = [one_head(grad, h) for h in range(heads)]
    query_pair = [
        jnp.concatenate(query_of[2 * n : 2 * n + 2], axis=0) for n in range(group)
    ]
    grad_pair = [jnp.concatenate(grad_of[2 * n : 2 * n + 2], axis=0) for n in range(group)]
    before = jnp.minimum(i, full_chunks)
    doubles = before // 2
    odd = before - 2 * doubles

    def fold(x, how):
        return how(x.reshape(x.shape[0] // 8, 8, chunk), axis=0)

    def pair_lanes(n):
        return slice(n * LANES, (n + 1) * LANES)

    def head_rows(h):
        return slice(h * half, (h + 1) * half)

    def sweep(tile):
        def quad(t, carry):
            start = pl.multiple_of(t * 4 * chunk, 4 * chunk)
            tile(start, start, 4 * chunk, False)
            return carry

        lax.fori_loop(0, doubles // 2, quad, 0)

        @pl.when(doubles % 2 == 1)
        def _():
            start = pl.multiple_of((doubles - 1) * 2 * chunk, 2 * chunk)
            tile(start, start, 2 * chunk, False)

        held = pl.multiple_of(doubles * 2 * chunk, chunk)

        @pl.when(odd == 1)
        def _():
            tile(held, held, 2 * chunk, True)

        @pl.when(odd == 0)
        def _():
            tile(pl.multiple_of(i * chunk, chunk), held, chunk, True)

    def score(start, held, size, masked):
        rows, to = pl.ds(start, size), pl.ds(held, size)
        if masked:
            key_row = lax.broadcasted_iota(jnp.int32, (size, chunk), 0) + start
            query_col = lax.broadcasted_iota(jnp.int32, (size, chunk), 1) + i * chunk
            seen = key_row <= query_col
        for h in range(heads):
            raw = dot(keys[rows, pair_lanes(h // 2)], query_of[h], NT)
            if masked:
                raw = jnp.where(seen, raw, -1e30)
            probs[h, to] = raw
            top_ref[h] = jnp.maximum(top_ref[h], fold(raw, jnp.max))

    sweep(score)
    top = [jnp.max(top_ref[h], axis=0, keepdims=True) for h in range(heads)]

    def mix(start, held, size, masked):
        rows, to = pl.ds(start, size), pl.ds(held, size)
        for h in range(heads):
            weight = jnp.exp(probs[h, to] - top[h])
            probs[h, to] = weight
            total_ref[h] += fold(weight, jnp.sum)
            mix_ref[head_rows(h)] += dot(values_t[head_rows(h), rows], weight.astype(LOW), NN)

    sweep(mix)
    inverse = [1.0 / jnp.sum(total_ref[h], axis=0, keepdims=True) for h in range(heads)]
    attended = jnp.concatenate(
        [mix_ref[head_rows(h)] * inverse[h] for h in range(heads)], axis=0
    )
    shared = grad.T.astype(WIDE) * attended
    inner = [jnp.sum(shared[head_rows(h)], axis=0, keepdims=True) for h in range(heads)]
    att_stage[slot] = attended.astype(LOW).T
    for copy in row_copies(0, slot):
        copy.start()

    def back(start, held, size, masked):
        rows, to = pl.ds(start, size), pl.ds(held, size)
        for n in range(group):
            value = values[rows, pair_lanes(n)]
            weights, grads = [], []
            for h in (2 * n, 2 * n + 1):
                weight = probs[h, to] * inverse[h]
                weight_grad = dot(value, grad_of[h], NT)
                score_grad = (weight * (weight_grad - inner[h])).astype(LOW)
                weights.append(weight.astype(LOW))
                grads.append(score_grad)
            value_sum[rows, pair_lanes(n)] += dot(
                jnp.concatenate(weights, axis=1), grad_pair[n], NN
            )
            key = keys[rows, pair_lanes(n)]
            back_ref[:, pair_lanes(n)] += dot(
                jnp.concatenate(grads, axis=0),
                jnp.concatenate([one_head(key, h) for h in range(2)], axis=0),
                TN,
            )
            key_sum[rows, pair_lanes(n)] += dot(
                jnp.concatenate(grads, axis=1), query_pair[n], NN
            )

    sweep(back)
    query_grad = turned(back_ref[...] * scale, tab, -1.0)
    query_stage[slot] = query_grad.astype(LOW)

    def column_sums(x):
        return jnp.sum(x.reshape(chunk // 8, 8, lanes), axis=0)

    @pl.when(i == 0)
    def _():
        sums_ref[...] = jnp.zeros(sums_ref.shape, WIDE)

    sums_ref[:, :lanes] += column_sums(query_grad)
    for copy in row_copies(1, slot):
        copy.start()

    @pl.when(i == chunks - 1)
    def _():
        @pl.loop(0, chunks)
        def _(n):
            rows = pl.ds(pl.multiple_of(n * chunk, chunk), chunk)
            key_grad = turned(key_sum[rows], tables(rows), -1.0)
            key_stage[rows] = key_grad.astype(LOW)
            value_stage[rows] = value_sum[rows].astype(LOW)
            sums_ref[:, lanes : 2 * lanes] += column_sums(key_grad)
            sums_ref[:, 2 * lanes :] += column_sums(value_sum[rows])
            for r in range(per):
                for copy in col_copies(n * per + r):
                    copy.start()

        for at in range(2):
            for which in range(2):
                for copy in row_copies(which, at):
                    copy.wait()

        @pl.loop(0, chunks * per)
        def _(n):
            for copy in col_copies(n):
                copy.wait()


def attention(qkv, grad, where, tabs, lanes, which, head_dim):
    rows = grad.shape[0]
    chunk, blk = CHUNK, BLK
    per, chunks, blocks = chunk // blk, rows // chunk, rows // blk
    group = lanes // LANES
    heads = 2 * group
    qkv_blocks = qkv.reshape(blocks, blk, qkv.shape[1])
    grad_blocks = grad.reshape(blocks, blk, grad.shape[1])

    def spec(columns, r):
        return pl.BlockSpec((1, blk, columns), lambda i, at: (at[i * per + r], 0, which))

    in_specs = [spec(3 * lanes, r) for r in range(per)] + [spec(lanes, r) for r in range(per)]
    in_specs += [pl.BlockSpec((rows, LANES), lambda i, at: (0, 0), pipeline_mode=pl.Buffered(1))] * 3
    operands = [qkv_blocks] * per + [grad_blocks] * per + list(tabs)
    kernel = functools.partial(
        attention_kernel,
        chunk=chunk,
        chunks=chunks,
        full_chunks=PROMPT // chunk,
        blk=blk,
        group=group,
        scale=1.0 / math.sqrt(head_dim),
    )
    attended, grads, sums = pl.pallas_call(
        kernel,
        out_shape=(
            jax.ShapeDtypeStruct((blocks, blk, lanes), LOW),
            jax.ShapeDtypeStruct((blocks, blk, 3 * lanes), LOW),
            jax.ShapeDtypeStruct((8, 3 * lanes), WIDE),
        ),
        grid_spec=pltpu.PrefetchScalarGridSpec(
            num_scalar_prefetch=1,
            grid=(chunks,),
            in_specs=in_specs,
            out_specs=[pl.BlockSpec(memory_space=pl.ANY)] * 2
            + [pl.BlockSpec((8, 3 * lanes), lambda i, at: (0, 0))],
            scratch_shapes=[
                pltpu.VMEM((rows, lanes), LOW),
                pltpu.VMEM((rows, lanes), LOW),
                pltpu.VMEM((lanes, rows), LOW),
                pltpu.VMEM((heads, PROMPT + chunk, chunk), WIDE),
                pltpu.VMEM((rows, lanes), WIDE),
                pltpu.VMEM((rows, lanes), WIDE),
                pltpu.VMEM((heads, 8, chunk), WIDE),
                pltpu.VMEM((heads, 8, chunk), WIDE),
                pltpu.VMEM((lanes, chunk), WIDE),
                pltpu.VMEM((chunk, lanes), WIDE),
                pltpu.VMEM((2, chunk, lanes), LOW),
                pltpu.VMEM((2, chunk, lanes), LOW),
                pltpu.VMEM((rows, lanes), LOW),
                pltpu.VMEM((rows, lanes), LOW),
                pltpu.SemaphoreType.DMA((2, 2, per)),
                pltpu.SemaphoreType.DMA((2, blocks)),
            ],
        ),
        compiler_params=pltpu.CompilerParams(
            dimension_semantics=("arbitrary",), vmem_limit_bytes=56 << 20
        ),
        cost_estimate=LITTLE,
        name="attention",
    )(where, *operands)
    return attended.reshape(rows, lanes), grads.reshape(rows, 3 * lanes), jnp.sum(sums, axis=0)


def after(value, *others):
    return lax.optimization_barrier((value,) + others)[0] if others else value


def ring_of(count):
    order = list(range(count // 2)) + list(range(count - 1, count // 2 - 1, -1))
    ahead = [(order[n], order[(n + 1) % count]) for n in range(count)]
    return order, ahead, [(b, a) for a, b in ahead]


def rank_of(offset, count):
    offset %= count
    if offset == 0 or 2 * offset == count:
        return max(2 * offset - 1, 0)
    return 2 * offset if 2 * offset < count else 2 * (count - offset) - 1


def ring_pieces(own, axis, gate=()):
    count = lax.axis_size(axis)
    _, ahead, behind = ring_of(count)
    pieces, half = [own], own.shape[0] // 2
    from_behind = from_ahead = own
    for _ in range(count // 2 - 1):
        from_behind = lax.ppermute(from_behind, axis, ahead)
        from_ahead = lax.ppermute(from_ahead, axis, behind)
        pieces += [from_behind, from_ahead]
    if gate:
        from_behind, from_ahead = after(from_behind, *gate), after(from_ahead, *gate)
        if count > 2:
            pieces[-2:] = [from_behind, from_ahead]
    far = [
        lax.ppermute(from_behind[:half], axis, ahead),
        lax.ppermute(from_ahead[half:], axis, behind),
    ]
    return pieces + far


def ring_reduce(part, axis, cuts=1, chained=False):
    count = lax.axis_size(axis)
    _, ahead, behind = ring_of(count)

    def plus(a, b):
        return (a.astype(WIDE) + b.astype(WIDE)).astype(LOW)

    def cut_rows(term, sizes):
        if isinstance(term, (list, tuple)):
            return term
        ends = [sum(sizes[: n + 1]) for n in range(len(sizes))]
        return [term[end - size : end] for end, size in zip(ends, sizes)]

    far = part(count - 1)
    half = sum(a.shape[0] for a in far) // 2 if isinstance(far, (list, tuple)) else far.shape[0] // 2
    far = cut_rows(far, [half, half])
    up, down = lax.ppermute(far[0], axis, ahead), lax.ppermute(far[1], axis, behind)
    hops = [(up, down)]
    if count == 2:
        return [(0, up), (half, down)], hops
    pieces = [half // cuts] * cuts
    to_ahead = cut_rows(part(count - 2), [half] + pieces)
    to_behind = cut_rows(part(count - 3), pieces + [half])
    got_up, got_down = {}, {}
    got_up[0] = lax.ppermute(plus(to_ahead[0], up), axis, ahead)
    got_down[half] = lax.ppermute(plus(to_behind[-1], down), axis, behind)
    hops.append((got_up[0], got_down[half]))
    for n in range(cuts):
        gate = hops[-1] if chained else ()
        at = n * (half // cuts)
        got_up[half + at] = lax.ppermute(after(to_ahead[1 + n], *gate), axis, ahead)
        got_down[at] = lax.ppermute(after(to_behind[n], *gate), axis, behind)
        hops.append((got_up[half + at], got_down[at]))
    if count == 4:
        return sorted(got_up.items()) + sorted(got_down.items()), hops
    up = jnp.concatenate([piece for _, piece in sorted(got_up.items())], axis=0)
    down = jnp.concatenate([piece for _, piece in sorted(got_down.items())], axis=0)
    for s in range(count // 2 - 2, 0, -1):
        up = lax.ppermute(plus(part(2 * s), up), axis, ahead)
        down = lax.ppermute(plus(part(2 * s - 1), down), axis, behind)
        hops.append((up, down))
    return [(0, up), (0, down)], hops


def ring_exchange(part, axis):
    count = lax.axis_size(axis)
    order, _, _ = ring_of(count)
    got = [None] * count
    got[0] = part(0)
    for offset in range(1, count):
        hops = [(order[n], order[(n + offset) % count]) for n in range(count)]
        got[rank_of(-offset, count)] = lax.ppermute(part(rank_of(offset, count)), axis, hops)
    return got


def exchange_steps(axes):
    steps = []
    for axis in axes:
        count, span = lax.axis_size(axis), 1
        while span < count:
            steps.append((axis, [(n, n ^ span) for n in range(count)]))
            span *= 2
    return steps


def exchange(values, steps):
    for axis, pairs in steps:
        values = values + lax.ppermute(values, axis, pairs)
    return values


def gelu_and_slope(h):
    inner_scale = math.sqrt(2.0 / math.pi)
    square = h * h
    t = jnp.tanh(h * (inner_scale + (inner_scale * 0.044715) * square))
    half = 0.5 * h
    rise = 0.5 + 0.5 * t
    bend = inner_scale + (3.0 * inner_scale * 0.044715) * square
    return (h * rise).astype(LOW), (rise + (half - half * t * t) * bend).astype(LOW)


def join_piece(pieces, spans, whole_ref):
    i = pl.program_id(0)
    for (first, span), piece in zip(spans, pieces):

        @pl.when((i >= first) & (i < first + span))
        def _(piece=piece):
            whole_ref[...] = piece[...]


def piece_blocks(pieces):
    tile, width = pieces[-1].shape
    spans, first = [], 0
    for piece in pieces:
        spans.append((first, piece.shape[0] // tile))
        first += piece.shape[0] // tile

    def spec(first, span):
        return pl.BlockSpec((tile, width), lambda i: (jnp.clip(i - first, 0, span - 1), 0))

    return tile, tuple(spans), [spec(*span) for span in spans]


def expand_kernel(*refs, spans, cols):
    w_ref, b_ref, act_ref, slope_ref, whole_ref = refs[len(spans) :]
    join_piece(refs[: len(spans)], spans, whole_ref)
    x = whole_ref[...]
    for n in range(w_ref.shape[1] // cols):
        at = slice(n * cols, (n + 1) * cols)
        act, slope = gelu_and_slope(dot(x, w_ref[:, at], NN) + b_ref[:, at])
        act_ref[:, at] = act
        slope_ref[:, at] = slope


def expand(pieces, w, b):
    width, hidden = w.shape
    tile, spans, specs = piece_blocks(pieces)
    rows = sum(piece.shape[0] for piece in pieces)
    by_row = pl.BlockSpec((tile, hidden), lambda i: (i, 0))
    out = jax.ShapeDtypeStruct((rows, hidden), LOW)
    return pl.pallas_call(
        functools.partial(expand_kernel, spans=spans, cols=min(512, hidden)),
        out_shape=(out, out, jax.ShapeDtypeStruct((rows, width), LOW)),
        grid=(rows // tile,),
        in_specs=specs
        + [
            pl.BlockSpec((width, hidden), lambda i: (0, 0), pipeline_mode=pl.Buffered(1)),
            pl.BlockSpec((1, hidden), lambda i: (0, 0)),
        ],
        out_specs=[by_row, by_row, pl.BlockSpec((tile, width), lambda i: (i, 0))],
        compiler_params=pltpu.CompilerParams(
            dimension_semantics=("arbitrary",), vmem_limit_bytes=48 << 20
        ),
        cost_estimate=pl.CostEstimate(
            flops=2 * rows * width * hidden,
            bytes_accessed=2 * rows * (2 * width + 2 * hidden),
            transcendentals=rows * hidden,
        ),
        name="expand",
    )(*pieces, w, b[None])


def slope_grad_kernel(*refs, spans, cols):
    pieces = refs[: len(spans)]
    w_ref, slope_ref, out_ref, whole_ref, sums_ref = refs[len(spans) :]
    join_piece(pieces, spans, whole_ref)

    @pl.when(pl.program_id(0) == 0)
    def _():
        sums_ref[...] = jnp.zeros(sums_ref.shape, WIDE)

    x = whole_ref[...]
    for n in range(w_ref.shape[1] // cols):
        at = slice(n * cols, (n + 1) * cols)
        value = dot(x, w_ref[:, at], NN) * slope_ref[:, at].astype(WIDE)
        out_ref[:, at] = value.astype(LOW)
        sums_ref[:, at] += jnp.sum(value.reshape(value.shape[0] // 8, 8, cols), axis=0)


def slope_grad(pieces, w, slope):
    width, hidden = w.shape
    tile, spans, specs = piece_blocks(pieces)
    first = sum(span for _, span in spans)
    by_row = pl.BlockSpec((tile, hidden), lambda i: (i, 0))
    grad, whole, sums = pl.pallas_call(
        functools.partial(slope_grad_kernel, spans=spans, cols=min(512, hidden)),
        out_shape=(
            jax.ShapeDtypeStruct((first * tile, hidden), LOW),
            jax.ShapeDtypeStruct((first * tile, width), LOW),
            jax.ShapeDtypeStruct((8, hidden), WIDE),
        ),
        grid=(first,),
        in_specs=specs
        + [
            pl.BlockSpec((width, hidden), lambda i: (0, 0), pipeline_mode=pl.Buffered(1)),
            by_row,
        ],
        out_specs=[
            by_row,
            pl.BlockSpec((tile, width), lambda i: (i, 0)),
            pl.BlockSpec((8, hidden), lambda i: (0, 0)),
        ],
        compiler_params=pltpu.CompilerParams(
            dimension_semantics=("arbitrary",), vmem_limit_bytes=48 << 20
        ),
        cost_estimate=pl.CostEstimate(
            flops=2 * first * tile * width * hidden,
            bytes_accessed=2 * first * tile * (2 * width + 2 * hidden),
            transcendentals=0,
        ),
        name="slope_grad",
    )(*pieces, w, slope)
    return grad, whole, jnp.sum(sums, axis=0)


def input_grad_kernel(*refs, terms, ranks):
    grads, weights = refs[: terms * ranks], refs[terms * ranks : terms * ranks + terms]
    rest = refs[terms * (ranks + 1) :]
    normed_refs, out_refs, sums_ref = rest[:ranks], list(rest[ranks:-1]), rest[-1]
    plain = weighted = 0.0
    for n in range(ranks):
        mine = grads[n * terms : (n + 1) * terms]
        total = sum(dot(g[...], w[...], NT) for g, w in zip(mine, weights))
        at = 0
        while at < total.shape[0]:
            out_ref = out_refs.pop(0)
            out_ref[...] = total[at : at + out_ref.shape[0]].astype(LOW)
            at += out_ref.shape[0]
        plain += jnp.sum(total, axis=0, keepdims=True)
        weighted += jnp.sum(total * normed_refs[n][...].astype(WIDE), axis=0, keepdims=True)
    sums_ref[0:1] = plain
    sums_ref[1:2] = weighted


def input_grad(grads, weights, normed, ranks, rows, cuts, cost):
    width = normed.shape[1]
    cols = 512
    keep = pl.Buffered(1)
    in_specs = [
        pl.BlockSpec((rows, g.shape[1]), lambda i, rank=rank: (rank, 0), pipeline_mode=keep)
        for rank in ranks
        for g in grads
    ]
    in_specs += [
        pl.BlockSpec((cols, g.shape[1]), lambda i, at=at: (i, at))
        for g, (_, at) in zip(grads, weights)
    ]
    in_specs += [pl.BlockSpec((rows, cols), lambda i, rank=rank: (rank, i)) for rank in ranks]
    sizes = [size for cut in cuts for size in cut]
    *parts, sums = pl.pallas_call(
        functools.partial(input_grad_kernel, terms=len(grads), ranks=len(ranks)),
        out_shape=[jax.ShapeDtypeStruct((size, width), LOW) for size in sizes]
        + [jax.ShapeDtypeStruct((2, width), WIDE)],
        grid=(width // cols,),
        in_specs=in_specs,
        out_specs=[pl.BlockSpec((size, cols), lambda i: (0, i)) for size in sizes]
        + [pl.BlockSpec((2, cols), lambda i: (0, i))],
        compiler_params=pltpu.CompilerParams(
            dimension_semantics=("arbitrary",), vmem_limit_bytes=58 << 20
        ),
        cost_estimate=cost,
        name="input_grad",
    )(*grads * len(ranks), *[w for w, _ in weights], *[normed] * len(ranks))
    return [[parts.pop(0) for _ in cut] for cut in cuts], sums


def place_kernel(*refs, starts, count, groups):
    pieces = refs[: count * groups]
    dense = refs[count * groups : count * groups + count + 1]
    rest = refs[count * (groups + 1) + 1 :]
    token_ref, bias_ref, own_ref = rest[:3]
    terms, out_ref, acc = rest[3:-2], rest[-2], rest[-1]
    acc[...] = token_ref[...].astype(WIDE) + bias_ref[...] + own_ref[...].astype(WIDE)
    for start, term in zip(starts, terms):
        acc[start : start + term.shape[0]] += term[...].astype(WIDE)
    steps = pl.num_programs(0)
    low_half = pl.program_id(0) * 2 < steps
    far = jnp.where(low_half, dense[count - 1][...], dense[count][...])
    total = acc[...]
    for rank in range(count):
        weight = dense[rank][...] if rank < count - 1 else far
        mine = [piece[...] for piece in pieces[rank * groups : (rank + 1) * groups]]
        total += dot(jnp.concatenate(mine, axis=1), weight, NT)
    out_ref[...] = total.astype(LOW)


def place_output(pieces, dense_pieces, tokens, bias, own, terms, count, groups):
    rows, width = tokens.shape
    cols = 512
    half = width // cols // 2
    whole = lambda a: pl.BlockSpec(a.shape, lambda i: (0, 0), pipeline_mode=pl.Buffered(1))
    in_specs = [whole(piece) for piece in pieces]
    depth = dense_pieces[0].shape[1]
    in_specs += [pl.BlockSpec((cols, depth), lambda i: (i, 0)) for _ in range(count - 1)]
    in_specs.append(pl.BlockSpec((cols, depth), lambda i: (jnp.minimum(i, half - 1), 0)))
    in_specs.append(pl.BlockSpec((cols, depth), lambda i: (jnp.maximum(i - half, 0), 0)))
    by_column = lambda n: pl.BlockSpec((n, cols), lambda i: (0, i))
    in_specs += [by_column(rows), by_column(1), by_column(rows)]
    in_specs += [by_column(term.shape[0]) for _, term in terms]
    return pl.pallas_call(
        functools.partial(
            place_kernel, starts=tuple(start for start, _ in terms), count=count, groups=groups
        ),
        out_shape=jax.ShapeDtypeStruct((rows, width), LOW),
        grid=(width // cols,),
        in_specs=in_specs,
        out_specs=by_column(rows),
        scratch_shapes=[pltpu.VMEM((rows, cols), WIDE)],
        compiler_params=pltpu.CompilerParams(
            dimension_semantics=("arbitrary",), vmem_limit_bytes=58 << 20
        ),
        cost_estimate=LITTLE,
        name="place_output",
    )(*pieces, *dense_pieces, tokens, bias, own, *[term for _, term in terms])


def token_grad_kernel(token_ref, grad_ref, own_ref, gain_ref, *refs, starts, tile):
    terms, out_ref, total = refs[:-2], refs[-2], refs[-1]
    first = pl.program_id(0) * tile
    total[...] = own_ref[...].astype(WIDE)
    for start, term in zip(starts, terms):
        size = min(tile, term.shape[0])
        for at in range(0, term.shape[0], size):

            @pl.when(first == (start + at) // tile * tile)
            def _(start=start, term=term, at=at, size=size):
                to = (start + at) % tile
                total[to : to + size] += term[at : at + size].astype(WIDE)

    x = token_ref[...].astype(WIDE)
    centred = x - jnp.mean(x, axis=-1, keepdims=True)
    rstd = lax.rsqrt(jnp.mean(centred * centred, axis=-1, keepdims=True) + 1e-05)
    xhat = centred * rstd
    scaled = total[...] * gain_ref[...]
    mean = jnp.mean(scaled, axis=-1, keepdims=True)
    along = jnp.mean(scaled * xhat, axis=-1, keepdims=True)
    out_ref[...] = (grad_ref[...].astype(WIDE) + rstd * (scaled - mean - xhat * along)).astype(LOW)


def token_grad(tokens, grad, own, gain, terms, tile):
    rows, width = tokens.shape
    by_row = pl.BlockSpec((tile, width), lambda i: (i, 0))
    whole = lambda a: pl.BlockSpec(a.shape, lambda i: (0, 0), pipeline_mode=pl.Buffered(1))
    return pl.pallas_call(
        functools.partial(
            token_grad_kernel, starts=tuple(start for start, _ in terms), tile=tile
        ),
        out_shape=jax.ShapeDtypeStruct((rows, width), LOW),
        grid=(rows // tile,),
        in_specs=[by_row, by_row, by_row, pl.BlockSpec((1, width), lambda i: (0, 0))]
        + [whole(term) for _, term in terms],
        out_specs=by_row,
        scratch_shapes=[pltpu.VMEM((tile, width), WIDE)],
        compiler_params=pltpu.CompilerParams(
            dimension_semantics=("arbitrary",), vmem_limit_bytes=48 << 20
        ),
        cost_estimate=LITTLE,
        name="token_grad",
    )(tokens, grad, own, gain[None], *[term for _, term in terms])


def pair_grad_kernel(x_ref, y_ref, a_ref, b_ref, out_ref):
    split = a_ref.shape[1]
    out_ref[:, :split] = dot(x_ref[...], a_ref[...], TN).astype(LOW)
    out_ref[:, split:] = dot(y_ref[...], b_ref[...], TN).astype(LOW)


def pair_grad(x, y, a, b):
    rows, width = x.shape
    columns = a.shape[1] + b.shape[1]
    tile = 512
    keep = pl.Buffered(1)
    return pl.pallas_call(
        pair_grad_kernel,
        out_shape=jax.ShapeDtypeStruct((width, columns), LOW),
        grid=(width // tile,),
        in_specs=[
            pl.BlockSpec((rows, tile), lambda i: (0, i)),
            pl.BlockSpec((rows, tile), lambda i: (0, i)),
            pl.BlockSpec(a.shape, lambda i: (0, 0), pipeline_mode=keep),
            pl.BlockSpec(b.shape, lambda i: (0, 0), pipeline_mode=keep),
        ],
        out_specs=pl.BlockSpec((tile, columns), lambda i: (i, 0)),
        compiler_params=pltpu.CompilerParams(
            dimension_semantics=("arbitrary",), vmem_limit_bytes=58 << 20
        ),
        cost_estimate=LITTLE,
        name="pair_grad",
    )(x, y, a, b)


def rope_tables(rows):
    place = lax.broadcasted_iota(jnp.int32, (rows, LANES), 0)
    lane = lax.broadcasted_iota(jnp.int32, (rows, LANES), 1)
    pos = jnp.where(place < PROMPT, place, PROMPT + (place - PROMPT) % CLEN)
    half = ROT // 2
    freq = 10000.0 ** (-2.0 * jnp.arange(half, dtype=WIDE) / ROT)
    angle = pos.astype(WIDE) * jnp.tile(freq, LANES // half)[None, :]
    dim = lane % (LANES // 2)
    cosine, sine = jnp.cos(angle), jnp.sin(angle)
    return [
        jnp.where(dim < ROT, cosine, 1.0),
        jnp.where((dim >= half) & (dim < ROT), sine, 0.0),
        jnp.where(dim < half, -sine, 0.0),
    ]


def shards(
    tokens,
    cotangent,
    block_table,
    ln_gain,
    ln_bias,
    w_qkv,
    b_qkv,
    w_dense,
    b_dense,
    w_fc1,
    b_fc1,
    w_fc2,
    b_fc2,
):
    _, local_rows, width = tokens.shape
    head_dim = width // HEADS
    count = lax.axis_size("ctx")
    me = lax.axis_index("ctx")
    rows = local_rows * count
    local_blocks = local_rows // BLK
    each = w_dense.shape[0]
    hidden = w_fc2.shape[0]
    gain, shift = ln_gain.astype(WIDE), ln_bias.astype(WIDE)

    def of_rank(whole, rank):
        return whole[rank * local_rows : (rank + 1) * local_rows]

    order, _, _ = ring_of(count)
    places = [0] * count
    for n, device in enumerate(order):
        places[device] = n
    places = jnp.asarray(places, jnp.int32)
    ranks = jnp.asarray([rank_of(n, count) for n in range(count)], jnp.int32)
    slots = jnp.arange(rows // BLK, dtype=jnp.int32)
    offset = (places[slots // local_blocks] - places[me]) % count
    held_at = ranks[offset] * local_blocks + slots % local_blocks
    hit = block_table[0][None, :] == slots[:, None]
    where = jnp.sum(jnp.where(hit, held_at[None, :], 0), axis=1).astype(jnp.int32)

    own_tokens = tokens[0].astype(WIDE)
    own_grad = cotangent[0]
    average = jnp.mean(own_tokens, axis=-1, keepdims=True)
    centred = own_tokens - average
    rstd = lax.rsqrt(jnp.mean(centred * centred, axis=-1, keepdims=True) + 1e-05)
    xhat = centred * rstd
    normed_own = (xhat * gain + shift).astype(LOW)

    def gather_rows(shard):
        return lax.all_gather(shard, "fsdp", axis=0, tiled=True)

    def scatter_rows(whole):
        return lax.psum_scatter(whole, "fsdp", scatter_dimension=0, tiled=True)

    lanes = 2 * LANES if each % (2 * LANES) == 0 else LANES
    groups = each // lanes

    def by_group(values):
        cut = values.reshape(-1, 3, groups, lanes)
        return jnp.swapaxes(cut, 1, 2).reshape(-1, 3 * each)

    tabs = rope_tables(rows)
    own_grad_sum = jnp.sum(own_grad.astype(WIDE), axis=0)
    fc1_bias = lax.dynamic_slice_in_dim(b_fc1, me * hidden, hidden, 0).astype(WIDE)
    early = (where, own_grad_sum, fc1_bias, *tabs)
    normed_pieces = ring_pieces(normed_own, "ctx", gate=early)
    attention_shard = jnp.concatenate([by_group(w_qkv), w_dense.T], axis=1)
    fc1_weight = gather_rows(w_fc1)
    fc2_turned = gather_rows(after(w_fc2.T, *normed_pieces[1:-2]))
    attention_weight = gather_rows(after(attention_shard, *normed_pieces[-2:]))
    qkv_weight, dense_turned = attention_weight[:, : 3 * each], attention_weight[:, 3 * each :]

    qkv_bias = lax.dynamic_slice_in_dim(b_qkv.reshape(3, width), me * each, each, 1)
    activated, slope, normed = expand(normed_pieces, fc1_weight, fc1_bias)

    sent_grad = after(own_grad, *normed_pieces[-2:])
    grad_pieces = ring_pieces(sent_grad, "ctx", gate=(activated,))
    ff_part = dot(activated, fc2_turned, NT).astype(LOW)
    ff_terms, ff_hops = ring_reduce(lambda rank: of_rank(ff_part, rank), "ctx", chained=True)
    first, second, last = ff_hops[0], ff_hops[min(1, len(ff_hops) - 1)], ff_hops[-1]

    gated = [after(piece, ff_part) for piece in grad_pieces]
    expanded_grad, grads, fc1_bias_part = slope_grad(gated, fc2_turned, slope)
    d_fc2_part = dot(after(grads, expanded_grad, *first), activated, TN).astype(LOW)
    d_fc2 = scatter_rows(d_fc2_part)
    qkv = dot(after(normed, d_fc2_part), qkv_weight, NN)
    qkv = (qkv + by_group(qkv_bias)[0].astype(WIDE)).astype(LOW)
    attended_grad = dot(after(grads, qkv, *second), dense_turned, NN).astype(LOW)
    gated = after(normed, attended_grad)
    d_fc1_part = dot(gated, expanded_grad, TN).astype(LOW)
    d_fc1 = scatter_rows(d_fc1_part)

    dense_pieces = ring_pieces(after(dense_turned, *second), "ctx")

    attended, qkv_grads, qkv_sums, d_attention, swapped = [], [], [], [], []
    ordered = (d_fc1_part,)
    for which in range(groups):
        got, got_grads, got_sums = attention(
            after(qkv, *ordered), attended_grad, where, tabs, lanes, which, head_dim
        )
        attended.append(got)
        qkv_grads.append(got_grads)
        qkv_sums.append(got_sums)
        if which < groups - 1:
            swapped.append(ring_exchange(lambda rank, got=got: of_rank(got, rank), "ctx"))
            gated = after(normed, d_fc2, *last, *dense_pieces[1:-2]) if which == 0 else normed
            d_part = pair_grad(gated, grads, got_grads, got)
            ordered = (d_part,)
            d_attention.append(scatter_rows(d_part))

    weights = [(attention_weight, which) for which in range(groups)] + [(fc1_weight, 0)]
    early_swaps = [piece for pieces in swapped for piece in pieces]
    turn = after(expanded_grad, d_fc1, *dense_pieces[-2:], *early_swaps, *attended)
    swapped.append(ring_exchange(lambda rank: of_rank(attended[-1], rank), "ctx"))
    half = local_rows // 2
    whole, far_cut, ahead_cut, behind_cut = [local_rows], [half, half], [half], [half]
    if count > 2:
        ahead_cut, behind_cut = [half, half], [half, half]
    cut_of = {0: whole, count - 2: ahead_cut, count - 3: behind_cut, count - 1: far_cut}

    def some_ranks(ranks, turn, cost=LITTLE):
        cuts = [cut_of.get(rank, whole) for rank in ranks]
        return input_grad(qkv_grads + [turn], weights, normed, ranks, local_rows, cuts, cost)

    far_part, far_sums = some_ranks([count - 1], turn)
    middle = list(range(count - 2, 0, -1))
    middle_sums, parts = 0.0, {count - 1: far_part[0]}
    turn = after(turn, *far_part[0], *swapped[-1])
    for n in range(0, len(middle), 2):
        some, some_sums = some_ranks(middle[n : n + 2], turn, MUCH)
        turn = after(turn, *[piece for pieces in some for piece in pieces])
        middle_sums = middle_sums + some_sums
        parts.update(zip(middle[n : n + 2], some))
    for rank, pieces in parts.items():
        if len(pieces) == 1:
            parts[rank] = pieces[0]

    grad_terms, hops = ring_reduce(lambda rank: parts[rank], "ctx")
    last_hops = [piece for hop in hops[1:3] for piece in hop]
    gated = after(normed, turn, *hops[0], *d_attention)
    d_part = pair_grad(gated, grads, qkv_grads[-1], attended[-1])
    d_attention.append(scatter_rows(d_part))
    [own_part], own_sums = some_ranks([0], after(turn, d_part), MUCH)
    d_qkv = jnp.concatenate(
        [part[:, : 3 * lanes].reshape(-1, 3, lanes) for part in d_attention], axis=2
    ).astype(WIDE)
    d_dense = jnp.concatenate([part[:, 3 * lanes :].T for part in d_attention], axis=0)
    d_dense = d_dense.astype(WIDE)

    qkv_bias_part = jnp.concatenate(
        [part.reshape(3, lanes) for part in qkv_sums], axis=1
    )
    qkv_bias_wide = lax.dynamic_update_slice_in_dim(
        jnp.zeros((3, width), WIDE), qkv_bias_part, me * each, 1
    ).reshape(-1)
    fc1_bias_wide = lax.dynamic_update_slice_in_dim(
        jnp.zeros((b_fc1.shape[0],), WIDE), fc1_bias_part, me * hidden, 0
    )
    small = jnp.concatenate(
        [
            (far_sums + middle_sums + own_sums).reshape(-1),
            qkv_bias_wide,
            own_grad_sum,
            fc1_bias_wide,
        ]
    )
    near, across = exchange_steps(("fsdp",)), exchange_steps(("ctx",))
    steps = near[:1] + across + near[1:]
    small = exchange(small, steps[:1])
    d_fc1, d_fc2 = d_fc1.astype(WIDE), d_fc2.T.astype(WIDE)
    output = place_output(
        [swapped[which][rank] for rank in range(count) for which in range(groups)],
        dense_pieces,
        after(tokens[0], *own_part),
        (b_dense.astype(WIDE) + b_fc2.astype(WIDE))[None],
        ff_part,
        ff_terms,
        count,
        groups,
    )
    small = exchange(after(small, output, *last_hops), steps[1:2])
    d_tokens = token_grad(
        after(tokens[0], output), own_grad, own_part[0], gain, grad_terms, local_rows // 4
    )
    small = exchange(after(small, d_tokens), steps[2:-1])
    small = after(small, d_fc1, d_fc2)
    axis, pairs = steps[-1]
    small = after(small, d_qkv, d_dense) + lax.ppermute(small, axis, pairs)
    d_shift, with_normed, d_b_qkv, d_b_out, d_b_fc1 = jnp.split(
        small, [width, 2 * width, 5 * width, 6 * width]
    )
    d_gain = (with_normed - shift * d_shift) / gain
    return (
        output[None],
        d_tokens[None],
        d_gain,
        d_shift,
        d_qkv,
        d_b_qkv,
        d_dense,
        d_b_out,
        d_fc1,
        d_b_fc1,
        d_fc2,
        d_b_out,
    )


def solution(mesh):
    in_specs = (
        P("fsdp", "ctx", None),
        P("fsdp", "ctx", None),
        P("fsdp", None),
        P(),
        P(),
        P("fsdp", None, "ctx"),
        P(),
        P("ctx", "fsdp"),
        P(),
        P("fsdp", "ctx"),
        P(),
        P("ctx", "fsdp"),
        P(),
    )
    out_specs = (
        P("fsdp", "ctx", None),
        P("fsdp", "ctx", None),
        P(),
        P(),
        P("fsdp", None, "ctx"),
        P(),
        P("ctx", "fsdp"),
        P(),
        P("fsdp", "ctx"),
        P(),
        P("ctx", "fsdp"),
        P(),
    )
    return jax.shard_map(shards, mesh=mesh, in_specs=in_specs, out_specs=out_specs, check_vma=False)
```

```python
import functools
import math

import jax
import jax.numpy as jnp
from jax import lax
from jax.experimental import pallas as pl
from jax.experimental.pallas import tpu as pltpu
from jax.sharding import PartitionSpec as P

HEADS = 32
ROT = 32
PROMPT = 2048
CLEN = 256
BLK = 64
CHUNK = 256
LANES = 128
NT = (((1,), (1,)), ((), ()))
NN = (((1,), (0,)), ((), ()))
TN = (((0,), (0,)), ((), ()))
LOW = jnp.bfloat16
WIDE = jnp.float32
LITTLE = pl.CostEstimate(flops=1000000, bytes_accessed=1000000, transcendentals=0)
MUCH = pl.CostEstimate(flops=100000000000, bytes_accessed=1000000, transcendentals=0)


def dot(left, right, dims):
    return lax.dot_general(left, right, dims, preferred_element_type=WIDE)


def attention_kernel(where_ref, *refs, chunk, chunks, full_chunks, blk, group, scale):
    per = chunk // blk
    qkv_in, g_in = refs[:per], refs[per : 2 * per]
    cos_ref, up_ref, down_ref, att_hbm, grad_hbm, sums_ref = refs[2 * per : 2 * per + 6]
    (
        keys,
        values,
        values_t,
        probs,
        key_sum,
        value_sum,
        top_ref,
        total_ref,
        mix_ref,
        back_ref,
        att_stage,
        query_stage,
        key_stage,
        value_stage,
        row_sem,
        col_sem,
    ) = refs[2 * per + 6 :]
    i = pl.program_id(0)
    slot = lax.rem(i, 2)
    half = LANES // 2
    lanes = group * LANES
    heads = 2 * group
    first = lax.broadcasted_iota(jnp.int32, (1, LANES), 1) < half

    def columns(part):
        return pl.ds(part * lanes, lanes)

    def row_copies(which, at):
        stage, target = ((att_stage, att_hbm), (query_stage, grad_hbm))[which]
        return [
            pltpu.make_async_copy(
                stage.at[at, pl.ds(r * blk, blk)],
                target.at[where_ref[i * per + r], :, columns(0)],
                row_sem.at[at, which, r],
            )
            for r in range(per)
        ]

    def col_copies(n):
        block = where_ref[n]
        rows = pl.ds(pl.multiple_of(n * blk, blk), blk)
        return (
            pltpu.make_async_copy(
                key_stage.at[rows], grad_hbm.at[block, :, columns(1)], col_sem.at[0, n]
            ),
            pltpu.make_async_copy(
                value_stage.at[rows], grad_hbm.at[block, :, columns(2)], col_sem.at[1, n]
            ),
        )

    def load(parts):
        return jnp.concatenate([part[0] for part in parts], axis=0)

    def tables(rows):
        return cos_ref[rows], up_ref[rows], down_ref[rows]

    quarter = ROT // 2

    def turned(x, tab, sign):
        return jnp.concatenate(
            [
                y * tab[0]
                + sign
                * (pltpu.roll(y, quarter, 1) * tab[1] + pltpu.roll(y, LANES - quarter, 1) * tab[2])
                for y in (x[:, n * LANES : (n + 1) * LANES] for n in range(group))
            ],
            axis=1,
        )

    def one_head(x, h):
        pair = x[:, (h // 2) * LANES : (h // 2 + 1) * LANES]
        nothing = jnp.zeros_like(pair)
        return jnp.where(first, pair, nothing) if h % 2 == 0 else jnp.where(first, nothing, pair)

    @pl.when(i >= 2)
    def _():
        for which in range(2):
            for copy in row_copies(which, slot):
                copy.wait()

    here = pl.ds(pl.multiple_of(i * chunk, chunk), chunk)
    tab = tables(here)
    qkv = load(qkv_in)
    query = (turned(qkv[:, :lanes].astype(WIDE), tab, 1.0) * scale).astype(LOW)
    key_new = turned(qkv[:, lanes : 2 * lanes].astype(WIDE), tab, 1.0)
    value_new = qkv[:, 2 * lanes :]
    grad = load(g_in)
    keys[here] = key_new.astype(LOW)
    values[here] = value_new
    values_t[:, here] = value_new.T
    key_sum[here] = jnp.zeros((chunk, lanes), WIDE)
    value_sum[here] = jnp.zeros((chunk, lanes), WIDE)
    top_ref[...] = jnp.full(top_ref.shape, -1e30, WIDE)
    total_ref[...] = jnp.zeros(total_ref.shape, WIDE)
    mix_ref[...] = jnp.zeros(mix_ref.shape, WIDE)
    back_ref[...] = jnp.zeros(back_ref.shape, WIDE)
    query_of = [one_head(query, h) for h in range(heads)]
    grad_of = [one_head(grad, h) for h in range(heads)]
    query_pair = [
        jnp.concatenate(query_of[2 * n : 2 * n + 2], axis=0) for n in range(group)
    ]
    grad_pair = [jnp.concatenate(grad_of[2 * n : 2 * n + 2], axis=0) for n in range(group)]
    before = jnp.minimum(i, full_chunks)
    doubles = before // 2
    odd = before - 2 * doubles

    def fold(x, how):
        return how(x.reshape(x.shape[0] // 8, 8, chunk), axis=0)

    def pair_lanes(n):
        return slice(n * LANES, (n + 1) * LANES)

    def head_rows(h):
        return slice(h * half, (h + 1) * half)

    def sweep(tile):
        def quad(t, carry):
            start = pl.multiple_of(t * 4 * chunk, 4 * chunk)
            tile(start, start, 4 * chunk, False)
            return carry

        lax.fori_loop(0, doubles // 2, quad, 0)

        @pl.when(doubles % 2 == 1)
        def _():
            start = pl.multiple_of((doubles - 1) * 2 * chunk, 2 * chunk)
            tile(start, start, 2 * chunk, False)

        held = pl.multiple_of(doubles * 2 * chunk, chunk)

        @pl.when(odd == 1)
        def _():
            tile(held, held, 2 * chunk, True)

        @pl.when(odd == 0)
        def _():
            tile(pl.multiple_of(i * chunk, chunk), held, chunk, True)

    def score(start, held, size, masked):
        rows, to = pl.ds(start, size), pl.ds(held, size)
        if masked:
            key_row = lax.broadcasted_iota(jnp.int32, (size, chunk), 0) + start
            query_col = lax.broadcasted_iota(jnp.int32, (size, chunk), 1) + i * chunk
            seen = key_row <= query_col
        for h in range(heads):
            raw = dot(keys[rows, pair_lanes(h // 2)], query_of[h], NT)
            if masked:
                raw = jnp.where(seen, raw, -1e30)
            probs[h, to] = raw
            top_ref[h] = jnp.maximum(top_ref[h], fold(raw, jnp.max))

    sweep(score)
    top = [jnp.max(top_ref[h], axis=0, keepdims=True) for h in range(heads)]

    def mix(start, held, size, masked):
        rows, to = pl.ds(start, size), pl.ds(held, size)
        for h in range(heads):
            weight = jnp.exp(probs[h, to] - top[h])
            probs[h, to] = weight
            total_ref[h] += fold(weight, jnp.sum)
            mix_ref[head_rows(h)] += dot(values_t[head_rows(h), rows], weight.astype(LOW), NN)

    sweep(mix)
    inverse = [1.0 / jnp.sum(total_ref[h], axis=0, keepdims=True) for h in range(heads)]
    attended = jnp.concatenate(
        [mix_ref[head_rows(h)] * inverse[h] for h in range(heads)], axis=0
    )
    shared = grad.T.astype(WIDE) * attended
    inner = [jnp.sum(shared[head_rows(h)], axis=0, keepdims=True) for h in range(heads)]
    att_stage[slot] = attended.astype(LOW).T
    for copy in row_copies(0, slot):
        copy.start()

    def back(start, held, size, masked):
        rows, to = pl.ds(start, size), pl.ds(held, size)
        for n in range(group):
            value = values[rows, pair_lanes(n)]
            weights, grads = [], []
            for h in (2 * n, 2 * n + 1):
                weight = probs[h, to] * inverse[h]
                weight_grad = dot(value, grad_of[h], NT)
                score_grad = (weight * (weight_grad - inner[h])).astype(LOW)
                weights.append(weight.astype(LOW))
                grads.append(score_grad)
            value_sum[rows, pair_lanes(n)] += dot(
                jnp.concatenate(weights, axis=1), grad_pair[n], NN
            )
            key = keys[rows, pair_lanes(n)]
            back_ref[:, pair_lanes(n)] += dot(
                jnp.concatenate(grads, axis=0),
                jnp.concatenate([one_head(key, h) for h in range(2)], axis=0),
                TN,
            )
            key_sum[rows, pair_lanes(n)] += dot(
                jnp.concatenate(grads, axis=1), query_pair[n], NN
            )

    sweep(back)
    query_grad = turned(back_ref[...] * scale, tab, -1.0)
    query_stage[slot] = query_grad.astype(LOW)

    def column_sums(x):
        return jnp.sum(x.reshape(chunk // 8, 8, lanes), axis=0)

    @pl.when(i == 0)
    def _():
        sums_ref[...] = jnp.zeros(sums_ref.shape, WIDE)

    sums_ref[:, :lanes] += column_sums(query_grad)
    for copy in row_copies(1, slot):
        copy.start()

    @pl.when(i == chunks - 1)
    def _():
        @pl.loop(0, chunks)
        def _(n):
            rows = pl.ds(pl.multiple_of(n * chunk, chunk), chunk)
            key_grad = turned(key_sum[rows], tables(rows), -1.0)
            key_stage[rows] = key_grad.astype(LOW)
            value_stage[rows] = value_sum[rows].astype(LOW)
            sums_ref[:, lanes : 2 * lanes] += column_sums(key_grad)
            sums_ref[:, 2 * lanes :] += column_sums(value_sum[rows])
            for r in range(per):
                for copy in col_copies(n * per + r):
                    copy.start()

        for at in range(2):
            for which in range(2):
                for copy in row_copies(which, at):
                    copy.wait()

        @pl.loop(0, chunks * per)
        def _(n):
            for copy in col_copies(n):
                copy.wait()


def attention(qkv, grad, where, tabs, lanes, which, head_dim):
    rows = grad.shape[0]
    chunk, blk = CHUNK, BLK
    per, chunks, blocks = chunk // blk, rows // chunk, rows // blk
    group = lanes // LANES
    heads = 2 * group
    qkv_blocks = qkv.reshape(blocks, blk, qkv.shape[1])
    grad_blocks = grad.reshape(blocks, blk, grad.shape[1])

    def spec(columns, r):
        return pl.BlockSpec((1, blk, columns), lambda i, at: (at[i * per + r], 0, which))

    in_specs = [spec(3 * lanes, r) for r in range(per)] + [spec(lanes, r) for r in range(per)]
    in_specs += [pl.BlockSpec((rows, LANES), lambda i, at: (0, 0), pipeline_mode=pl.Buffered(1))] * 3
    operands = [qkv_blocks] * per + [grad_blocks] * per + list(tabs)
    kernel = functools.partial(
        attention_kernel,
        chunk=chunk,
        chunks=chunks,
        full_chunks=PROMPT // chunk,
        blk=blk,
        group=group,
        scale=1.0 / math.sqrt(head_dim),
    )
    attended, grads, sums = pl.pallas_call(
        kernel,
        out_shape=(
            jax.ShapeDtypeStruct((blocks, blk, lanes), LOW),
            jax.ShapeDtypeStruct((blocks, blk, 3 * lanes), LOW),
            jax.ShapeDtypeStruct((8, 3 * lanes), WIDE),
        ),
        grid_spec=pltpu.PrefetchScalarGridSpec(
            num_scalar_prefetch=1,
            grid=(chunks,),
            in_specs=in_specs,
            out_specs=[pl.BlockSpec(memory_space=pl.ANY)] * 2
            + [pl.BlockSpec((8, 3 * lanes), lambda i, at: (0, 0))],
            scratch_shapes=[
                pltpu.VMEM((rows, lanes), LOW),
                pltpu.VMEM((rows, lanes), LOW),
                pltpu.VMEM((lanes, rows), LOW),
                pltpu.VMEM((heads, PROMPT + chunk, chunk), WIDE),
                pltpu.VMEM((rows, lanes), WIDE),
                pltpu.VMEM((rows, lanes), WIDE),
                pltpu.VMEM((heads, 8, chunk), WIDE),
                pltpu.VMEM((heads, 8, chunk), WIDE),
                pltpu.VMEM((lanes, chunk), WIDE),
                pltpu.VMEM((chunk, lanes), WIDE),
                pltpu.VMEM((2, chunk, lanes), LOW),
                pltpu.VMEM((2, chunk, lanes), LOW),
                pltpu.VMEM((rows, lanes), LOW),
                pltpu.VMEM((rows, lanes), LOW),
                pltpu.SemaphoreType.DMA((2, 2, per)),
                pltpu.SemaphoreType.DMA((2, blocks)),
            ],
        ),
        compiler_params=pltpu.CompilerParams(
            dimension_semantics=("arbitrary",), vmem_limit_bytes=56 << 20
        ),
        cost_estimate=LITTLE,
        name="attention",
    )(where, *operands)
    return attended.reshape(rows, lanes), grads.reshape(rows, 3 * lanes), jnp.sum(sums, axis=0)


def after(value, *others):
    return lax.optimization_barrier((value,) + others)[0] if others else value


def ring_of(count):
    order = list(range(count // 2)) + list(range(count - 1, count // 2 - 1, -1))
    ahead = [(order[n], order[(n + 1) % count]) for n in range(count)]
    return order, ahead, [(b, a) for a, b in ahead]


def rank_of(offset, count):
    offset %= count
    if offset == 0 or 2 * offset == count:
        return max(2 * offset - 1, 0)
    return 2 * offset if 2 * offset < count else 2 * (count - offset) - 1


def ring_pieces(own, axis, gate=()):
    count = lax.axis_size(axis)
    _, ahead, behind = ring_of(count)
    pieces, half = [own], own.shape[0] // 2
    from_behind = from_ahead = own
    for _ in range(count // 2 - 1):
        from_behind = lax.ppermute(from_behind, axis, ahead)
        from_ahead = lax.ppermute(from_ahead, axis, behind)
        pieces += [from_behind, from_ahead]
    if gate:
        from_behind, from_ahead = after(from_behind, *gate), after(from_ahead, *gate)
        if count > 2:
            pieces[-2:] = [from_behind, from_ahead]
    far = [
        lax.ppermute(from_behind[:half], axis, ahead),
        lax.ppermute(from_ahead[half:], axis, behind),
    ]
    return pieces + far


def ring_reduce(part, axis, cuts=1, chained=False):
    count = lax.axis_size(axis)
    _, ahead, behind = ring_of(count)

    def plus(a, b):
        return (a.astype(WIDE) + b.astype(WIDE)).astype(LOW)

    def cut_rows(term, sizes):
        if isinstance(term, (list, tuple)):
            return term
        ends = [sum(sizes[: n + 1]) for n in range(len(sizes))]
        return [term[end - size : end] for end, size in zip(ends, sizes)]

    far = part(count - 1)
    half = sum(a.shape[0] for a in far) // 2 if isinstance(far, (list, tuple)) else far.shape[0] // 2
    far = cut_rows(far, [half, half])
    up, down = lax.ppermute(far[0], axis, ahead), lax.ppermute(far[1], axis, behind)
    hops = [(up, down)]
    if count == 2:
        return [(0, up), (half, down)], hops
    pieces = [half // cuts] * cuts
    to_ahead = cut_rows(part(count - 2), [half] + pieces)
    to_behind = cut_rows(part(count - 3), pieces + [half])
    got_up, got_down = {}, {}
    got_up[0] = lax.ppermute(plus(to_ahead[0], up), axis, ahead)
    got_down[half] = lax.ppermute(plus(to_behind[-1], down), axis, behind)
    hops.append((got_up[0], got_down[half]))
    for n in range(cuts):
        gate = hops[-1] if chained else ()
        at = n * (half // cuts)
        got_up[half + at] = lax.ppermute(after(to_ahead[1 + n], *gate), axis, ahead)
        got_down[at] = lax.ppermute(after(to_behind[n], *gate), axis, behind)
        hops.append((got_up[half + at], got_down[at]))
    if count == 4:
        return sorted(got_up.items()) + sorted(got_down.items()), hops
    up = jnp.concatenate([piece for _, piece in sorted(got_up.items())], axis=0)
    down = jnp.concatenate([piece for _, piece in sorted(got_down.items())], axis=0)
    for s in range(count // 2 - 2, 0, -1):
        up = lax.ppermute(plus(part(2 * s), up), axis, ahead)
        down = lax.ppermute(plus(part(2 * s - 1), down), axis, behind)
        hops.append((up, down))
    return [(0, up), (0, down)], hops


def ring_exchange(part, axis):
    count = lax.axis_size(axis)
    order, _, _ = ring_of(count)
    got = [None] * count
    got[0] = part(0)
    for offset in range(1, count):
        hops = [(order[n], order[(n + offset) % count]) for n in range(count)]
        got[rank_of(-offset, count)] = lax.ppermute(part(rank_of(offset, count)), axis, hops)
    return got


def exchange_steps(axes):
    steps = []
    for axis in axes:
        count, span = lax.axis_size(axis), 1
        while span < count:
            steps.append((axis, [(n, n ^ span) for n in range(count)]))
            span *= 2
    return steps


def exchange(values, steps):
    for axis, pairs in steps:
        values = values + lax.ppermute(values, axis, pairs)
    return values


def gelu_and_slope(h):
    inner_scale = math.sqrt(2.0 / math.pi)
    square = h * h
    t = jnp.tanh(h * (inner_scale + (inner_scale * 0.044715) * square))
    half = 0.5 * h
    rise = 0.5 + 0.5 * t
    bend = inner_scale + (3.0 * inner_scale * 0.044715) * square
    return (h * rise).astype(LOW), (rise + (half - half * t * t) * bend).astype(LOW)


def join_piece(pieces, spans, whole_ref):
    i = pl.program_id(0)
    for (first, span), piece in zip(spans, pieces):

        @pl.when((i >= first) & (i < first + span))
        def _(piece=piece):
            whole_ref[...] = piece[...]


def piece_blocks(pieces):
    tile, width = pieces[-1].shape
    spans, first = [], 0
    for piece in pieces:
        spans.append((first, piece.shape[0] // tile))
        first += piece.shape[0] // tile

    def spec(first, span):
        return pl.BlockSpec((tile, width), lambda i: (jnp.clip(i - first, 0, span - 1), 0))

    return tile, tuple(spans), [spec(*span) for span in spans]


def expand_kernel(*refs, spans, cols):
    w_ref, b_ref, act_ref, slope_ref, whole_ref = refs[len(spans) :]
    join_piece(refs[: len(spans)], spans, whole_ref)
    x = whole_ref[...]
    for n in range(w_ref.shape[1] // cols):
        at = slice(n * cols, (n + 1) * cols)
        act, slope = gelu_and_slope(dot(x, w_ref[:, at], NN) + b_ref[:, at])
        act_ref[:, at] = act
        slope_ref[:, at] = slope


def expand(pieces, w, b):
    width, hidden = w.shape
    tile, spans, specs = piece_blocks(pieces)
    rows = sum(piece.shape[0] for piece in pieces)
    by_row = pl.BlockSpec((tile, hidden), lambda i: (i, 0))
    out = jax.ShapeDtypeStruct((rows, hidden), LOW)
    return pl.pallas_call(
        functools.partial(expand_kernel, spans=spans, cols=min(512, hidden)),
        out_shape=(out, out, jax.ShapeDtypeStruct((rows, width), LOW)),
        grid=(rows // tile,),
        in_specs=specs
        + [
            pl.BlockSpec((width, hidden), lambda i: (0, 0), pipeline_mode=pl.Buffered(1)),
            pl.BlockSpec((1, hidden), lambda i: (0, 0)),
        ],
        out_specs=[by_row, by_row, pl.BlockSpec((tile, width), lambda i: (i, 0))],
        compiler_params=pltpu.CompilerParams(
            dimension_semantics=("arbitrary",), vmem_limit_bytes=48 << 20
        ),
        cost_estimate=pl.CostEstimate(
            flops=2 * rows * width * hidden,
            bytes_accessed=2 * rows * (2 * width + 2 * hidden),
            transcendentals=rows * hidden,
        ),
        name="expand",
    )(*pieces, w, b[None])


def slope_grad_kernel(*refs, spans, cols):
    pieces = refs[: len(spans)]
    w_ref, slope_ref, out_ref, whole_ref, sums_ref = refs[len(spans) :]
    join_piece(pieces, spans, whole_ref)

    @pl.when(pl.program_id(0) == 0)
    def _():
        sums_ref[...] = jnp.zeros(sums_ref.shape, WIDE)

    x = whole_ref[...]
    for n in range(w_ref.shape[1] // cols):
        at = slice(n * cols, (n + 1) * cols)
        value = dot(x, w_ref[:, at], NN) * slope_ref[:, at].astype(WIDE)
        out_ref[:, at] = value.astype(LOW)
        sums_ref[:, at] += jnp.sum(value.reshape(value.shape[0] // 8, 8, cols), axis=0)


def slope_grad(pieces, w, slope):
    width, hidden = w.shape
    tile, spans, specs = piece_blocks(pieces)
    first = sum(span for _, span in spans)
    by_row = pl.BlockSpec((tile, hidden), lambda i: (i, 0))
    grad, whole, sums = pl.pallas_call(
        functools.partial(slope_grad_kernel, spans=spans, cols=min(512, hidden)),
        out_shape=(
            jax.ShapeDtypeStruct((first * tile, hidden), LOW),
            jax.ShapeDtypeStruct((first * tile, width), LOW),
            jax.ShapeDtypeStruct((8, hidden), WIDE),
        ),
        grid=(first,),
        in_specs=specs
        + [
            pl.BlockSpec((width, hidden), lambda i: (0, 0), pipeline_mode=pl.Buffered(1)),
            by_row,
        ],
        out_specs=[
            by_row,
            pl.BlockSpec((tile, width), lambda i: (i, 0)),
            pl.BlockSpec((8, hidden), lambda i: (0, 0)),
        ],
        compiler_params=pltpu.CompilerParams(
            dimension_semantics=("arbitrary",), vmem_limit_bytes=48 << 20
        ),
        cost_estimate=pl.CostEstimate(
            flops=2 * first * tile * width * hidden,
            bytes_accessed=2 * first * tile * (2 * width + 2 * hidden),
            transcendentals=0,
        ),
        name="slope_grad",
    )(*pieces, w, slope)
    return grad, whole, jnp.sum(sums, axis=0)


def input_grad_kernel(*refs, terms, ranks):
    grads, weights = refs[: terms * ranks], refs[terms * ranks : terms * ranks + terms]
    rest = refs[terms * (ranks + 1) :]
    normed_refs, out_refs, sums_ref = rest[:ranks], list(rest[ranks:-1]), rest[-1]
    plain = weighted = 0.0
    for n in range(ranks):
        mine = grads[n * terms : (n + 1) * terms]
        total = sum(dot(g[...], w[...], NT) for g, w in zip(mine, weights))
        at = 0
        while at < total.shape[0]:
            out_ref = out_refs.pop(0)
            out_ref[...] = total[at : at + out_ref.shape[0]].astype(LOW)
            at += out_ref.shape[0]
        plain += jnp.sum(total, axis=0, keepdims=True)
        weighted += jnp.sum(total * normed_refs[n][...].astype(WIDE), axis=0, keepdims=True)
    sums_ref[0:1] = plain
    sums_ref[1:2] = weighted


def input_grad(grads, weights, normed, ranks, rows, cuts, cost):
    width = normed.shape[1]
    cols = 512
    keep = pl.Buffered(1)
    in_specs = [
        pl.BlockSpec((rows, g.shape[1]), lambda i, rank=rank: (rank, 0), pipeline_mode=keep)
        for rank in ranks
        for g in grads
    ]
    in_specs += [
        pl.BlockSpec((cols, g.shape[1]), lambda i, at=at: (i, at))
        for g, (_, at) in zip(grads, weights)
    ]
    in_specs += [pl.BlockSpec((rows, cols), lambda i, rank=rank: (rank, i)) for rank in ranks]
    sizes = [size for cut in cuts for size in cut]
    *parts, sums = pl.pallas_call(
        functools.partial(input_grad_kernel, terms=len(grads), ranks=len(ranks)),
        out_shape=[jax.ShapeDtypeStruct((size, width), LOW) for size in sizes]
        + [jax.ShapeDtypeStruct((2, width), WIDE)],
        grid=(width // cols,),
        in_specs=in_specs,
        out_specs=[pl.BlockSpec((size, cols), lambda i: (0, i)) for size in sizes]
        + [pl.BlockSpec((2, cols), lambda i: (0, i))],
        compiler_params=pltpu.CompilerParams(
            dimension_semantics=("arbitrary",), vmem_limit_bytes=58 << 20
        ),
        cost_estimate=cost,
        name="input_grad",
    )(*grads * len(ranks), *[w for w, _ in weights], *[normed] * len(ranks))
    return [[parts.pop(0) for _ in cut] for cut in cuts], sums


def place_kernel(*refs, starts, count, groups):
    pieces = refs[: count * groups]
    dense = refs[count * groups : count * groups + count + 1]
    rest = refs[count * (groups + 1) + 1 :]
    token_ref, bias_ref, own_ref = rest[:3]
    terms, out_ref, acc = rest[3:-2], rest[-2], rest[-1]
    acc[...] = token_ref[...].astype(WIDE) + bias_ref[...] + own_ref[...].astype(WIDE)
    for start, term in zip(starts, terms):
        acc[start : start + term.shape[0]] += term[...].astype(WIDE)
    steps = pl.num_programs(0)
    low_half = pl.program_id(0) * 2 < steps
    far = jnp.where(low_half, dense[count - 1][...], dense[count][...])
    total = acc[...]
    for rank in range(count):
        weight = dense[rank][...] if rank < count - 1 else far
        mine = [piece[...] for piece in pieces[rank * groups : (rank + 1) * groups]]
        total += dot(jnp.concatenate(mine, axis=1), weight, NT)
    out_ref[...] = total.astype(LOW)


def place_output(pieces, dense_pieces, tokens, bias, own, terms, count, groups):
    rows, width = tokens.shape
    cols = 512
    half = width // cols // 2
    whole = lambda a: pl.BlockSpec(a.shape, lambda i: (0, 0), pipeline_mode=pl.Buffered(1))
    in_specs = [whole(piece) for piece in pieces]
    depth = dense_pieces[0].shape[1]
    in_specs += [pl.BlockSpec((cols, depth), lambda i: (i, 0)) for _ in range(count - 1)]
    in_specs.append(pl.BlockSpec((cols, depth), lambda i: (jnp.minimum(i, half - 1), 0)))
    in_specs.append(pl.BlockSpec((cols, depth), lambda i: (jnp.maximum(i - half, 0), 0)))
    by_column = lambda n: pl.BlockSpec((n, cols), lambda i: (0, i))
    in_specs += [by_column(rows), by_column(1), by_column(rows)]
    in_specs += [by_column(term.shape[0]) for _, term in terms]
    return pl.pallas_call(
        functools.partial(
            place_kernel, starts=tuple(start for start, _ in terms), count=count, groups=groups
        ),
        out_shape=jax.ShapeDtypeStruct((rows, width), LOW),
        grid=(width // cols,),
        in_specs=in_specs,
        out_specs=by_column(rows),
        scratch_shapes=[pltpu.VMEM((rows, cols), WIDE)],
        compiler_params=pltpu.CompilerParams(
            dimension_semantics=("arbitrary",), vmem_limit_bytes=58 << 20
        ),
        cost_estimate=LITTLE,
        name="place_output",
    )(*pieces, *dense_pieces, tokens, bias, own, *[term for _, term in terms])


def token_grad_kernel(token_ref, grad_ref, own_ref, gain_ref, *refs, starts, tile):
    terms, out_ref, total = refs[:-2], refs[-2], refs[-1]
    first = pl.program_id(0) * tile
    total[...] = own_ref[...].astype(WIDE)
    for start, term in zip(starts, terms):
        size = min(tile, term.shape[0])
        for at in range(0, term.shape[0], size):

            @pl.when(first == (start + at) // tile * tile)
            def _(start=start, term=term, at=at, size=size):
                to = (start + at) % tile
                total[to : to + size] += term[at : at + size].astype(WIDE)

    x = token_ref[...].astype(WIDE)
    centred = x - jnp.mean(x, axis=-1, keepdims=True)
    rstd = lax.rsqrt(jnp.mean(centred * centred, axis=-1, keepdims=True) + 1e-05)
    xhat = centred * rstd
    scaled = total[...] * gain_ref[...]
    mean = jnp.mean(scaled, axis=-1, keepdims=True)
    along = jnp.mean(scaled * xhat, axis=-1, keepdims=True)
    out_ref[...] = (grad_ref[...].astype(WIDE) + rstd * (scaled - mean - xhat * along)).astype(LOW)


def token_grad(tokens, grad, own, gain, terms, tile):
    rows, width = tokens.shape
    by_row = pl.BlockSpec((tile, width), lambda i: (i, 0))
    whole = lambda a: pl.BlockSpec(a.shape, lambda i: (0, 0), pipeline_mode=pl.Buffered(1))
    return pl.pallas_call(
        functools.partial(
            token_grad_kernel, starts=tuple(start for start, _ in terms), tile=tile
        ),
        out_shape=jax.ShapeDtypeStruct((rows, width), LOW),
        grid=(rows // tile,),
        in_specs=[by_row, by_row, by_row, pl.BlockSpec((1, width), lambda i: (0, 0))]
        + [whole(term) for _, term in terms],
        out_specs=by_row,
        scratch_shapes=[pltpu.VMEM((tile, width), WIDE)],
        compiler_params=pltpu.CompilerParams(
            dimension_semantics=("arbitrary",), vmem_limit_bytes=48 << 20
        ),
        cost_estimate=LITTLE,
        name="token_grad",
    )(tokens, grad, own, gain[None], *[term for _, term in terms])


def pair_grad_kernel(x_ref, y_ref, a_ref, b_ref, out_ref):
    split = a_ref.shape[1]
    out_ref[:, :split] = dot(x_ref[...], a_ref[...], TN).astype(LOW)
    out_ref[:, split:] = dot(y_ref[...], b_ref[...], TN).astype(LOW)


def pair_grad(x, y, a, b):
    rows, width = x.shape
    columns = a.shape[1] + b.shape[1]
    tile = 512
    keep = pl.Buffered(1)
    return pl.pallas_call(
        pair_grad_kernel,
        out_shape=jax.ShapeDtypeStruct((width, columns), LOW),
        grid=(width // tile,),
        in_specs=[
            pl.BlockSpec((rows, tile), lambda i: (0, i)),
            pl.BlockSpec((rows, tile), lambda i: (0, i)),
            pl.BlockSpec(a.shape, lambda i: (0, 0), pipeline_mode=keep),
            pl.BlockSpec(b.shape, lambda i: (0, 0), pipeline_mode=keep),
        ],
        out_specs=pl.BlockSpec((tile, columns), lambda i: (i, 0)),
        compiler_params=pltpu.CompilerParams(
            dimension_semantics=("arbitrary",), vmem_limit_bytes=58 << 20
        ),
        cost_estimate=LITTLE,
        name="pair_grad",
    )(x, y, a, b)


def rope_tables(rows):
    place = lax.broadcasted_iota(jnp.int32, (rows, LANES), 0)
    lane = lax.broadcasted_iota(jnp.int32, (rows, LANES), 1)
    pos = jnp.where(place < PROMPT, place, PROMPT + (place - PROMPT) % CLEN)
    half = ROT // 2
    freq = 10000.0 ** (-2.0 * jnp.arange(half, dtype=WIDE) / ROT)
    angle = pos.astype(WIDE) * jnp.tile(freq, LANES // half)[None, :]
    dim = lane % (LANES // 2)
    cosine, sine = jnp.cos(angle), jnp.sin(angle)
    return [
        jnp.where(dim < ROT, cosine, 1.0),
        jnp.where((dim >= half) & (dim < ROT), sine, 0.0),
        jnp.where(dim < half, -sine, 0.0),
    ]


def shards(
    tokens,
    cotangent,
    block_table,
    ln_gain,
    ln_bias,
    w_qkv,
    b_qkv,
    w_dense,
    b_dense,
    w_fc1,
    b_fc1,
    w_fc2,
    b_fc2,
):
    _, local_rows, width = tokens.shape
    head_dim = width // HEADS
    count = lax.axis_size("ctx")
    me = lax.axis_index("ctx")
    rows = local_rows * count
    local_blocks = local_rows // BLK
    each = w_dense.shape[0]
    hidden = w_fc2.shape[0]
    gain, shift = ln_gain.astype(WIDE), ln_bias.astype(WIDE)

    def of_rank(whole, rank):
        return whole[rank * local_rows : (rank + 1) * local_rows]

    order, _, _ = ring_of(count)
    places = [0] * count
    for n, device in enumerate(order):
        places[device] = n
    places = jnp.asarray(places, jnp.int32)
    ranks = jnp.asarray([rank_of(n, count) for n in range(count)], jnp.int32)
    slots = jnp.arange(rows // BLK, dtype=jnp.int32)
    offset = (places[slots // local_blocks] - places[me]) % count
    held_at = ranks[offset] * local_blocks + slots % local_blocks
    hit = block_table[0][None, :] == slots[:, None]
    where = jnp.sum(jnp.where(hit, held_at[None, :], 0), axis=1).astype(jnp.int32)

    own_tokens = tokens[0].astype(WIDE)
    own_grad = cotangent[0]
    average = jnp.mean(own_tokens, axis=-1, keepdims=True)
    centred = own_tokens - average
    rstd = lax.rsqrt(jnp.mean(centred * centred, axis=-1, keepdims=True) + 1e-05)
    xhat = centred * rstd
    normed_own = (xhat * gain + shift).astype(LOW)

    def gather_rows(shard):
        return lax.all_gather(shard, "fsdp", axis=0, tiled=True)

    def scatter_rows(whole):
        return lax.psum_scatter(whole, "fsdp", scatter_dimension=0, tiled=True)

    lanes = 2 * LANES if each % (2 * LANES) == 0 else LANES
    groups = each // lanes

    def by_group(values):
        cut = values.reshape(-1, 3, groups, lanes)
        return jnp.swapaxes(cut, 1, 2).reshape(-1, 3 * each)

    tabs = rope_tables(rows)
    own_grad_sum = jnp.sum(own_grad.astype(WIDE), axis=0)
    fc1_bias = lax.dynamic_slice_in_dim(b_fc1, me * hidden, hidden, 0).astype(WIDE)
    early = (where, own_grad_sum, fc1_bias, *tabs)
    normed_pieces = ring_pieces(normed_own, "ctx", gate=early)
    attention_shard = jnp.concatenate([by_group(w_qkv), w_dense.T], axis=1)
    fc1_weight = gather_rows(w_fc1)
    fc2_turned = gather_rows(after(w_fc2.T, *normed_pieces[1:-2]))
    attention_weight = gather_rows(after(attention_shard, *normed_pieces[-2:]))
    qkv_weight, dense_turned = attention_weight[:, : 3 * each], attention_weight[:, 3 * each :]

    qkv_bias = lax.dynamic_slice_in_dim(b_qkv.reshape(3, width), me * each, each, 1)
    activated, slope, normed = expand(normed_pieces, fc1_weight, fc1_bias)

    sent_grad = after(own_grad, *normed_pieces[-2:])
    grad_pieces = ring_pieces(sent_grad, "ctx", gate=(activated,))
    ff_part = dot(activated, fc2_turned, NT).astype(LOW)
    ff_terms, ff_hops = ring_reduce(lambda rank: of_rank(ff_part, rank), "ctx", chained=True)
    first, second, last = ff_hops[0], ff_hops[min(1, len(ff_hops) - 1)], ff_hops[-1]

    gated = [after(piece, ff_part) for piece in grad_pieces]
    expanded_grad, grads, fc1_bias_part = slope_grad(gated, fc2_turned, slope)
    d_fc2_part = dot(after(grads, expanded_grad, *first), activated, TN).astype(LOW)
    d_fc2 = scatter_rows(d_fc2_part)
    qkv = dot(after(normed, d_fc2_part), qkv_weight, NN)
    qkv = (qkv + by_group(qkv_bias)[0].astype(WIDE)).astype(LOW)
    attended_grad = dot(after(grads, qkv, *second), dense_turned, NN).astype(LOW)
    gated = after(normed, attended_grad)
    d_fc1_part = dot(gated, expanded_grad, TN).astype(LOW)
    d_fc1 = scatter_rows(d_fc1_part)


    attended, qkv_grads, qkv_sums, d_attention, swapped = [], [], [], [], []
    ordered = (d_fc1_part,)
    for which in range(groups):
        got, got_grads, got_sums = attention(
            after(qkv, *ordered), attended_grad, where, tabs, lanes, which, head_dim
        )
        if which == 0:
            dense_pieces = ring_pieces(after(dense_turned, *second), "ctx", gate=(got,))
        attended.append(got)
        qkv_grads.append(got_grads)
        qkv_sums.append(got_sums)
        if which < groups - 1:
            swapped.append(ring_exchange(lambda rank, got=got: of_rank(got, rank), "ctx"))
            gated = after(normed, d_fc2, *last, *dense_pieces[1:-2]) if which == 0 else normed
            d_part = pair_grad(gated, grads, got_grads, got)
            ordered = (d_part,)
            d_attention.append(scatter_rows(d_part))

    weights = [(attention_weight, which) for which in range(groups)] + [(fc1_weight, 0)]
    early_swaps = [piece for pieces in swapped for piece in pieces]
    turn = after(expanded_grad, d_fc1, *dense_pieces[-2:], *early_swaps, *attended)
    swapped.append(ring_exchange(lambda rank: of_rank(attended[-1], rank), "ctx"))
    half = local_rows // 2
    whole, far_cut, ahead_cut, behind_cut = [local_rows], [half, half], [half], [half]
    if count > 2:
        ahead_cut, behind_cut = [half, half], [half, half]
    cut_of = {0: whole, count - 2: ahead_cut, count - 3: behind_cut, count - 1: far_cut}

    def some_ranks(ranks, turn, cost=LITTLE):
        cuts = [cut_of.get(rank, whole) for rank in ranks]
        return input_grad(qkv_grads + [turn], weights, normed, ranks, local_rows, cuts, cost)

    far_part, far_sums = some_ranks([count - 1], turn)
    middle = list(range(count - 2, 0, -1))
    middle_sums, parts = 0.0, {count - 1: far_part[0]}
    turn = after(turn, *far_part[0], *swapped[-1])
    for n in range(0, len(middle), 2):
        some, some_sums = some_ranks(middle[n : n + 2], turn, MUCH)
        turn = after(turn, *[piece for pieces in some for piece in pieces])
        middle_sums = middle_sums + some_sums
        parts.update(zip(middle[n : n + 2], some))
    for rank, pieces in parts.items():
        if len(pieces) == 1:
            parts[rank] = pieces[0]

    grad_terms, hops = ring_reduce(lambda rank: parts[rank], "ctx")
    last_hops = [piece for hop in hops[1:3] for piece in hop]
    gated = after(normed, turn, *hops[0], *d_attention)
    d_part = pair_grad(gated, grads, qkv_grads[-1], attended[-1])
    d_attention.append(scatter_rows(d_part))
    [own_part], own_sums = some_ranks([0], after(turn, d_part), MUCH)
    d_qkv = jnp.concatenate(
        [part[:, : 3 * lanes].reshape(-1, 3, lanes) for part in d_attention], axis=2
    ).astype(WIDE)
    d_dense = jnp.concatenate([part[:, 3 * lanes :].T for part in d_attention], axis=0)
    d_dense = d_dense.astype(WIDE)

    qkv_bias_part = jnp.concatenate(
        [part.reshape(3, lanes) for part in qkv_sums], axis=1
    )
    qkv_bias_wide = lax.dynamic_update_slice_in_dim(
        jnp.zeros((3, width), WIDE), qkv_bias_part, me * each, 1
    ).reshape(-1)
    fc1_bias_wide = lax.dynamic_update_slice_in_dim(
        jnp.zeros((b_fc1.shape[0],), WIDE), fc1_bias_part, me * hidden, 0
    )
    small = jnp.concatenate(
        [
            (far_sums + middle_sums + own_sums).reshape(-1),
            qkv_bias_wide,
            own_grad_sum,
            fc1_bias_wide,
        ]
    )
    near, across = exchange_steps(("fsdp",)), exchange_steps(("ctx",))
    steps = near[:1] + across + near[1:]
    small = exchange(small, steps[:1])
    d_fc1, d_fc2 = d_fc1.astype(WIDE), d_fc2.T.astype(WIDE)
    output = place_output(
        [swapped[which][rank] for rank in range(count) for which in range(groups)],
        dense_pieces,
        after(tokens[0], *own_part),
        (b_dense.astype(WIDE) + b_fc2.astype(WIDE))[None],
        ff_part,
        ff_terms,
        count,
        groups,
    )
    small = exchange(after(small, output, *last_hops), steps[1:2])
    d_tokens = token_grad(
        after(tokens[0], output), own_grad, own_part[0], gain, grad_terms, local_rows // 4
    )
    small = exchange(after(small, d_tokens), steps[2:-1])
    small = after(small, d_fc1, d_fc2)
    axis, pairs = steps[-1]
    small = after(small, d_qkv, d_dense) + lax.ppermute(small, axis, pairs)
    d_shift, with_normed, d_b_qkv, d_b_out, d_b_fc1 = jnp.split(
        small, [width, 2 * width, 5 * width, 6 * width]
    )
    d_gain = (with_normed - shift * d_shift) / gain
    return (
        output[None],
        d_tokens[None],
        d_gain,
        d_shift,
        d_qkv,
        d_b_qkv,
        d_dense,
        d_b_out,
        d_fc1,
        d_b_fc1,
        d_fc2,
        d_b_out,
    )


def solution(mesh):
    in_specs = (
        P("fsdp", "ctx", None),
        P("fsdp", "ctx", None),
        P("fsdp", None),
        P(),
        P(),
        P("fsdp", None, "ctx"),
        P(),
        P("ctx", "fsdp"),
        P(),
        P("fsdp", "ctx"),
        P(),
        P("ctx", "fsdp"),
        P(),
    )
    out_specs = (
        P("fsdp", "ctx", None),
        P("fsdp", "ctx", None),
        P(),
        P(),
        P("fsdp", None, "ctx"),
        P(),
        P("ctx", "fsdp"),
        P(),
        P("fsdp", "ctx"),
        P(),
        P("ctx", "fsdp"),
        P(),
    )
    return jax.shard_map(shards, mesh=mesh, in_specs=in_specs, out_specs=out_specs, check_vma=False)
```

```python
import functools
import math

import jax
import jax.numpy as jnp
from jax import lax
from jax.experimental import pallas as pl
from jax.experimental.pallas import tpu as pltpu
from jax.sharding import PartitionSpec as P

HEADS = 32
ROT = 32
PROMPT = 2048
CLEN = 256
BLK = 64
CHUNK = 256
LANES = 128
NT = (((1,), (1,)), ((), ()))
NN = (((1,), (0,)), ((), ()))
TN = (((0,), (0,)), ((), ()))
LOW = jnp.bfloat16
WIDE = jnp.float32
LITTLE = pl.CostEstimate(flops=1000000, bytes_accessed=1000000, transcendentals=0)
MUCH = pl.CostEstimate(flops=100000000000, bytes_accessed=1000000, transcendentals=0)


def dot(left, right, dims):
    return lax.dot_general(left, right, dims, preferred_element_type=WIDE)


def attention_kernel(where_ref, *refs, chunk, chunks, full_chunks, blk, group, scale):
    per = chunk // blk
    qkv_in, g_in = refs[:per], refs[per : 2 * per]
    cos_ref, up_ref, down_ref, att_hbm, grad_hbm, sums_ref = refs[2 * per : 2 * per + 6]
    (
        keys,
        values,
        values_t,
        probs,
        key_sum,
        value_sum,
        top_ref,
        total_ref,
        mix_ref,
        back_ref,
        att_stage,
        query_stage,
        key_stage,
        value_stage,
        row_sem,
        col_sem,
    ) = refs[2 * per + 6 :]
    i = pl.program_id(0)
    slot = lax.rem(i, 2)
    half = LANES // 2
    lanes = group * LANES
    heads = 2 * group
    first = lax.broadcasted_iota(jnp.int32, (1, LANES), 1) < half

    def columns(part):
        return pl.ds(part * lanes, lanes)

    def row_copies(which, at):
        stage, target = ((att_stage, att_hbm), (query_stage, grad_hbm))[which]
        return [
            pltpu.make_async_copy(
                stage.at[at, pl.ds(r * blk, blk)],
                target.at[where_ref[i * per + r], :, columns(0)],
                row_sem.at[at, which, r],
            )
            for r in range(per)
        ]

    def col_copies(n):
        block = where_ref[n]
        rows = pl.ds(pl.multiple_of(n * blk, blk), blk)
        return (
            pltpu.make_async_copy(
                key_stage.at[rows], grad_hbm.at[block, :, columns(1)], col_sem.at[0, n]
            ),
            pltpu.make_async_copy(
                value_stage.at[rows], grad_hbm.at[block, :, columns(2)], col_sem.at[1, n]
            ),
        )

    def load(parts):
        return jnp.concatenate([part[0] for part in parts], axis=0)

    def tables(rows):
        return cos_ref[rows], up_ref[rows], down_ref[rows]

    quarter = ROT // 2

    def turned(x, tab, sign):
        return jnp.concatenate(
            [
                y * tab[0]
                + sign
                * (pltpu.roll(y, quarter, 1) * tab[1] + pltpu.roll(y, LANES - quarter, 1) * tab[2])
                for y in (x[:, n * LANES : (n + 1) * LANES] for n in range(group))
            ],
            axis=1,
        )

    def one_head(x, h):
        pair = x[:, (h // 2) * LANES : (h // 2 + 1) * LANES]
        nothing = jnp.zeros_like(pair)
        return jnp.where(first, pair, nothing) if h % 2 == 0 else jnp.where(first, nothing, pair)

    @pl.when(i >= 2)
    def _():
        for which in range(2):
            for copy in row_copies(which, slot):
                copy.wait()

    here = pl.ds(pl.multiple_of(i * chunk, chunk), chunk)
    tab = tables(here)
    qkv = load(qkv_in)
    query = (turned(qkv[:, :lanes].astype(WIDE), tab, 1.0) * scale).astype(LOW)
    key_new = turned(qkv[:, lanes : 2 * lanes].astype(WIDE), tab, 1.0)
    value_new = qkv[:, 2 * lanes :]
    grad = load(g_in)
    keys[here] = key_new.astype(LOW)
    values[here] = value_new
    values_t[:, here] = value_new.T
    key_sum[here] = jnp.zeros((chunk, lanes), WIDE)
    value_sum[here] = jnp.zeros((chunk, lanes), WIDE)
    top_ref[...] = jnp.full(top_ref.shape, -1e30, WIDE)
    total_ref[...] = jnp.zeros(total_ref.shape, WIDE)
    mix_ref[...] = jnp.zeros(mix_ref.shape, WIDE)
    back_ref[...] = jnp.zeros(back_ref.shape, WIDE)
    query_of = [one_head(query, h) for h in range(heads)]
    grad_of = [one_head(grad, h) for h in range(heads)]
    query_pair = [
        jnp.concatenate(query_of[2 * n : 2 * n + 2], axis=0) for n in range(group)
    ]
    grad_pair = [jnp.concatenate(grad_of[2 * n : 2 * n + 2], axis=0) for n in range(group)]
    before = jnp.minimum(i, full_chunks)
    doubles = before // 2
    odd = before - 2 * doubles

    def fold(x, how):
        return how(x.reshape(x.shape[0] // 8, 8, chunk), axis=0)

    def pair_lanes(n):
        return slice(n * LANES, (n + 1) * LANES)

    def head_rows(h):
        return slice(h * half, (h + 1) * half)

    def sweep(tile):
        def quad(t, carry):
            start = pl.multiple_of(t * 4 * chunk, 4 * chunk)
            tile(start, start, 4 * chunk, False)
            return carry

        lax.fori_loop(0, doubles // 2, quad, 0)

        @pl.when(doubles % 2 == 1)
        def _():
            start = pl.multiple_of((doubles - 1) * 2 * chunk, 2 * chunk)
            tile(start, start, 2 * chunk, False)

        held = pl.multiple_of(doubles * 2 * chunk, chunk)

        @pl.when(odd == 1)
        def _():
            tile(held, held, 2 * chunk, True)

        @pl.when(odd == 0)
        def _():
            tile(pl.multiple_of(i * chunk, chunk), held, chunk, True)

    def score(start, held, size, masked):
        rows, to = pl.ds(start, size), pl.ds(held, size)
        if masked:
            key_row = lax.broadcasted_iota(jnp.int32, (size, chunk), 0) + start
            query_col = lax.broadcasted_iota(jnp.int32, (size, chunk), 1) + i * chunk
            seen = key_row <= query_col
        for h in range(heads):
            raw = dot(keys[rows, pair_lanes(h // 2)], query_of[h], NT)
            if masked:
                raw = jnp.where(seen, raw, -1e30)
            probs[h, to] = raw
            top_ref[h] = jnp.maximum(top_ref[h], fold(raw, jnp.max))

    sweep(score)
    top = [jnp.max(top_ref[h], axis=0, keepdims=True) for h in range(heads)]

    def mix(start, held, size, masked):
        rows, to = pl.ds(start, size), pl.ds(held, size)
        for h in range(heads):
            weight = jnp.exp(probs[h, to] - top[h])
            probs[h, to] = weight
            total_ref[h] += fold(weight, jnp.sum)
            mix_ref[head_rows(h)] += dot(values_t[head_rows(h), rows], weight.astype(LOW), NN)

    sweep(mix)
    inverse = [1.0 / jnp.sum(total_ref[h], axis=0, keepdims=True) for h in range(heads)]
    attended = jnp.concatenate(
        [mix_ref[head_rows(h)] * inverse[h] for h in range(heads)], axis=0
    )
    shared = grad.T.astype(WIDE) * attended
    inner = [jnp.sum(shared[head_rows(h)], axis=0, keepdims=True) for h in range(heads)]
    att_stage[slot] = attended.astype(LOW).T
    for copy in row_copies(0, slot):
        copy.start()

    def back(start, held, size, masked):
        rows, to = pl.ds(start, size), pl.ds(held, size)
        for n in range(group):
            value = values[rows, pair_lanes(n)]
            weights, grads = [], []
            for h in (2 * n, 2 * n + 1):
                weight = probs[h, to] * inverse[h]
                weight_grad = dot(value, grad_of[h], NT)
                score_grad = (weight * (weight_grad - inner[h])).astype(LOW)
                weights.append(weight.astype(LOW))
                grads.append(score_grad)
            value_sum[rows, pair_lanes(n)] += dot(
                jnp.concatenate(weights, axis=1), grad_pair[n], NN
            )
            key = keys[rows, pair_lanes(n)]
            back_ref[:, pair_lanes(n)] += dot(
                jnp.concatenate(grads, axis=0),
                jnp.concatenate([one_head(key, h) for h in range(2)], axis=0),
                TN,
            )
            key_sum[rows, pair_lanes(n)] += dot(
                jnp.concatenate(grads, axis=1), query_pair[n], NN
            )

    sweep(back)
    query_grad = turned(back_ref[...] * scale, tab, -1.0)
    query_stage[slot] = query_grad.astype(LOW)

    def column_sums(x):
        return jnp.sum(x.reshape(chunk // 8, 8, lanes), axis=0)

    @pl.when(i == 0)
    def _():
        sums_ref[...] = jnp.zeros(sums_ref.shape, WIDE)

    sums_ref[:, :lanes] += column_sums(query_grad)
    for copy in row_copies(1, slot):
        copy.start()

    @pl.when(i == chunks - 1)
    def _():
        @pl.loop(0, chunks)
        def _(n):
            rows = pl.ds(pl.multiple_of(n * chunk, chunk), chunk)
            key_grad = turned(key_sum[rows], tables(rows), -1.0)
            key_stage[rows] = key_grad.astype(LOW)
            value_stage[rows] = value_sum[rows].astype(LOW)
            sums_ref[:, lanes : 2 * lanes] += column_sums(key_grad)
            sums_ref[:, 2 * lanes :] += column_sums(value_sum[rows])
            for r in range(per):
                for copy in col_copies(n * per + r):
                    copy.start()

        for at in range(2):
            for which in range(2):
                for copy in row_copies(which, at):
                    copy.wait()

        @pl.loop(0, chunks * per)
        def _(n):
            for copy in col_copies(n):
                copy.wait()


def attention(qkv, grad, where, tabs, lanes, which, head_dim):
    rows = grad.shape[0]
    chunk, blk = CHUNK, BLK
    per, chunks, blocks = chunk // blk, rows // chunk, rows // blk
    group = lanes // LANES
    heads = 2 * group
    qkv_blocks = qkv.reshape(blocks, blk, qkv.shape[1])
    grad_blocks = grad.reshape(blocks, blk, grad.shape[1])

    def spec(columns, r):
        return pl.BlockSpec((1, blk, columns), lambda i, at: (at[i * per + r], 0, which))

    in_specs = [spec(3 * lanes, r) for r in range(per)] + [spec(lanes, r) for r in range(per)]
    in_specs += [pl.BlockSpec((rows, LANES), lambda i, at: (0, 0), pipeline_mode=pl.Buffered(1))] * 3
    operands = [qkv_blocks] * per + [grad_blocks] * per + list(tabs)
    kernel = functools.partial(
        attention_kernel,
        chunk=chunk,
        chunks=chunks,
        full_chunks=PROMPT // chunk,
        blk=blk,
        group=group,
        scale=1.0 / math.sqrt(head_dim),
    )
    attended, grads, sums = pl.pallas_call(
        kernel,
        out_shape=(
            jax.ShapeDtypeStruct((blocks, blk, lanes), LOW),
            jax.ShapeDtypeStruct((blocks, blk, 3 * lanes), LOW),
            jax.ShapeDtypeStruct((8, 3 * lanes), WIDE),
        ),
        grid_spec=pltpu.PrefetchScalarGridSpec(
            num_scalar_prefetch=1,
            grid=(chunks,),
            in_specs=in_specs,
            out_specs=[pl.BlockSpec(memory_space=pl.ANY)] * 2
            + [pl.BlockSpec((8, 3 * lanes), lambda i, at: (0, 0))],
            scratch_shapes=[
                pltpu.VMEM((rows, lanes), LOW),
                pltpu.VMEM((rows, lanes), LOW),
                pltpu.VMEM((lanes, rows), LOW),
                pltpu.VMEM((heads, PROMPT + chunk, chunk), WIDE),
                pltpu.VMEM((rows, lanes), WIDE),
                pltpu.VMEM((rows, lanes), WIDE),
                pltpu.VMEM((heads, 8, chunk), WIDE),
                pltpu.VMEM((heads, 8, chunk), WIDE),
                pltpu.VMEM((lanes, chunk), WIDE),
                pltpu.VMEM((chunk, lanes), WIDE),
                pltpu.VMEM((2, chunk, lanes), LOW),
                pltpu.VMEM((2, chunk, lanes), LOW),
                pltpu.VMEM((rows, lanes), LOW),
                pltpu.VMEM((rows, lanes), LOW),
                pltpu.SemaphoreType.DMA((2, 2, per)),
                pltpu.SemaphoreType.DMA((2, blocks)),
            ],
        ),
        compiler_params=pltpu.CompilerParams(
            dimension_semantics=("arbitrary",), vmem_limit_bytes=56 << 20
        ),
        cost_estimate=LITTLE,
        name="attention",
    )(where, *operands)
    return attended.reshape(rows, lanes), grads.reshape(rows, 3 * lanes), jnp.sum(sums, axis=0)


def after(value, *others):
    return lax.optimization_barrier((value,) + others)[0] if others else value


def ring_of(count):
    order = list(range(count // 2)) + list(range(count - 1, count // 2 - 1, -1))
    ahead = [(order[n], order[(n + 1) % count]) for n in range(count)]
    return order, ahead, [(b, a) for a, b in ahead]


def rank_of(offset, count):
    offset %= count
    if offset == 0 or 2 * offset == count:
        return max(2 * offset - 1, 0)
    return 2 * offset if 2 * offset < count else 2 * (count - offset) - 1


def ring_pieces(own, axis, gate=()):
    count = lax.axis_size(axis)
    _, ahead, behind = ring_of(count)
    pieces, half = [own], own.shape[0] // 2
    from_behind = from_ahead = own
    for _ in range(count // 2 - 1):
        from_behind = lax.ppermute(from_behind, axis, ahead)
        from_ahead = lax.ppermute(from_ahead, axis, behind)
        pieces += [from_behind, from_ahead]
    if gate:
        from_behind, from_ahead = after(from_behind, *gate), after(from_ahead, *gate)
        if count > 2:
            pieces[-2:] = [from_behind, from_ahead]
    far = [
        lax.ppermute(from_behind[:half], axis, ahead),
        lax.ppermute(from_ahead[half:], axis, behind),
    ]
    return pieces + far


def ring_reduce(part, axis, cuts=1, chained=False):
    count = lax.axis_size(axis)
    _, ahead, behind = ring_of(count)

    def plus(a, b):
        return (a.astype(WIDE) + b.astype(WIDE)).astype(LOW)

    def cut_rows(term, sizes):
        if isinstance(term, (list, tuple)):
            return term
        ends = [sum(sizes[: n + 1]) for n in range(len(sizes))]
        return [term[end - size : end] for end, size in zip(ends, sizes)]

    far = part(count - 1)
    half = sum(a.shape[0] for a in far) // 2 if isinstance(far, (list, tuple)) else far.shape[0] // 2
    far = cut_rows(far, [half, half])
    up, down = lax.ppermute(far[0], axis, ahead), lax.ppermute(far[1], axis, behind)
    hops = [(up, down)]
    if count == 2:
        return [(0, up), (half, down)], hops
    pieces = [half // cuts] * cuts
    to_ahead = cut_rows(part(count - 2), [half] + pieces)
    to_behind = cut_rows(part(count - 3), pieces + [half])
    got_up, got_down = {}, {}
    got_up[0] = lax.ppermute(plus(to_ahead[0], up), axis, ahead)
    got_down[half] = lax.ppermute(plus(to_behind[-1], down), axis, behind)
    hops.append((got_up[0], got_down[half]))
    for n in range(cuts):
        gate = hops[-1] if chained else ()
        at = n * (half // cuts)
        got_up[half + at] = lax.ppermute(after(to_ahead[1 + n], *gate), axis, ahead)
        got_down[at] = lax.ppermute(after(to_behind[n], *gate), axis, behind)
        hops.append((got_up[half + at], got_down[at]))
    if count == 4:
        return sorted(got_up.items()) + sorted(got_down.items()), hops
    up = jnp.concatenate([piece for _, piece in sorted(got_up.items())], axis=0)
    down = jnp.concatenate([piece for _, piece in sorted(got_down.items())], axis=0)
    for s in range(count // 2 - 2, 0, -1):
        up = lax.ppermute(plus(part(2 * s), up), axis, ahead)
        down = lax.ppermute(plus(part(2 * s - 1), down), axis, behind)
        hops.append((up, down))
    return [(0, up), (0, down)], hops


def ring_exchange(part, axis):
    count = lax.axis_size(axis)
    order, _, _ = ring_of(count)
    got = [None] * count
    got[0] = part(0)
    for offset in range(1, count):
        hops = [(order[n], order[(n + offset) % count]) for n in range(count)]
        got[rank_of(-offset, count)] = lax.ppermute(part(rank_of(offset, count)), axis, hops)
    return got


def exchange_steps(axis, spans):
    steps, count = [], lax.axis_size(axis)
    spans = [span for span in spans if span < count]
    while spans:
        step, spans = spans[:2], spans[2:]
        steps.append((axis, step + [step[0] + step[1]] if len(step) == 2 else step))
    return steps


def exchange(values, step, gate=()):
    axis, flips = step
    count = lax.axis_size(axis)
    got = [lax.ppermute(values, axis, [(n, n ^ flip) for n in range(count)]) for flip in flips]
    total = after(values, *gate) + got[0]
    return total + (got[1] + got[2]) if len(got) == 3 else total


def gelu_and_slope(h):
    inner_scale = math.sqrt(2.0 / math.pi)
    square = h * h
    t = jnp.tanh(h * (inner_scale + (inner_scale * 0.044715) * square))
    half = 0.5 * h
    rise = 0.5 + 0.5 * t
    bend = inner_scale + (3.0 * inner_scale * 0.044715) * square
    return (h * rise).astype(LOW), (rise + (half - half * t * t) * bend).astype(LOW)


def join_piece(pieces, spans, whole_ref):
    i = pl.program_id(0)
    for (first, span), piece in zip(spans, pieces):

        @pl.when((i >= first) & (i < first + span))
        def _(piece=piece):
            whole_ref[...] = piece[...]


def piece_blocks(pieces):
    tile, width = pieces[-1].shape
    spans, first = [], 0
    for piece in pieces:
        spans.append((first, piece.shape[0] // tile))
        first += piece.shape[0] // tile

    def spec(first, span):
        return pl.BlockSpec((tile, width), lambda i: (jnp.clip(i - first, 0, span - 1), 0))

    return tile, tuple(spans), [spec(*span) for span in spans]


def expand_kernel(*refs, spans, cols):
    w_ref, b_ref, act_ref, slope_ref, whole_ref = refs[len(spans) :]
    join_piece(refs[: len(spans)], spans, whole_ref)
    x = whole_ref[...]
    for n in range(w_ref.shape[1] // cols):
        at = slice(n * cols, (n + 1) * cols)
        act, slope = gelu_and_slope(dot(x, w_ref[:, at], NN) + b_ref[:, at])
        act_ref[:, at] = act
        slope_ref[:, at] = slope


def expand(pieces, w, b):
    width, hidden = w.shape
    tile, spans, specs = piece_blocks(pieces)
    rows = sum(piece.shape[0] for piece in pieces)
    by_row = pl.BlockSpec((tile, hidden), lambda i: (i, 0))
    out = jax.ShapeDtypeStruct((rows, hidden), LOW)
    return pl.pallas_call(
        functools.partial(expand_kernel, spans=spans, cols=min(512, hidden)),
        out_shape=(out, out, jax.ShapeDtypeStruct((rows, width), LOW)),
        grid=(rows // tile,),
        in_specs=specs
        + [
            pl.BlockSpec((width, hidden), lambda i: (0, 0), pipeline_mode=pl.Buffered(1)),
            pl.BlockSpec((1, hidden), lambda i: (0, 0)),
        ],
        out_specs=[by_row, by_row, pl.BlockSpec((tile, width), lambda i: (i, 0))],
        compiler_params=pltpu.CompilerParams(
            dimension_semantics=("arbitrary",), vmem_limit_bytes=48 << 20
        ),
        cost_estimate=pl.CostEstimate(
            flops=2 * rows * width * hidden,
            bytes_accessed=2 * rows * (2 * width + 2 * hidden),
            transcendentals=rows * hidden,
        ),
        name="expand",
    )(*pieces, w, b[None])


def slope_grad_kernel(*refs, spans, cols):
    pieces = refs[: len(spans)]
    w_ref, slope_ref, out_ref, whole_ref, sums_ref = refs[len(spans) :]
    join_piece(pieces, spans, whole_ref)

    @pl.when(pl.program_id(0) == 0)
    def _():
        sums_ref[...] = jnp.zeros(sums_ref.shape, WIDE)

    x = whole_ref[...]
    for n in range(w_ref.shape[1] // cols):
        at = slice(n * cols, (n + 1) * cols)
        value = dot(x, w_ref[:, at], NN) * slope_ref[:, at].astype(WIDE)
        out_ref[:, at] = value.astype(LOW)
        sums_ref[:, at] += jnp.sum(value.reshape(value.shape[0] // 8, 8, cols), axis=0)


def slope_grad(pieces, w, slope):
    width, hidden = w.shape
    tile, spans, specs = piece_blocks(pieces)
    first = sum(span for _, span in spans)
    by_row = pl.BlockSpec((tile, hidden), lambda i: (i, 0))
    grad, whole, sums = pl.pallas_call(
        functools.partial(slope_grad_kernel, spans=spans, cols=min(512, hidden)),
        out_shape=(
            jax.ShapeDtypeStruct((first * tile, hidden), LOW),
            jax.ShapeDtypeStruct((first * tile, width), LOW),
            jax.ShapeDtypeStruct((8, hidden), WIDE),
        ),
        grid=(first,),
        in_specs=specs
        + [
            pl.BlockSpec((width, hidden), lambda i: (0, 0), pipeline_mode=pl.Buffered(1)),
            by_row,
        ],
        out_specs=[
            by_row,
            pl.BlockSpec((tile, width), lambda i: (i, 0)),
            pl.BlockSpec((8, hidden), lambda i: (0, 0)),
        ],
        compiler_params=pltpu.CompilerParams(
            dimension_semantics=("arbitrary",), vmem_limit_bytes=48 << 20
        ),
        cost_estimate=pl.CostEstimate(
            flops=2 * first * tile * width * hidden,
            bytes_accessed=2 * first * tile * (2 * width + 2 * hidden),
            transcendentals=0,
        ),
        name="slope_grad",
    )(*pieces, w, slope)
    return grad, whole, jnp.sum(sums, axis=0)


def input_grad_kernel(*refs, terms, ranks):
    grads, weights = refs[: terms * ranks], refs[terms * ranks : terms * ranks + terms]
    rest = refs[terms * (ranks + 1) :]
    normed_refs, out_refs, sums_ref = rest[:ranks], list(rest[ranks:-1]), rest[-1]
    plain = weighted = 0.0
    for n in range(ranks):
        mine = grads[n * terms : (n + 1) * terms]
        total = sum(dot(g[...], w[...], NT) for g, w in zip(mine, weights))
        at = 0
        while at < total.shape[0]:
            out_ref = out_refs.pop(0)
            out_ref[...] = total[at : at + out_ref.shape[0]].astype(LOW)
            at += out_ref.shape[0]
        plain += jnp.sum(total, axis=0, keepdims=True)
        weighted += jnp.sum(total * normed_refs[n][...].astype(WIDE), axis=0, keepdims=True)
    sums_ref[0:1] = plain
    sums_ref[1:2] = weighted


def input_grad(grads, weights, normed, ranks, rows, cuts, cost):
    width = normed.shape[1]
    cols = 512
    keep = pl.Buffered(1)
    in_specs = [
        pl.BlockSpec((rows, g.shape[1]), lambda i, rank=rank: (rank, 0), pipeline_mode=keep)
        for rank in ranks
        for g in grads
    ]
    in_specs += [
        pl.BlockSpec((cols, g.shape[1]), lambda i, at=at: (i, at))
        for g, (_, at) in zip(grads, weights)
    ]
    in_specs += [pl.BlockSpec((rows, cols), lambda i, rank=rank: (rank, i)) for rank in ranks]
    sizes = [size for cut in cuts for size in cut]
    *parts, sums = pl.pallas_call(
        functools.partial(input_grad_kernel, terms=len(grads), ranks=len(ranks)),
        out_shape=[jax.ShapeDtypeStruct((size, width), LOW) for size in sizes]
        + [jax.ShapeDtypeStruct((2, width), WIDE)],
        grid=(width // cols,),
        in_specs=in_specs,
        out_specs=[pl.BlockSpec((size, cols), lambda i: (0, i)) for size in sizes]
        + [pl.BlockSpec((2, cols), lambda i: (0, i))],
        compiler_params=pltpu.CompilerParams(
            dimension_semantics=("arbitrary",), vmem_limit_bytes=58 << 20
        ),
        cost_estimate=cost,
        name="input_grad",
    )(*grads * len(ranks), *[w for w, _ in weights], *[normed] * len(ranks))
    return [[parts.pop(0) for _ in cut] for cut in cuts], sums


def place_kernel(*refs, starts, count, groups):
    pieces = refs[: count * groups]
    dense = refs[count * groups : count * groups + count + 1]
    rest = refs[count * (groups + 1) + 1 :]
    token_ref, bias_ref, own_ref = rest[:3]
    terms, out_ref, acc = rest[3:-2], rest[-2], rest[-1]
    acc[...] = token_ref[...].astype(WIDE) + bias_ref[...] + own_ref[...].astype(WIDE)
    for start, term in zip(starts, terms):
        acc[start : start + term.shape[0]] += term[...].astype(WIDE)
    steps = pl.num_programs(0)
    low_half = pl.program_id(0) * 2 < steps
    far = jnp.where(low_half, dense[count - 1][...], dense[count][...])
    total = acc[...]
    for rank in range(count):
        weight = dense[rank][...] if rank < count - 1 else far
        mine = [piece[...] for piece in pieces[rank * groups : (rank + 1) * groups]]
        total += dot(jnp.concatenate(mine, axis=1), weight, NT)
    out_ref[...] = total.astype(LOW)


def place_output(pieces, dense_pieces, tokens, bias, own, terms, count, groups):
    rows, width = tokens.shape
    cols = 512
    half = width // cols // 2
    whole = lambda a: pl.BlockSpec(a.shape, lambda i: (0, 0), pipeline_mode=pl.Buffered(1))
    in_specs = [whole(piece) for piece in pieces]
    depth = dense_pieces[0].shape[1]
    in_specs += [pl.BlockSpec((cols, depth), lambda i: (i, 0)) for _ in range(count - 1)]
    in_specs.append(pl.BlockSpec((cols, depth), lambda i: (jnp.minimum(i, half - 1), 0)))
    in_specs.append(pl.BlockSpec((cols, depth), lambda i: (jnp.maximum(i - half, 0), 0)))
    by_column = lambda n: pl.BlockSpec((n, cols), lambda i: (0, i))
    in_specs += [by_column(rows), by_column(1), by_column(rows)]
    in_specs += [by_column(term.shape[0]) for _, term in terms]
    return pl.pallas_call(
        functools.partial(
            place_kernel, starts=tuple(start for start, _ in terms), count=count, groups=groups
        ),
        out_shape=jax.ShapeDtypeStruct((rows, width), LOW),
        grid=(width // cols,),
        in_specs=in_specs,
        out_specs=by_column(rows),
        scratch_shapes=[pltpu.VMEM((rows, cols), WIDE)],
        compiler_params=pltpu.CompilerParams(
            dimension_semantics=("arbitrary",), vmem_limit_bytes=58 << 20
        ),
        cost_estimate=LITTLE,
        name="place_output",
    )(*pieces, *dense_pieces, tokens, bias, own, *[term for _, term in terms])


def token_grad_kernel(token_ref, grad_ref, own_ref, gain_ref, *refs, starts, tile):
    terms, out_ref, total = refs[:-2], refs[-2], refs[-1]
    first = pl.program_id(0) * tile
    total[...] = own_ref[...].astype(WIDE)
    for start, term in zip(starts, terms):
        size = min(tile, term.shape[0])
        for at in range(0, term.shape[0], size):

            @pl.when(first == (start + at) // tile * tile)
            def _(start=start, term=term, at=at, size=size):
                to = (start + at) % tile
                total[to : to + size] += term[at : at + size].astype(WIDE)

    x = token_ref[...].astype(WIDE)
    centred = x - jnp.mean(x, axis=-1, keepdims=True)
    rstd = lax.rsqrt(jnp.mean(centred * centred, axis=-1, keepdims=True) + 1e-05)
    xhat = centred * rstd
    scaled = total[...] * gain_ref[...]
    mean = jnp.mean(scaled, axis=-1, keepdims=True)
    along = jnp.mean(scaled * xhat, axis=-1, keepdims=True)
    out_ref[...] = (grad_ref[...].astype(WIDE) + rstd * (scaled - mean - xhat * along)).astype(LOW)


def token_grad(tokens, grad, own, gain, terms, tile):
    rows, width = tokens.shape
    by_row = pl.BlockSpec((tile, width), lambda i: (i, 0))
    whole = lambda a: pl.BlockSpec(a.shape, lambda i: (0, 0), pipeline_mode=pl.Buffered(1))
    return pl.pallas_call(
        functools.partial(
            token_grad_kernel, starts=tuple(start for start, _ in terms), tile=tile
        ),
        out_shape=jax.ShapeDtypeStruct((rows, width), LOW),
        grid=(rows // tile,),
        in_specs=[by_row, by_row, by_row, pl.BlockSpec((1, width), lambda i: (0, 0))]
        + [whole(term) for _, term in terms],
        out_specs=by_row,
        scratch_shapes=[pltpu.VMEM((tile, width), WIDE)],
        compiler_params=pltpu.CompilerParams(
            dimension_semantics=("arbitrary",), vmem_limit_bytes=48 << 20
        ),
        cost_estimate=LITTLE,
        name="token_grad",
    )(tokens, grad, own, gain[None], *[term for _, term in terms])


def pair_grad_kernel(x_ref, y_ref, a_ref, b_ref, out_ref):
    split = a_ref.shape[1]
    out_ref[:, :split] = dot(x_ref[...], a_ref[...], TN).astype(LOW)
    out_ref[:, split:] = dot(y_ref[...], b_ref[...], TN).astype(LOW)


def pair_grad(x, y, a, b):
    rows, width = x.shape
    columns = a.shape[1] + b.shape[1]
    tile = 512
    keep = pl.Buffered(1)
    return pl.pallas_call(
        pair_grad_kernel,
        out_shape=jax.ShapeDtypeStruct((width, columns), LOW),
        grid=(width // tile,),
        in_specs=[
            pl.BlockSpec((rows, tile), lambda i: (0, i)),
            pl.BlockSpec((rows, tile), lambda i: (0, i)),
            pl.BlockSpec(a.shape, lambda i: (0, 0), pipeline_mode=keep),
            pl.BlockSpec(b.shape, lambda i: (0, 0), pipeline_mode=keep),
        ],
        out_specs=pl.BlockSpec((tile, columns), lambda i: (i, 0)),
        compiler_params=pltpu.CompilerParams(
            dimension_semantics=("arbitrary",), vmem_limit_bytes=58 << 20
        ),
        cost_estimate=LITTLE,
        name="pair_grad",
    )(x, y, a, b)


def rope_tables(rows):
    place = lax.broadcasted_iota(jnp.int32, (rows, LANES), 0)
    lane = lax.broadcasted_iota(jnp.int32, (rows, LANES), 1)
    pos = jnp.where(place < PROMPT, place, PROMPT + (place - PROMPT) % CLEN)
    half = ROT // 2
    freq = 10000.0 ** (-2.0 * jnp.arange(half, dtype=WIDE) / ROT)
    angle = pos.astype(WIDE) * jnp.tile(freq, LANES // half)[None, :]
    dim = lane % (LANES // 2)
    cosine, sine = jnp.cos(angle), jnp.sin(angle)
    return [
        jnp.where(dim < ROT, cosine, 1.0),
        jnp.where((dim >= half) & (dim < ROT), sine, 0.0),
        jnp.where(dim < half, -sine, 0.0),
    ]


def shards(
    tokens,
    cotangent,
    block_table,
    ln_gain,
    ln_bias,
    w_qkv,
    b_qkv,
    w_dense,
    b_dense,
    w_fc1,
    b_fc1,
    w_fc2,
    b_fc2,
):
    _, local_rows, width = tokens.shape
    head_dim = width // HEADS
    count = lax.axis_size("ctx")
    me = lax.axis_index("ctx")
    rows = local_rows * count
    local_blocks = local_rows // BLK
    each = w_dense.shape[0]
    hidden = w_fc2.shape[0]
    gain, shift = ln_gain.astype(WIDE), ln_bias.astype(WIDE)

    def of_rank(whole, rank):
        return whole[rank * local_rows : (rank + 1) * local_rows]

    order, _, _ = ring_of(count)
    places = [0] * count
    for n, device in enumerate(order):
        places[device] = n
    places = jnp.asarray(places, jnp.int32)
    ranks = jnp.asarray([rank_of(n, count) for n in range(count)], jnp.int32)
    slots = jnp.arange(rows // BLK, dtype=jnp.int32)
    offset = (places[slots // local_blocks] - places[me]) % count
    held_at = ranks[offset] * local_blocks + slots % local_blocks
    hit = block_table[0][None, :] == slots[:, None]
    where = jnp.sum(jnp.where(hit, held_at[None, :], 0), axis=1).astype(jnp.int32)

    own_tokens = tokens[0].astype(WIDE)
    own_grad = cotangent[0]
    average = jnp.mean(own_tokens, axis=-1, keepdims=True)
    centred = own_tokens - average
    rstd = lax.rsqrt(jnp.mean(centred * centred, axis=-1, keepdims=True) + 1e-05)
    xhat = centred * rstd
    normed_own = (xhat * gain + shift).astype(LOW)

    def gather_rows(shard):
        return lax.all_gather(shard, "fsdp", axis=0, tiled=True)

    def scatter_rows(whole):
        return lax.psum_scatter(whole, "fsdp", scatter_dimension=0, tiled=True)

    lanes = 2 * LANES if each % (2 * LANES) == 0 else LANES
    groups = each // lanes

    def by_group(values):
        cut = values.reshape(-1, 3, groups, lanes)
        return jnp.swapaxes(cut, 1, 2).reshape(-1, 3 * each)

    tabs = rope_tables(rows)
    own_grad_sum = jnp.sum(own_grad.astype(WIDE), axis=0)
    fc1_bias = lax.dynamic_slice_in_dim(b_fc1, me * hidden, hidden, 0).astype(WIDE)
    early = (where, own_grad_sum, fc1_bias, *tabs)
    normed_pieces = ring_pieces(normed_own, "ctx", gate=early)
    attention_shard = jnp.concatenate([by_group(w_qkv), w_dense.T], axis=1)
    fc1_weight = gather_rows(w_fc1)
    fc2_turned = gather_rows(after(w_fc2.T, *normed_pieces[1:-2]))
    attention_weight = gather_rows(after(attention_shard, *normed_pieces[-2:]))
    qkv_weight, dense_turned = attention_weight[:, : 3 * each], attention_weight[:, 3 * each :]

    qkv_bias = lax.dynamic_slice_in_dim(b_qkv.reshape(3, width), me * each, each, 1)
    activated, slope, normed = expand(normed_pieces, fc1_weight, fc1_bias)

    sent_grad = after(own_grad, *normed_pieces[-2:])
    grad_pieces = ring_pieces(sent_grad, "ctx", gate=(activated,))
    ff_part = dot(activated, fc2_turned, NT).astype(LOW)
    ff_terms, ff_hops = ring_reduce(lambda rank: of_rank(ff_part, rank), "ctx", chained=True)
    first, second, last = ff_hops[0], ff_hops[min(1, len(ff_hops) - 1)], ff_hops[-1]

    gated = [after(piece, ff_part) for piece in grad_pieces]
    expanded_grad, grads, fc1_bias_part = slope_grad(gated, fc2_turned, slope)
    d_fc2_part = dot(after(grads, expanded_grad, *first), activated, TN).astype(LOW)
    d_fc2 = scatter_rows(d_fc2_part)
    qkv = dot(after(normed, d_fc2_part), qkv_weight, NN)
    qkv = (qkv + by_group(qkv_bias)[0].astype(WIDE)).astype(LOW)
    attended_grad = dot(after(grads, qkv, *second), dense_turned, NN).astype(LOW)
    gated = after(normed, attended_grad)
    d_fc1_part = dot(gated, expanded_grad, TN).astype(LOW)
    d_fc1 = scatter_rows(d_fc1_part)


    attended, qkv_grads, qkv_sums, d_attention, swapped = [], [], [], [], []
    ordered = (d_fc1_part,)
    for which in range(groups):
        got, got_grads, got_sums = attention(
            after(qkv, *ordered), attended_grad, where, tabs, lanes, which, head_dim
        )
        if which == 0:
            dense_pieces = ring_pieces(after(dense_turned, *second), "ctx", gate=(got,))
        attended.append(got)
        qkv_grads.append(got_grads)
        qkv_sums.append(got_sums)
        if which < groups - 1:
            swapped.append(ring_exchange(lambda rank, got=got: of_rank(got, rank), "ctx"))
            gated = after(normed, d_fc2, *last, *dense_pieces[1:-2]) if which == 0 else normed
            d_part = pair_grad(gated, grads, got_grads, got)
            ordered = (d_part,)
            d_attention.append(scatter_rows(d_part))

    weights = [(attention_weight, which) for which in range(groups)] + [(fc1_weight, 0)]
    early_swaps = [piece for pieces in swapped for piece in pieces]
    turn = after(expanded_grad, d_fc1, *dense_pieces[-2:], *early_swaps, *attended)
    swapped.append(ring_exchange(lambda rank: of_rank(attended[-1], rank), "ctx"))
    half = local_rows // 2
    whole, far_cut, ahead_cut, behind_cut = [local_rows], [half, half], [half], [half]
    if count > 2:
        ahead_cut, behind_cut = [half, half], [half, half]
    cut_of = {0: whole, count - 2: ahead_cut, count - 3: behind_cut, count - 1: far_cut}

    def some_ranks(ranks, turn, cost=LITTLE):
        cuts = [cut_of.get(rank, whole) for rank in ranks]
        return input_grad(qkv_grads + [turn], weights, normed, ranks, local_rows, cuts, cost)

    far_part, far_sums = some_ranks([count - 1], turn)
    middle = list(range(count - 2, 0, -1))
    middle_sums, parts = 0.0, {count - 1: far_part[0]}
    turn = after(turn, *far_part[0], *swapped[-1])
    for n in range(0, len(middle), 2):
        some, some_sums = some_ranks(middle[n : n + 2], turn, MUCH)
        turn = after(turn, *[piece for pieces in some for piece in pieces])
        middle_sums = middle_sums + some_sums
        parts.update(zip(middle[n : n + 2], some))
    for rank, pieces in parts.items():
        if len(pieces) == 1:
            parts[rank] = pieces[0]

    grad_terms, hops = ring_reduce(lambda rank: parts[rank], "ctx")
    last_hops = [piece for hop in hops[1:3] for piece in hop]
    gated = after(normed, turn, *hops[0], *d_attention)
    d_part = pair_grad(gated, grads, qkv_grads[-1], attended[-1])
    d_attention.append(scatter_rows(d_part))
    [own_part], own_sums = some_ranks([0], after(turn, d_part), MUCH)
    d_qkv = jnp.concatenate(
        [part[:, : 3 * lanes].reshape(-1, 3, lanes) for part in d_attention], axis=2
    ).astype(WIDE)
    d_dense = jnp.concatenate([part[:, 3 * lanes :].T for part in d_attention], axis=0)
    d_dense = d_dense.astype(WIDE)

    qkv_bias_part = jnp.concatenate(
        [part.reshape(3, lanes) for part in qkv_sums], axis=1
    )
    qkv_bias_wide = lax.dynamic_update_slice_in_dim(
        jnp.zeros((3, width), WIDE), qkv_bias_part, me * each, 1
    ).reshape(-1)
    fc1_bias_wide = lax.dynamic_update_slice_in_dim(
        jnp.zeros((b_fc1.shape[0],), WIDE), fc1_bias_part, me * hidden, 0
    )
    small = jnp.concatenate(
        [
            (far_sums + middle_sums + own_sums).reshape(-1),
            qkv_bias_wide,
            own_grad_sum,
            fc1_bias_wide,
        ]
    )
    doubled = [2**n for n in range(1, 30)]
    steps = exchange_steps("fsdp", [1]) + exchange_steps("ctx", [1] + doubled)
    steps += exchange_steps("fsdp", doubled)
    small = exchange(small, steps[0])
    d_fc1, d_fc2 = d_fc1.astype(WIDE), d_fc2.T.astype(WIDE)
    output = place_output(
        [swapped[which][rank] for rank in range(count) for which in range(groups)],
        dense_pieces,
        after(tokens[0], *own_part),
        (b_dense.astype(WIDE) + b_fc2.astype(WIDE))[None],
        ff_part,
        ff_terms,
        count,
        groups,
    )
    small = exchange(after(small, output, *last_hops), steps[1])
    d_tokens = token_grad(
        after(tokens[0], output), own_grad, own_part[0], gain, grad_terms, local_rows // 4
    )
    for step in steps[2:-1]:
        small = exchange(small, step)
    small = exchange(after(small, d_tokens), steps[-1], (d_fc1, d_fc2, d_qkv, d_dense))
    d_shift, with_normed, d_b_qkv, d_b_out, d_b_fc1 = jnp.split(
        small, [width, 2 * width, 5 * width, 6 * width]
    )
    d_gain = (with_normed - shift * d_shift) / gain
    return (
        output[None],
        d_tokens[None],
        d_gain,
        d_shift,
        d_qkv,
        d_b_qkv,
        d_dense,
        d_b_out,
        d_fc1,
        d_b_fc1,
        d_fc2,
        d_b_out,
    )


def solution(mesh):
    in_specs = (
        P("fsdp", "ctx", None),
        P("fsdp", "ctx", None),
        P("fsdp", None),
        P(),
        P(),
        P("fsdp", None, "ctx"),
        P(),
        P("ctx", "fsdp"),
        P(),
        P("fsdp", "ctx"),
        P(),
        P("ctx", "fsdp"),
        P(),
    )
    out_specs = (
        P("fsdp", "ctx", None),
        P("fsdp", "ctx", None),
        P(),
        P(),
        P("fsdp", None, "ctx"),
        P(),
        P("ctx", "fsdp"),
        P(),
        P("fsdp", "ctx"),
        P(),
        P("ctx", "fsdp"),
        P(),
    )
    return jax.shard_map(shards, mesh=mesh, in_specs=in_specs, out_specs=out_specs, check_vma=False)
```

```python
import functools
import math

import jax
import jax.numpy as jnp
from jax import lax
from jax.experimental import pallas as pl
from jax.experimental.pallas import tpu as pltpu
from jax.sharding import PartitionSpec as P

HEADS = 32
ROT = 32
PROMPT = 2048
CLEN = 256
BLK = 64
CHUNK = 256
LANES = 128
NT = (((1,), (1,)), ((), ()))
NN = (((1,), (0,)), ((), ()))
TN = (((0,), (0,)), ((), ()))
LOW = jnp.bfloat16
WIDE = jnp.float32
LITTLE = pl.CostEstimate(flops=1000000, bytes_accessed=1000000, transcendentals=0)
MUCH = pl.CostEstimate(flops=100000000000, bytes_accessed=1000000, transcendentals=0)


def dot(left, right, dims):
    return lax.dot_general(left, right, dims, preferred_element_type=WIDE)


def attention_kernel(where_ref, *refs, chunk, chunks, full_chunks, blk, group, scale):
    per = chunk // blk
    qkv_in, g_in = refs[:per], refs[per : 2 * per]
    cos_ref, up_ref, down_ref, att_hbm, grad_hbm, sums_ref = refs[2 * per : 2 * per + 6]
    (
        keys,
        values,
        values_t,
        probs,
        key_sum,
        value_sum,
        top_ref,
        total_ref,
        mix_ref,
        back_ref,
        att_stage,
        query_stage,
        key_stage,
        value_stage,
        row_sem,
        col_sem,
    ) = refs[2 * per + 6 :]
    i = pl.program_id(0)
    slot = lax.rem(i, 2)
    half = LANES // 2
    lanes = group * LANES
    heads = 2 * group
    first = lax.broadcasted_iota(jnp.int32, (1, LANES), 1) < half

    def columns(part):
        return pl.ds(part * lanes, lanes)

    def row_copies(which, at):
        stage, target = ((att_stage, att_hbm), (query_stage, grad_hbm))[which]
        return [
            pltpu.make_async_copy(
                stage.at[at, pl.ds(r * blk, blk)],
                target.at[where_ref[i * per + r], :, columns(0)],
                row_sem.at[at, which, r],
            )
            for r in range(per)
        ]

    def col_copies(n):
        block = where_ref[n]
        rows = pl.ds(pl.multiple_of(n * blk, blk), blk)
        return (
            pltpu.make_async_copy(
                key_stage.at[rows], grad_hbm.at[block, :, columns(1)], col_sem.at[0, n]
            ),
            pltpu.make_async_copy(
                value_stage.at[rows], grad_hbm.at[block, :, columns(2)], col_sem.at[1, n]
            ),
        )

    def load(parts):
        return jnp.concatenate([part[0] for part in parts], axis=0)

    def tables(rows):
        return cos_ref[rows], up_ref[rows], down_ref[rows]

    quarter = ROT // 2

    def turned(x, tab, sign):
        return jnp.concatenate(
            [
                y * tab[0]
                + sign
                * (pltpu.roll(y, quarter, 1) * tab[1] + pltpu.roll(y, LANES - quarter, 1) * tab[2])
                for y in (x[:, n * LANES : (n + 1) * LANES] for n in range(group))
            ],
            axis=1,
        )

    def one_head(x, h):
        pair = x[:, (h // 2) * LANES : (h // 2 + 1) * LANES]
        nothing = jnp.zeros_like(pair)
        return jnp.where(first, pair, nothing) if h % 2 == 0 else jnp.where(first, nothing, pair)

    @pl.when(i >= 2)
    def _():
        for which in range(2):
            for copy in row_copies(which, slot):
                copy.wait()

    here = pl.ds(pl.multiple_of(i * chunk, chunk), chunk)
    tab = tables(here)
    qkv = load(qkv_in)
    query = (turned(qkv[:, :lanes].astype(WIDE), tab, 1.0) * scale).astype(LOW)
    key_new = turned(qkv[:, lanes : 2 * lanes].astype(WIDE), tab, 1.0)
    value_new = qkv[:, 2 * lanes :]
    grad = load(g_in)
    keys[here] = key_new.astype(LOW)
    values[here] = value_new
    values_t[:, here] = value_new.T
    key_sum[here] = jnp.zeros((chunk, lanes), WIDE)
    value_sum[here] = jnp.zeros((chunk, lanes), WIDE)
    top_ref[...] = jnp.full(top_ref.shape, -1e30, WIDE)
    total_ref[...] = jnp.zeros(total_ref.shape, WIDE)
    mix_ref[...] = jnp.zeros(mix_ref.shape, WIDE)
    back_ref[...] = jnp.zeros(back_ref.shape, WIDE)
    query_of = [one_head(query, h) for h in range(heads)]
    grad_of = [one_head(grad, h) for h in range(heads)]
    query_pair = [
        jnp.concatenate(query_of[2 * n : 2 * n + 2], axis=0) for n in range(group)
    ]
    grad_pair = [jnp.concatenate(grad_of[2 * n : 2 * n + 2], axis=0) for n in range(group)]
    before = jnp.minimum(i, full_chunks)
    doubles = before // 2
    odd = before - 2 * doubles

    def fold(x, how):
        return how(x.reshape(x.shape[0] // 8, 8, chunk), axis=0)

    def pair_lanes(n):
        return slice(n * LANES, (n + 1) * LANES)

    def head_rows(h):
        return slice(h * half, (h + 1) * half)

    def sweep(tile):
        def quad(t, carry):
            start = pl.multiple_of(t * 4 * chunk, 4 * chunk)
            tile(start, start, 4 * chunk, False)
            return carry

        lax.fori_loop(0, doubles // 2, quad, 0)

        @pl.when(doubles % 2 == 1)
        def _():
            start = pl.multiple_of((doubles - 1) * 2 * chunk, 2 * chunk)
            tile(start, start, 2 * chunk, False)

        held = pl.multiple_of(doubles * 2 * chunk, chunk)

        @pl.when(odd == 1)
        def _():
            tile(held, held, 2 * chunk, True)

        @pl.when(odd == 0)
        def _():
            tile(pl.multiple_of(i * chunk, chunk), held, chunk, True)

    def score(start, held, size, masked):
        rows, to = pl.ds(start, size), pl.ds(held, size)
        if masked:
            key_row = lax.broadcasted_iota(jnp.int32, (size, chunk), 0) + start
            query_col = lax.broadcasted_iota(jnp.int32, (size, chunk), 1) + i * chunk
            seen = key_row <= query_col
        for h in range(heads):
            raw = dot(keys[rows, pair_lanes(h // 2)], query_of[h], NT)
            if masked:
                raw = jnp.where(seen, raw, -1e30)
            probs[h, to] = raw
            top_ref[h] = jnp.maximum(top_ref[h], fold(raw, jnp.max))

    sweep(score)
    top = [jnp.max(top_ref[h], axis=0, keepdims=True) for h in range(heads)]

    def mix(start, held, size, masked):
        rows, to = pl.ds(start, size), pl.ds(held, size)
        for h in range(heads):
            weight = jnp.exp(probs[h, to] - top[h])
            probs[h, to] = weight
            total_ref[h] += fold(weight, jnp.sum)
            mix_ref[head_rows(h)] += dot(values_t[head_rows(h), rows], weight.astype(LOW), NN)

    sweep(mix)
    inverse = [1.0 / jnp.sum(total_ref[h], axis=0, keepdims=True) for h in range(heads)]
    attended = jnp.concatenate(
        [mix_ref[head_rows(h)] * inverse[h] for h in range(heads)], axis=0
    )
    shared = grad.T.astype(WIDE) * attended
    inner = [jnp.sum(shared[head_rows(h)], axis=0, keepdims=True) for h in range(heads)]
    att_stage[slot] = attended.astype(LOW).T
    for copy in row_copies(0, slot):
        copy.start()

    def back(start, held, size, masked):
        rows, to = pl.ds(start, size), pl.ds(held, size)
        for n in range(group):
            value = values[rows, pair_lanes(n)]
            weights, grads = [], []
            for h in (2 * n, 2 * n + 1):
                weight = probs[h, to] * inverse[h]
                weight_grad = dot(value, grad_of[h], NT)
                score_grad = (weight * (weight_grad - inner[h])).astype(LOW)
                weights.append(weight.astype(LOW))
                grads.append(score_grad)
            value_sum[rows, pair_lanes(n)] += dot(
                jnp.concatenate(weights, axis=1), grad_pair[n], NN
            )
            key = keys[rows, pair_lanes(n)]
            back_ref[:, pair_lanes(n)] += dot(
                jnp.concatenate(grads, axis=0),
                jnp.concatenate([one_head(key, h) for h in range(2)], axis=0),
                TN,
            )
            key_sum[rows, pair_lanes(n)] += dot(
                jnp.concatenate(grads, axis=1), query_pair[n], NN
            )

    sweep(back)
    query_grad = turned(back_ref[...] * scale, tab, -1.0)
    query_stage[slot] = query_grad.astype(LOW)

    def column_sums(x):
        return jnp.sum(x.reshape(chunk // 8, 8, lanes), axis=0)

    @pl.when(i == 0)
    def _():
        sums_ref[...] = jnp.zeros(sums_ref.shape, WIDE)

    sums_ref[:, :lanes] += column_sums(query_grad)
    for copy in row_copies(1, slot):
        copy.start()

    @pl.when(i == chunks - 1)
    def _():
        @pl.loop(0, chunks)
        def _(n):
            rows = pl.ds(pl.multiple_of(n * chunk, chunk), chunk)
            key_grad = turned(key_sum[rows], tables(rows), -1.0)
            key_stage[rows] = key_grad.astype(LOW)
            value_stage[rows] = value_sum[rows].astype(LOW)
            sums_ref[:, lanes : 2 * lanes] += column_sums(key_grad)
            sums_ref[:, 2 * lanes :] += column_sums(value_sum[rows])
            for r in range(per):
                for copy in col_copies(n * per + r):
                    copy.start()

        for at in range(2):
            for which in range(2):
                for copy in row_copies(which, at):
                    copy.wait()

        @pl.loop(0, chunks * per)
        def _(n):
            for copy in col_copies(n):
                copy.wait()


def attention(qkv, grad, where, tabs, lanes, which, head_dim):
    rows = grad.shape[0]
    chunk, blk = CHUNK, BLK
    per, chunks, blocks = chunk // blk, rows // chunk, rows // blk
    group = lanes // LANES
    heads = 2 * group
    qkv_blocks = qkv.reshape(blocks, blk, qkv.shape[1])
    grad_blocks = grad.reshape(blocks, blk, grad.shape[1])

    def spec(columns, r):
        return pl.BlockSpec((1, blk, columns), lambda i, at: (at[i * per + r], 0, which))

    in_specs = [spec(3 * lanes, r) for r in range(per)] + [spec(lanes, r) for r in range(per)]
    in_specs += [pl.BlockSpec((rows, LANES), lambda i, at: (0, 0), pipeline_mode=pl.Buffered(1))] * 3
    operands = [qkv_blocks] * per + [grad_blocks] * per + list(tabs)
    kernel = functools.partial(
        attention_kernel,
        chunk=chunk,
        chunks=chunks,
        full_chunks=PROMPT // chunk,
        blk=blk,
        group=group,
        scale=1.0 / math.sqrt(head_dim),
    )
    attended, grads, sums = pl.pallas_call(
        kernel,
        out_shape=(
            jax.ShapeDtypeStruct((blocks, blk, lanes), LOW),
            jax.ShapeDtypeStruct((blocks, blk, 3 * lanes), LOW),
            jax.ShapeDtypeStruct((8, 3 * lanes), WIDE),
        ),
        grid_spec=pltpu.PrefetchScalarGridSpec(
            num_scalar_prefetch=1,
            grid=(chunks,),
            in_specs=in_specs,
            out_specs=[pl.BlockSpec(memory_space=pl.ANY)] * 2
            + [pl.BlockSpec((8, 3 * lanes), lambda i, at: (0, 0))],
            scratch_shapes=[
                pltpu.VMEM((rows, lanes), LOW),
                pltpu.VMEM((rows, lanes), LOW),
                pltpu.VMEM((lanes, rows), LOW),
                pltpu.VMEM((heads, PROMPT + chunk, chunk), WIDE),
                pltpu.VMEM((rows, lanes), WIDE),
                pltpu.VMEM((rows, lanes), WIDE),
                pltpu.VMEM((heads, 8, chunk), WIDE),
                pltpu.VMEM((heads, 8, chunk), WIDE),
                pltpu.VMEM((lanes, chunk), WIDE),
                pltpu.VMEM((chunk, lanes), WIDE),
                pltpu.VMEM((2, chunk, lanes), LOW),
                pltpu.VMEM((2, chunk, lanes), LOW),
                pltpu.VMEM((rows, lanes), LOW),
                pltpu.VMEM((rows, lanes), LOW),
                pltpu.SemaphoreType.DMA((2, 2, per)),
                pltpu.SemaphoreType.DMA((2, blocks)),
            ],
        ),
        compiler_params=pltpu.CompilerParams(
            dimension_semantics=("arbitrary",), vmem_limit_bytes=56 << 20
        ),
        cost_estimate=LITTLE,
        name="attention",
    )(where, *operands)
    return attended.reshape(rows, lanes), grads.reshape(rows, 3 * lanes), jnp.sum(sums, axis=0)


def after(value, *others):
    return lax.optimization_barrier((value,) + others)[0] if others else value


def ring_of(count):
    order = list(range(count // 2)) + list(range(count - 1, count // 2 - 1, -1))
    ahead = [(order[n], order[(n + 1) % count]) for n in range(count)]
    return order, ahead, [(b, a) for a, b in ahead]


def rank_of(offset, count):
    offset %= count
    if offset == 0 or 2 * offset == count:
        return max(2 * offset - 1, 0)
    return 2 * offset if 2 * offset < count else 2 * (count - offset) - 1


def ring_pieces(own, axis, gate=()):
    count = lax.axis_size(axis)
    _, ahead, behind = ring_of(count)
    pieces, half = [own], own.shape[0] // 2
    from_behind = from_ahead = own
    for _ in range(count // 2 - 1):
        from_behind = lax.ppermute(from_behind, axis, ahead)
        from_ahead = lax.ppermute(from_ahead, axis, behind)
        pieces += [from_behind, from_ahead]
    if gate:
        from_behind, from_ahead = after(from_behind, *gate), after(from_ahead, *gate)
        if count > 2:
            pieces[-2:] = [from_behind, from_ahead]
    far = [
        lax.ppermute(from_behind[:half], axis, ahead),
        lax.ppermute(from_ahead[half:], axis, behind),
    ]
    return pieces + far


def ring_reduce(part, axis, cuts=1, chained=False):
    count = lax.axis_size(axis)
    _, ahead, behind = ring_of(count)

    def plus(a, b):
        return (a.astype(WIDE) + b.astype(WIDE)).astype(LOW)

    def cut_rows(term, sizes):
        if isinstance(term, (list, tuple)):
            return term
        ends = [sum(sizes[: n + 1]) for n in range(len(sizes))]
        return [term[end - size : end] for end, size in zip(ends, sizes)]

    far = part(count - 1)
    half = sum(a.shape[0] for a in far) // 2 if isinstance(far, (list, tuple)) else far.shape[0] // 2
    far = cut_rows(far, [half, half])
    up, down = lax.ppermute(far[0], axis, ahead), lax.ppermute(far[1], axis, behind)
    hops = [(up, down)]
    if count == 2:
        return [(0, up), (half, down)], hops
    pieces = [half // cuts] * cuts
    to_ahead = cut_rows(part(count - 2), [half] + pieces)
    to_behind = cut_rows(part(count - 3), pieces + [half])
    got_up, got_down = {}, {}
    got_up[0] = lax.ppermute(plus(to_ahead[0], up), axis, ahead)
    got_down[half] = lax.ppermute(plus(to_behind[-1], down), axis, behind)
    hops.append((got_up[0], got_down[half]))
    for n in range(cuts):
        gate = hops[-1] if chained else ()
        at = n * (half // cuts)
        got_up[half + at] = lax.ppermute(after(to_ahead[1 + n], *gate), axis, ahead)
        got_down[at] = lax.ppermute(after(to_behind[n], *gate), axis, behind)
        hops.append((got_up[half + at], got_down[at]))
    if count == 4:
        return sorted(got_up.items()) + sorted(got_down.items()), hops
    up = jnp.concatenate([piece for _, piece in sorted(got_up.items())], axis=0)
    down = jnp.concatenate([piece for _, piece in sorted(got_down.items())], axis=0)
    for s in range(count // 2 - 2, 0, -1):
        up = lax.ppermute(plus(part(2 * s), up), axis, ahead)
        down = lax.ppermute(plus(part(2 * s - 1), down), axis, behind)
        hops.append((up, down))
    return [(0, up), (0, down)], hops


def ring_exchange(part, axis):
    count = lax.axis_size(axis)
    order, _, _ = ring_of(count)
    got = [None] * count
    got[0] = part(0)
    for offset in range(1, count):
        hops = [(order[n], order[(n + offset) % count]) for n in range(count)]
        got[rank_of(-offset, count)] = lax.ppermute(part(rank_of(offset, count)), axis, hops)
    return got


def exchange_steps(axis, spans):
    steps, count = [], lax.axis_size(axis)
    spans = [span for span in spans if span < count]
    while spans:
        step, spans = spans[:2], spans[2:]
        steps.append((axis, step + [step[0] + step[1]] if len(step) == 2 else step))
    return steps


def exchange(values, step, gate=()):
    axis, flips = step
    count = lax.axis_size(axis)
    got = [lax.ppermute(values, axis, [(n, n ^ flip) for n in range(count)]) for flip in flips]
    total = after(values, *gate) + got[0]
    return total + (got[1] + got[2]) if len(got) == 3 else total


def gelu_and_slope(h):
    inner_scale = math.sqrt(2.0 / math.pi)
    square = h * h
    t = jnp.tanh(h * (inner_scale + (inner_scale * 0.044715) * square))
    half = 0.5 * h
    rise = 0.5 + 0.5 * t
    bend = inner_scale + (3.0 * inner_scale * 0.044715) * square
    return (h * rise).astype(LOW), (rise + (half - half * t * t) * bend).astype(LOW)


def join_piece(pieces, spans, whole_ref):
    i = pl.program_id(0)
    for (first, span), piece in zip(spans, pieces):

        @pl.when((i >= first) & (i < first + span))
        def _(piece=piece):
            whole_ref[...] = piece[...]


def piece_blocks(pieces):
    tile, width = pieces[-1].shape
    spans, first = [], 0
    for piece in pieces:
        spans.append((first, piece.shape[0] // tile))
        first += piece.shape[0] // tile

    def spec(first, span):
        return pl.BlockSpec((tile, width), lambda i: (jnp.clip(i - first, 0, span - 1), 0))

    return tile, tuple(spans), [spec(*span) for span in spans]


def expand_kernel(*refs, spans, cols):
    w_ref, b_ref, act_ref, slope_ref, whole_ref = refs[len(spans) :]
    join_piece(refs[: len(spans)], spans, whole_ref)
    x = whole_ref[...]
    for n in range(w_ref.shape[1] // cols):
        at = slice(n * cols, (n + 1) * cols)
        act, slope = gelu_and_slope(dot(x, w_ref[:, at], NN) + b_ref[:, at])
        act_ref[:, at] = act
        slope_ref[:, at] = slope


def expand(pieces, w, b):
    width, hidden = w.shape
    tile, spans, specs = piece_blocks(pieces)
    rows = sum(piece.shape[0] for piece in pieces)
    by_row = pl.BlockSpec((tile, hidden), lambda i: (i, 0))
    out = jax.ShapeDtypeStruct((rows, hidden), LOW)
    return pl.pallas_call(
        functools.partial(expand_kernel, spans=spans, cols=min(512, hidden)),
        out_shape=(out, out, jax.ShapeDtypeStruct((rows, width), LOW)),
        grid=(rows // tile,),
        in_specs=specs
        + [
            pl.BlockSpec((width, hidden), lambda i: (0, 0), pipeline_mode=pl.Buffered(1)),
            pl.BlockSpec((1, hidden), lambda i: (0, 0)),
        ],
        out_specs=[by_row, by_row, pl.BlockSpec((tile, width), lambda i: (i, 0))],
        compiler_params=pltpu.CompilerParams(
            dimension_semantics=("arbitrary",), vmem_limit_bytes=48 << 20
        ),
        cost_estimate=pl.CostEstimate(
            flops=2 * rows * width * hidden,
            bytes_accessed=2 * rows * (2 * width + 2 * hidden),
            transcendentals=rows * hidden,
        ),
        name="expand",
    )(*pieces, w, b[None])


def slope_grad_kernel(*refs, spans, cols):
    pieces = refs[: len(spans)]
    w_ref, slope_ref, out_ref, whole_ref, sums_ref = refs[len(spans) :]
    join_piece(pieces, spans, whole_ref)

    @pl.when(pl.program_id(0) == 0)
    def _():
        sums_ref[...] = jnp.zeros(sums_ref.shape, WIDE)

    x = whole_ref[...]
    for n in range(w_ref.shape[1] // cols):
        at = slice(n * cols, (n + 1) * cols)
        value = dot(x, w_ref[:, at], NN) * slope_ref[:, at].astype(WIDE)
        out_ref[:, at] = value.astype(LOW)
        sums_ref[:, at] += jnp.sum(value.reshape(value.shape[0] // 8, 8, cols), axis=0)


def slope_grad(pieces, w, slope):
    width, hidden = w.shape
    tile, spans, specs = piece_blocks(pieces)
    first = sum(span for _, span in spans)
    by_row = pl.BlockSpec((tile, hidden), lambda i: (i, 0))
    grad, whole, sums = pl.pallas_call(
        functools.partial(slope_grad_kernel, spans=spans, cols=min(512, hidden)),
        out_shape=(
            jax.ShapeDtypeStruct((first * tile, hidden), LOW),
            jax.ShapeDtypeStruct((first * tile, width), LOW),
            jax.ShapeDtypeStruct((8, hidden), WIDE),
        ),
        grid=(first,),
        in_specs=specs
        + [
            pl.BlockSpec((width, hidden), lambda i: (0, 0), pipeline_mode=pl.Buffered(1)),
            by_row,
        ],
        out_specs=[
            by_row,
            pl.BlockSpec((tile, width), lambda i: (i, 0)),
            pl.BlockSpec((8, hidden), lambda i: (0, 0)),
        ],
        compiler_params=pltpu.CompilerParams(
            dimension_semantics=("arbitrary",), vmem_limit_bytes=48 << 20
        ),
        cost_estimate=pl.CostEstimate(
            flops=2 * first * tile * width * hidden,
            bytes_accessed=2 * first * tile * (2 * width + 2 * hidden),
            transcendentals=0,
        ),
        name="slope_grad",
    )(*pieces, w, slope)
    return grad, whole, jnp.sum(sums, axis=0)


def input_grad_kernel(*refs, terms, ranks):
    grads, weights = refs[: terms * ranks], refs[terms * ranks : terms * ranks + terms]
    rest = refs[terms * (ranks + 1) :]
    normed_refs, out_refs, sums_ref = rest[:ranks], list(rest[ranks:-1]), rest[-1]
    plain = weighted = 0.0
    for n in range(ranks):
        mine = grads[n * terms : (n + 1) * terms]
        total = sum(dot(g[...], w[...], NT) for g, w in zip(mine, weights))
        at = 0
        while at < total.shape[0]:
            out_ref = out_refs.pop(0)
            out_ref[...] = total[at : at + out_ref.shape[0]].astype(LOW)
            at += out_ref.shape[0]
        plain += jnp.sum(total, axis=0, keepdims=True)
        weighted += jnp.sum(total * normed_refs[n][...].astype(WIDE), axis=0, keepdims=True)
    sums_ref[0:1] = plain
    sums_ref[1:2] = weighted


def input_grad(grads, weights, normed, ranks, rows, cuts, cost):
    width = normed.shape[1]
    cols = 512
    keep = pl.Buffered(1)
    in_specs = [
        pl.BlockSpec((rows, g.shape[1]), lambda i, rank=rank: (rank, 0), pipeline_mode=keep)
        for rank in ranks
        for g in grads
    ]
    in_specs += [
        pl.BlockSpec((cols, g.shape[1]), lambda i, at=at: (i, at))
        for g, (_, at) in zip(grads, weights)
    ]
    in_specs += [pl.BlockSpec((rows, cols), lambda i, rank=rank: (rank, i)) for rank in ranks]
    sizes = [size for cut in cuts for size in cut]
    *parts, sums = pl.pallas_call(
        functools.partial(input_grad_kernel, terms=len(grads), ranks=len(ranks)),
        out_shape=[jax.ShapeDtypeStruct((size, width), LOW) for size in sizes]
        + [jax.ShapeDtypeStruct((2, width), WIDE)],
        grid=(width // cols,),
        in_specs=in_specs,
        out_specs=[pl.BlockSpec((size, cols), lambda i: (0, i)) for size in sizes]
        + [pl.BlockSpec((2, cols), lambda i: (0, i))],
        compiler_params=pltpu.CompilerParams(
            dimension_semantics=("arbitrary",), vmem_limit_bytes=58 << 20
        ),
        cost_estimate=cost,
        name="input_grad",
    )(*grads * len(ranks), *[w for w, _ in weights], *[normed] * len(ranks))
    return [[parts.pop(0) for _ in cut] for cut in cuts], sums


def place_kernel(*refs, starts, count, groups):
    pieces = refs[: count * groups]
    dense = refs[count * groups : count * groups + count + 1]
    rest = refs[count * (groups + 1) + 1 :]
    token_ref, bias_ref, own_ref = rest[:3]
    terms, out_ref, acc = rest[3:-2], rest[-2], rest[-1]
    acc[...] = token_ref[...].astype(WIDE) + bias_ref[...] + own_ref[...].astype(WIDE)
    for start, term in zip(starts, terms):
        acc[start : start + term.shape[0]] += term[...].astype(WIDE)
    steps = pl.num_programs(0)
    low_half = pl.program_id(0) * 2 < steps
    far = jnp.where(low_half, dense[count - 1][...], dense[count][...])
    total = acc[...]
    for rank in range(count):
        weight = dense[rank][...] if rank < count - 1 else far
        mine = [piece[...] for piece in pieces[rank * groups : (rank + 1) * groups]]
        total += dot(jnp.concatenate(mine, axis=1), weight, NT)
    out_ref[...] = total.astype(LOW)


def place_output(pieces, dense_pieces, tokens, bias, own, terms, count, groups):
    rows, width = tokens.shape
    cols = 512
    half = width // cols // 2
    whole = lambda a: pl.BlockSpec(a.shape, lambda i: (0, 0), pipeline_mode=pl.Buffered(1))
    in_specs = [whole(piece) for piece in pieces]
    depth = dense_pieces[0].shape[1]
    in_specs += [pl.BlockSpec((cols, depth), lambda i: (i, 0)) for _ in range(count - 1)]
    in_specs.append(pl.BlockSpec((cols, depth), lambda i: (jnp.minimum(i, half - 1), 0)))
    in_specs.append(pl.BlockSpec((cols, depth), lambda i: (jnp.maximum(i - half, 0), 0)))
    by_column = lambda n: pl.BlockSpec((n, cols), lambda i: (0, i))
    in_specs += [by_column(rows), by_column(1), by_column(rows)]
    in_specs += [by_column(term.shape[0]) for _, term in terms]
    return pl.pallas_call(
        functools.partial(
            place_kernel, starts=tuple(start for start, _ in terms), count=count, groups=groups
        ),
        out_shape=jax.ShapeDtypeStruct((rows, width), LOW),
        grid=(width // cols,),
        in_specs=in_specs,
        out_specs=by_column(rows),
        scratch_shapes=[pltpu.VMEM((rows, cols), WIDE)],
        compiler_params=pltpu.CompilerParams(
            dimension_semantics=("arbitrary",), vmem_limit_bytes=58 << 20
        ),
        cost_estimate=LITTLE,
        name="place_output",
    )(*pieces, *dense_pieces, tokens, bias, own, *[term for _, term in terms])


def token_grad_kernel(token_ref, grad_ref, own_ref, gain_ref, *refs, starts, tile):
    terms, out_ref, total = refs[:-2], refs[-2], refs[-1]
    first = pl.program_id(0) * tile
    total[...] = own_ref[...].astype(WIDE)
    for start, term in zip(starts, terms):
        size = min(tile, term.shape[0])
        for at in range(0, term.shape[0], size):

            @pl.when(first == (start + at) // tile * tile)
            def _(start=start, term=term, at=at, size=size):
                to = (start + at) % tile
                total[to : to + size] += term[at : at + size].astype(WIDE)

    x = token_ref[...].astype(WIDE)
    centred = x - jnp.mean(x, axis=-1, keepdims=True)
    rstd = lax.rsqrt(jnp.mean(centred * centred, axis=-1, keepdims=True) + 1e-05)
    xhat = centred * rstd
    scaled = total[...] * gain_ref[...]
    mean = jnp.mean(scaled, axis=-1, keepdims=True)
    along = jnp.mean(scaled * xhat, axis=-1, keepdims=True)
    out_ref[...] = (grad_ref[...].astype(WIDE) + rstd * (scaled - mean - xhat * along)).astype(LOW)


def token_grad(tokens, grad, own, gain, terms, tile):
    rows, width = tokens.shape
    by_row = pl.BlockSpec((tile, width), lambda i: (i, 0))
    whole = lambda a: pl.BlockSpec(a.shape, lambda i: (0, 0), pipeline_mode=pl.Buffered(1))
    return pl.pallas_call(
        functools.partial(
            token_grad_kernel, starts=tuple(start for start, _ in terms), tile=tile
        ),
        out_shape=jax.ShapeDtypeStruct((rows, width), LOW),
        grid=(rows // tile,),
        in_specs=[by_row, by_row, by_row, pl.BlockSpec((1, width), lambda i: (0, 0))]
        + [whole(term) for _, term in terms],
        out_specs=by_row,
        scratch_shapes=[pltpu.VMEM((tile, width), WIDE)],
        compiler_params=pltpu.CompilerParams(
            dimension_semantics=("arbitrary",), vmem_limit_bytes=48 << 20
        ),
        cost_estimate=LITTLE,
        name="token_grad",
    )(tokens, grad, own, gain[None], *[term for _, term in terms])


def pair_grad_kernel(x_ref, y_ref, a_ref, b_ref, out_ref):
    split = a_ref.shape[1]
    out_ref[:, :split] = dot(x_ref[...], a_ref[...], TN).astype(LOW)
    out_ref[:, split:] = dot(y_ref[...], b_ref[...], TN).astype(LOW)


def pair_grad(x, y, a, b):
    rows, width = x.shape
    columns = a.shape[1] + b.shape[1]
    tile = 512
    keep = pl.Buffered(1)
    return pl.pallas_call(
        pair_grad_kernel,
        out_shape=jax.ShapeDtypeStruct((width, columns), LOW),
        grid=(width // tile,),
        in_specs=[
            pl.BlockSpec((rows, tile), lambda i: (0, i)),
            pl.BlockSpec((rows, tile), lambda i: (0, i)),
            pl.BlockSpec(a.shape, lambda i: (0, 0), pipeline_mode=keep),
            pl.BlockSpec(b.shape, lambda i: (0, 0), pipeline_mode=keep),
        ],
        out_specs=pl.BlockSpec((tile, columns), lambda i: (i, 0)),
        compiler_params=pltpu.CompilerParams(
            dimension_semantics=("arbitrary",), vmem_limit_bytes=58 << 20
        ),
        cost_estimate=LITTLE,
        name="pair_grad",
    )(x, y, a, b)


def rope_tables(rows):
    place = lax.broadcasted_iota(jnp.int32, (rows, LANES), 0)
    lane = lax.broadcasted_iota(jnp.int32, (rows, LANES), 1)
    pos = jnp.where(place < PROMPT, place, PROMPT + (place - PROMPT) % CLEN)
    half = ROT // 2
    freq = 10000.0 ** (-2.0 * jnp.arange(half, dtype=WIDE) / ROT)
    angle = pos.astype(WIDE) * jnp.tile(freq, LANES // half)[None, :]
    dim = lane % (LANES // 2)
    cosine, sine = jnp.cos(angle), jnp.sin(angle)
    return [
        jnp.where(dim < ROT, cosine, 1.0),
        jnp.where((dim >= half) & (dim < ROT), sine, 0.0),
        jnp.where(dim < half, -sine, 0.0),
    ]


def shards(
    tokens,
    cotangent,
    block_table,
    ln_gain,
    ln_bias,
    w_qkv,
    b_qkv,
    w_dense,
    b_dense,
    w_fc1,
    b_fc1,
    w_fc2,
    b_fc2,
):
    _, local_rows, width = tokens.shape
    head_dim = width // HEADS
    count = lax.axis_size("ctx")
    me = lax.axis_index("ctx")
    rows = local_rows * count
    local_blocks = local_rows // BLK
    each = w_dense.shape[0]
    hidden = w_fc2.shape[0]
    gain, shift = ln_gain.astype(WIDE), ln_bias.astype(WIDE)

    def of_rank(whole, rank):
        return whole[rank * local_rows : (rank + 1) * local_rows]

    order, _, _ = ring_of(count)
    places = [0] * count
    for n, device in enumerate(order):
        places[device] = n
    places = jnp.asarray(places, jnp.int32)
    ranks = jnp.asarray([rank_of(n, count) for n in range(count)], jnp.int32)
    slots = jnp.arange(rows // BLK, dtype=jnp.int32)
    offset = (places[slots // local_blocks] - places[me]) % count
    held_at = ranks[offset] * local_blocks + slots % local_blocks
    hit = block_table[0][None, :] == slots[:, None]
    where = jnp.sum(jnp.where(hit, held_at[None, :], 0), axis=1).astype(jnp.int32)

    own_tokens = tokens[0].astype(WIDE)
    own_grad = cotangent[0]
    average = jnp.mean(own_tokens, axis=-1, keepdims=True)
    centred = own_tokens - average
    rstd = lax.rsqrt(jnp.mean(centred * centred, axis=-1, keepdims=True) + 1e-05)
    xhat = centred * rstd
    normed_own = (xhat * gain + shift).astype(LOW)

    def gather_rows(shard):
        return lax.all_gather(shard, "fsdp", axis=0, tiled=True)

    def scatter_rows(whole):
        return lax.psum_scatter(whole, "fsdp", scatter_dimension=0, tiled=True)

    lanes = 2 * LANES if each % (2 * LANES) == 0 else LANES
    groups = each // lanes

    def by_group(values):
        cut = values.reshape(-1, 3, groups, lanes)
        return jnp.swapaxes(cut, 1, 2).reshape(-1, 3 * each)

    tabs = rope_tables(rows)
    own_grad_sum = jnp.sum(own_grad.astype(WIDE), axis=0)
    fc1_bias = lax.dynamic_slice_in_dim(b_fc1, me * hidden, hidden, 0).astype(WIDE)
    early = (where, own_grad_sum, fc1_bias, *tabs)
    normed_pieces = ring_pieces(normed_own, "ctx", gate=early)
    attention_shard = jnp.concatenate([by_group(w_qkv), w_dense.T], axis=1)
    fc1_weight = gather_rows(w_fc1)
    fc2_turned = gather_rows(after(w_fc2.T, *normed_pieces[1:-2]))
    attention_weight = gather_rows(after(attention_shard, *normed_pieces[-2:]))
    qkv_weight, dense_turned = attention_weight[:, : 3 * each], attention_weight[:, 3 * each :]

    qkv_bias = lax.dynamic_slice_in_dim(b_qkv.reshape(3, width), me * each, each, 1)
    activated, slope, normed = expand(normed_pieces, fc1_weight, fc1_bias)

    sent_grad = after(own_grad, *normed_pieces[-2:])
    grad_pieces = ring_pieces(sent_grad, "ctx", gate=(activated,))
    ff_part = dot(activated, fc2_turned, NT).astype(LOW)
    ff_terms, ff_hops = ring_reduce(lambda rank: of_rank(ff_part, rank), "ctx", chained=True)
    first, second, last = ff_hops[0], ff_hops[min(1, len(ff_hops) - 1)], ff_hops[-1]

    gated = [after(piece, ff_part) for piece in grad_pieces]
    expanded_grad, grads, fc1_bias_part = slope_grad(gated, fc2_turned, slope)
    d_fc2_part = dot(after(grads, expanded_grad, *first), activated, TN).astype(LOW)
    d_fc2 = scatter_rows(d_fc2_part)
    qkv = dot(after(normed, d_fc2_part), qkv_weight, NN)
    qkv = (qkv + by_group(qkv_bias)[0].astype(WIDE)).astype(LOW)
    attended_grad = dot(after(grads, qkv, *second), dense_turned, NN).astype(LOW)
    gated = after(normed, attended_grad)
    d_fc1_part = dot(gated, expanded_grad, TN).astype(LOW)
    d_fc1 = scatter_rows(d_fc1_part)


    attended, qkv_grads, qkv_sums, d_attention, swapped = [], [], [], [], []
    ordered = (d_fc1_part,)
    for which in range(groups):
        got, got_grads, got_sums = attention(
            after(qkv, *ordered), attended_grad, where, tabs, lanes, which, head_dim
        )
        if which == 0:
            dense_pieces = ring_pieces(after(dense_turned, *second), "ctx", gate=(got,))
        attended.append(got)
        qkv_grads.append(got_grads)
        qkv_sums.append(got_sums)
        if which < groups - 1:
            swapped.append(ring_exchange(lambda rank, got=got: of_rank(got, rank), "ctx"))
            gated = after(normed, d_fc2, *last, *dense_pieces[1:-2]) if which == 0 else normed
            d_part = pair_grad(gated, grads, got_grads, got)
            ordered = (d_part,)
            d_attention.append(scatter_rows(d_part))

    weights = [(attention_weight, which) for which in range(groups)] + [(fc1_weight, 0)]
    early_swaps = [piece for pieces in swapped for piece in pieces]
    turn = after(expanded_grad, d_fc1, *dense_pieces[-2:], *early_swaps, *attended)
    swapped.append(ring_exchange(lambda rank: of_rank(attended[-1], rank), "ctx"))
    half = local_rows // 2
    whole, far_cut, ahead_cut, behind_cut = [local_rows], [half, half], [half], [half]
    if count > 2:
        ahead_cut, behind_cut = [half, half], [half, half]
    cut_of = {0: whole, count - 2: ahead_cut, count - 3: behind_cut, count - 1: far_cut}

    def some_ranks(ranks, turn, cost=LITTLE):
        cuts = [cut_of.get(rank, whole) for rank in ranks]
        return input_grad(qkv_grads + [turn], weights, normed, ranks, local_rows, cuts, cost)

    far_part, far_sums = some_ranks([count - 1], turn)
    middle = list(range(count - 2, 0, -1))
    middle_sums, parts = 0.0, {count - 1: far_part[0]}
    turn = after(turn, *far_part[0], *swapped[-1])
    for n in range(0, len(middle), 2):
        some, some_sums = some_ranks(middle[n : n + 2], turn, MUCH)
        turn = after(turn, *[piece for pieces in some for piece in pieces])
        middle_sums = middle_sums + some_sums
        parts.update(zip(middle[n : n + 2], some))
    for rank, pieces in parts.items():
        if len(pieces) == 1:
            parts[rank] = pieces[0]

    grad_terms, hops = ring_reduce(lambda rank: parts[rank], "ctx")
    last_hops = [piece for hop in hops[1:3] for piece in hop]
    gated = after(normed, turn, *hops[0], *d_attention)
    d_part = pair_grad(gated, grads, qkv_grads[-1], attended[-1])
    d_attention.append(scatter_rows(d_part))
    [own_part], own_sums = some_ranks([0], after(turn, d_part), MUCH)
    d_qkv = jnp.concatenate(
        [part[:, : 3 * lanes].reshape(-1, 3, lanes) for part in d_attention], axis=2
    ).astype(WIDE)
    d_dense = jnp.concatenate([part[:, 3 * lanes :].T for part in d_attention], axis=0)
    d_dense = d_dense.astype(WIDE)

    qkv_bias_part = jnp.concatenate(
        [part.reshape(3, lanes) for part in qkv_sums], axis=1
    )
    qkv_bias_wide = lax.dynamic_update_slice_in_dim(
        jnp.zeros((3, width), WIDE), qkv_bias_part, me * each, 1
    ).reshape(-1)
    fc1_bias_wide = lax.dynamic_update_slice_in_dim(
        jnp.zeros((b_fc1.shape[0],), WIDE), fc1_bias_part, me * hidden, 0
    )
    small = jnp.concatenate(
        [
            (far_sums + middle_sums + own_sums).reshape(-1),
            qkv_bias_wide,
            own_grad_sum,
            fc1_bias_wide,
        ]
    )
    doubled = [2**n for n in range(1, 30)]
    steps = exchange_steps("fsdp", [1]) + exchange_steps("ctx", [1] + doubled)
    for span in doubled:
        steps += exchange_steps("fsdp", [span])
    small = exchange(small, steps[0])
    output = place_output(
        [swapped[which][rank] for rank in range(count) for which in range(groups)],
        dense_pieces,
        after(tokens[0], *own_part),
        (b_dense.astype(WIDE) + b_fc2.astype(WIDE))[None],
        ff_part,
        ff_terms,
        count,
        groups,
    )
    small = exchange(after(small, output, *last_hops), steps[1])
    d_tokens = token_grad(
        after(tokens[0], output), own_grad, own_part[0], gain, grad_terms, local_rows // 4
    )
    d_fc1, d_fc2 = after(d_fc1, small).astype(WIDE), after(d_fc2, small).T.astype(WIDE)
    small = after(small, d_tokens)
    for step in steps[2:-1]:
        small = exchange(small, step)
    small = exchange(after(small, d_fc1, d_fc2), steps[-1], (d_qkv, d_dense))
    d_shift, with_normed, d_b_qkv, d_b_out, d_b_fc1 = jnp.split(
        small, [width, 2 * width, 5 * width, 6 * width]
    )
    d_gain = (with_normed - shift * d_shift) / gain
    return (
        output[None],
        d_tokens[None],
        d_gain,
        d_shift,
        d_qkv,
        d_b_qkv,
        d_dense,
        d_b_out,
        d_fc1,
        d_b_fc1,
        d_fc2,
        d_b_out,
    )


def solution(mesh):
    in_specs = (
        P("fsdp", "ctx", None),
        P("fsdp", "ctx", None),
        P("fsdp", None),
        P(),
        P(),
        P("fsdp", None, "ctx"),
        P(),
        P("ctx", "fsdp"),
        P(),
        P("fsdp", "ctx"),
        P(),
        P("ctx", "fsdp"),
        P(),
    )
    out_specs = (
        P("fsdp", "ctx", None),
        P("fsdp", "ctx", None),
        P(),
        P(),
        P("fsdp", None, "ctx"),
        P(),
        P("ctx", "fsdp"),
        P(),
        P("fsdp", "ctx"),
        P(),
        P("ctx", "fsdp"),
        P(),
    )
    return jax.shard_map(shards, mesh=mesh, in_specs=in_specs, out_specs=out_specs, check_vma=False)
```
